32 devices in a mesh: stream: 2 (over x), dp: 16 (over z, y, core).
Axes of the slice: x: 2, y: 2, z: 4, core: 2. Of those that a mesh axis runs over, the one named last changes fastest.
Arguments:
- inputs: bfloat16 [2, 6144, 768], P('stream', 'dp'), may hold values from -6 to 6
- lengths: int32 [2, 16, 2], P(None, 'dp'), may hold values from 64 to 256, as said below
- cotangent: bfloat16 [6144, 768], P('dp'), may hold values from -6 to 6
- attn_in: bfloat16 [2, 3, 768, 768], P('stream'), may hold values from -0.21875 to 0.21875
- attn_out: bfloat16 [2, 768, 768], P('stream'), may hold values from -0.875 to 0.875
- cross_first: bfloat16 [2, 768, 768], P('stream'), may hold values from -0.21875 to 0.21875
- cross_second: bfloat16 [2, 768, 768], P('stream'), may hold values from -0.875 to 0.875
- ffn_in: bfloat16 [2, 768, 3072], P('stream'), may hold values from -0.21875 to 0.21875
- ffn_out: bfloat16 [2, 3072, 768], P('stream'), may hold values from -0.109375 to 0.109375
- gains: bfloat16 [5, 768], replicated, may hold values from 0.5 to 1.5
- biases: bfloat16 [24, 768], replicated, may hold values from -1.25 to 1.25
Outputs:
- layer_out: bfloat16 [2, 6144, 768], P('stream', 'dp')
- grad_inputs: float32 [2, 6144, 768], P('stream', 'dp')
- grad_attn_in: float32 [2, 3, 768, 768], P('stream', None, 'dp')
- grad_attn_out: float32 [2, 768, 768], P('stream', 'dp')
- grad_cross_first: float32 [2, 768, 768], P('stream', 'dp')
- grad_cross_second: float32 [2, 768, 768], P('stream', 'dp')
- grad_ffn_in: float32 [2, 768, 3072], P('stream', 'dp')
- grad_ffn_out: float32 [2, 3072, 768], P('stream', 'dp')
- grad_gains: float32 [5, 768], P(None, 'dp')
- grad_biases: float32 [24, 768], P(None, 'dp')
The draws below stay inside these ranges and needn't reach their ends.
Inputs may be any that keep to these rules, and one draw needn't show every extreme that they name: lengths[s, i, 0] lies between 64 and 128, lengths[s, i, 1] between 129 and 256; some pair group has full-length sequences in both buckets on both sides.
All inputs are finite; a program needn't handle non-finite values.
Results may differ from the reference program's by a relative error of at most 0.025.
Values may be sent and summed in bfloat16 or wider, within the bound.
A program may use at most 384 MiB of HBM per device.

```python
import jax
import jax.numpy as jnp
from jax import lax

D = 768
HDIM = 64
FF = 3072
SHORT = 128
LONG = 256
ROWS_ALL = 6144
N_DP = 16


def draw_lengths(key, part):
    short_key, long_key = jax.random.split(jax.random.fold_in(key, 11))
    short_len = jax.random.randint(short_key, (2, N_DP), SHORT // 2, SHORT + 1)
    long_len = jax.random.randint(long_key, (2, N_DP), SHORT + 1, LONG + 1)
    short_len = short_len.at[:, 0].set(SHORT)
    long_len = long_len.at[:, 0].set(LONG)
    return jnp.stack([short_len, long_len], axis=-1).astype(jnp.int32)


def steps_of(own_key, extent, pieces, least, largest):
    loudness = 1.0
    for dim, blocks in pieces:
        steps = jax.random.uniform(jax.random.fold_in(jax.random.fold_in(own_key, 6), dim), (blocks,), jnp.float32, least / len(pieces), largest / len(pieces))
        loudness = loudness * jnp.repeat(jnp.exp(steps), extent[dim] // blocks).reshape((-1,) + (1,) * (len(extent) - 1 - dim))
    return loudness


def gaussian(rng, extent, width, bound, cuts=(), held_as=jnp.bfloat16):
    array = width * jax.random.normal(rng, extent, jnp.float32)
    if cuts:
        array = array * steps_of(rng, extent, cuts, -0.22, 0.18)
    return jnp.clip(array, -bound, bound).astype(held_as)


def setup_inputs(seed: int = 0) -> dict:
    seeds = jax.random.split(jax.random.key(seed), 12)
    return {
        "inputs": gaussian(seeds[0], (2, ROWS_ALL, D), 1.0, 6.0, ((0, 2), (1, 16))),
        "lengths": draw_lengths(jax.random.fold_in(seeds[11], 71), 0),
        "cotangent": gaussian(seeds[2], (ROWS_ALL, D), 1.0, 6.0, ((0, 16),)),
        "attn_in": gaussian(seeds[3], (2, 3, D, D), D ** -0.5, 0.21875, ((0, 2),)),
        "attn_out": gaussian(seeds[4], (2, D, D), (D // 16) ** -0.5, 0.875, ((0, 2),)),
        "cross_first": gaussian(seeds[5], (2, D, D), D ** -0.5, 0.21875, ((0, 2),)),
        "cross_second": gaussian(seeds[6], (2, D, D), (D // 16) ** -0.5, 0.875, ((0, 2),)),
        "ffn_in": gaussian(seeds[7], (2, D, FF), D ** -0.5, 0.21875, ((0, 2),)),
        "ffn_out": gaussian(seeds[8], (2, FF, D), FF ** -0.5, 0.109375, ((0, 2),)),
        "gains": jnp.clip(1.0 + 0.1 * jax.random.normal(seeds[9], (5, D), jnp.float32), 0.5, 1.5).astype(jnp.bfloat16),
        "biases": gaussian(seeds[10], (24, D), 0.2, 1.25),
    }


@jax.custom_vjp
def low(v):
    return lax.optimization_barrier(v.astype(jnp.bfloat16)).astype(jnp.float32)

@jax.custom_vjp
def low_back(v):
    return v

def low_keep(v):
    return (low(v), None)

def low_pass(kept, grad):
    return (grad,)

def back_keep(v):
    return (v, None)

def back_low(kept, grad):
    return (low(grad),)
low.defvjp(low_keep, low_pass)
low_back.defvjp(back_keep, back_low)
eps_norm = 1e-05

def hi_dot(left_mat, right_mat):
    return jnp.dot(left_mat, right_mat, precision=lax.Precision.HIGHEST)

def norm_rows(tensor, norm_gain, norm_shift):
    centre = tensor - lax.optimization_barrier(jnp.mean(tensor, axis=-1, keepdims=True))
    spread = lax.optimization_barrier(jnp.mean(centre * centre, axis=-1, keepdims=True))
    return centre * lax.rsqrt(spread + eps_norm) * norm_gain + norm_shift

def key_mask(row_count, key_count, length, causal):
    columns = lax.broadcasted_iota(jnp.int32, (row_count, key_count), 1)
    allowed = columns < length
    if causal:
        allowed = allowed & (columns <= lax.broadcasted_iota(jnp.int32, (row_count, key_count), 0))
    return allowed

def attend(queries, key_rows, values, allowed):
    heads_q = queries.reshape(queries.shape[0], -1, HDIM)
    heads_k = key_rows.reshape(key_rows.shape[0], -1, HDIM)
    heads_v = values.reshape(values.shape[0], -1, HDIM)
    scores = low_back(jnp.einsum('qhd,khd->hqk', heads_q, heads_k, precision=lax.Precision.HIGHEST) * HDIM ** (-0.5))
    scores = jnp.where(allowed[None], scores, -1e+30)
    softmaxed = low(jax.nn.softmax(scores, axis=-1))
    attended = jnp.einsum('hqk,khd->qhd', softmaxed, heads_v, precision=lax.Precision.HIGHEST)
    return attended.reshape(queries.shape[0], -1)

def self_block(row_block, length, causal, w_proj, w_out, vectors):
    bias_q, bias_v, bias_o, norm_gain, norm_shift = vectors
    low_rows = low(row_block)
    queries = low(low_back(hi_dot(low_rows, w_proj[0]) + bias_q))
    key_rows = low(low_back(hi_dot(low_rows, w_proj[1])))
    values = low(low_back(hi_dot(low_rows, w_proj[2]) + bias_v))
    allowed = key_mask(row_block.shape[0], row_block.shape[0], length, causal)
    attended = low(low_back(attend(queries, key_rows, values, allowed)))
    branch = low_back(hi_dot(attended, w_out) + bias_o)
    return norm_rows(row_block + branch, norm_gain, norm_shift)

def ffn_block(hidden, w_in, w_out, vectors):
    bias_in, bias_out, norm_gain, norm_shift = vectors
    inner_act = low_back(hi_dot(low(hidden), w_in) + bias_in)
    active = low(jax.nn.gelu(inner_act, approximate=False))
    branch = low_back(hi_dot(active, w_out) + bias_out)
    return norm_rows(hidden + branch, norm_gain, norm_shift)

def cross_block(hidden, key_rows, values, src_len, w_query, w_out, vectors):
    bias_q, bias_v, bias_o, norm_gain, norm_shift = vectors
    queries = low(low_back(hi_dot(low(hidden), w_query) + bias_q))
    allowed = key_mask(hidden.shape[0], key_rows.shape[0], src_len, False)
    attended = low(low_back(attend(queries, key_rows, values, allowed) + bias_v))
    branch = low_back(hi_dot(attended, w_out) + bias_o)
    return norm_rows(hidden + branch, norm_gain, norm_shift)

def pair_layers(params, source, target, src_len, tgt_len):
    attn_in, attn_out, cross_first, cross_second, ffn_in, ffn_out, gains, biases = params
    enc_self = (biases[0], biases[1], biases[2], gains[0], biases[3])
    enc_ffn = (biases[4:8].reshape(-1), biases[8], gains[1], biases[9])
    dec_self = (biases[10], biases[11], biases[12], gains[2], biases[13])
    dec_cross = (biases[14], biases[15], biases[16], gains[3], biases[17])
    dec_ffn = (biases[18:22].reshape(-1), biases[22], gains[4], biases[23])
    h_one = self_block(source, src_len, False, attn_in[0], attn_out[0], enc_self)
    memory = ffn_block(h_one, ffn_in[0], ffn_out[0], enc_ffn)
    low_memory = low(memory)
    key_rows = low(low_back(hi_dot(low_memory, cross_first[0])))
    values = low(low_back(hi_dot(low_memory, cross_second[0])))
    d_one = self_block(target, tgt_len, True, attn_in[1], attn_out[1], dec_self)
    d_two = cross_block(d_one, key_rows, values, src_len, cross_first[1], cross_second[1], dec_cross)
    decoded = ffn_block(d_two, ffn_in[1], ffn_out[1], dec_ffn)
    return (memory, decoded)

def reference(inputs, lengths, cotangent, attn_in, attn_out, cross_first, cross_second, ffn_in, ffn_out, gains, biases):
    params = tuple((weight.astype(jnp.float32) for weight in (attn_in, attn_out, cross_first, cross_second, ffn_in, ffn_out, gains, biases)))
    model_width = inputs.shape[-1]
    device_rows = SHORT + LONG
    streams = inputs.astype(jnp.float32).reshape(2, N_DP, device_rows, model_width)

    def forward(params, streams):

        def run_bucket(sources, targets, src_lens, tgt_lens):

            def one_pair(carry_in, entry_now):
                return (carry_in, jax.checkpoint(pair_layers)(params, entry_now[0], entry_now[1], entry_now[2], entry_now[3]))
            unused, bucket_out = lax.scan(one_pair, jnp.zeros((), jnp.float32), (sources, targets, src_lens, tgt_lens))
            return bucket_out
        short_out = run_bucket(streams[0, :, :SHORT], streams[1, :, :SHORT], lengths[0, :, 0], lengths[1, :, 0])
        long_out = run_bucket(streams[0, :, SHORT:], streams[1, :, SHORT:], lengths[0, :, 1], lengths[1, :, 1])
        memory = jnp.concatenate([short_out[0], long_out[0]], axis=1)
        decoded = jnp.concatenate([short_out[1], long_out[1]], axis=1)
        return (memory, decoded)
    (memory, decoded), pullback = jax.vjp(forward, params, streams)
    grad_params, grad_streams = pullback((jnp.zeros_like(memory), cotangent.astype(jnp.float32).reshape(N_DP, device_rows, model_width)))
    layer_out = jnp.stack([memory, decoded]).reshape(2, N_DP * device_rows, model_width).astype(jnp.bfloat16)
    grad_inputs = grad_streams.reshape(2, N_DP * device_rows, model_width)
    return (layer_out, grad_inputs, grad_params[0], grad_params[1], grad_params[2], grad_params[3], grad_params[4], grad_params[5], grad_params[6], grad_params[7])
```

```python
import functools

import jax
import jax.numpy as jnp
from jax import lax
from jax.experimental import pallas as pl
from jax.experimental.pallas import tpu as pltpu
from jax.sharding import PartitionSpec as P

HDIM = 64
SHORT = 128
LONG = 256
MESH = pl.DeviceIdType.MESH
bf16, f32 = jnp.bfloat16, jnp.float32
PIECE = 48


def rs_kernel(nz, chunks, g_ref, vec_ref, *refs):
    out_refs = refs[:7]
    (keep, crecv, yrecv, zrecv, vbuf, vzbuf,
     keep_sem, csend, crecv_sem, ysend, yrecv_sem, zsend, zrecv_sem,
     vsend, vrecv_sem, vzsend, vzrecv_sem) = refs[7:]
    me = lax.axis_index("dp")
    st = lax.axis_index("stream")
    z, y, c = me // 4, (me // 2) % 2, me % 2
    core_id = {"dp": z * 4 + y * 2 + (1 - c)}
    y_id = {"dp": z * 4 + (1 - y) * 2 + c}
    x_id = {"stream": 1 - st}

    def z_id(dz):
        return {"dp": lax.rem(z + dz, nz) * 4 + y * 2 + c}

    barrier = pltpu.get_barrier_semaphore()
    peers = [core_id, y_id, x_id] + [z_id(d) for d in range(1, nz)]
    for p in peers:
        pl.semaphore_signal(barrier, inc=1, device_id=p, device_id_type=MESH)
    pl.semaphore_wait(barrier, len(peers))

    def rcopy(src, dst, ss, rs, dev):
        return pltpu.make_async_remote_copy(src_ref=src, dst_ref=dst, send_sem=ss, recv_sem=rs,
                                            device_id=dev, device_id_type=MESH)
    n = len(chunks)
    starts = [sum(chunks[:i]) for i in range(n)]
    rows = [pl.ds(starts[i] * PIECE, chunks[i] * PIECE) for i in range(n)]
    ccopy = [rcopy(g_ref.at[:, :, 1 - c, rows[i]], crecv.at[:, :, rows[i]], csend.at[i], crecv_sem.at[i], core_id) for i in range(n)]
    kcopy = [pltpu.make_async_copy(g_ref.at[:, :, c, rows[i]], keep.at[:, :, rows[i]], keep_sem.at[i]) for i in range(n)]
    ycopy = [rcopy(crecv.at[:, 1 - y, rows[i]], yrecv.at[:, rows[i]], ysend.at[i], yrecv_sem.at[i], y_id) for i in range(n)]
    zcopy = [[rcopy(yrecv.at[lax.rem(z + d, nz), rows[i]], zrecv.at[d - 1, rows[i]], zsend.at[i, d - 1], zrecv_sem.at[i, d - 1], z_id(d))
              for d in range(1, nz)] for i in range(n)]
    vcopy = [rcopy(vbuf.at[0], vbuf.at[1], vsend.at[0], vrecv_sem.at[0], core_id),
             rcopy(vbuf.at[2], vbuf.at[3], vsend.at[1], vrecv_sem.at[1], y_id)]
    vz = [rcopy(vbuf.at[4], vzbuf.at[d - 1], vzsend.at[d - 1], vzrecv_sem.at[d - 1], z_id(d)) for d in range(1, nz)]
    vx = rcopy(vbuf.at[5], vbuf.at[6], vsend.at[2], vrecv_sem.at[2], x_id)
    vbuf[0] = vec_ref[...]
    vcopy[0].start()
    for i in range(n):
        ccopy[i].start()
        kcopy[i].start()

    def c_add(i):
        ccopy[i].wait()
        kcopy[i].wait()
        for p in range(starts[i], starts[i] + chunks[i]):
            def bodyf(j, carry):
                zz, yy = j // 2, j % 2
                sl = pl.ds(p * PIECE, PIECE)
                crecv[zz, yy, sl] = (crecv[zz, yy, sl].astype(f32) + keep[zz, yy, sl].astype(f32)).astype(bf16)
                return carry
            lax.fori_loop(0, nz * 2, bodyf, 0)
        ycopy[i].start()

    def y_add(i):
        ycopy[i].wait()
        for p in range(starts[i], starts[i] + chunks[i]):
            def bodyf(zz, carry):
                sl = pl.ds(p * PIECE, PIECE)
                yrecv[zz, sl] = (yrecv[zz, sl].astype(f32) + crecv[zz, y, sl].astype(f32)).astype(bf16)
                return carry
            lax.fori_loop(0, nz, bodyf, 0)
        for d in range(1, nz):
            zcopy[i][d - 1].start()

    def z_add(i):
        for d in range(1, nz):
            zcopy[i][d - 1].wait()
        for p in range(starts[i], starts[i] + chunks[i]):
            sl = pl.ds(p * PIECE, PIECE)
            tot = yrecv[z, sl].astype(f32)
            for d in range(1, nz):
                tot = tot + zrecv[d - 1, sl].astype(f32)
            if p < 4:
                out_refs[0][pl.ds(p * PIECE, PIECE)] = tot
            elif p < 8:
                out_refs[1][:, pl.ds((p - 4) * 768, 768)] = tot
            elif p < 11:
                out_refs[p - 6][...] = tot
            else:
                out_refs[5][p - 11] = tot

    for t in range(n + 2):
        if t < n:
            c_add(t)
        if 1 <= t <= n:
            y_add(t - 1)
        if t == 0:
            vcopy[0].wait()
            vbuf[2] = vbuf[0] + vbuf[1]
            vcopy[1].start()
        if t == 1:
            vcopy[1].wait()
            vbuf[4] = vbuf[2] + vbuf[3]
            for cp in vz:
                cp.start()
        if t == 2:
            for cp in vz:
                cp.wait()
            tot = vbuf[4]
            for d in range(1, nz):
                tot = tot + vzbuf[d - 1]
            vbuf[5] = tot
            vx.start()
        if t >= 2:
            z_add(t - 2)
    vx.wait()
    out_refs[6][...] = vbuf[5] + vbuf[6]


def reduce_scatter(nz, g, vec, chunks=(2,) * 7):
    n = len(chunks)
    r = g.shape[3]
    w = g.shape[4]
    shapes = [(192, w), (48, 4 * w), (48, w), (48, w), (48, w), (3, 48, w), vec.shape]
    return pl.pallas_call(
        functools.partial(rs_kernel, nz, chunks),
        out_shape=[jax.ShapeDtypeStruct(s, f32) for s in shapes],
        in_specs=[pl.BlockSpec(memory_space=pl.ANY), pl.BlockSpec(memory_space=pltpu.VMEM)],
        out_specs=[pl.BlockSpec(memory_space=pltpu.VMEM)] * 7,
        scratch_shapes=[
            pltpu.VMEM((nz, 2, r, w), bf16), pltpu.VMEM((nz, 2, r, w), bf16),
            pltpu.VMEM((nz, r, w), bf16), pltpu.VMEM((nz - 1, r, w), bf16),
            pltpu.VMEM((7,) + vec.shape, f32), pltpu.VMEM((nz - 1,) + vec.shape, f32),
            pltpu.SemaphoreType.DMA((n,)), pltpu.SemaphoreType.DMA((n,)), pltpu.SemaphoreType.DMA((n,)),
            pltpu.SemaphoreType.DMA((n,)), pltpu.SemaphoreType.DMA((n,)),
            pltpu.SemaphoreType.DMA((n, nz - 1)), pltpu.SemaphoreType.DMA((n, nz - 1)),
            pltpu.SemaphoreType.DMA((3,)), pltpu.SemaphoreType.DMA((3,)),
            pltpu.SemaphoreType.DMA((nz - 1,)), pltpu.SemaphoreType.DMA((nz - 1,)),
        ],
        compiler_params=pltpu.CompilerParams(collective_id=0, has_side_effects=True, vmem_limit_bytes=56 << 20),
    )(g, vec)


eps_norm = 1e-05
low_type = jnp.bfloat16
wide_type = jnp.float32


def as_sent(shard):
    return jax.tree.map(lambda a: a.astype(jnp.bfloat16) if a.dtype == jnp.float32 else a, shard)


def shifted(shard, axis, by):
    count = lax.axis_size(axis)
    pairs = [(i, i + by) for i in range(count) if 0 <= i + by < count]
    return lax.ppermute(shard, axis, pairs)


def matmul(left_mat, right_mat):
    return jnp.dot(left_mat, right_mat, preferred_element_type=wide_type)


def matmul_tn(left_mat, right_mat):
    return lax.dot_general(
        left_mat, right_mat, (((0,), (0,)), ((), ())), preferred_element_type=wide_type
    )


def matmul_nt(left_mat, right_mat):
    return lax.dot_general(
        left_mat, right_mat, (((1,), (1,)), ((), ())), preferred_element_type=wide_type
    )


def column_sum(tensor):
    return jnp.sum(tensor.astype(wide_type), axis=0)


def norm_rows(tensor, norm_gain, norm_shift):
    centre = tensor - jnp.mean(tensor, axis=-1, keepdims=True)
    spread = jnp.mean(centre * centre, axis=-1, keepdims=True)
    return centre * lax.rsqrt(spread + eps_norm) * norm_gain + norm_shift


def norm_back(tensor, norm_gain, norm_shift, upstream):
    unused, pullback = jax.vjp(norm_rows, tensor, norm_gain, norm_shift)
    return pullback(upstream)


def gelu_exact(tensor):
    return jax.nn.gelu(tensor, approximate=False)


def key_mask(row_count, key_count, length, causal):
    columns = lax.broadcasted_iota(jnp.int32, (row_count, key_count), 1)
    allowed = columns < length
    if causal:
        allowed = allowed & (columns <= lax.broadcasted_iota(jnp.int32, (row_count, key_count), 0))
    return allowed


def split_heads(tensor):
    return tensor.reshape(tensor.shape[0], -1, HDIM)


def attend_scores(queries, key_rows, allowed):
    scores = jnp.einsum(
        "qhd,khd->hqk",
        split_heads(queries),
        split_heads(key_rows),
        preferred_element_type=wide_type,
    )
    return jnp.where(allowed[None], scores * HDIM ** (-0.5), -1e30)


def attend_forward(queries, key_rows, values, allowed):
    scores = attend_scores(queries, key_rows, allowed)
    row_max = jnp.max(scores, axis=-1, keepdims=True)
    log_total = row_max + jnp.log(jnp.sum(jnp.exp(scores - row_max), axis=-1, keepdims=True))
    softmaxed = jnp.exp(scores - log_total).astype(low_type)
    attended = jnp.einsum(
        "hqk,khd->qhd", softmaxed, split_heads(values), preferred_element_type=wide_type
    )
    return (attended.reshape(queries.shape[0], -1), log_total)


def attend_backward(queries, key_rows, values, allowed, log_total, upstream):
    softmaxed = jnp.exp(attend_scores(queries, key_rows, allowed) - log_total)
    grad_heads = split_heads(upstream)
    grad_values = jnp.einsum(
        "hqk,qhd->khd", softmaxed.astype(low_type), grad_heads, preferred_element_type=wide_type
    )
    grad_probs = jnp.einsum(
        "qhd,khd->hqk", grad_heads, split_heads(values), preferred_element_type=wide_type
    )
    grad_scores = (
        softmaxed * (grad_probs - jnp.sum(softmaxed * grad_probs, axis=-1, keepdims=True))
    ).astype(low_type)
    scale_factor = HDIM ** (-0.5)
    grad_queries = (
        jnp.einsum(
            "hqk,khd->qhd", grad_scores, split_heads(key_rows), preferred_element_type=wide_type
        )
        * scale_factor
    )
    grad_keys = (
        jnp.einsum(
            "hqk,qhd->khd", grad_scores, split_heads(queries), preferred_element_type=wide_type
        )
        * scale_factor
    )
    key_count = key_rows.shape[0]
    return (
        grad_queries.reshape(queries.shape[0], -1),
        grad_keys.reshape(key_count, -1),
        grad_values.reshape(key_count, -1),
    )


def self_forward(row_block, length, causal, w_proj, w_out, vectors):
    bias_q, bias_v, bias_o, norm_gain, norm_shift = vectors
    row_count = row_block.shape[0]
    offsets = jnp.stack([bias_q, jnp.zeros_like(bias_q), bias_v])[:, None, :]
    projected = (
        jnp.einsum("rd,cde->cre", row_block, w_proj, preferred_element_type=wide_type) + offsets
    ).astype(low_type)
    allowed = key_mask(row_count, row_count, length, causal)
    attended, log_total = attend_forward(projected[0], projected[1], projected[2], allowed)
    attended = attended.astype(low_type)
    summed = row_block.astype(wide_type) + matmul(attended, w_out) + bias_o
    return (norm_rows(summed, norm_gain, norm_shift), (projected, log_total, attended, summed))


def self_backward(row_block, length, causal, w_proj, w_out, vectors, saved_fwd, upstream):
    projected, log_total, attended, summed = saved_fwd
    row_count = row_block.shape[0]
    grad_sum, grad_gain, grad_shift = norm_back(summed, vectors[3], vectors[4], upstream)
    grad_branch = grad_sum.astype(low_type)
    grad_attended = matmul_nt(grad_branch, w_out).astype(low_type)
    allowed = key_mask(row_count, row_count, length, causal)
    grad_q, grad_k, grad_v = attend_backward(
        projected[0], projected[1], projected[2], allowed, log_total, grad_attended
    )
    grad_proj = jnp.stack([grad_q, grad_k, grad_v]).astype(low_type)
    grad_rows = grad_sum + jnp.einsum(
        "cre,cde->rd", grad_proj, w_proj, preferred_element_type=wide_type
    )
    weight_grads = (
        jnp.einsum("rd,cre->cde", row_block, grad_proj, preferred_element_type=wide_type),
        matmul_tn(attended, grad_branch),
    )
    vector_grads = (
        column_sum(grad_proj[0]),
        column_sum(grad_proj[2]),
        column_sum(grad_branch),
        grad_gain,
        grad_shift,
    )
    return (grad_rows, weight_grads, vector_grads)


def ffn_forward(hidden, w_in, w_out, vectors):
    bias_in, bias_out, norm_gain, norm_shift = vectors
    low_hidden = hidden.astype(low_type)
    inner_act = matmul(low_hidden, w_in) + bias_in
    active = gelu_exact(inner_act).astype(low_type)
    summed = hidden + matmul(active, w_out) + bias_out
    return (norm_rows(summed, norm_gain, norm_shift), (low_hidden, inner_act, active, summed))


def ffn_backward(w_in, w_out, vectors, saved_fwd, upstream):
    low_hidden, inner_act, active, summed = saved_fwd
    grad_sum, grad_gain, grad_shift = norm_back(summed, vectors[2], vectors[3], upstream)
    grad_branch = grad_sum.astype(low_type)
    unused, pullback = jax.vjp(gelu_exact, inner_act)
    grad_inner = pullback(matmul_nt(grad_branch, w_out))[0].astype(low_type)
    grad_hidden = grad_sum + matmul_nt(grad_inner, w_in)
    weight_grads = (matmul_tn(low_hidden, grad_inner), matmul_tn(active, grad_branch))
    vector_grads = (column_sum(grad_inner), column_sum(grad_branch), grad_gain, grad_shift)
    return (grad_hidden, weight_grads, vector_grads)


def cross_forward(hidden, memory, src_len, w_query, w_out, vectors):
    bias_q, bias_v, bias_o, norm_gain, norm_shift = vectors
    low_hidden = hidden.astype(low_type)
    queries = (matmul(low_hidden, w_query) + bias_q).astype(low_type)
    allowed = key_mask(hidden.shape[0], memory.shape[1], src_len, False)
    attended, log_total = attend_forward(queries, memory[0], memory[1], allowed)
    attended = (attended + bias_v).astype(low_type)
    summed = hidden + matmul(attended, w_out) + bias_o
    return (
        norm_rows(summed, norm_gain, norm_shift),
        (low_hidden, queries, log_total, attended, summed),
    )


def cross_backward(memory, src_len, w_query, w_out, vectors, saved_fwd, upstream):
    low_hidden, queries, log_total, attended, summed = saved_fwd
    grad_sum, grad_gain, grad_shift = norm_back(summed, vectors[3], vectors[4], upstream)
    grad_branch = grad_sum.astype(low_type)
    grad_attended = matmul_nt(grad_branch, w_out).astype(low_type)
    allowed = key_mask(queries.shape[0], memory.shape[1], src_len, False)
    grad_q, grad_k, grad_v = attend_backward(
        queries, memory[0], memory[1], allowed, log_total, grad_attended
    )
    grad_query = grad_q.astype(low_type)
    grad_memory = jnp.stack([grad_k, grad_v]).astype(low_type)
    grad_hidden = grad_sum + matmul_nt(grad_query, w_query)
    weight_grads = (matmul_tn(low_hidden, grad_query), matmul_tn(attended, grad_branch))
    vector_grads = (
        column_sum(grad_query),
        column_sum(grad_attended),
        column_sum(grad_branch),
        grad_gain,
        grad_shift,
    )
    return (grad_hidden, grad_memory, weight_grads, vector_grads)


def self_vectors(gain_rows, bias_rows, decoder):
    base_row = 10 if decoder else 0
    gain_row = 2 if decoder else 0
    return (
        bias_rows[base_row],
        bias_rows[base_row + 1],
        bias_rows[base_row + 2],
        gain_rows[gain_row],
        bias_rows[base_row + 3],
    )


def ffn_vectors(gain_rows, bias_rows, decoder):
    base_row = 18 if decoder else 4
    gain_row = 4 if decoder else 1
    return (
        bias_rows[base_row : base_row + 4].reshape(-1),
        bias_rows[base_row + 4],
        gain_rows[gain_row],
        bias_rows[base_row + 5],
    )


def cross_vectors(gain_rows, bias_rows):
    return (bias_rows[14], bias_rows[15], bias_rows[16], gain_rows[3], bias_rows[17])


def self_plan(decoder, vector_grads):
    base_row = 10 if decoder else 0
    gain_row = 2 if decoder else 0
    return (
        ("biases", base_row, vector_grads[0]),
        ("biases", base_row + 1, vector_grads[1]),
        ("biases", base_row + 2, vector_grads[2]),
        ("gains", gain_row, vector_grads[3]),
        ("biases", base_row + 3, vector_grads[4]),
    )


def ffn_plan(decoder, vector_grads):
    base_row = 18 if decoder else 4
    gain_row = 4 if decoder else 1
    return (
        ("biases", base_row, vector_grads[0]),
        ("biases", base_row + 4, vector_grads[1]),
        ("gains", gain_row, vector_grads[2]),
        ("biases", base_row + 5, vector_grads[3]),
    )


def cross_plan(vector_grads):
    return (
        ("biases", 14, vector_grads[0]),
        ("biases", 15, vector_grads[1]),
        ("biases", 16, vector_grads[2]),
        ("gains", 3, vector_grads[3]),
        ("biases", 17, vector_grads[4]),
    )


def accumulate(totals, weight_names, weight_grads, vector_plan):
    merged = dict(totals)
    for key_name, tensor in zip(weight_names, weight_grads):
        merged[key_name] = merged[key_name] + tensor
    for table_name, row_at, tensor in vector_plan:
        table_now = merged[table_name]
        row_block = tensor.reshape(-1, table_now.shape[1])
        merged[table_name] = table_now.at[row_at : row_at + row_block.shape[0]].add(row_block)
    return merged


def updated(progress, key_name, position, tensor):
    copied = dict(progress)
    copied[key_name] = [
        tensor if slot_index == position else entry_now
        for slot_index, entry_now in enumerate(progress[key_name])
    ]
    return copied


def with_totals(progress, totals):
    copied = dict(progress)
    copied["totals"] = totals
    return copied


def forward_pass(tensor):
    return jax.tree.map(
        lambda part, own: part.astype(own.dtype), shifted(as_sent(tensor), "stream", 1), tensor
    )


def backward_pass(tensor):
    return jax.tree.map(
        lambda part, own: part.astype(own.dtype), shifted(as_sent(tensor), "stream", -1), tensor
    )


def keep_same(progress):
    return progress


def body(
    inputs,
    lengths,
    cotangent,
    attn_in,
    attn_out,
    cross_first,
    cross_second,
    ffn_in,
    ffn_out,
    gains,
    biases,
):
    own_rows = inputs[0]
    model_width = own_rows.shape[1]
    hidden_width = ffn_in.shape[2]
    head_count = model_width // HDIM
    row_sizes = (SHORT, LONG)
    bucket_spans = ((0, SHORT), (SHORT, SHORT + LONG))
    row_pieces = [own_rows[start_row:stop_row] for start_row, stop_row in bucket_spans]
    grad_pieces = [
        cotangent[start_row:stop_row].astype(wide_type) for start_row, stop_row in bucket_spans
    ]
    src_lens = [lengths[0, 0, bucket_idx] for bucket_idx in range(2)]
    tgt_lens = [lengths[1, 0, bucket_idx] for bucket_idx in range(2)]
    w_proj = attn_in[0]
    w_attn_out = attn_out[0]
    w_first = cross_first[0]
    w_second = cross_second[0]
    w_ffn_in = ffn_in[0]
    w_ffn_out = ffn_out[0]
    gain_rows = gains.astype(wide_type)
    bias_rows = biases.astype(wide_type)
    enc_self = self_vectors(gain_rows, bias_rows, False)
    enc_ffn = ffn_vectors(gain_rows, bias_rows, False)
    dec_self = self_vectors(gain_rows, bias_rows, True)
    dec_ffn = ffn_vectors(gain_rows, bias_rows, True)
    dec_cross = cross_vectors(gain_rows, bias_rows)
    is_decoder = lax.axis_index("stream") == 1

    def blank_self(size_rows):
        return (
            jnp.zeros((3, size_rows, model_width), low_type),
            jnp.zeros((head_count, size_rows, 1), wide_type),
            jnp.zeros((size_rows, model_width), low_type),
            jnp.zeros((size_rows, model_width), wide_type),
        )

    def blank_ffn(size_rows):
        return (
            jnp.zeros((size_rows, model_width), low_type),
            jnp.zeros((size_rows, hidden_width), wide_type),
            jnp.zeros((size_rows, hidden_width), low_type),
            jnp.zeros((size_rows, model_width), wide_type),
        )

    def blank_cross(size_rows):
        return (
            jnp.zeros((size_rows, model_width), low_type),
            jnp.zeros((size_rows, model_width), low_type),
            jnp.zeros((head_count, size_rows, 1), wide_type),
            jnp.zeros((size_rows, model_width), low_type),
            jnp.zeros((size_rows, model_width), wide_type),
        )

    progress = {
        "out": [jnp.zeros((size_rows, model_width), low_type) for size_rows in row_sizes],
        "grad_in": [jnp.zeros((size_rows, model_width), wide_type) for size_rows in row_sizes],
        "send": [jnp.zeros((2, size_rows, model_width), low_type) for size_rows in row_sizes],
        "memory": [jnp.zeros((2, size_rows, model_width), low_type) for size_rows in row_sizes],
        "grad_send": [jnp.zeros((2, size_rows, model_width), low_type) for size_rows in row_sizes],
        "grad_memory": [
            jnp.zeros((2, size_rows, model_width), low_type) for size_rows in row_sizes
        ],
        "mid": [jnp.zeros((size_rows, model_width), wide_type) for size_rows in row_sizes],
        "grad_mid": [jnp.zeros((size_rows, model_width), wide_type) for size_rows in row_sizes],
        "totals": {
            "proj": jnp.zeros(w_proj.shape, wide_type),
            "attn_out": jnp.zeros(w_attn_out.shape, wide_type),
            "first": jnp.zeros(w_first.shape, wide_type),
            "second": jnp.zeros(w_second.shape, wide_type),
            "ffn_in": jnp.zeros(w_ffn_in.shape, wide_type),
            "ffn_out": jnp.zeros(w_ffn_out.shape, wide_type),
            "gains": jnp.zeros(gains.shape, wide_type),
            "biases": jnp.zeros(biases.shape, wide_type),
        },
    }
    progress["self_saved"] = [blank_self(size_rows) for size_rows in row_sizes]
    progress["ffn_saved"] = [blank_ffn(size_rows) for size_rows in row_sizes]
    progress["cross_saved"] = [blank_cross(size_rows) for size_rows in row_sizes]

    def encoder_core(micro_idx):
        h_one, self_saved = self_forward(
            row_pieces[micro_idx], src_lens[micro_idx], False, w_proj, w_attn_out, enc_self
        )
        encoded, ffn_saved = ffn_forward(h_one, w_ffn_in, w_ffn_out, enc_ffn)
        return (encoded.astype(low_type), self_saved, ffn_saved)

    def encoder_forward_step(progress, micro_idx):
        low_memory, self_saved, ffn_saved = encoder_core(micro_idx)
        memory = jnp.stack([matmul(low_memory, w_first), matmul(low_memory, w_second)]).astype(
            low_type
        )
        progress = updated(progress, "out", micro_idx, low_memory)
        progress = updated(progress, "send", micro_idx, memory)
        progress = updated(progress, "self_saved", micro_idx, self_saved)
        progress = updated(progress, "ffn_saved", micro_idx, ffn_saved)
        return progress

    def decoder_head(micro_idx):
        return self_forward(
            row_pieces[micro_idx], tgt_lens[micro_idx], True, w_proj, w_attn_out, dec_self
        )

    def decoder_tail(mid_rows, memory, micro_idx):
        crossed, cross_saved = cross_forward(
            mid_rows, memory, src_lens[micro_idx], w_first, w_second, dec_cross
        )
        decoded, ffn_saved = ffn_forward(crossed, w_ffn_in, w_ffn_out, dec_ffn)
        return (decoded, cross_saved, ffn_saved)

    def decoder_head_step(progress, micro_idx):
        mid_rows, self_saved = decoder_head(micro_idx)
        progress = updated(progress, "mid", micro_idx, mid_rows)
        progress = updated(progress, "self_saved", micro_idx, self_saved)
        return progress

    def decoder_tail_step(progress, micro_idx):
        decoded, cross_saved, ffn_saved = decoder_tail(
            progress["mid"][micro_idx], progress["memory"][micro_idx], micro_idx
        )
        progress = updated(progress, "out", micro_idx, decoded.astype(low_type))
        progress = updated(progress, "cross_saved", micro_idx, cross_saved)
        progress = updated(progress, "ffn_saved", micro_idx, ffn_saved)
        return progress

    def decoder_back_step(progress, micro_idx):
        memory = progress["memory"][micro_idx]
        self_saved = progress["self_saved"][micro_idx]
        cross_saved = progress["cross_saved"][micro_idx]
        ffn_saved = progress["ffn_saved"][micro_idx]
        grad_h_two, ffn_w, ffn_v = ffn_backward(
            w_ffn_in, w_ffn_out, dec_ffn, ffn_saved, grad_pieces[micro_idx]
        )
        grad_h_one, grad_memory, cross_w, cross_v = cross_backward(
            memory, src_lens[micro_idx], w_first, w_second, dec_cross, cross_saved, grad_h_two
        )
        grad_rows, self_w, self_v = self_backward(
            row_pieces[micro_idx],
            tgt_lens[micro_idx],
            True,
            w_proj,
            w_attn_out,
            dec_self,
            self_saved,
            grad_h_one,
        )
        totals = accumulate(
            progress["totals"],
            ("ffn_in", "ffn_out", "first", "second", "proj", "attn_out"),
            ffn_w + cross_w + self_w,
            ffn_plan(True, ffn_v) + cross_plan(cross_v) + self_plan(True, self_v),
        )
        progress = updated(progress, "grad_in", micro_idx, grad_rows)
        progress = updated(progress, "grad_send", micro_idx, grad_memory)
        return with_totals(progress, totals)

    def encoder_top_step(progress, micro_idx):
        low_memory = progress["out"][micro_idx]
        ffn_saved = progress["ffn_saved"][micro_idx]
        grad_memory = progress["grad_memory"][micro_idx]
        grad_encoded = matmul_nt(grad_memory[0], w_first) + matmul_nt(grad_memory[1], w_second)
        grad_h_one, ffn_w, ffn_v = ffn_backward(
            w_ffn_in, w_ffn_out, enc_ffn, ffn_saved, grad_encoded
        )
        projections = (matmul_tn(low_memory, grad_memory[0]), matmul_tn(low_memory, grad_memory[1]))
        totals = accumulate(
            progress["totals"],
            ("first", "second", "ffn_in", "ffn_out"),
            projections + ffn_w,
            ffn_plan(False, ffn_v),
        )
        progress = updated(progress, "grad_mid", micro_idx, grad_h_one)
        return with_totals(progress, totals)

    def encoder_bottom_step(progress, micro_idx):
        self_saved = progress["self_saved"][micro_idx]
        grad_rows, self_w, self_v = self_backward(
            row_pieces[micro_idx],
            src_lens[micro_idx],
            False,
            w_proj,
            w_attn_out,
            enc_self,
            self_saved,
            progress["grad_mid"][micro_idx],
        )
        totals = accumulate(
            progress["totals"], ("proj", "attn_out"), self_w, self_plan(False, self_v)
        )
        progress = updated(progress, "grad_in", micro_idx, grad_rows)
        return with_totals(progress, totals)

    def enc_zero(progress):
        return encoder_forward_step(progress, 0)

    def dec_zero(progress):
        return decoder_head_step(progress, 0)

    def enc_one(progress):
        return encoder_forward_step(progress, 1)

    def dec_one(progress):
        return decoder_tail_step(decoder_head_step(progress, 1), 0)

    def dec_two(progress):
        return decoder_back_step(decoder_tail_step(progress, 1), 1)

    def enc_three(progress):
        return encoder_bottom_step(encoder_top_step(progress, 1), 1)

    def dec_three(progress):
        return decoder_back_step(progress, 0)

    def enc_four(progress):
        return encoder_top_step(progress, 0)

    def enc_five(progress):
        return encoder_bottom_step(progress, 0)

    progress = lax.cond(is_decoder, dec_zero, enc_zero, progress)
    progress = updated(progress, "memory", 0, forward_pass(progress["send"][0]))
    progress = lax.cond(is_decoder, dec_one, enc_one, progress)
    progress = updated(progress, "memory", 1, forward_pass(progress["send"][1]))
    progress = lax.cond(is_decoder, dec_two, keep_same, progress)
    progress = updated(progress, "grad_memory", 1, backward_pass(progress["grad_send"][1]))
    progress = lax.cond(is_decoder, dec_three, enc_three, progress)
    progress = updated(progress, "grad_memory", 0, backward_pass(progress["grad_send"][0]))
    progress = lax.cond(is_decoder, keep_same, enc_four, progress)
    progress = lax.cond(is_decoder, keep_same, enc_five, progress)
    totals = progress["totals"]
    dp_size = lax.axis_size("dp")
    if dp_size % 4 == 0 and model_width // dp_size == PIECE:
        nz = dp_size // 4
        split = lambda t: t.astype(low_type).reshape(nz, 2, 2, -1, t.shape[-1])
        parts = [
            split(totals["ffn_out"]),
            split(totals["ffn_in"]).reshape(nz, 2, 2, PIECE, 4, model_width).swapaxes(3, 4).reshape(nz, 2, 2, 4 * PIECE, model_width),
            split(totals["second"]),
            split(totals["first"]),
            split(totals["attn_out"]),
        ] + [split(totals["proj"][j]) for j in range(3)]
        packed = jnp.concatenate(parts, axis=3)
        rows = jnp.concatenate([totals["gains"], totals["biases"], jnp.zeros((3, model_width), f32)])
        s_out, s_in, s_second, s_first, s_attn, s_proj, rows = reduce_scatter(nz, packed, rows, (1,) * 14)
        owned = (s_proj, s_attn, s_first, s_second, s_in, s_out)
        own_cols = lax.dynamic_slice_in_dim(rows, lax.axis_index("dp") * PIECE, PIECE, 1)
        owned_gains, owned_biases = own_cols[:5], own_cols[5:29]
    else:
        owned = (
            lax.psum_scatter(totals["proj"], "dp", scatter_dimension=1, tiled=True),
            lax.psum_scatter(totals["attn_out"], "dp", scatter_dimension=0, tiled=True),
            lax.psum_scatter(totals["first"], "dp", scatter_dimension=0, tiled=True),
            lax.psum_scatter(totals["second"], "dp", scatter_dimension=0, tiled=True),
            lax.psum_scatter(totals["ffn_in"], "dp", scatter_dimension=0, tiled=True),
            lax.psum_scatter(totals["ffn_out"], "dp", scatter_dimension=0, tiled=True),
            lax.psum_scatter(totals["gains"], "dp", scatter_dimension=1, tiled=True),
            lax.psum_scatter(totals["biases"], "dp", scatter_dimension=1, tiled=True),
        )
        owned_gains, owned_biases = lax.psum((owned[6], owned[7]), "stream")
    layer_out = jnp.concatenate(progress["out"], axis=0)[None]
    grad_inputs = jnp.concatenate(progress["grad_in"], axis=0)[None]
    return (
        layer_out,
        grad_inputs,
        owned[0][None],
        owned[1][None],
        owned[2][None],
        owned[3][None],
        owned[4][None],
        owned[5][None],
        owned_gains,
        owned_biases,
    )


def solution(mesh):
    return jax.shard_map(
        body,
        mesh=mesh,
        in_specs=(
            P("stream", "dp", None),
            P(None, "dp", None),
            P("dp", None),
            P("stream", None, None, None),
            P("stream", None, None),
            P("stream", None, None),
            P("stream", None, None),
            P("stream", None, None),
            P("stream", None, None),
            P(),
            P(),
        ),
        out_specs=(
            P("stream", "dp", None),
            P("stream", "dp", None),
            P("stream", None, "dp", None),
            P("stream", "dp", None),
            P("stream", "dp", None),
            P("stream", "dp", None),
            P("stream", "dp", None),
            P("stream", "dp", None),
            P(None, "dp"),
            P(None, "dp"),
        ),
        check_vma=False,
    )
```

```python
import functools

import jax
import jax.numpy as jnp
from jax import lax
from jax.experimental import pallas as pl
from jax.experimental.pallas import tpu as pltpu
from jax.sharding import PartitionSpec as P

HDIM = 64
SHORT = 128
LONG = 256
ROWS = SHORT + LONG
PIECE = 48
PIECES = 14
MESH = pl.DeviceIdType.MESH
bf16, f32 = jnp.bfloat16, jnp.float32
VMEM_LIMIT = 64 << 20


def dot_nn(a, b):
    return jnp.dot(a, b, preferred_element_type=f32)


def dot_nt(a, b):
    return lax.dot_general(a, b, (((1,), (1,)), ((), ())), preferred_element_type=f32)


def dot_tn(a, b):
    return lax.dot_general(a, b, (((0,), (0,)), ((), ())), preferred_element_type=f32)


def cols(j, width):
    return pl.ds(pl.multiple_of(j * width, width), width)


def step_kernel(
    nz, width, hidden,
    lens, vec, bias_in, x_hbm, cot_hbm, wproj_hbm, wo_hbm, wfirst_hbm, wsecond_hbm, win_hbm, wout_hbm,
    out_rows, out_grad, out_own, out_z, out_vec,
    wproj, wo, wfirst, wsecond, win, wout, wx,
    xb, up, mem, obuf, hlow, dg, kv, acc, grad, u_self, u_cross, u_ffn, gr, grp, lt, ltp, ysend, yrecv, gmem, vg, vbuf, vzbuf,
    load_sem, wx_send, wx_recv, mem_send, mem_recv, gm_send, gm_recv, gk_send, gk_recv, lt_send, lt_recv, gr_send, gr_recv,
    y_send, y_recv, z_send, z_recv, own_sem, io_sem, v_send, v_recv, vz_send, vz_recv,
):
    st = lax.axis_index("stream")
    me = lax.axis_index("dp")
    z, y, c = me // 4, (me // 2) % 2, me % 2
    is_dec = st == 1
    is_enc = st == 0
    core_id = {"dp": z * 4 + y * 2 + (1 - c)}
    y_id = {"dp": z * 4 + (1 - y) * 2 + c}
    x_id = {"stream": 1 - st}
    tiles = width // 256
    slots = hidden // width

    def z_id(d):
        return {"dp": lax.rem(z + d, nz) * 4 + y * 2 + c}

    def remote(src, dst, ss, rs, dev):
        return pltpu.make_async_remote_copy(
            src_ref=src, dst_ref=dst, send_sem=ss, recv_sem=rs, device_id=dev, device_id_type=MESH)

    loads = [
        pltpu.make_async_copy(src, dst, load_sem.at[i])
        for i, (src, dst) in enumerate((
            (x_hbm, xb), (wproj_hbm, wproj), (wo_hbm, wo), (wfirst_hbm, wfirst), (wsecond_hbm, wsecond),
            (win_hbm, win), (wout_hbm, wout)))
    ]
    for cp in loads:
        cp.start()
    cot_load = pltpu.make_async_copy(cot_hbm, up, load_sem.at[7])

    @pl.when(is_dec)
    def _():
        cot_load.start()

    barrier = pltpu.get_barrier_semaphore()
    peers = [core_id, y_id, x_id] + [z_id(d) for d in range(1, nz)]
    for p in peers:
        pl.semaphore_signal(barrier, inc=1, device_id=p, device_id_type=MESH)
    pl.semaphore_wait(barrier, len(peers))

    half = width // 2
    quarter = y * 2 + c
    wx_first = remote(wfirst_hbm.at[pl.ds(c * half, half)], wx.at[quarter], wx_send.at[0], wx_recv.at[0], x_id)
    wx_second = remote(wsecond_hbm.at[pl.ds(c * half, half)], wx.at[quarter], wx_send.at[0], wx_recv.at[0], x_id)
    wx_y = remote(wx.at[quarter], wx.at[quarter], wx_send.at[1], wx_recv.at[1], y_id)
    wx_c0 = remote(wx.at[quarter], wx.at[quarter], wx_send.at[2], wx_recv.at[2], core_id)
    far = (1 - y) * 2 + c
    wx_c1 = remote(wx.at[far], wx.at[far], wx_send.at[3], wx_recv.at[3], core_id)

    @pl.when(is_enc & (y == 0))
    def _():
        wx_first.start()

    @pl.when(is_enc & (y == 1))
    def _():
        wx_second.start()

    lt_copy = [remote(lt.at[i, :, :, 1 - c], ltp.at[i], lt_send.at[i], lt_recv.at[i], core_id) for i in range(9)]
    gr_copy = [remote(gr.at[i], grp.at[i], gr_send.at[i], gr_recv.at[i], core_id) for i in range(11)]
    mem_copy = remote(xb, mem, mem_send, mem_recv, x_id)
    gm_copy = remote(gmem, up, gm_send, gm_recv, x_id)
    gk_copy = [remote(kv.at[0], gr.at[6], gk_send.at[0], gk_recv.at[0], x_id),
               remote(kv.at[1], gr.at[5], gk_send.at[1], gk_recv.at[1], x_id)]
    vg[...] = jnp.zeros_like(vg)

    def row_loop(block, body):
        def step(i, carry):
            body(pl.ds(pl.multiple_of(i * block, block), block))
            return carry
        lax.fori_loop(0, ROWS // block, step, 0)

    def vrow(r):
        return vec[pl.ds(r, 1), :]

    def transposed(i, value):
        lt[i] = value.T.reshape(nz, 2, 2, PIECE, ROWS)

    def col_sum(slot, row):
        def step(i, carry):
            block = slot[pl.ds(pl.multiple_of(i * 64, 64), 64), :].astype(f32)
            return carry + jnp.sum(block.reshape(8, 8, width), axis=0)
        total = lax.fori_loop(0, ROWS // 64, step, jnp.zeros((8, width), f32))
        vg[pl.ds(row, 1), :] = jnp.sum(total, axis=0, keepdims=True)

    def norm_forward(sum_ref, add_bias, gain, shift, out_low, keep_wide):
        def body(rows):
            u = grad[rows, :] + acc[rows, :] + vrow(add_bias)
            sum_ref[rows, :] = u
            centre = u - jnp.mean(u, axis=-1, keepdims=True)
            spread = jnp.mean(centre * centre, axis=-1, keepdims=True)
            h = centre * lax.rsqrt(spread + 1e-05) * vrow(gain) + vrow(shift)
            if keep_wide:
                grad[rows, :] = h
            out_low[rows, :] = h.astype(bf16)
        row_loop(32, body)

    def norm_backward(sum_ref, source, gain, shift, slot):
        def step(i, carry):
            rows = pl.ds(pl.multiple_of(i * 32, 32), 32)
            r = source[rows, :].astype(f32)
            u = sum_ref[rows, :]
            centre = u - jnp.mean(u, axis=-1, keepdims=True)
            spread = jnp.mean(centre * centre, axis=-1, keepdims=True)
            inv = lax.rsqrt(spread + 1e-05)
            uhat = centre * inv
            t = r * vrow(gain)
            gu = (t - jnp.mean(t, axis=-1, keepdims=True) - uhat * jnp.mean(t * uhat, axis=-1, keepdims=True)) * inv
            grad[rows, :] = gu
            slot[rows, :] = gu.astype(bf16)
            return (carry[0] + jnp.sum((r * uhat).reshape(4, 8, width), axis=0),
                    carry[1] + jnp.sum(r.reshape(4, 8, width), axis=0))
        zero = jnp.zeros((8, width), f32)
        total = lax.fori_loop(0, ROWS // 32, step, (zero, zero))
        vg[pl.ds(gain, 1), :] = jnp.sum(total[0], axis=0, keepdims=True)
        vg[pl.ds(shift, 1), :] = jnp.sum(total[1], axis=0, keepdims=True)

    def masked_scores(q_half, k2, n, length, diagonal):
        s = dot_nt(q_half, k2) * (HDIM ** -0.5)
        column = lax.broadcasted_iota(jnp.int32, (n, n), 1)
        row = lax.broadcasted_iota(jnp.int32, (n, n), 0)
        return jnp.where((column < length) & (column <= row + diagonal), s, -1e30)

    def softmax(s):
        e = jnp.exp(s - jnp.max(s, axis=-1, keepdims=True))
        return e * (1.0 / jnp.sum(e, axis=-1, keepdims=True))

    buckets = ((0, SHORT), (SHORT, LONG))

    def halves(n):
        lane = lax.broadcasted_iota(jnp.int32, (n, 2 * HDIM), 1)
        return lane < HDIM

    def attend_forward(q_ref, k_ref, v_ref, len_at, diagonal, bias_row, out_ref):
        for b, (r0, n) in enumerate(buckets):
            rows = pl.ds(r0, n)
            length = lens[len_at + b]
            first = halves(n)

            def step(p, carry, rows=rows, n=n, length=length, first=first):
                at = cols(p, 2 * HDIM)
                q2, k2, v2 = q_ref[rows, at], k_ref[rows, at], v_ref[rows, at]
                zero = jnp.zeros_like(q2)
                parts = []
                for lanes in (first, ~first):
                    prob = softmax(masked_scores(jnp.where(lanes, q2, zero), k2, n, length, diagonal))
                    parts.append(dot_nn(prob.astype(bf16), v2))
                att = jnp.where(first, parts[0], parts[1])
                if bias_row is not None:
                    att = att + vec[pl.ds(bias_row, 1), at]
                out_ref[rows, at] = att.astype(bf16)
                return carry
            lax.fori_loop(0, width // (2 * HDIM), step, 0)

    def attend_backward(b, q_ref, k_ref, v_ref, len_at, diagonal):
        r0, n = buckets[b]
        rows = pl.ds(r0, n)
        length = lens[len_at + b]
        first = halves(n)
        scale = HDIM ** -0.5

        def step(p, carry):
            at = cols(p, 2 * HDIM)
            q2, k2, v2, go2 = q_ref[rows, at], k_ref[rows, at], v_ref[rows, at], obuf[rows, at]
            zero = jnp.zeros_like(q2)
            got = []
            for lanes in (first, ~first):
                prob = softmax(masked_scores(jnp.where(lanes, q2, zero), k2, n, length, diagonal))
                gv = dot_tn(prob.astype(bf16), go2)
                gp = dot_nt(jnp.where(lanes, go2, zero), v2)
                gs = (prob * (gp - jnp.sum(prob * gp, axis=-1, keepdims=True))).astype(bf16)
                got.append((dot_nn(gs, k2), dot_tn(gs, q2), gv))
            q_ref[rows, at] = (jnp.where(first, got[0][0], got[1][0]) * scale).astype(bf16)
            k_ref[rows, at] = (jnp.where(first, got[0][1], got[1][1]) * scale).astype(bf16)
            v_ref[rows, at] = jnp.where(first, got[0][2], got[1][2]).astype(bf16)
            return carry
        lax.fori_loop(0, width // (2 * HDIM), step, 0)

    q_ref, k_ref, v_ref = gr.at[8], gr.at[9], gr.at[10]
    diagonal = (1 - st) * 4096

    loads[0].wait()
    loads[1].wait()
    bias_at = 5 + 10 * st

    def project(i, carry):
        which, t = i // tiles, i % tiles
        at = cols(t, 256)
        value = dot_nn(xb[...], wproj[which, :, at])
        bias = vec[pl.ds(bias_at + which // 2, 1), at] * jnp.where(which == 1, 0.0, 1.0)
        gr[8 + which, :, at] = (value + bias).astype(bf16)
        return carry
    lax.fori_loop(0, 3 * tiles, project, 0)
    transposed(4, xb[...])
    lt_copy[4].start()

    def load_residual(rows):
        grad[rows, :] = xb[rows, :].astype(f32)
    row_loop(64, load_residual)

    attend_forward(q_ref, k_ref, v_ref, 2 * st, diagonal, None, obuf)
    loads[2].wait()

    def by_tiles(fn):
        def step(t, carry):
            fn(t)
            return carry
        lax.fori_loop(0, tiles, step, 0)

    def self_out(t):
        acc[:, cols(t, 256)] = dot_nn(obuf[...], wo[:, cols(t, 256)])
    by_tiles(self_out)
    norm_forward(u_self, bias_at + 2, 2 * st, bias_at + 3, hlow, True)
    transposed(5, obuf[...])
    lt_copy[5].start()

    loads[3].wait()
    loads[4].wait()

    @pl.when(is_dec)
    def _():
        wx_first.wait_recv()
        wx_y.start()
        wx_c0.start()

        def cross_query(t):
            at = cols(t, 256)
            gr[6, :, at] = (dot_nn(hlow[...], wfirst[:, at]) + vec[pl.ds(19, 1), at]).astype(bf16)
        by_tiles(cross_query)
        transposed(8, hlow[...])
        lt_copy[8].start()
        wx_y.wait()
        wx_c1.start()
        wx_c0.wait()
        wx_c1.wait()
        mem_copy.wait_recv()

        def memory_kv(i, carry):
            which, t = i // tiles, i % tiles
            at = cols(t, 256)
            value = dot_nn(mem[:, pl.ds(0, half)], wx[2 * which, :, at]) + dot_nn(mem[:, pl.ds(half, half)], wx[2 * which + 1, :, at])
            kv[which, :, at] = value.astype(bf16)
            return carry
        lax.fori_loop(0, 2 * tiles, memory_kv, 0)
        attend_forward(gr.at[6], kv.at[0], kv.at[1], 0, 4096, 20, obuf)

        def cross_out(t):
            acc[:, cols(t, 256)] = dot_nn(obuf[...], wsecond[:, cols(t, 256)])
        by_tiles(cross_out)
        norm_forward(u_cross, 21, 3, 22, hlow, True)
        transposed(7, obuf[...])
        lt_copy[7].start()

    loads[5].wait()
    loads[6].wait()

    def ffn_slot(j, carry):
        def tile(t, carry2):
            at = cols(t, 256)
            wide = pl.ds(pl.multiple_of(j * width + t * 256, 256), 256)
            acc[:, at] = dot_nn(hlow[...], win[:, wide])

            def activate(rows):
                zv = acc[rows, at] + bias_in[pl.ds(st, 1), wide]
                cdf = 0.5 * (1.0 + lax.erf(zv * (0.5 ** 0.5)))
                pdf = jnp.exp(-0.5 * zv * zv) * 0.3989422804014327
                gr[1 + j, rows, at] = (zv * cdf).astype(bf16)
                dg[j, rows, at] = (cdf + zv * pdf).astype(bf16)
            row_loop(64, activate)
            return carry2
        lax.fori_loop(0, tiles, tile, 0)
        turned = gr[1 + j].T.reshape(2, 2, 4, PIECE, ROWS)
        for k in range(4):
            lt[k, j] = turned[:, :, k]
        return carry
    lax.fori_loop(0, slots, ffn_slot, 0)
    for k in range(4):
        lt_copy[k].start()

    def ffn_out(t):
        at = cols(t, 256)
        total = dot_nn(gr[1], wout[pl.ds(0, width), at])
        for j in range(1, slots):
            total = total + dot_nn(gr[1 + j], wout[pl.ds(j * width, width), at])
        acc[:, at] = total
    by_tiles(ffn_out)
    ffn_at = 5 + 8 + 14 * st
    norm_forward(u_ffn, ffn_at, 1 + 3 * st, ffn_at + 1, xb, False)

    @pl.when(is_enc)
    def _():
        mem_copy.start()
    rows_copy = pltpu.make_async_copy(xb, out_rows, io_sem.at[0])
    rows_copy.start()
    transposed(6, hlow[...])
    lt_copy[6].start()

    @pl.when(is_enc)
    def _():
        transposed(7, xb[...])
        lt_copy[7].start()
        gm_copy.wait_recv()

    @pl.when(is_dec)
    def _():
        cot_load.wait()

    norm_backward(u_ffn, up, 1 + 3 * st, ffn_at + 1, gr.at[0])
    gr_copy[0].start()

    def ffn_inner(j, carry):
        def tile(t, carry2):
            at = cols(t, 256)
            wide = pl.ds(pl.multiple_of(j * width + t * 256, 256), 256)
            acc[:, at] = dot_nt(gr[0], wout[wide, :])

            def scale(rows):
                gr[1 + j, rows, at] = (acc[rows, at] * dg[j, rows, at].astype(f32)).astype(bf16)
            row_loop(64, scale)
            return carry2
        lax.fori_loop(0, tiles, tile, 0)
        remote(gr.at[1 + j], grp.at[1 + j], gr_send.at[1 + j], gr_recv.at[1 + j], core_id).start()
        return carry
    lax.fori_loop(0, slots, ffn_inner, 0)

    def ffn_input(t):
        at = cols(t, 256)
        total = grad[:, at]
        for j in range(slots):
            total = total + dot_nt(gr[1 + j], win[at, pl.ds(j * width, width)])
        grad[:, at] = total
    by_tiles(ffn_input)

    @pl.when(is_dec)
    def _():
        norm_backward(u_cross, grad, 3, 22, gr.at[5])
        gr_copy[5].start()

        def cross_up(t):
            at = cols(t, 256)
            obuf[:, at] = dot_nt(gr[5], wsecond[at, :]).astype(bf16)
        by_tiles(cross_up)
        col_sum(obuf, 20)
        for b in range(2):
            attend_backward(b, gr.at[6], kv.at[0], kv.at[1], 0, 4096)

        def memory_half(h, carry):
            at = cols(h, half)
            gmem[:, at] = (dot_nt(kv[0], wx[h]) + dot_nt(kv[1], wx[2 + h])).astype(bf16)
            return carry
        lax.fori_loop(0, 2, memory_half, 0)
        gm_copy.start()
        gk_copy[0].start()
        gk_copy[1].start()
        gr_copy[6].start()
        col_sum(gr.at[6], 19)
        col_sum(gr.at[5], 21)

        def cross_input(t):
            at = cols(t, 256)
            grad[:, at] = grad[:, at] + dot_nt(gr[6], wfirst[at, :])
        by_tiles(cross_input)


    def y_copy(i):
        return remote(ysend.at[i], yrecv.at[i], y_send.at[i], y_recv.at[i], y_id)

    def z_copy(i, d):
        return remote(yrecv.at[i, lax.rem(z + d, nz)], out_z.at[d - 1, i], z_send.at[i, d - 1], z_recv.at[i, d - 1], z_id(d))

    def product(left, slot, yy, at):
        mine = lt[left, :, yy, c].reshape(nz * PIECE, ROWS)
        theirs = ltp[left, :, yy].reshape(nz * PIECE, ROWS)
        return dot_nn(mine, gr[slot, :, at]) + dot_nn(theirs, grp[slot, :, at])

    def send_piece(i, left, slot):
        def tile(t):
            at = cols(t, 256)
            ysend[i, :, :, at] = product(left, slot, 1 - y, at).astype(bf16).reshape(nz, PIECE, 256)
        by_tiles(tile)
        y_copy(i).start()

    def keep_piece(i, left, slot):
        y_copy(i).wait()

        def tile(t):
            at = cols(t, 256)
            total = yrecv[i, :, :, at].reshape(nz * PIECE, 256).astype(f32) + product(left, slot, y, at)
            yrecv[i, :, :, at] = total.astype(bf16).reshape(nz, PIECE, 256)
        by_tiles(tile)
        for d in range(1, nz):
            z_copy(i, d).start()
        pltpu.make_async_copy(yrecv.at[i, z], out_own.at[i], own_sem.at[i]).start()

    def loop(lo, hi, fn):
        def step(i, carry):
            fn(i)
            return carry
        lax.fori_loop(lo, hi, step, 0)

    for i in (0, 1, 2, 3, 6):
        lt_copy[i].wait()
    gr_copy[0].wait()
    loop(0, 4, lambda i: send_piece(i, i, 0))
    for j in range(slots):
        gr_copy[1 + j].wait()
    loop(4, 8, lambda i: send_piece(i, 6, i - 3))

    norm_backward(u_self, grad, 2 * st, bias_at + 3, gr.at[7])
    gr_copy[7].start()

    def self_up(t):
        at = cols(t, 256)
        obuf[:, at] = dot_nt(gr[7], wo[at, :]).astype(bf16)
    by_tiles(self_up)
    loop(0, 1, lambda i: keep_piece(i, i, 0))
    attend_backward(0, q_ref, k_ref, v_ref, 2 * st, diagonal)
    loop(1, 2, lambda i: keep_piece(i, i, 0))
    attend_backward(1, q_ref, k_ref, v_ref, 2 * st, diagonal)
    for j in range(3):
        gr_copy[8 + j].start()

    @pl.when(is_enc)
    def _():
        gk_copy[0].wait_recv()
        gk_copy[1].wait_recv()
        gr_copy[5].start()
        gr_copy[6].start()

    def self_input(t):
        at = cols(t, 256)
        total = grad[:, at]
        for j in range(3):
            total = total + dot_nt(gr[8 + j], wproj[j, at, :])
        grad[:, at] = total
    by_tiles(self_input)
    grad_copy = pltpu.make_async_copy(grad, out_grad, io_sem.at[1])
    grad_copy.start()
    loop(2, 4, lambda i: keep_piece(i, i, 0))
    for i in (4, 5, 7):
        lt_copy[i].wait()

    @pl.when(is_dec)
    def _():
        lt_copy[8].wait()
    for i in range(5, 11):
        gr_copy[i].wait()
    first_left = 7 + st
    rest = ((8, 7, 5), (9, first_left, 6), (10, 5, 7), (11, 4, 8), (12, 4, 9), (13, 4, 10))
    for i, left, slot in rest:
        send_piece(i, left, slot)

    col_sum(gr.at[0], ffn_at)
    loop(0, slots, lambda j: col_sum(gr.at[1 + j], ffn_at - 4 + j))
    col_sum(gr.at[7], bias_at + 2)
    col_sum(gr.at[8], bias_at)
    col_sum(gr.at[10], bias_at + 1)
    v_copy = [remote(vbuf.at[0], vbuf.at[1], v_send.at[0], v_recv.at[0], core_id),
              remote(vbuf.at[2], vbuf.at[3], v_send.at[1], v_recv.at[1], y_id),
              remote(vbuf.at[5], vbuf.at[6], v_send.at[2], v_recv.at[2], x_id)]
    vz_copy = [remote(vbuf.at[4], vzbuf.at[d - 1], vz_send.at[d - 1], vz_recv.at[d - 1], z_id(d)) for d in range(1, nz)]
    vbuf[0] = vg[...]
    v_copy[0].start()
    loop(4, 5, lambda i: keep_piece(i, 6, i - 3))
    v_copy[0].wait()
    vbuf[2] = vbuf[0] + vbuf[1]
    v_copy[1].start()
    loop(5, 6, lambda i: keep_piece(i, 6, i - 3))
    v_copy[1].wait()
    vbuf[4] = vbuf[2] + vbuf[3]
    for cp in vz_copy:
        cp.start()
    loop(6, 8, lambda i: keep_piece(i, 6, i - 3))
    for cp in vz_copy:
        cp.wait()
    total = vbuf[4]
    for d in range(1, nz):
        total = total + vzbuf[d - 1]
    vbuf[5] = total
    v_copy[2].start()
    for i, left, slot in rest:
        keep_piece(i, left, slot)
    v_copy[2].wait()
    out_vec[...] = vbuf[5] + vbuf[6]

    def finish(i):
        for d in range(1, nz):
            z_copy(i, d).wait()
        pltpu.make_async_copy(yrecv.at[i, z], out_own.at[i], own_sem.at[i]).wait()
    loop(0, PIECES, finish)
    rows_copy.wait()
    grad_copy.wait()

    @pl.when(is_enc)
    def _():
        wx_first.wait_send()
        mem_copy.wait_send()

    @pl.when(is_dec)
    def _():
        gm_copy.wait_send()
        gk_copy[0].wait_send()
        gk_copy[1].wait_send()


def last_kernel(nz, width, rows_in, grad_in, own, parts, rows_out, grad_out, *outs):
    rows_out[...] = rows_in[...]
    grad_out[...] = grad_in[...]
    for i in range(PIECES):
        total = own[i].astype(f32)
        for d in range(nz - 1):
            total = total + parts[d, i].astype(f32)
        if i < 4:
            outs[0][pl.ds(i * PIECE, PIECE), :] = total
        elif i < 8:
            outs[1][:, pl.ds((i - 4) * width, width)] = total
        elif i < 11:
            outs[i - 6][...] = total
        else:
            outs[5][i - 11] = total


def whole_step(nz, lens, vec, bias_in, x, cot, wproj, wo, wfirst, wsecond, win, wout):
    width = x.shape[1]
    hidden = win.shape[1]
    half = width // 2
    any_space = pl.BlockSpec(memory_space=pl.ANY)
    vmem = pl.BlockSpec(memory_space=pltpu.VMEM)
    dma = pltpu.SemaphoreType.DMA
    slots = hidden // width
    results = pl.pallas_call(
        functools.partial(step_kernel, nz, width, hidden),
        out_shape=[
            jax.ShapeDtypeStruct((ROWS, width), bf16),
            jax.ShapeDtypeStruct((ROWS, width), f32),
            jax.ShapeDtypeStruct((PIECES, PIECE, width), bf16),
            jax.ShapeDtypeStruct((nz - 1, PIECES, PIECE, width), bf16),
            jax.ShapeDtypeStruct(vec.shape, f32),
        ],
        in_specs=[pl.BlockSpec(memory_space=pltpu.SMEM), vmem, vmem] + [any_space] * 8,
        out_specs=[any_space] * 4 + [vmem],
        scratch_shapes=[
            pltpu.VMEM(wproj.shape, bf16), pltpu.VMEM(wo.shape, bf16), pltpu.VMEM(wfirst.shape, bf16),
            pltpu.VMEM(wsecond.shape, bf16), pltpu.VMEM(win.shape, bf16), pltpu.VMEM(wout.shape, bf16),
            pltpu.VMEM((4, half, width), bf16),
            pltpu.VMEM((ROWS, width), bf16),
            pltpu.VMEM((ROWS, width), bf16),
            pltpu.VMEM((ROWS, width), bf16),
            pltpu.VMEM((ROWS, width), bf16),
            pltpu.VMEM((ROWS, width), bf16),
            pltpu.VMEM((slots, ROWS, width), bf16),
            pltpu.VMEM((2, ROWS, width), bf16),
            pltpu.VMEM((ROWS, width), f32),
            pltpu.VMEM((ROWS, width), f32),
            pltpu.VMEM((ROWS, width), f32),
            pltpu.VMEM((ROWS, width), f32),
            pltpu.VMEM((ROWS, width), f32),
            pltpu.VMEM((11, ROWS, width), bf16),
            pltpu.VMEM((11, ROWS, width), bf16),
            pltpu.VMEM((9, nz, 2, 2, PIECE, ROWS), bf16),
            pltpu.VMEM((9, nz, 2, PIECE, ROWS), bf16),
            pltpu.VMEM((PIECES, nz, PIECE, width), bf16),
            pltpu.VMEM((PIECES, nz, PIECE, width), bf16),
            pltpu.VMEM((ROWS, width), bf16),
            pltpu.VMEM(vec.shape, f32),
            pltpu.VMEM((7,) + vec.shape, f32),
            pltpu.VMEM((nz - 1,) + vec.shape, f32),
            dma((8,)), dma((4,)), dma((4,)), dma, dma, dma, dma, dma((2,)), dma((2,)),
            dma((9,)), dma((9,)), dma((11,)), dma((11,)),
            dma((PIECES,)), dma((PIECES,)), dma((PIECES, nz - 1)), dma((PIECES, nz - 1)), dma((PIECES,)), dma((2,)),
            dma((3,)), dma((3,)), dma((nz - 1,)), dma((nz - 1,)),
        ],
        compiler_params=pltpu.CompilerParams(collective_id=0, has_side_effects=True, vmem_limit_bytes=VMEM_LIMIT),
        name="step",
    )(lens, vec, bias_in, x, cot, wproj, wo, wfirst, wsecond, win, wout)
    rows, grad, own, parts, vec_sum = results
    shapes = [(4 * PIECE, width), (PIECE, hidden), (PIECE, width), (PIECE, width), (PIECE, width), (3, PIECE, width)]
    outs = pl.pallas_call(
        functools.partial(last_kernel, nz, width),
        out_shape=[jax.ShapeDtypeStruct(rows.shape, bf16), jax.ShapeDtypeStruct(grad.shape, f32)]
        + [jax.ShapeDtypeStruct(s, f32) for s in shapes],
        in_specs=[vmem] * 4,
        out_specs=[vmem] * 8,
        compiler_params=pltpu.CompilerParams(vmem_limit_bytes=32 << 20),
        name="last",
    )(rows, grad, own, parts)
    return list(outs) + [vec_sum]


eps_norm = 1e-05
low_type = jnp.bfloat16
wide_type = jnp.float32


def as_sent(shard):
    return jax.tree.map(lambda a: a.astype(jnp.bfloat16) if a.dtype == jnp.float32 else a, shard)


def shifted(shard, axis, by):
    count = lax.axis_size(axis)
    pairs = [(i, i + by) for i in range(count) if 0 <= i + by < count]
    return lax.ppermute(shard, axis, pairs)


def matmul(left_mat, right_mat):
    return jnp.dot(left_mat, right_mat, preferred_element_type=wide_type)


def matmul_tn(left_mat, right_mat):
    return lax.dot_general(
        left_mat, right_mat, (((0,), (0,)), ((), ())), preferred_element_type=wide_type
    )


def matmul_nt(left_mat, right_mat):
    return lax.dot_general(
        left_mat, right_mat, (((1,), (1,)), ((), ())), preferred_element_type=wide_type
    )


def column_sum(tensor):
    return jnp.sum(tensor.astype(wide_type), axis=0)


def norm_rows(tensor, norm_gain, norm_shift):
    centre = tensor - jnp.mean(tensor, axis=-1, keepdims=True)
    spread = jnp.mean(centre * centre, axis=-1, keepdims=True)
    return centre * lax.rsqrt(spread + eps_norm) * norm_gain + norm_shift


def norm_back(tensor, norm_gain, norm_shift, upstream):
    unused, pullback = jax.vjp(norm_rows, tensor, norm_gain, norm_shift)
    return pullback(upstream)


def gelu_exact(tensor):
    return jax.nn.gelu(tensor, approximate=False)


def key_mask(row_count, key_count, length, causal):
    columns = lax.broadcasted_iota(jnp.int32, (row_count, key_count), 1)
    allowed = columns < length
    if causal:
        allowed = allowed & (columns <= lax.broadcasted_iota(jnp.int32, (row_count, key_count), 0))
    return allowed


def split_heads(tensor):
    return tensor.reshape(tensor.shape[0], -1, HDIM)


def attend_scores(queries, key_rows, allowed):
    scores = jnp.einsum(
        "qhd,khd->hqk",
        split_heads(queries),
        split_heads(key_rows),
        preferred_element_type=wide_type,
    )
    return jnp.where(allowed[None], scores * HDIM ** (-0.5), -1e30)


def attend_forward(queries, key_rows, values, allowed):
    scores = attend_scores(queries, key_rows, allowed)
    row_max = jnp.max(scores, axis=-1, keepdims=True)
    log_total = row_max + jnp.log(jnp.sum(jnp.exp(scores - row_max), axis=-1, keepdims=True))
    softmaxed = jnp.exp(scores - log_total).astype(low_type)
    attended = jnp.einsum(
        "hqk,khd->qhd", softmaxed, split_heads(values), preferred_element_type=wide_type
    )
    return (attended.reshape(queries.shape[0], -1), log_total)


def attend_backward(queries, key_rows, values, allowed, log_total, upstream):
    softmaxed = jnp.exp(attend_scores(queries, key_rows, allowed) - log_total)
    grad_heads = split_heads(upstream)
    grad_values = jnp.einsum(
        "hqk,qhd->khd", softmaxed.astype(low_type), grad_heads, preferred_element_type=wide_type
    )
    grad_probs = jnp.einsum(
        "qhd,khd->hqk", grad_heads, split_heads(values), preferred_element_type=wide_type
    )
    grad_scores = (
        softmaxed * (grad_probs - jnp.sum(softmaxed * grad_probs, axis=-1, keepdims=True))
    ).astype(low_type)
    scale_factor = HDIM ** (-0.5)
    grad_queries = (
        jnp.einsum(
            "hqk,khd->qhd", grad_scores, split_heads(key_rows), preferred_element_type=wide_type
        )
        * scale_factor
    )
    grad_keys = (
        jnp.einsum(
            "hqk,qhd->khd", grad_scores, split_heads(queries), preferred_element_type=wide_type
        )
        * scale_factor
    )
    key_count = key_rows.shape[0]
    return (
        grad_queries.reshape(queries.shape[0], -1),
        grad_keys.reshape(key_count, -1),
        grad_values.reshape(key_count, -1),
    )


def self_forward(row_block, length, causal, w_proj, w_out, vectors):
    bias_q, bias_v, bias_o, norm_gain, norm_shift = vectors
    row_count = row_block.shape[0]
    offsets = jnp.stack([bias_q, jnp.zeros_like(bias_q), bias_v])[:, None, :]
    projected = (
        jnp.einsum("rd,cde->cre", row_block, w_proj, preferred_element_type=wide_type) + offsets
    ).astype(low_type)
    allowed = key_mask(row_count, row_count, length, causal)
    attended, log_total = attend_forward(projected[0], projected[1], projected[2], allowed)
    attended = attended.astype(low_type)
    summed = row_block.astype(wide_type) + matmul(attended, w_out) + bias_o
    return (norm_rows(summed, norm_gain, norm_shift), (projected, log_total, attended, summed))


def self_backward(row_block, length, causal, w_proj, w_out, vectors, saved_fwd, upstream):
    projected, log_total, attended, summed = saved_fwd
    row_count = row_block.shape[0]
    grad_sum, grad_gain, grad_shift = norm_back(summed, vectors[3], vectors[4], upstream)
    grad_branch = grad_sum.astype(low_type)
    grad_attended = matmul_nt(grad_branch, w_out).astype(low_type)
    allowed = key_mask(row_count, row_count, length, causal)
    grad_q, grad_k, grad_v = attend_backward(
        projected[0], projected[1], projected[2], allowed, log_total, grad_attended
    )
    grad_proj = jnp.stack([grad_q, grad_k, grad_v]).astype(low_type)
    grad_rows = grad_sum + jnp.einsum(
        "cre,cde->rd", grad_proj, w_proj, preferred_element_type=wide_type
    )
    weight_grads = (
        jnp.einsum("rd,cre->cde", row_block, grad_proj, preferred_element_type=wide_type),
        matmul_tn(attended, grad_branch),
    )
    vector_grads = (
        column_sum(grad_proj[0]),
        column_sum(grad_proj[2]),
        column_sum(grad_branch),
        grad_gain,
        grad_shift,
    )
    return (grad_rows, weight_grads, vector_grads)


def ffn_forward(hidden, w_in, w_out, vectors):
    bias_in, bias_out, norm_gain, norm_shift = vectors
    low_hidden = hidden.astype(low_type)
    inner_act = matmul(low_hidden, w_in) + bias_in
    active = gelu_exact(inner_act).astype(low_type)
    summed = hidden + matmul(active, w_out) + bias_out
    return (norm_rows(summed, norm_gain, norm_shift), (low_hidden, inner_act, active, summed))


def ffn_backward(w_in, w_out, vectors, saved_fwd, upstream):
    low_hidden, inner_act, active, summed = saved_fwd
    grad_sum, grad_gain, grad_shift = norm_back(summed, vectors[2], vectors[3], upstream)
    grad_branch = grad_sum.astype(low_type)
    unused, pullback = jax.vjp(gelu_exact, inner_act)
    grad_inner = pullback(matmul_nt(grad_branch, w_out))[0].astype(low_type)
    grad_hidden = grad_sum + matmul_nt(grad_inner, w_in)
    weight_grads = (matmul_tn(low_hidden, grad_inner), matmul_tn(active, grad_branch))
    vector_grads = (column_sum(grad_inner), column_sum(grad_branch), grad_gain, grad_shift)
    return (grad_hidden, weight_grads, vector_grads)


def cross_forward(hidden, memory, src_len, w_query, w_out, vectors):
    bias_q, bias_v, bias_o, norm_gain, norm_shift = vectors
    low_hidden = hidden.astype(low_type)
    queries = (matmul(low_hidden, w_query) + bias_q).astype(low_type)
    allowed = key_mask(hidden.shape[0], memory.shape[1], src_len, False)
    attended, log_total = attend_forward(queries, memory[0], memory[1], allowed)
    attended = (attended + bias_v).astype(low_type)
    summed = hidden + matmul(attended, w_out) + bias_o
    return (
        norm_rows(summed, norm_gain, norm_shift),
        (low_hidden, queries, log_total, attended, summed),
    )


def cross_backward(memory, src_len, w_query, w_out, vectors, saved_fwd, upstream):
    low_hidden, queries, log_total, attended, summed = saved_fwd
    grad_sum, grad_gain, grad_shift = norm_back(summed, vectors[3], vectors[4], upstream)
    grad_branch = grad_sum.astype(low_type)
    grad_attended = matmul_nt(grad_branch, w_out).astype(low_type)
    allowed = key_mask(queries.shape[0], memory.shape[1], src_len, False)
    grad_q, grad_k, grad_v = attend_backward(
        queries, memory[0], memory[1], allowed, log_total, grad_attended
    )
    grad_query = grad_q.astype(low_type)
    grad_memory = jnp.stack([grad_k, grad_v]).astype(low_type)
    grad_hidden = grad_sum + matmul_nt(grad_query, w_query)
    weight_grads = (matmul_tn(low_hidden, grad_query), matmul_tn(attended, grad_branch))
    vector_grads = (
        column_sum(grad_query),
        column_sum(grad_attended),
        column_sum(grad_branch),
        grad_gain,
        grad_shift,
    )
    return (grad_hidden, grad_memory, weight_grads, vector_grads)


def self_vectors(gain_rows, bias_rows, decoder):
    base_row = 10 if decoder else 0
    gain_row = 2 if decoder else 0
    return (
        bias_rows[base_row],
        bias_rows[base_row + 1],
        bias_rows[base_row + 2],
        gain_rows[gain_row],
        bias_rows[base_row + 3],
    )


def ffn_vectors(gain_rows, bias_rows, decoder):
    base_row = 18 if decoder else 4
    gain_row = 4 if decoder else 1
    return (
        bias_rows[base_row : base_row + 4].reshape(-1),
        bias_rows[base_row + 4],
        gain_rows[gain_row],
        bias_rows[base_row + 5],
    )


def cross_vectors(gain_rows, bias_rows):
    return (bias_rows[14], bias_rows[15], bias_rows[16], gain_rows[3], bias_rows[17])


def self_plan(decoder, vector_grads):
    base_row = 10 if decoder else 0
    gain_row = 2 if decoder else 0
    return (
        ("biases", base_row, vector_grads[0]),
        ("biases", base_row + 1, vector_grads[1]),
        ("biases", base_row + 2, vector_grads[2]),
        ("gains", gain_row, vector_grads[3]),
        ("biases", base_row + 3, vector_grads[4]),
    )


def ffn_plan(decoder, vector_grads):
    base_row = 18 if decoder else 4
    gain_row = 4 if decoder else 1
    return (
        ("biases", base_row, vector_grads[0]),
        ("biases", base_row + 4, vector_grads[1]),
        ("gains", gain_row, vector_grads[2]),
        ("biases", base_row + 5, vector_grads[3]),
    )


def cross_plan(vector_grads):
    return (
        ("biases", 14, vector_grads[0]),
        ("biases", 15, vector_grads[1]),
        ("biases", 16, vector_grads[2]),
        ("gains", 3, vector_grads[3]),
        ("biases", 17, vector_grads[4]),
    )


def accumulate(totals, weight_names, weight_grads, vector_plan):
    merged = dict(totals)
    for key_name, tensor in zip(weight_names, weight_grads):
        merged[key_name] = merged[key_name] + tensor
    for table_name, row_at, tensor in vector_plan:
        table_now = merged[table_name]
        row_block = tensor.reshape(-1, table_now.shape[1])
        merged[table_name] = table_now.at[row_at : row_at + row_block.shape[0]].add(row_block)
    return merged


def updated(progress, key_name, position, tensor):
    copied = dict(progress)
    copied[key_name] = [
        tensor if slot_index == position else entry_now
        for slot_index, entry_now in enumerate(progress[key_name])
    ]
    return copied


def with_totals(progress, totals):
    copied = dict(progress)
    copied["totals"] = totals
    return copied


def forward_pass(tensor):
    return jax.tree.map(
        lambda part, own: part.astype(own.dtype), shifted(as_sent(tensor), "stream", 1), tensor
    )


def backward_pass(tensor):
    return jax.tree.map(
        lambda part, own: part.astype(own.dtype), shifted(as_sent(tensor), "stream", -1), tensor
    )


def keep_same(progress):
    return progress


def plain_body(
    inputs,
    lengths,
    cotangent,
    attn_in,
    attn_out,
    cross_first,
    cross_second,
    ffn_in,
    ffn_out,
    gains,
    biases,
):
    own_rows = inputs[0]
    model_width = own_rows.shape[1]
    hidden_width = ffn_in.shape[2]
    head_count = model_width // HDIM
    row_sizes = (SHORT, LONG)
    bucket_spans = ((0, SHORT), (SHORT, SHORT + LONG))
    row_pieces = [own_rows[start_row:stop_row] for start_row, stop_row in bucket_spans]
    grad_pieces = [
        cotangent[start_row:stop_row].astype(wide_type) for start_row, stop_row in bucket_spans
    ]
    src_lens = [lengths[0, 0, bucket_idx] for bucket_idx in range(2)]
    tgt_lens = [lengths[1, 0, bucket_idx] for bucket_idx in range(2)]
    w_proj = attn_in[0]
    w_attn_out = attn_out[0]
    w_first = cross_first[0]
    w_second = cross_second[0]
    w_ffn_in = ffn_in[0]
    w_ffn_out = ffn_out[0]
    gain_rows = gains.astype(wide_type)
    bias_rows = biases.astype(wide_type)
    enc_self = self_vectors(gain_rows, bias_rows, False)
    enc_ffn = ffn_vectors(gain_rows, bias_rows, False)
    dec_self = self_vectors(gain_rows, bias_rows, True)
    dec_ffn = ffn_vectors(gain_rows, bias_rows, True)
    dec_cross = cross_vectors(gain_rows, bias_rows)
    is_decoder = lax.axis_index("stream") == 1

    def blank_self(size_rows):
        return (
            jnp.zeros((3, size_rows, model_width), low_type),
            jnp.zeros((head_count, size_rows, 1), wide_type),
            jnp.zeros((size_rows, model_width), low_type),
            jnp.zeros((size_rows, model_width), wide_type),
        )

    def blank_ffn(size_rows):
        return (
            jnp.zeros((size_rows, model_width), low_type),
            jnp.zeros((size_rows, hidden_width), wide_type),
            jnp.zeros((size_rows, hidden_width), low_type),
            jnp.zeros((size_rows, model_width), wide_type),
        )

    def blank_cross(size_rows):
        return (
            jnp.zeros((size_rows, model_width), low_type),
            jnp.zeros((size_rows, model_width), low_type),
            jnp.zeros((head_count, size_rows, 1), wide_type),
            jnp.zeros((size_rows, model_width), low_type),
            jnp.zeros((size_rows, model_width), wide_type),
        )

    progress = {
        "out": [jnp.zeros((size_rows, model_width), low_type) for size_rows in row_sizes],
        "grad_in": [jnp.zeros((size_rows, model_width), wide_type) for size_rows in row_sizes],
        "send": [jnp.zeros((2, size_rows, model_width), low_type) for size_rows in row_sizes],
        "memory": [jnp.zeros((2, size_rows, model_width), low_type) for size_rows in row_sizes],
        "grad_send": [jnp.zeros((2, size_rows, model_width), low_type) for size_rows in row_sizes],
        "grad_memory": [
            jnp.zeros((2, size_rows, model_width), low_type) for size_rows in row_sizes
        ],
        "mid": [jnp.zeros((size_rows, model_width), wide_type) for size_rows in row_sizes],
        "grad_mid": [jnp.zeros((size_rows, model_width), wide_type) for size_rows in row_sizes],
        "totals": {
            "proj": jnp.zeros(w_proj.shape, wide_type),
            "attn_out": jnp.zeros(w_attn_out.shape, wide_type),
            "first": jnp.zeros(w_first.shape, wide_type),
            "second": jnp.zeros(w_second.shape, wide_type),
            "ffn_in": jnp.zeros(w_ffn_in.shape, wide_type),
            "ffn_out": jnp.zeros(w_ffn_out.shape, wide_type),
            "gains": jnp.zeros(gains.shape, wide_type),
            "biases": jnp.zeros(biases.shape, wide_type),
        },
    }
    progress["self_saved"] = [blank_self(size_rows) for size_rows in row_sizes]
    progress["ffn_saved"] = [blank_ffn(size_rows) for size_rows in row_sizes]
    progress["cross_saved"] = [blank_cross(size_rows) for size_rows in row_sizes]

    def encoder_core(micro_idx):
        h_one, self_saved = self_forward(
            row_pieces[micro_idx], src_lens[micro_idx], False, w_proj, w_attn_out, enc_self
        )
        encoded, ffn_saved = ffn_forward(h_one, w_ffn_in, w_ffn_out, enc_ffn)
        return (encoded.astype(low_type), self_saved, ffn_saved)

    def encoder_forward_step(progress, micro_idx):
        low_memory, self_saved, ffn_saved = encoder_core(micro_idx)
        memory = jnp.stack([matmul(low_memory, w_first), matmul(low_memory, w_second)]).astype(
            low_type
        )
        progress = updated(progress, "out", micro_idx, low_memory)
        progress = updated(progress, "send", micro_idx, memory)
        progress = updated(progress, "self_saved", micro_idx, self_saved)
        progress = updated(progress, "ffn_saved", micro_idx, ffn_saved)
        return progress

    def decoder_head(micro_idx):
        return self_forward(
            row_pieces[micro_idx], tgt_lens[micro_idx], True, w_proj, w_attn_out, dec_self
        )

    def decoder_tail(mid_rows, memory, micro_idx):
        crossed, cross_saved = cross_forward(
            mid_rows, memory, src_lens[micro_idx], w_first, w_second, dec_cross
        )
        decoded, ffn_saved = ffn_forward(crossed, w_ffn_in, w_ffn_out, dec_ffn)
        return (decoded, cross_saved, ffn_saved)

    def decoder_head_step(progress, micro_idx):
        mid_rows, self_saved = decoder_head(micro_idx)
        progress = updated(progress, "mid", micro_idx, mid_rows)
        progress = updated(progress, "self_saved", micro_idx, self_saved)
        return progress

    def decoder_tail_step(progress, micro_idx):
        decoded, cross_saved, ffn_saved = decoder_tail(
            progress["mid"][micro_idx], progress["memory"][micro_idx], micro_idx
        )
        progress = updated(progress, "out", micro_idx, decoded.astype(low_type))
        progress = updated(progress, "cross_saved", micro_idx, cross_saved)
        progress = updated(progress, "ffn_saved", micro_idx, ffn_saved)
        return progress

    def decoder_back_step(progress, micro_idx):
        memory = progress["memory"][micro_idx]
        self_saved = progress["self_saved"][micro_idx]
        cross_saved = progress["cross_saved"][micro_idx]
        ffn_saved = progress["ffn_saved"][micro_idx]
        grad_h_two, ffn_w, ffn_v = ffn_backward(
            w_ffn_in, w_ffn_out, dec_ffn, ffn_saved, grad_pieces[micro_idx]
        )
        grad_h_one, grad_memory, cross_w, cross_v = cross_backward(
            memory, src_lens[micro_idx], w_first, w_second, dec_cross, cross_saved, grad_h_two
        )
        grad_rows, self_w, self_v = self_backward(
            row_pieces[micro_idx],
            tgt_lens[micro_idx],
            True,
            w_proj,
            w_attn_out,
            dec_self,
            self_saved,
            grad_h_one,
        )
        totals = accumulate(
            progress["totals"],
            ("ffn_in", "ffn_out", "first", "second", "proj", "attn_out"),
            ffn_w + cross_w + self_w,
            ffn_plan(True, ffn_v) + cross_plan(cross_v) + self_plan(True, self_v),
        )
        progress = updated(progress, "grad_in", micro_idx, grad_rows)
        progress = updated(progress, "grad_send", micro_idx, grad_memory)
        return with_totals(progress, totals)

    def encoder_top_step(progress, micro_idx):
        low_memory = progress["out"][micro_idx]
        ffn_saved = progress["ffn_saved"][micro_idx]
        grad_memory = progress["grad_memory"][micro_idx]
        grad_encoded = matmul_nt(grad_memory[0], w_first) + matmul_nt(grad_memory[1], w_second)
        grad_h_one, ffn_w, ffn_v = ffn_backward(
            w_ffn_in, w_ffn_out, enc_ffn, ffn_saved, grad_encoded
        )
        projections = (matmul_tn(low_memory, grad_memory[0]), matmul_tn(low_memory, grad_memory[1]))
        totals = accumulate(
            progress["totals"],
            ("first", "second", "ffn_in", "ffn_out"),
            projections + ffn_w,
            ffn_plan(False, ffn_v),
        )
        progress = updated(progress, "grad_mid", micro_idx, grad_h_one)
        return with_totals(progress, totals)

    def encoder_bottom_step(progress, micro_idx):
        self_saved = progress["self_saved"][micro_idx]
        grad_rows, self_w, self_v = self_backward(
            row_pieces[micro_idx],
            src_lens[micro_idx],
            False,
            w_proj,
            w_attn_out,
            enc_self,
            self_saved,
            progress["grad_mid"][micro_idx],
        )
        totals = accumulate(
            progress["totals"], ("proj", "attn_out"), self_w, self_plan(False, self_v)
        )
        progress = updated(progress, "grad_in", micro_idx, grad_rows)
        return with_totals(progress, totals)

    def enc_zero(progress):
        return encoder_forward_step(progress, 0)

    def dec_zero(progress):
        return decoder_head_step(progress, 0)

    def enc_one(progress):
        return encoder_forward_step(progress, 1)

    def dec_one(progress):
        return decoder_tail_step(decoder_head_step(progress, 1), 0)

    def dec_two(progress):
        return decoder_back_step(decoder_tail_step(progress, 1), 1)

    def enc_three(progress):
        return encoder_bottom_step(encoder_top_step(progress, 1), 1)

    def dec_three(progress):
        return decoder_back_step(progress, 0)

    def enc_four(progress):
        return encoder_top_step(progress, 0)

    def enc_five(progress):
        return encoder_bottom_step(progress, 0)

    progress = lax.cond(is_decoder, dec_zero, enc_zero, progress)
    progress = updated(progress, "memory", 0, forward_pass(progress["send"][0]))
    progress = lax.cond(is_decoder, dec_one, enc_one, progress)
    progress = updated(progress, "memory", 1, forward_pass(progress["send"][1]))
    progress = lax.cond(is_decoder, dec_two, keep_same, progress)
    progress = updated(progress, "grad_memory", 1, backward_pass(progress["grad_send"][1]))
    progress = lax.cond(is_decoder, dec_three, enc_three, progress)
    progress = updated(progress, "grad_memory", 0, backward_pass(progress["grad_send"][0]))
    progress = lax.cond(is_decoder, keep_same, enc_four, progress)
    progress = lax.cond(is_decoder, keep_same, enc_five, progress)
    totals = progress["totals"]
    owned = (
        lax.psum_scatter(totals["proj"], "dp", scatter_dimension=1, tiled=True),
        lax.psum_scatter(totals["attn_out"], "dp", scatter_dimension=0, tiled=True),
        lax.psum_scatter(totals["first"], "dp", scatter_dimension=0, tiled=True),
        lax.psum_scatter(totals["second"], "dp", scatter_dimension=0, tiled=True),
        lax.psum_scatter(totals["ffn_in"], "dp", scatter_dimension=0, tiled=True),
        lax.psum_scatter(totals["ffn_out"], "dp", scatter_dimension=0, tiled=True),
        lax.psum_scatter(totals["gains"], "dp", scatter_dimension=1, tiled=True),
        lax.psum_scatter(totals["biases"], "dp", scatter_dimension=1, tiled=True),
    )
    owned_gains, owned_biases = lax.psum((owned[6], owned[7]), "stream")
    layer_out = jnp.concatenate(progress["out"], axis=0)[None]
    grad_inputs = jnp.concatenate(progress["grad_in"], axis=0)[None]
    return (
        layer_out,
        grad_inputs,
        owned[0][None],
        owned[1][None],
        owned[2][None],
        owned[3][None],
        owned[4][None],
        owned[5][None],
        owned_gains,
        owned_biases,
    )


def fused_body(inputs, lengths, cotangent, attn_in, attn_out, cross_first, cross_second, ffn_in, ffn_out, gains, biases):
    nz = lax.axis_size("dp") // 4
    vec = jnp.concatenate([gains, biases, jnp.zeros((3, gains.shape[1]), gains.dtype)]).astype(f32)
    bias_in = jnp.stack([biases[4:8].reshape(-1), biases[18:22].reshape(-1)]).astype(f32)
    rows, grad, s_out, s_in, s_second, s_first, s_attn, s_proj, vec_sum = whole_step(
        nz, lengths.reshape(-1), vec, bias_in, inputs[0], cotangent, attn_in[0], attn_out[0],
        cross_first[0], cross_second[0], ffn_in[0], ffn_out[0])
    own_cols = lax.dynamic_slice_in_dim(vec_sum, lax.axis_index("dp") * PIECE, PIECE, 1)
    return (rows[None], grad[None], s_proj[None], s_attn[None], s_first[None], s_second[None],
            s_in[None], s_out[None], own_cols[:5], own_cols[5:29])


def solution(mesh):
    def body(*args):
        width = args[0].shape[2]
        fits = mesh.shape["dp"] * PIECE == width and args[0].shape[1] == ROWS and args[7].shape[2] == 4 * width
        return (fused_body if fits else plain_body)(*args)
    return jax.shard_map(
        body,
        mesh=mesh,
        in_specs=(
            P("stream", "dp", None),
            P(None, "dp", None),
            P("dp", None),
            P("stream", None, None, None),
            P("stream", None, None),
            P("stream", None, None),
            P("stream", None, None),
            P("stream", None, None),
            P("stream", None, None),
            P(),
            P(),
        ),
        out_specs=(
            P("stream", "dp", None),
            P("stream", "dp", None),
            P("stream", None, "dp", None),
            P("stream", "dp", None),
            P("stream", "dp", None),
            P("stream", "dp", None),
            P("stream", "dp", None),
            P("stream", "dp", None),
            P(None, "dp"),
            P(None, "dp"),
        ),
        check_vma=False,
    )
```

```python
import functools

import jax
import jax.numpy as jnp
from jax import lax
from jax.experimental import pallas as pl
from jax.experimental.pallas import tpu as pltpu
from jax.sharding import PartitionSpec as P

HDIM = 64
SHORT = 128
LONG = 256
ROWS = SHORT + LONG
PIECE = 48
PIECES = 14
SEND_SLOTS = 8
WX_CHUNKS = 4
MESH = pl.DeviceIdType.MESH
bf16, f32 = jnp.bfloat16, jnp.float32
VMEM_LIMIT = 64 << 20


def dot_nn(a, b):
    return jnp.dot(a, b, preferred_element_type=f32)


def dot_nt(a, b):
    return lax.dot_general(a, b, (((1,), (1,)), ((), ())), preferred_element_type=f32)


def dot_tn(a, b):
    return lax.dot_general(a, b, (((0,), (0,)), ((), ())), preferred_element_type=f32)


def cols(j, width):
    return pl.ds(pl.multiple_of(j * width, width), width)


def step_kernel(
    width, hidden,
    lengths, gains, biases, x_hbm, cot_hbm, wproj_hbm, wo_hbm, wfirst_hbm, wsecond_hbm, win_hbm, wout_hbm,
    out_rows, out_grad, out_own, out_part, out_vec,
    vec, bias_in, wproj, wo, wfirst, wsecond, win, wout, wx,
    xb, up, mem, obuf, hlow, dg, kv, acc, grad, hw, u_self, u_cross, u_ffn, gr, grp, lt, ltp, one_send, one_recv, two_recv, gmem, vg, vbuf,
    load_sem, wx_send, wx_recv, mem_send, mem_recv, gm_send, gm_recv, gk_send, gk_recv, lt_send, lt_recv, gr_send, gr_recv,
    sem_send, sem_recv, own_sem, io_sem, v_send, v_recv,
):
    st = lax.axis_index("stream")
    me = lax.axis_index("dp")
    z, y, c = me // 4, (me // 2) % 2, me % 2
    is_dec = st == 1
    is_enc = st == 0
    core_id = {"dp": z * 4 + y * 2 + (1 - c)}
    y_id = {"dp": z * 4 + (1 - y) * 2 + c}
    x_id = {"stream": 1 - st}
    tiles = width // 256
    slots = hidden // width

    zh, zl = z // 2, z % 2

    def z_id(other):
        return {"dp": other * 4 + y * 2 + c}
    near_id = z_id(zh * 2 + 1 - zl)
    far_id = z_id((1 - zh) * 2 + zl)

    def remote(src, dst, ss, rs, dev):
        return pltpu.make_async_remote_copy(
            src_ref=src, dst_ref=dst, send_sem=ss, recv_sem=rs, device_id=dev, device_id_type=MESH)

    loads = [
        pltpu.make_async_copy(src, dst, load_sem.at[i])
        for i, (src, dst) in enumerate((
            (x_hbm, xb), (wproj_hbm, wproj), (wo_hbm, wo), (win_hbm, win), (wout_hbm, wout),
            (wfirst_hbm, wfirst), (wsecond_hbm, wsecond)))
    ]
    cot_load = pltpu.make_async_copy(cot_hbm, up, load_sem.at[7])
    loads[0].start()
    loads[1].start()

    barrier = pltpu.get_barrier_semaphore()
    peers = [core_id, y_id, x_id, near_id, far_id]
    for p in peers:
        pl.semaphore_signal(barrier, inc=1, device_id=p, device_id_type=MESH)

    lens = [lengths[i // 2, 0, i % 2] for i in range(4)]
    own_lens = [jnp.where(is_dec, lens[2 + i], lens[i]) for i in range(2)]
    vec[pl.ds(0, 5), :] = gains[...].astype(f32)
    vec[pl.ds(5, 24), :] = biases[...].astype(f32)
    for i in range(slots):
        for s in range(2):
            bias_in[pl.ds(s, 1), pl.ds(i * width, width)] = vec[pl.ds(9 + 14 * s + i, 1), :]
    vg[...] = jnp.zeros_like(vg)
    pl.semaphore_wait(barrier, len(peers))

    half = width // 2
    chunk = half // WX_CHUNKS
    quarter = y * 2 + c
    far = (1 - y) * 2 + c

    def wx_from(source, h):
        return remote(source.at[pl.ds(c * half + h * chunk, chunk)], wx.at[quarter, pl.ds(h * chunk, chunk)],
                      wx_send.at[h], wx_recv.at[h], x_id)

    def wx_pass(at, h, sem, dev):
        ref = wx.at[at, pl.ds(h * chunk, chunk)]
        return remote(ref, ref, wx_send.at[sem * WX_CHUNKS + h], wx_recv.at[sem * WX_CHUNKS + h], dev)
    wx_first = [wx_from(wfirst_hbm, h) for h in range(WX_CHUNKS)]
    wx_y = [wx_pass(quarter, h, 1, y_id) for h in range(WX_CHUNKS)]
    wx_near = [wx_pass(quarter, h, 2, core_id) for h in range(WX_CHUNKS)]
    wx_far = [wx_pass(far, h, 3, core_id) for h in range(WX_CHUNKS)]

    @pl.when(is_enc & (y == 0))
    def _():
        for h in range(WX_CHUNKS):
            wx_first[h].start()

    @pl.when(is_enc & (y == 1))
    def _():
        for h in range(WX_CHUNKS):
            wx_from(wsecond_hbm, h).start()
    loads[0].wait()
    loads[1].wait()
    for cp in loads[2:]:
        cp.start()

    @pl.when(is_dec)
    def _():
        cot_load.start()

    lt_copy = [remote(lt.at[i, :, :, :, 1 - c], ltp.at[i], lt_send.at[i], lt_recv.at[i], core_id) for i in range(9)]
    gr_copy = [remote(gr.at[i], grp.at[i], gr_send.at[i], gr_recv.at[i], core_id) for i in range(11)]
    buckets = ((0, SHORT), (SHORT, LONG))
    short, long, both = (0,), (1,), (0, 1)

    def span(bs):
        return buckets[bs[0]][0], sum(buckets[b][1] for b in bs)

    def at_rows(bs):
        return pl.ds(*span(bs))
    mem_copy = [remote(xb.at[at_rows((b,))], mem.at[at_rows((b,))], mem_send.at[b], mem_recv.at[b], x_id) for b in range(2)]
    gm_copy = [remote(gmem.at[at_rows((b,))], up.at[at_rows((b,))], gm_send.at[b], gm_recv.at[b], x_id) for b in range(2)]
    gk_copy = [remote(kv.at[0], gr.at[6], gk_send.at[0], gk_recv.at[0], x_id),
               remote(kv.at[1], gr.at[5], gk_send.at[1], gk_recv.at[1], x_id)]

    def row_loop(bs, block, body, unroll=1):
        r0, n = span(bs)

        def step(i, carry):
            body(pl.ds(pl.multiple_of(r0 + i * block, block), block))
            return carry
        lax.fori_loop(0, n // block, step, 0, unroll=unroll)

    def vrow(r):
        return vec[pl.ds(r, 1), :]

    def transposed(i, bs, ref):
        r0, n = span(bs)
        lt[i, :, :, :, :, :, pl.ds(r0, n)] = ref[pl.ds(r0, n), :].T.reshape(2, 2, 2, 2, PIECE, n)

    def transposed_active(bs):
        r0, n = span(bs)

        def step(j, carry):
            turned = gr[1 + j, pl.ds(r0, n), :].T.reshape(2, 2, 4, PIECE, n)
            for k in range(4):
                lt[k, j // 2, j % 2, :, :, :, pl.ds(r0, n)] = turned[:, :, k]
            return carry
        lax.fori_loop(0, slots, step, 0)

    def col_sum(slot, row):
        def step(i, carry):
            block = slot[pl.ds(pl.multiple_of(i * 64, 64), 64), :].astype(f32)
            return carry + jnp.sum(block.reshape(8, 8, width), axis=0)
        total = lax.fori_loop(0, ROWS // 64, step, jnp.zeros((8, width), f32))
        vg[pl.ds(row, 1), :] = jnp.sum(total, axis=0, keepdims=True)

    def norm_forward(bs, residual, sum_ref, add_bias, gain, shift, out_low, out_wide):
        def body(rows):
            u = residual[rows, :].astype(f32) + acc[rows, :] + vrow(add_bias)
            sum_ref[rows, :] = u
            centre = u - jnp.mean(u, axis=-1, keepdims=True)
            spread = jnp.mean(centre * centre, axis=-1, keepdims=True)
            h = centre * lax.rsqrt(spread + 1e-05) * vrow(gain) + vrow(shift)
            if out_wide is not None:
                out_wide[rows, :] = h
            out_low[rows, :] = h.astype(bf16)
        row_loop(bs, 32, body, 4)

    def norm_backward(bs, sum_ref, source, gain, shift, out_wide, slot):
        r0, n = span(bs)

        def step(i, carry):
            rows = pl.ds(pl.multiple_of(r0 + i * 32, 32), 32)
            r = source[rows, :].astype(f32)
            u = sum_ref[rows, :]
            centre = u - jnp.mean(u, axis=-1, keepdims=True)
            spread = jnp.mean(centre * centre, axis=-1, keepdims=True)
            inv = lax.rsqrt(spread + 1e-05)
            uhat = centre * inv
            t = r * vrow(gain)
            gu = (t - jnp.mean(t, axis=-1, keepdims=True) - uhat * jnp.mean(t * uhat, axis=-1, keepdims=True)) * inv
            out_wide[rows, :] = gu
            slot[rows, :] = gu.astype(bf16)
            return (carry[0] + jnp.sum((r * uhat).reshape(4, 8, width), axis=0),
                    carry[1] + jnp.sum(r.reshape(4, 8, width), axis=0))
        zero = jnp.zeros((8, width), f32)
        total = lax.fori_loop(0, n // 32, step, (zero, zero), unroll=4)
        for row, part in ((gain, total[0]), (shift, total[1])):
            vg[pl.ds(row, 1), :] = vg[pl.ds(row, 1), :] + jnp.sum(part, axis=0, keepdims=True)

    def masked_scores(q_half, k2, n, length, diagonal):
        s = dot_nt(q_half, k2) * (HDIM ** -0.5)
        column = lax.broadcasted_iota(jnp.int32, (n, n), 1)
        row = lax.broadcasted_iota(jnp.int32, (n, n), 0)
        return jnp.where((column < length) & (column <= row + diagonal), s, -1e30)

    def softmax(s):
        e = jnp.exp(s - jnp.max(s, axis=-1, keepdims=True))
        return e * (1.0 / jnp.sum(e, axis=-1, keepdims=True))

    def halves(n):
        lane = lax.broadcasted_iota(jnp.int32, (n, 2 * HDIM), 1)
        return lane < HDIM

    def head_loop(bs, body):
        pairs = {short: 3, long: 2, both: 1}[bs]

        def step(p, carry):
            body([(b, pl.ds(pl.multiple_of((p * pairs + i) * 2 * HDIM, 2 * HDIM), 2 * HDIM)) for b in bs for i in range(pairs)])
            return carry
        lax.fori_loop(0, width // (2 * HDIM * pairs), step, 0)

    def attend_forward(bs, q_ref, k_ref, v_ref, lengths_at, diagonal, bias_row, out_ref):
        def body(units):
            work = []
            for b, at in units:
                r0, n = buckets[b]
                rows = pl.ds(r0, n)
                q2, k2 = q_ref[rows, at], k_ref[rows, at]
                first = halves(n)
                for lanes in (first, ~first):
                    work.append(masked_scores(jnp.where(lanes, q2, jnp.zeros_like(q2)), k2, n, lengths_at[b], diagonal))
            work = [softmax(s).astype(bf16) for s in work]
            work = [dot_nn(prob, v_ref[pl.ds(*buckets[units[i // 2][0]]), units[i // 2][1]]) for i, prob in enumerate(work)]
            for i, (b, at) in enumerate(units):
                r0, n = buckets[b]
                att = jnp.where(halves(n), work[2 * i], work[2 * i + 1])
                if bias_row is not None:
                    att = att + vec[pl.ds(bias_row, 1), at]
                out_ref[pl.ds(r0, n), at] = att.astype(bf16)
        head_loop(bs, body)

    def attend_backward(bs, q_ref, k_ref, v_ref, lengths_at, diagonal):
        scale = HDIM ** -0.5

        def body(units):
            scores, ups = [], []
            for b, at in units:
                r0, n = buckets[b]
                rows = pl.ds(r0, n)
                q2, k2, v2, go2 = q_ref[rows, at], k_ref[rows, at], v_ref[rows, at], obuf[rows, at]
                first = halves(n)
                zero = jnp.zeros_like(q2)
                for lanes in (first, ~first):
                    scores.append(masked_scores(jnp.where(lanes, q2, zero), k2, n, lengths_at[b], diagonal))
                    ups.append(dot_nt(jnp.where(lanes, go2, zero), v2))
            probs = [softmax(s) for s in scores]
            gs = [(p * (gp - jnp.sum(p * gp, axis=-1, keepdims=True))).astype(bf16) for p, gp in zip(probs, ups)]
            for i, (b, at) in enumerate(units):
                r0, n = buckets[b]
                rows = pl.ds(r0, n)
                q2, k2, go2 = q_ref[rows, at], k_ref[rows, at], obuf[rows, at]
                first = halves(n)
                two = (2 * i, 2 * i + 1)
                gv = [dot_tn(probs[u].astype(bf16), go2) for u in two]
                gq = [dot_nn(gs[u], k2) for u in two]
                gk = [dot_tn(gs[u], q2) for u in two]
                q_ref[rows, at] = (jnp.where(first, gq[0], gq[1]) * scale).astype(bf16)
                k_ref[rows, at] = (jnp.where(first, gk[0], gk[1]) * scale).astype(bf16)
                v_ref[rows, at] = jnp.where(first, gv[0], gv[1]).astype(bf16)
        head_loop(bs, body)

    q_ref, k_ref, v_ref = gr.at[8], gr.at[9], gr.at[10]
    diagonal = (1 - st) * 4096
    bias_at = 5 + 10 * st
    ffn_at = 13 + 14 * st
    ffn_gain = 1 + 3 * st

    def by_tiles(fn):
        def step(t, carry):
            fn(cols(t, 256))
            return carry
        lax.fori_loop(0, tiles, step, 0)

    def self_project(bs):
        rows = at_rows(bs)

        def project(i, carry):
            which, t = i // tiles, i % tiles
            at = cols(t, 256)
            value = dot_nn(xb[rows, :], wproj[which, :, at])
            bias = vec[pl.ds(bias_at + which // 2, 1), at] * jnp.where(which == 1, 0.0, 1.0)
            gr[8 + which, rows, at] = (value + bias).astype(bf16)
            return carry
        lax.fori_loop(0, 3 * tiles, project, 0)

    def self_output(bs):
        rows = at_rows(bs)

        def tile(at):
            acc[rows, at] = dot_nn(obuf[rows, :], wo[:, at])
        by_tiles(tile)
        norm_forward(bs, xb, u_self, bias_at + 2, 2 * st, bias_at + 3, hlow, grad)

    def ffn_forward(bs, residual):
        r0, n = span(bs)
        rows = pl.ds(r0, n)

        def ffn_slot(j, carry):
            def tile(t, carry2):
                at = cols(t, 256)
                wide = pl.ds(pl.multiple_of(j * width + t * 256, 256), 256)
                acc[rows, at] = dot_nn(hlow[rows, :], win[:, wide])

                def activate(block):
                    zv = acc[block, at] + bias_in[pl.ds(st, 1), wide]
                    cdf = 0.5 * (1.0 + lax.erf(zv * (0.5 ** 0.5)))
                    pdf = jnp.exp(-0.5 * zv * zv) * 0.3989422804014327
                    gr[1 + j, block, at] = (zv * cdf).astype(bf16)
                    dg[j, block, at] = (cdf + zv * pdf).astype(bf16)
                row_loop(bs, 64, activate)
                return carry2
            lax.fori_loop(0, tiles, tile, 0)
            return carry
        lax.fori_loop(0, slots, ffn_slot, 0)

        def ffn_out(at):
            total = dot_nn(gr[1, rows, :], wout[pl.ds(0, width), at])
            for j in range(1, slots):
                total = total + dot_nn(gr[1 + j, rows, :], wout[pl.ds(j * width, width), at])
            acc[rows, at] = total
        by_tiles(ffn_out)
        norm_forward(bs, residual, u_ffn, ffn_at, ffn_gain, ffn_at + 1, xb, None)

    def ffn_inner(bs, lo, hi):
        r0, n = span(bs)
        rows = pl.ds(r0, n)

        def ffn_inner_slot(j, carry):
            def tile(t, carry2):
                at = cols(t, 256)
                wide = pl.ds(pl.multiple_of(j * width + t * 256, 256), 256)
                acc[rows, at] = dot_nt(gr[0, rows, :], wout[wide, :])

                def scale(block):
                    gr[1 + j, block, at] = (acc[block, at] * dg[j, block, at].astype(f32)).astype(bf16)
                row_loop(bs, 64, scale)
                return carry2
            lax.fori_loop(0, tiles, tile, 0)
            if bs == long:
                remote(gr.at[1 + j], grp.at[1 + j], gr_send.at[1 + j], gr_recv.at[1 + j], core_id).start()
            return carry
        lax.fori_loop(lo, hi, ffn_inner_slot, 0)

    def ffn_input(bs):
        rows = at_rows(bs)

        def tile(at):
            total = grad[rows, at]
            for j in range(slots):
                total = total + dot_nt(gr[1 + j, rows, :], win[at, pl.ds(j * width, width)])
            grad[rows, at] = total
        by_tiles(tile)

    def cross_forward(bs):
        rows = at_rows(bs)

        def memory_kv(i, carry):
            which, t = i // tiles, i % tiles
            at = cols(t, 256)
            value = dot_nn(mem[rows, pl.ds(0, half)], wx[2 * which, :, at]) + dot_nn(mem[rows, pl.ds(half, half)], wx[2 * which + 1, :, at])
            kv[which, rows, at] = value.astype(bf16)
            return carry
        lax.fori_loop(0, 2 * tiles, memory_kv, 0)
        attend_forward(bs, gr.at[6], kv.at[0], kv.at[1], lens[:2], 4096, 20, obuf)

        def cross_out(at):
            acc[rows, at] = dot_nn(obuf[rows, :], wsecond[:, at])
        by_tiles(cross_out)
        norm_forward(bs, grad, u_cross, 21, 3, 22, hlow, hw)
        transposed(7, bs, obuf)

    def cross_backward(bs):
        rows = at_rows(bs)
        norm_backward(bs, u_cross, grad, 3, 22, hw, gr.at[5])

        def cross_up(at):
            obuf[rows, at] = dot_nt(gr[5, rows, :], wsecond[at, :]).astype(bf16)
        by_tiles(cross_up)
        attend_backward(bs, gr.at[6], kv.at[0], kv.at[1], lens[:2], 4096)

        def memory_half(h, carry):
            at = cols(h, half)
            gmem[rows, at] = (dot_nt(kv[0, rows, :], wx[h]) + dot_nt(kv[1, rows, :], wx[2 + h])).astype(bf16)
            return carry
        lax.fori_loop(0, 2, memory_half, 0)
        gm_copy[bs[0]].start()

    def cross_input(at):
        grad[:, at] = hw[:, at] + dot_nt(gr[6], wfirst[at, :])

    def first_copy(i, z_first):
        return remote(one_send.at[i % SEND_SLOTS], one_recv.at[i], sem_send.at[i, 0], sem_recv.at[i, 0], near_id if z_first else y_id)

    def second_copy(i, z_first):
        source = one_recv.at[i, 1 - zh] if z_first else one_recv.at[i, :, 1 - zl]
        return remote(source, two_recv.at[i], sem_send.at[i, 1], sem_recv.at[i, 1], far_id if z_first else near_id)

    def third_copy(i, z_first):
        source = two_recv.at[i, 1 - y if z_first else 1 - zh]
        return remote(source, out_part.at[i], sem_send.at[i, 2], sem_recv.at[i, 2], y_id if z_first else far_id)

    def own_copy(i, z_first):
        return pltpu.make_async_copy(two_recv.at[i, y if z_first else zh], out_own.at[i], own_sem.at[i])

    def product(left, slot, z_first, other, at):
        if z_first:
            zz = 1 - zl if other else zl
            mine, theirs = lt[left, :, zz, :, c], ltp[left, :, zz]
        else:
            yy = 1 - y if other else y
            mine, theirs = lt[left, :, :, yy, c], ltp[left, :, :, yy]
        shape = (4 * PIECE, ROWS)
        return dot_nn(mine.reshape(shape), gr[slot, :, at]) + dot_nn(theirs.reshape(shape), grp[slot, :, at])

    def send_piece(i, left, slot, z_first=False):
        def tile(at):
            one_send[i % SEND_SLOTS, :, :, :, at] = product(left, slot, z_first, True, at).astype(bf16).reshape(2, 2, PIECE, 256)
        by_tiles(tile)
        first_copy(i, z_first).start()

    def keep_piece(i, left, slot, z_first=False):
        first_copy(i, z_first).wait()

        def tile(at):
            total = one_recv[i, :, :, :, at].reshape(4 * PIECE, 256).astype(f32) + product(left, slot, z_first, False, at)
            one_recv[i, :, :, :, at] = total.astype(bf16).reshape(2, 2, PIECE, 256)
        by_tiles(tile)
        second_copy(i, z_first).start()

    def pass_piece(i, z_first=False):
        second_copy(i, z_first).wait()
        for k in range(2):
            mine = one_recv[i, zh, k] if z_first else one_recv[i, k, zl]
            two_recv[i, k] = (two_recv[i, k].astype(f32) + mine.astype(f32)).astype(bf16)
        third_copy(i, z_first).start()
        own_copy(i, z_first).start()

    def loop(lo, hi, fn):
        def step(i, carry):
            fn(i)
            return carry
        lax.fori_loop(lo, hi, step, 0)

    def wait_active():
        for i in range(4):
            lt_copy[i].wait()
        gr_copy[0].wait()

    def first_sends():
        loop(2, 3, lambda i: send_piece(i, i, 0))
        loop(0, 1, lambda i: send_piece(i, i, 0, True))
        loop(3, 4, lambda i: send_piece(i, i, 0))
        loop(1, 2, lambda i: send_piece(i, i, 0, True))

    @pl.when(is_enc)
    def _():
        again = pltpu.make_async_copy(x_hbm, mem, load_sem.at[8])
        again.start()
        for bs in (short, long):
            self_project(bs)
            attend_forward(bs, q_ref, k_ref, v_ref, own_lens, diagonal, None, obuf)
            if bs == short:
                loads[2].wait()
            self_output(bs)
            if bs == short:
                loads[3].wait()
                loads[4].wait()
            ffn_forward(bs, grad)
            mem_copy[bs[0]].start()
        transposed_active(both)
        for k in range(4):
            lt_copy[k].start()
        again.wait()
        for i, ref in ((4, mem), (5, obuf), (6, hlow), (7, xb)):
            transposed(i, both, ref)
            lt_copy[i].start()
        loads[5].wait()
        loads[6].wait()
        for bs in (short, long):
            gm_copy[bs[0]].wait_recv()
            norm_backward(bs, u_ffn, up, ffn_gain, ffn_at + 1, grad, gr.at[0])
            if bs == short:
                ffn_inner(bs, 0, slots)
                ffn_input(bs)
        gr_copy[0].start()
        ffn_inner(long, 0, 2)
        wait_active()
        first_sends()
        ffn_inner(long, 2, slots)
        ffn_input(long)

    @pl.when(is_dec)
    def _():
        self_project(both)
        transposed(4, both, xb)
        lt_copy[4].start()

        def wx_forward(h):
            wx_first[h].wait_recv()
            wx_y[h].start()
            wx_near[h].start()
        wx_forward(0)
        attend_forward(both, q_ref, k_ref, v_ref, own_lens, diagonal, None, obuf)
        wx_forward(1)
        loads[2].wait()
        self_output(both)
        wx_forward(2)
        for cp in loads[3:]:
            cp.wait()

        def cross_query(at):
            gr[6, :, at] = (dot_nn(hlow[...], wfirst[:, at]) + vec[pl.ds(19, 1), at]).astype(bf16)
        by_tiles(cross_query)
        wx_forward(3)
        transposed(5, both, obuf)
        lt_copy[5].start()
        transposed(8, both, hlow)
        lt_copy[8].start()
        cot_load.wait()
        for h in range(WX_CHUNKS):
            wx_y[h].wait()
            wx_far[h].start()
        for h in range(WX_CHUNKS):
            wx_near[h].wait()
            wx_far[h].wait()
        for bs in (short, long):
            mem_copy[bs[0]].wait_recv()
            cross_forward(bs)
            ffn_forward(bs, hw)
            transposed_active(bs)
            norm_backward(bs, u_ffn, up, ffn_gain, ffn_at + 1, grad, gr.at[0])
            ffn_inner(bs, 0, slots)
            ffn_input(bs)
            cross_backward(bs)
        gr_copy[0].start()
        for k in range(4):
            lt_copy[k].start()
        transposed(6, both, hlow)
        lt_copy[6].start()
        lt_copy[7].start()
        wait_active()
        first_sends()
        gr_copy[5].start()
        gr_copy[6].start()
        by_tiles(cross_input)
        col_sum(obuf, 20)
        col_sum(gr.at[6], 19)
        col_sum(gr.at[5], 21)

    rows_copy = pltpu.make_async_copy(xb, out_rows, io_sem.at[0])
    rows_copy.start()
    lt_copy[6].wait()
    for j in range(slots):
        gr_copy[1 + j].wait()
    loop(4, 8, lambda i: send_piece(i, 6, i - 3))

    norm_backward(both, u_self, grad, 2 * st, bias_at + 3, hw, gr.at[7])
    gr_copy[7].start()

    def self_up(at):
        obuf[:, at] = dot_nt(gr[7], wo[at, :]).astype(bf16)
    by_tiles(self_up)
    loop(2, 3, lambda i: keep_piece(i, i, 0))
    loop(0, 1, lambda i: keep_piece(i, i, 0, True))
    attend_backward(both, q_ref, k_ref, v_ref, own_lens, diagonal)
    for j in range(3):
        gr_copy[8 + j].start()

    @pl.when(is_dec)
    def _():
        gk_copy[0].start()
        gk_copy[1].start()
    loop(3, 4, lambda i: keep_piece(i, i, 0))
    loop(1, 2, lambda i: keep_piece(i, i, 0, True))
    loop(2, 3, lambda i: pass_piece(i))
    loop(0, 1, lambda i: pass_piece(i, True))

    def self_input(at):
        total = hw[:, at]
        for j in range(3):
            total = total + dot_nt(gr[8 + j], wproj[j, at, :])
        hw[:, at] = total
    by_tiles(self_input)
    grad_copy = pltpu.make_async_copy(hw, out_grad, io_sem.at[1])
    grad_copy.start()
    loop(4, 5, lambda i: keep_piece(i, 6, i - 3))
    for i in (4, 5, 7):
        lt_copy[i].wait()

    @pl.when(is_dec)
    def _():
        lt_copy[8].wait()
    for i in range(7, 11):
        gr_copy[i].wait()
    first_left = 7 + st
    rest = ((8, 5, 7), (9, 4, 8), (10, 4, 9), (11, 4, 10), (12, 7, 5), (13, first_left, 6))

    col_sum(gr.at[0], ffn_at)
    loop(0, slots, lambda j: col_sum(gr.at[1 + j], ffn_at - 4 + j))
    col_sum(gr.at[7], bias_at + 2)
    col_sum(gr.at[8], bias_at)
    col_sum(gr.at[10], bias_at + 1)
    v_copy = [remote(vbuf.at[2 * k], vbuf.at[2 * k + 1], v_send.at[k], v_recv.at[k], dev)
              for k, dev in enumerate((core_id, y_id, near_id, far_id, x_id))]
    vbuf[0] = vg[...]

    def v_next(k):
        v_copy[k].wait()
        vbuf[2 * k + 2] = vbuf[2 * k] + vbuf[2 * k + 1]
        v_copy[k + 1].start()
    v_copy[0].start()
    for i, left, slot in rest[:2]:
        send_piece(i, left, slot)
    v_next(0)
    for i, left, slot in rest[2:4]:
        send_piece(i, left, slot)
    loop(3, 4, lambda i: pass_piece(i))
    loop(1, 2, lambda i: pass_piece(i, True))
    loop(5, 6, lambda i: keep_piece(i, 6, i - 3))
    loop(4, 5, lambda i: pass_piece(i))

    @pl.when(is_enc)
    def _():
        gk_copy[0].wait_recv()
        gk_copy[1].wait_recv()
        gr_copy[5].start()
        gr_copy[6].start()
    loop(6, 7, lambda i: keep_piece(i, 6, i - 3))
    for i in range(5, 7):
        gr_copy[i].wait()
    for i, left, slot in rest[4:]:
        send_piece(i, left, slot)
    loop(5, 6, lambda i: pass_piece(i))
    loop(7, 8, lambda i: keep_piece(i, 6, i - 3))
    loop(6, 7, lambda i: pass_piece(i))
    for k, (i, left, slot) in enumerate(rest):
        keep_piece(i, left, slot)
        pass_piece(i - 1)
        if 2 <= k <= 4:
            v_next(k - 1)
    pass_piece(13)
    v_copy[4].wait()
    out_vec[...] = vbuf[8] + vbuf[9]

    def finish(i, z_first=False):
        third_copy(i, z_first).wait()
        own_copy(i, z_first).wait()
    loop(0, 2, lambda i: finish(i, True))
    loop(2, PIECES, finish)
    rows_copy.wait()
    grad_copy.wait()

    @pl.when(is_enc)
    def _():
        for h in range(WX_CHUNKS):
            wx_first[h].wait_send()
        for h in range(2):
            mem_copy[h].wait_send()

    @pl.when(is_dec)
    def _():
        for h in range(2):
            gm_copy[h].wait_send()
            gk_copy[h].wait_send()


def last_kernel(width, rows_in, grad_in, own, parts, vec_sum, rows_out, grad_out, *refs):
    outs, (rows_buf, grad_buf, own_buf, part_buf, sums, in_sem, through_sem, out_sem) = refs[:8], refs[8:]
    into = [pltpu.make_async_copy(rows_in, rows_buf, through_sem.at[0]), pltpu.make_async_copy(grad_in, grad_buf, through_sem.at[1])]
    through = [pltpu.make_async_copy(rows_buf, rows_out, out_sem.at[PIECES]),
               pltpu.make_async_copy(grad_buf, grad_out, out_sem.at[PIECES + 1])]
    for cp in into:
        cp.start()
    loads = [(pltpu.make_async_copy(own.at[i], own_buf.at[i], in_sem.at[i, 0]),
              pltpu.make_async_copy(parts.at[i], part_buf.at[i], in_sem.at[i, 1])) for i in range(PIECES)]
    for pair in loads:
        for cp in pair:
            cp.start()
    shift = lax.rem(width - lax.axis_index("dp") * PIECE, width)
    turned = pltpu.roll(vec_sum[...], shift, 1)
    outs[6][...] = turned[:5, :PIECE]
    outs[7][...] = turned[5:29, :PIECE]
    for cp, out in zip(into, through):
        cp.wait()
        out.start()
    stores = []
    for i in range(PIECES):
        for cp in loads[i]:
            cp.wait()
        sums[i] = own_buf[i].astype(f32) + part_buf[i].astype(f32)
        if i < 4:
            target = outs[0].at[pl.ds(i * PIECE, PIECE), :]
        elif i < 8:
            target = outs[1].at[:, pl.ds((i - 4) * width, width)]
        elif i == 8:
            target = outs[4]
        elif i < 12:
            target = outs[5].at[i - 9]
        else:
            target = outs[i - 10]
        stores.append(pltpu.make_async_copy(sums.at[i], target, out_sem.at[i]))
        stores[-1].start()
    for cp in stores + through:
        cp.wait()


def whole_step(lengths, gains, biases, x, cot, wproj, wo, wfirst, wsecond, win, wout):
    width = x.shape[1]
    hidden = win.shape[1]
    half = width // 2
    any_space = pl.BlockSpec(memory_space=pl.ANY)
    vmem = pl.BlockSpec(memory_space=pltpu.VMEM)
    dma = pltpu.SemaphoreType.DMA
    slots = hidden // width
    small = (32, width)
    results = pl.pallas_call(
        functools.partial(step_kernel, width, hidden),
        out_shape=[
            jax.ShapeDtypeStruct((ROWS, width), bf16),
            jax.ShapeDtypeStruct((ROWS, width), f32),
            jax.ShapeDtypeStruct((PIECES, PIECE, width), bf16),
            jax.ShapeDtypeStruct((PIECES, PIECE, width), bf16),
            jax.ShapeDtypeStruct(small, f32),
        ],
        in_specs=[pl.BlockSpec(memory_space=pltpu.SMEM), vmem, vmem] + [any_space] * 8,
        out_specs=[any_space] * 4 + [vmem],
        scratch_shapes=[
            pltpu.VMEM(small, f32), pltpu.VMEM((2, hidden), f32),
            pltpu.VMEM(wproj.shape, bf16), pltpu.VMEM(wo.shape, bf16), pltpu.VMEM(wfirst.shape, bf16),
            pltpu.VMEM(wsecond.shape, bf16), pltpu.VMEM(win.shape, bf16), pltpu.VMEM(wout.shape, bf16),
            pltpu.VMEM((4, half, width), bf16),
            pltpu.VMEM((ROWS, width), bf16),
            pltpu.VMEM((ROWS, width), bf16),
            pltpu.VMEM((ROWS, width), bf16),
            pltpu.VMEM((ROWS, width), bf16),
            pltpu.VMEM((ROWS, width), bf16),
            pltpu.VMEM((slots, ROWS, width), bf16),
            pltpu.VMEM((2, ROWS, width), bf16),
            pltpu.VMEM((ROWS, width), f32),
            pltpu.VMEM((ROWS, width), f32),
            pltpu.VMEM((ROWS, width), f32),
            pltpu.VMEM((ROWS, width), f32),
            pltpu.VMEM((ROWS, width), f32),
            pltpu.VMEM((ROWS, width), f32),
            pltpu.VMEM((11, ROWS, width), bf16),
            pltpu.VMEM((11, ROWS, width), bf16),
            pltpu.VMEM((9, 2, 2, 2, 2, PIECE, ROWS), bf16),
            pltpu.VMEM((9, 2, 2, 2, PIECE, ROWS), bf16),
            pltpu.VMEM((SEND_SLOTS, 2, 2, PIECE, width), bf16),
            pltpu.VMEM((PIECES, 2, 2, PIECE, width), bf16),
            pltpu.VMEM((PIECES, 2, PIECE, width), bf16),
            pltpu.VMEM((ROWS, width), bf16),
            pltpu.VMEM(small, f32),
            pltpu.VMEM((10,) + small, f32),
            dma((9,)), dma((4 * WX_CHUNKS,)), dma((4 * WX_CHUNKS,)), dma((2,)), dma((2,)), dma((2,)), dma((2,)), dma((2,)), dma((2,)),
            dma((9,)), dma((9,)), dma((11,)), dma((11,)),
            dma((PIECES, 3)), dma((PIECES, 3)), dma((PIECES,)), dma((2,)), dma((5,)), dma((5,)),
        ],
        compiler_params=pltpu.CompilerParams(collective_id=0, has_side_effects=True, vmem_limit_bytes=VMEM_LIMIT),
        name="step",
    )(lengths, gains, biases, x, cot, wproj, wo, wfirst, wsecond, win, wout)
    shapes = [(4 * PIECE, width), (PIECE, hidden), (PIECE, width), (PIECE, width), (PIECE, width), (3, PIECE, width),
              (5, PIECE), (24, PIECE)]
    return pl.pallas_call(
        functools.partial(last_kernel, width),
        out_shape=[jax.ShapeDtypeStruct((ROWS, width), bf16), jax.ShapeDtypeStruct((ROWS, width), f32)]
        + [jax.ShapeDtypeStruct(shape, f32) for shape in shapes],
        in_specs=[any_space] * 4 + [vmem],
        out_specs=[any_space] * 8 + [vmem] * 2,
        scratch_shapes=[
            pltpu.VMEM((ROWS, width), bf16), pltpu.VMEM((ROWS, width), f32),
            pltpu.VMEM((PIECES, PIECE, width), bf16), pltpu.VMEM((PIECES, PIECE, width), bf16),
            pltpu.VMEM((PIECES, PIECE, width), f32), dma((PIECES, 2)), dma((2,)), dma((PIECES + 2,)),
        ],
        compiler_params=pltpu.CompilerParams(vmem_limit_bytes=VMEM_LIMIT),
        name="last",
    )(*results)


eps_norm = 1e-05
low_type = jnp.bfloat16
wide_type = jnp.float32


def as_sent(shard):
    return jax.tree.map(lambda a: a.astype(jnp.bfloat16) if a.dtype == jnp.float32 else a, shard)


def shifted(shard, axis, by):
    count = lax.axis_size(axis)
    pairs = [(i, i + by) for i in range(count) if 0 <= i + by < count]
    return lax.ppermute(shard, axis, pairs)


def matmul(left_mat, right_mat):
    return jnp.dot(left_mat, right_mat, preferred_element_type=wide_type)


def matmul_tn(left_mat, right_mat):
    return lax.dot_general(
        left_mat, right_mat, (((0,), (0,)), ((), ())), preferred_element_type=wide_type
    )


def matmul_nt(left_mat, right_mat):
    return lax.dot_general(
        left_mat, right_mat, (((1,), (1,)), ((), ())), preferred_element_type=wide_type
    )


def column_sum(tensor):
    return jnp.sum(tensor.astype(wide_type), axis=0)


def norm_rows(tensor, norm_gain, norm_shift):
    centre = tensor - jnp.mean(tensor, axis=-1, keepdims=True)
    spread = jnp.mean(centre * centre, axis=-1, keepdims=True)
    return centre * lax.rsqrt(spread + eps_norm) * norm_gain + norm_shift


def norm_back(tensor, norm_gain, norm_shift, upstream):
    unused, pullback = jax.vjp(norm_rows, tensor, norm_gain, norm_shift)
    return pullback(upstream)


def gelu_exact(tensor):
    return jax.nn.gelu(tensor, approximate=False)


def key_mask(row_count, key_count, length, causal):
    columns = lax.broadcasted_iota(jnp.int32, (row_count, key_count), 1)
    allowed = columns < length
    if causal:
        allowed = allowed & (columns <= lax.broadcasted_iota(jnp.int32, (row_count, key_count), 0))
    return allowed


def split_heads(tensor):
    return tensor.reshape(tensor.shape[0], -1, HDIM)


def attend_scores(queries, key_rows, allowed):
    scores = jnp.einsum(
        "qhd,khd->hqk",
        split_heads(queries),
        split_heads(key_rows),
        preferred_element_type=wide_type,
    )
    return jnp.where(allowed[None], scores * HDIM ** (-0.5), -1e30)


def attend_forward(queries, key_rows, values, allowed):
    scores = attend_scores(queries, key_rows, allowed)
    row_max = jnp.max(scores, axis=-1, keepdims=True)
    log_total = row_max + jnp.log(jnp.sum(jnp.exp(scores - row_max), axis=-1, keepdims=True))
    softmaxed = jnp.exp(scores - log_total).astype(low_type)
    attended = jnp.einsum(
        "hqk,khd->qhd", softmaxed, split_heads(values), preferred_element_type=wide_type
    )
    return (attended.reshape(queries.shape[0], -1), log_total)


def attend_backward(queries, key_rows, values, allowed, log_total, upstream):
    softmaxed = jnp.exp(attend_scores(queries, key_rows, allowed) - log_total)
    grad_heads = split_heads(upstream)
    grad_values = jnp.einsum(
        "hqk,qhd->khd", softmaxed.astype(low_type), grad_heads, preferred_element_type=wide_type
    )
    grad_probs = jnp.einsum(
        "qhd,khd->hqk", grad_heads, split_heads(values), preferred_element_type=wide_type
    )
    grad_scores = (
        softmaxed * (grad_probs - jnp.sum(softmaxed * grad_probs, axis=-1, keepdims=True))
    ).astype(low_type)
    scale_factor = HDIM ** (-0.5)
    grad_queries = (
        jnp.einsum(
            "hqk,khd->qhd", grad_scores, split_heads(key_rows), preferred_element_type=wide_type
        )
        * scale_factor
    )
    grad_keys = (
        jnp.einsum(
            "hqk,qhd->khd", grad_scores, split_heads(queries), preferred_element_type=wide_type
        )
        * scale_factor
    )
    key_count = key_rows.shape[0]
    return (
        grad_queries.reshape(queries.shape[0], -1),
        grad_keys.reshape(key_count, -1),
        grad_values.reshape(key_count, -1),
    )


def self_forward(row_block, length, causal, w_proj, w_out, vectors):
    bias_q, bias_v, bias_o, norm_gain, norm_shift = vectors
    row_count = row_block.shape[0]
    offsets = jnp.stack([bias_q, jnp.zeros_like(bias_q), bias_v])[:, None, :]
    projected = (
        jnp.einsum("rd,cde->cre", row_block, w_proj, preferred_element_type=wide_type) + offsets
    ).astype(low_type)
    allowed = key_mask(row_count, row_count, length, causal)
    attended, log_total = attend_forward(projected[0], projected[1], projected[2], allowed)
    attended = attended.astype(low_type)
    summed = row_block.astype(wide_type) + matmul(attended, w_out) + bias_o
    return (norm_rows(summed, norm_gain, norm_shift), (projected, log_total, attended, summed))


def self_backward(row_block, length, causal, w_proj, w_out, vectors, saved_fwd, upstream):
    projected, log_total, attended, summed = saved_fwd
    row_count = row_block.shape[0]
    grad_sum, grad_gain, grad_shift = norm_back(summed, vectors[3], vectors[4], upstream)
    grad_branch = grad_sum.astype(low_type)
    grad_attended = matmul_nt(grad_branch, w_out).astype(low_type)
    allowed = key_mask(row_count, row_count, length, causal)
    grad_q, grad_k, grad_v = attend_backward(
        projected[0], projected[1], projected[2], allowed, log_total, grad_attended
    )
    grad_proj = jnp.stack([grad_q, grad_k, grad_v]).astype(low_type)
    grad_rows = grad_sum + jnp.einsum(
        "cre,cde->rd", grad_proj, w_proj, preferred_element_type=wide_type
    )
    weight_grads = (
        jnp.einsum("rd,cre->cde", row_block, grad_proj, preferred_element_type=wide_type),
        matmul_tn(attended, grad_branch),
    )
    vector_grads = (
        column_sum(grad_proj[0]),
        column_sum(grad_proj[2]),
        column_sum(grad_branch),
        grad_gain,
        grad_shift,
    )
    return (grad_rows, weight_grads, vector_grads)


def ffn_forward(hidden, w_in, w_out, vectors):
    bias_in, bias_out, norm_gain, norm_shift = vectors
    low_hidden = hidden.astype(low_type)
    inner_act = matmul(low_hidden, w_in) + bias_in
    active = gelu_exact(inner_act).astype(low_type)
    summed = hidden + matmul(active, w_out) + bias_out
    return (norm_rows(summed, norm_gain, norm_shift), (low_hidden, inner_act, active, summed))


def ffn_backward(w_in, w_out, vectors, saved_fwd, upstream):
    low_hidden, inner_act, active, summed = saved_fwd
    grad_sum, grad_gain, grad_shift = norm_back(summed, vectors[2], vectors[3], upstream)
    grad_branch = grad_sum.astype(low_type)
    unused, pullback = jax.vjp(gelu_exact, inner_act)
    grad_inner = pullback(matmul_nt(grad_branch, w_out))[0].astype(low_type)
    grad_hidden = grad_sum + matmul_nt(grad_inner, w_in)
    weight_grads = (matmul_tn(low_hidden, grad_inner), matmul_tn(active, grad_branch))
    vector_grads = (column_sum(grad_inner), column_sum(grad_branch), grad_gain, grad_shift)
    return (grad_hidden, weight_grads, vector_grads)


def cross_forward(hidden, memory, src_len, w_query, w_out, vectors):
    bias_q, bias_v, bias_o, norm_gain, norm_shift = vectors
    low_hidden = hidden.astype(low_type)
    queries = (matmul(low_hidden, w_query) + bias_q).astype(low_type)
    allowed = key_mask(hidden.shape[0], memory.shape[1], src_len, False)
    attended, log_total = attend_forward(queries, memory[0], memory[1], allowed)
    attended = (attended + bias_v).astype(low_type)
    summed = hidden + matmul(attended, w_out) + bias_o
    return (
        norm_rows(summed, norm_gain, norm_shift),
        (low_hidden, queries, log_total, attended, summed),
    )


def cross_backward(memory, src_len, w_query, w_out, vectors, saved_fwd, upstream):
    low_hidden, queries, log_total, attended, summed = saved_fwd
    grad_sum, grad_gain, grad_shift = norm_back(summed, vectors[3], vectors[4], upstream)
    grad_branch = grad_sum.astype(low_type)
    grad_attended = matmul_nt(grad_branch, w_out).astype(low_type)
    allowed = key_mask(queries.shape[0], memory.shape[1], src_len, False)
    grad_q, grad_k, grad_v = attend_backward(
        queries, memory[0], memory[1], allowed, log_total, grad_attended
    )
    grad_query = grad_q.astype(low_type)
    grad_memory = jnp.stack([grad_k, grad_v]).astype(low_type)
    grad_hidden = grad_sum + matmul_nt(grad_query, w_query)
    weight_grads = (matmul_tn(low_hidden, grad_query), matmul_tn(attended, grad_branch))
    vector_grads = (
        column_sum(grad_query),
        column_sum(grad_attended),
        column_sum(grad_branch),
        grad_gain,
        grad_shift,
    )
    return (grad_hidden, grad_memory, weight_grads, vector_grads)


def self_vectors(gain_rows, bias_rows, decoder):
    base_row = 10 if decoder else 0
    gain_row = 2 if decoder else 0
    return (
        bias_rows[base_row],
        bias_rows[base_row + 1],
        bias_rows[base_row + 2],
        gain_rows[gain_row],
        bias_rows[base_row + 3],
    )


def ffn_vectors(gain_rows, bias_rows, decoder):
    base_row = 18 if decoder else 4
    gain_row = 4 if decoder else 1
    return (
        bias_rows[base_row : base_row + 4].reshape(-1),
        bias_rows[base_row + 4],
        gain_rows[gain_row],
        bias_rows[base_row + 5],
    )


def cross_vectors(gain_rows, bias_rows):
    return (bias_rows[14], bias_rows[15], bias_rows[16], gain_rows[3], bias_rows[17])


def self_plan(decoder, vector_grads):
    base_row = 10 if decoder else 0
    gain_row = 2 if decoder else 0
    return (
        ("biases", base_row, vector_grads[0]),
        ("biases", base_row + 1, vector_grads[1]),
        ("biases", base_row + 2, vector_grads[2]),
        ("gains", gain_row, vector_grads[3]),
        ("biases", base_row + 3, vector_grads[4]),
    )


def ffn_plan(decoder, vector_grads):
    base_row = 18 if decoder else 4
    gain_row = 4 if decoder else 1
    return (
        ("biases", base_row, vector_grads[0]),
        ("biases", base_row + 4, vector_grads[1]),
        ("gains", gain_row, vector_grads[2]),
        ("biases", base_row + 5, vector_grads[3]),
    )


def cross_plan(vector_grads):
    return (
        ("biases", 14, vector_grads[0]),
        ("biases", 15, vector_grads[1]),
        ("biases", 16, vector_grads[2]),
        ("gains", 3, vector_grads[3]),
        ("biases", 17, vector_grads[4]),
    )


def accumulate(totals, weight_names, weight_grads, vector_plan):
    merged = dict(totals)
    for key_name, tensor in zip(weight_names, weight_grads):
        merged[key_name] = merged[key_name] + tensor
    for table_name, row_at, tensor in vector_plan:
        table_now = merged[table_name]
        row_block = tensor.reshape(-1, table_now.shape[1])
        merged[table_name] = table_now.at[row_at : row_at + row_block.shape[0]].add(row_block)
    return merged


def updated(progress, key_name, position, tensor):
    copied = dict(progress)
    copied[key_name] = [
        tensor if slot_index == position else entry_now
        for slot_index, entry_now in enumerate(progress[key_name])
    ]
    return copied


def with_totals(progress, totals):
    copied = dict(progress)
    copied["totals"] = totals
    return copied


def forward_pass(tensor):
    return jax.tree.map(
        lambda part, own: part.astype(own.dtype), shifted(as_sent(tensor), "stream", 1), tensor
    )


def backward_pass(tensor):
    return jax.tree.map(
        lambda part, own: part.astype(own.dtype), shifted(as_sent(tensor), "stream", -1), tensor
    )


def keep_same(progress):
    return progress


def plain_body(
    inputs,
    lengths,
    cotangent,
    attn_in,
    attn_out,
    cross_first,
    cross_second,
    ffn_in,
    ffn_out,
    gains,
    biases,
):
    own_rows = inputs[0]
    model_width = own_rows.shape[1]
    hidden_width = ffn_in.shape[2]
    head_count = model_width // HDIM
    row_sizes = (SHORT, LONG)
    bucket_spans = ((0, SHORT), (SHORT, SHORT + LONG))
    row_pieces = [own_rows[start_row:stop_row] for start_row, stop_row in bucket_spans]
    grad_pieces = [
        cotangent[start_row:stop_row].astype(wide_type) for start_row, stop_row in bucket_spans
    ]
    src_lens = [lengths[0, 0, bucket_idx] for bucket_idx in range(2)]
    tgt_lens = [lengths[1, 0, bucket_idx] for bucket_idx in range(2)]
    w_proj = attn_in[0]
    w_attn_out = attn_out[0]
    w_first = cross_first[0]
    w_second = cross_second[0]
    w_ffn_in = ffn_in[0]
    w_ffn_out = ffn_out[0]
    gain_rows = gains.astype(wide_type)
    bias_rows = biases.astype(wide_type)
    enc_self = self_vectors(gain_rows, bias_rows, False)
    enc_ffn = ffn_vectors(gain_rows, bias_rows, False)
    dec_self = self_vectors(gain_rows, bias_rows, True)
    dec_ffn = ffn_vectors(gain_rows, bias_rows, True)
    dec_cross = cross_vectors(gain_rows, bias_rows)
    is_decoder = lax.axis_index("stream") == 1

    def blank_self(size_rows):
        return (
            jnp.zeros((3, size_rows, model_width), low_type),
            jnp.zeros((head_count, size_rows, 1), wide_type),
            jnp.zeros((size_rows, model_width), low_type),
            jnp.zeros((size_rows, model_width), wide_type),
        )

    def blank_ffn(size_rows):
        return (
            jnp.zeros((size_rows, model_width), low_type),
            jnp.zeros((size_rows, hidden_width), wide_type),
            jnp.zeros((size_rows, hidden_width), low_type),
            jnp.zeros((size_rows, model_width), wide_type),
        )

    def blank_cross(size_rows):
        return (
            jnp.zeros((size_rows, model_width), low_type),
            jnp.zeros((size_rows, model_width), low_type),
            jnp.zeros((head_count, size_rows, 1), wide_type),
            jnp.zeros((size_rows, model_width), low_type),
            jnp.zeros((size_rows, model_width), wide_type),
        )

    progress = {
        "out": [jnp.zeros((size_rows, model_width), low_type) for size_rows in row_sizes],
        "grad_in": [jnp.zeros((size_rows, model_width), wide_type) for size_rows in row_sizes],
        "send": [jnp.zeros((2, size_rows, model_width), low_type) for size_rows in row_sizes],
        "memory": [jnp.zeros((2, size_rows, model_width), low_type) for size_rows in row_sizes],
        "grad_send": [jnp.zeros((2, size_rows, model_width), low_type) for size_rows in row_sizes],
        "grad_memory": [
            jnp.zeros((2, size_rows, model_width), low_type) for size_rows in row_sizes
        ],
        "mid": [jnp.zeros((size_rows, model_width), wide_type) for size_rows in row_sizes],
        "grad_mid": [jnp.zeros((size_rows, model_width), wide_type) for size_rows in row_sizes],
        "totals": {
            "proj": jnp.zeros(w_proj.shape, wide_type),
            "attn_out": jnp.zeros(w_attn_out.shape, wide_type),
            "first": jnp.zeros(w_first.shape, wide_type),
            "second": jnp.zeros(w_second.shape, wide_type),
            "ffn_in": jnp.zeros(w_ffn_in.shape, wide_type),
            "ffn_out": jnp.zeros(w_ffn_out.shape, wide_type),
            "gains": jnp.zeros(gains.shape, wide_type),
            "biases": jnp.zeros(biases.shape, wide_type),
        },
    }
    progress["self_saved"] = [blank_self(size_rows) for size_rows in row_sizes]
    progress["ffn_saved"] = [blank_ffn(size_rows) for size_rows in row_sizes]
    progress["cross_saved"] = [blank_cross(size_rows) for size_rows in row_sizes]

    def encoder_core(micro_idx):
        h_one, self_saved = self_forward(
            row_pieces[micro_idx], src_lens[micro_idx], False, w_proj, w_attn_out, enc_self
        )
        encoded, ffn_saved = ffn_forward(h_one, w_ffn_in, w_ffn_out, enc_ffn)
        return (encoded.astype(low_type), self_saved, ffn_saved)

    def encoder_forward_step(progress, micro_idx):
        low_memory, self_saved, ffn_saved = encoder_core(micro_idx)
        memory = jnp.stack([matmul(low_memory, w_first), matmul(low_memory, w_second)]).astype(
            low_type
        )
        progress = updated(progress, "out", micro_idx, low_memory)
        progress = updated(progress, "send", micro_idx, memory)
        progress = updated(progress, "self_saved", micro_idx, self_saved)
        progress = updated(progress, "ffn_saved", micro_idx, ffn_saved)
        return progress

    def decoder_head(micro_idx):
        return self_forward(
            row_pieces[micro_idx], tgt_lens[micro_idx], True, w_proj, w_attn_out, dec_self
        )

    def decoder_tail(mid_rows, memory, micro_idx):
        crossed, cross_saved = cross_forward(
            mid_rows, memory, src_lens[micro_idx], w_first, w_second, dec_cross
        )
        decoded, ffn_saved = ffn_forward(crossed, w_ffn_in, w_ffn_out, dec_ffn)
        return (decoded, cross_saved, ffn_saved)

    def decoder_head_step(progress, micro_idx):
        mid_rows, self_saved = decoder_head(micro_idx)
        progress = updated(progress, "mid", micro_idx, mid_rows)
        progress = updated(progress, "self_saved", micro_idx, self_saved)
        return progress

    def decoder_tail_step(progress, micro_idx):
        decoded, cross_saved, ffn_saved = decoder_tail(
            progress["mid"][micro_idx], progress["memory"][micro_idx], micro_idx
        )
        progress = updated(progress, "out", micro_idx, decoded.astype(low_type))
        progress = updated(progress, "cross_saved", micro_idx, cross_saved)
        progress = updated(progress, "ffn_saved", micro_idx, ffn_saved)
        return progress

    def decoder_back_step(progress, micro_idx):
        memory = progress["memory"][micro_idx]
        self_saved = progress["self_saved"][micro_idx]
        cross_saved = progress["cross_saved"][micro_idx]
        ffn_saved = progress["ffn_saved"][micro_idx]
        grad_h_two, ffn_w, ffn_v = ffn_backward(
            w_ffn_in, w_ffn_out, dec_ffn, ffn_saved, grad_pieces[micro_idx]
        )
        grad_h_one, grad_memory, cross_w, cross_v = cross_backward(
            memory, src_lens[micro_idx], w_first, w_second, dec_cross, cross_saved, grad_h_two
        )
        grad_rows, self_w, self_v = self_backward(
            row_pieces[micro_idx],
            tgt_lens[micro_idx],
            True,
            w_proj,
            w_attn_out,
            dec_self,
            self_saved,
            grad_h_one,
        )
        totals = accumulate(
            progress["totals"],
            ("ffn_in", "ffn_out", "first", "second", "proj", "attn_out"),
            ffn_w + cross_w + self_w,
            ffn_plan(True, ffn_v) + cross_plan(cross_v) + self_plan(True, self_v),
        )
        progress = updated(progress, "grad_in", micro_idx, grad_rows)
        progress = updated(progress, "grad_send", micro_idx, grad_memory)
        return with_totals(progress, totals)

    def encoder_top_step(progress, micro_idx):
        low_memory = progress["out"][micro_idx]
        ffn_saved = progress["ffn_saved"][micro_idx]
        grad_memory = progress["grad_memory"][micro_idx]
        grad_encoded = matmul_nt(grad_memory[0], w_first) + matmul_nt(grad_memory[1], w_second)
        grad_h_one, ffn_w, ffn_v = ffn_backward(
            w_ffn_in, w_ffn_out, enc_ffn, ffn_saved, grad_encoded
        )
        projections = (matmul_tn(low_memory, grad_memory[0]), matmul_tn(low_memory, grad_memory[1]))
        totals = accumulate(
            progress["totals"],
            ("first", "second", "ffn_in", "ffn_out"),
            projections + ffn_w,
            ffn_plan(False, ffn_v),
        )
        progress = updated(progress, "grad_mid", micro_idx, grad_h_one)
        return with_totals(progress, totals)

    def encoder_bottom_step(progress, micro_idx):
        self_saved = progress["self_saved"][micro_idx]
        grad_rows, self_w, self_v = self_backward(
            row_pieces[micro_idx],
            src_lens[micro_idx],
            False,
            w_proj,
            w_attn_out,
            enc_self,
            self_saved,
            progress["grad_mid"][micro_idx],
        )
        totals = accumulate(
            progress["totals"], ("proj", "attn_out"), self_w, self_plan(False, self_v)
        )
        progress = updated(progress, "grad_in", micro_idx, grad_rows)
        return with_totals(progress, totals)

    def enc_zero(progress):
        return encoder_forward_step(progress, 0)

    def dec_zero(progress):
        return decoder_head_step(progress, 0)

    def enc_one(progress):
        return encoder_forward_step(progress, 1)

    def dec_one(progress):
        return decoder_tail_step(decoder_head_step(progress, 1), 0)

    def dec_two(progress):
        return decoder_back_step(decoder_tail_step(progress, 1), 1)

    def enc_three(progress):
        return encoder_bottom_step(encoder_top_step(progress, 1), 1)

    def dec_three(progress):
        return decoder_back_step(progress, 0)

    def enc_four(progress):
        return encoder_top_step(progress, 0)

    def enc_five(progress):
        return encoder_bottom_step(progress, 0)

    progress = lax.cond(is_decoder, dec_zero, enc_zero, progress)
    progress = updated(progress, "memory", 0, forward_pass(progress["send"][0]))
    progress = lax.cond(is_decoder, dec_one, enc_one, progress)
    progress = updated(progress, "memory", 1, forward_pass(progress["send"][1]))
    progress = lax.cond(is_decoder, dec_two, keep_same, progress)
    progress = updated(progress, "grad_memory", 1, backward_pass(progress["grad_send"][1]))
    progress = lax.cond(is_decoder, dec_three, enc_three, progress)
    progress = updated(progress, "grad_memory", 0, backward_pass(progress["grad_send"][0]))
    progress = lax.cond(is_decoder, keep_same, enc_four, progress)
    progress = lax.cond(is_decoder, keep_same, enc_five, progress)
    totals = progress["totals"]
    owned = (
        lax.psum_scatter(totals["proj"], "dp", scatter_dimension=1, tiled=True),
        lax.psum_scatter(totals["attn_out"], "dp", scatter_dimension=0, tiled=True),
        lax.psum_scatter(totals["first"], "dp", scatter_dimension=0, tiled=True),
        lax.psum_scatter(totals["second"], "dp", scatter_dimension=0, tiled=True),
        lax.psum_scatter(totals["ffn_in"], "dp", scatter_dimension=0, tiled=True),
        lax.psum_scatter(totals["ffn_out"], "dp", scatter_dimension=0, tiled=True),
        lax.psum_scatter(totals["gains"], "dp", scatter_dimension=1, tiled=True),
        lax.psum_scatter(totals["biases"], "dp", scatter_dimension=1, tiled=True),
    )
    owned_gains, owned_biases = lax.psum((owned[6], owned[7]), "stream")
    layer_out = jnp.concatenate(progress["out"], axis=0)[None]
    grad_inputs = jnp.concatenate(progress["grad_in"], axis=0)[None]
    return (
        layer_out,
        grad_inputs,
        owned[0][None],
        owned[1][None],
        owned[2][None],
        owned[3][None],
        owned[4][None],
        owned[5][None],
        owned_gains,
        owned_biases,
    )


def fused_body(inputs, lengths, cotangent, attn_in, attn_out, cross_first, cross_second, ffn_in, ffn_out, gains, biases):
    rows, grad, s_out, s_in, s_second, s_first, s_attn, s_proj, own_gains, own_biases = whole_step(
        lengths, gains, biases, inputs[0], cotangent, attn_in[0], attn_out[0],
        cross_first[0], cross_second[0], ffn_in[0], ffn_out[0])
    return (rows[None], grad[None], s_proj[None], s_attn[None], s_first[None], s_second[None],
            s_in[None], s_out[None], own_gains, own_biases)


def solution(mesh):
    def body(*args):
        width = args[0].shape[2]
        fits = mesh.shape["dp"] * PIECE == width and args[0].shape[1] == ROWS and args[7].shape[2] == 4 * width
        return (fused_body if fits else plain_body)(*args)
    return jax.shard_map(
        body,
        mesh=mesh,
        in_specs=(
            P("stream", "dp", None),
            P(None, "dp", None),
            P("dp", None),
            P("stream", None, None, None),
            P("stream", None, None),
            P("stream", None, None),
            P("stream", None, None),
            P("stream", None, None),
            P("stream", None, None),
            P(),
            P(),
        ),
        out_specs=(
            P("stream", "dp", None),
            P("stream", "dp", None),
            P("stream", None, "dp", None),
            P("stream", "dp", None),
            P("stream", "dp", None),
            P("stream", "dp", None),
            P("stream", "dp", None),
            P("stream", "dp", None),
            P(None, "dp"),
            P(None, "dp"),
        ),
        check_vma=False,
    )
```

```python
import functools

import jax
import jax.numpy as jnp
from jax import lax
from jax.experimental import pallas as pl
from jax.experimental.pallas import tpu as pltpu
from jax.sharding import PartitionSpec as P

HDIM = 64
SHORT = 128
LONG = 256
ROWS = SHORT + LONG
PIECE = 48
PIECES = 14
VEC_ROWS = 24
SEND_SLOTS = 8
WX_CHUNKS = 4
MESH = pl.DeviceIdType.MESH
bf16, f32 = jnp.bfloat16, jnp.float32
VMEM_LIMIT = 64 << 20


def dot_nn(a, b):
    return jnp.dot(a, b, preferred_element_type=f32)


def dot_nt(a, b):
    return lax.dot_general(a, b, (((1,), (1,)), ((), ())), preferred_element_type=f32)


def dot_tn(a, b):
    return lax.dot_general(a, b, (((0,), (0,)), ((), ())), preferred_element_type=f32)


def cols(j, width):
    return pl.ds(pl.multiple_of(j * width, width), width)


def step_kernel(
    width, hidden,
    lengths, gains, biases, x_hbm, cot_hbm, wproj_hbm, wo_hbm, wfirst_hbm, wsecond_hbm, win_hbm, wout_hbm,
    out_rows, out_grad, out_own, out_part, out_vec,
    vec, bias_in, wproj, wo, wfirst, wsecond, win, wout, wx,
    xb, up, mem, obuf, hlow, dg, kv, acc, grad, hw, u_self, u_cross, u_ffn, gr, grp, lt, ltp, one_send, one_recv, two_recv, gmem, vg, vbuf, vboth,
    load_sem, wx_send, wx_recv, mem_send, mem_recv, gm_send, gm_recv, gk_send, gk_recv, lt_send, lt_recv, gr_send, gr_recv,
    sem_send, sem_recv, own_sem, io_sem, v_send, v_recv,
):
    st = lax.axis_index("stream")
    me = lax.axis_index("dp")
    z, y, c = me // 4, (me // 2) % 2, me % 2
    is_dec = st == 1
    is_enc = st == 0
    core_id = {"dp": z * 4 + y * 2 + (1 - c)}
    y_id = {"dp": z * 4 + (1 - y) * 2 + c}
    x_id = {"stream": 1 - st}
    tiles = width // 256
    slots = hidden // width

    zh, zl = z // 2, z % 2

    def z_id(other):
        return {"dp": other * 4 + y * 2 + c}
    near_id = z_id(zh * 2 + 1 - zl)
    far_id = z_id((1 - zh) * 2 + zl)

    def remote(src, dst, ss, rs, dev):
        return pltpu.make_async_remote_copy(
            src_ref=src, dst_ref=dst, send_sem=ss, recv_sem=rs, device_id=dev, device_id_type=MESH)

    loads = [
        pltpu.make_async_copy(src, dst, load_sem.at[i])
        for i, (src, dst) in enumerate((
            (x_hbm, xb), (wproj_hbm, wproj), (wo_hbm, wo), (win_hbm, win), (wout_hbm, wout),
            (wfirst_hbm, wfirst), (wsecond_hbm, wsecond)))
    ]
    cot_load = pltpu.make_async_copy(cot_hbm, up, load_sem.at[7])
    loads[0].start()
    loads[1].start()

    barrier = pltpu.get_barrier_semaphore()
    peers = [core_id, y_id, x_id, near_id, far_id]
    for p in peers:
        pl.semaphore_signal(barrier, inc=1, device_id=p, device_id_type=MESH)

    lens = [lengths[i // 2, 0, i % 2] for i in range(4)]
    own_lens = [jnp.where(is_dec, lens[2 + i], lens[i]) for i in range(2)]
    vec[pl.ds(0, 5), :] = gains[...].astype(f32)
    vec[pl.ds(5, 24), :] = biases[...].astype(f32)
    for i in range(slots):
        for s in range(2):
            bias_in[pl.ds(s, 1), pl.ds(i * width, width)] = vec[pl.ds(9 + 14 * s + i, 1), :]
    vg[...] = jnp.zeros_like(vg)
    pl.semaphore_wait(barrier, len(peers))

    half = width // 2
    chunk = half // WX_CHUNKS
    quarter = y * 2 + c
    far = (1 - y) * 2 + c

    def wx_from(source, h):
        return remote(source.at[pl.ds(c * half + h * chunk, chunk)], wx.at[quarter, pl.ds(h * chunk, chunk)],
                      wx_send.at[h], wx_recv.at[h], x_id)

    def wx_pass(at, h, sem, dev):
        ref = wx.at[at, pl.ds(h * chunk, chunk)]
        return remote(ref, ref, wx_send.at[sem * WX_CHUNKS + h], wx_recv.at[sem * WX_CHUNKS + h], dev)
    wx_first = [wx_from(wfirst_hbm, h) for h in range(WX_CHUNKS)]
    wx_y = [wx_pass(quarter, h, 1, y_id) for h in range(WX_CHUNKS)]
    wx_near = [wx_pass(quarter, h, 2, core_id) for h in range(WX_CHUNKS)]
    wx_far = [wx_pass(far, h, 3, core_id) for h in range(WX_CHUNKS)]

    @pl.when(is_enc & (y == 0))
    def _():
        for h in range(WX_CHUNKS):
            wx_first[h].start()

    @pl.when(is_enc & (y == 1))
    def _():
        for h in range(WX_CHUNKS):
            wx_from(wsecond_hbm, h).start()
    loads[0].wait()
    loads[1].wait()
    for cp in loads[2:]:
        cp.start()

    @pl.when(is_dec)
    def _():
        cot_load.start()

    gain_row = lambda r: pl.ds(r - 2 * st, 1)
    bias_row_of = lambda r: pl.ds(r - 2 - 10 * st, 1)
    lt_copy = [remote(lt.at[i, :, :, :, 1 - c], ltp.at[i], lt_send.at[i], lt_recv.at[i], core_id) for i in range(9)]
    gr_copy = {i: remote(gr.at[i], grp.at[i], gr_send.at[i], gr_recv.at[i], core_id) for i in range(5, 11)}
    buckets = ((0, SHORT), (SHORT, LONG))
    short, long, both = (0,), (1,), (0, 1)

    def span(bs):
        return buckets[bs[0]][0], sum(buckets[b][1] for b in bs)

    def at_rows(bs):
        return pl.ds(*span(bs))
    mem_copy = [remote(xb.at[at_rows((b,))], mem.at[at_rows((b,))], mem_send.at[b], mem_recv.at[b], x_id) for b in range(2)]
    gm_copy = [remote(gmem.at[at_rows((b,))], up.at[at_rows((b,))], gm_send.at[b], gm_recv.at[b], x_id) for b in range(2)]
    gk_copy = [remote(kv.at[0], gr.at[6], gk_send.at[0], gk_recv.at[0], x_id),
               remote(kv.at[1], gr.at[5], gk_send.at[1], gk_recv.at[1], x_id)]

    gr_first = [remote(gr.at[0, at_rows((b,))], grp.at[0, at_rows((b,))], gr_send.at[11 * b], gr_recv.at[11 * b], core_id)
                for b in range(2)]

    def row_loop(bs, block, body, unroll=1):
        r0, n = span(bs)

        def step(i, carry):
            body(pl.ds(pl.multiple_of(r0 + i * block, block), block))
            return carry
        lax.fori_loop(0, n // block, step, 0, unroll=unroll)

    def vrow(r):
        return vec[pl.ds(r, 1), :]

    def transposed(i, bs, ref):
        r0, n = span(bs)
        lt[i, :, :, :, :, :, pl.ds(r0, n)] = ref[pl.ds(r0, n), :].T.reshape(2, 2, 2, 2, PIECE, n)

    def transposed_active(bs):
        r0, n = span(bs)

        def step(j, carry):
            turned = gr[1 + j, pl.ds(r0, n), :].T.reshape(2, 2, 4, PIECE, n)
            for k in range(4):
                lt[k, j // 2, j % 2, :, :, :, pl.ds(r0, n)] = turned[:, :, k]
            return carry
        lax.fori_loop(0, slots, step, 0)

    def col_sum(slot, row):
        def step(i, carry):
            block = slot[pl.ds(pl.multiple_of(i * 64, 64), 64), :].astype(f32)
            return carry + jnp.sum(block.reshape(8, 8, width), axis=0)
        total = lax.fori_loop(0, ROWS // 64, step, jnp.zeros((8, width), f32))
        vg[bias_row_of(row), :] = jnp.sum(total, axis=0, keepdims=True)

    def norm_forward(bs, residual, sum_ref, add_bias, gain, shift, out_low, out_wide):
        def body(rows):
            u = residual[rows, :].astype(f32) + acc[rows, :] + vrow(add_bias)
            sum_ref[rows, :] = u
            centre = u - jnp.mean(u, axis=-1, keepdims=True)
            spread = jnp.mean(centre * centre, axis=-1, keepdims=True)
            h = centre * lax.rsqrt(spread + 1e-05) * vrow(gain) + vrow(shift)
            if out_wide is not None:
                out_wide[rows, :] = h
            out_low[rows, :] = h.astype(bf16)
        row_loop(bs, 32, body, 4)

    def norm_backward(bs, sum_ref, source, gain, shift, out_wide, slot):
        r0, n = span(bs)

        def step(i, carry):
            rows = pl.ds(pl.multiple_of(r0 + i * 32, 32), 32)
            r = source[rows, :].astype(f32)
            u = sum_ref[rows, :]
            centre = u - jnp.mean(u, axis=-1, keepdims=True)
            spread = jnp.mean(centre * centre, axis=-1, keepdims=True)
            inv = lax.rsqrt(spread + 1e-05)
            uhat = centre * inv
            t = r * vrow(gain)
            gu = (t - jnp.mean(t, axis=-1, keepdims=True) - uhat * jnp.mean(t * uhat, axis=-1, keepdims=True)) * inv
            out_wide[rows, :] = gu
            slot[rows, :] = gu.astype(bf16)
            return (carry[0] + jnp.sum((r * uhat).reshape(4, 8, width), axis=0),
                    carry[1] + jnp.sum(r.reshape(4, 8, width), axis=0))
        zero = jnp.zeros((8, width), f32)
        total = lax.fori_loop(0, n // 32, step, (zero, zero), unroll=4)
        for row, part in ((gain_row(gain), total[0]), (bias_row_of(shift), total[1])):
            vg[row, :] = vg[row, :] + jnp.sum(part, axis=0, keepdims=True)

    def masked_scores(q_half, k2, n, length, diagonal):
        s = dot_nt(q_half, k2)
        column = lax.broadcasted_iota(jnp.int32, (n, n), 1)
        row = lax.broadcasted_iota(jnp.int32, (n, n), 0)
        return jnp.where((column < length) & (column <= row + diagonal), s, -1e30)

    def softmax(s):
        e = jnp.exp(s - jnp.max(s, axis=-1, keepdims=True))
        return e * (1.0 / jnp.sum(e, axis=-1, keepdims=True))

    def halves(n):
        lane = lax.broadcasted_iota(jnp.int32, (n, 2 * HDIM), 1)
        return lane < HDIM

    def head_loop(bs, body, lo=0, hi=None):
        pairs = {short: 3, long: 2, both: 1}[bs]

        def step(p, carry):
            body([(b, pl.ds(pl.multiple_of((p * pairs + i) * 2 * HDIM, 2 * HDIM), 2 * HDIM)) for b in bs for i in range(pairs)])
            return carry
        lax.fori_loop(lo, width // (2 * HDIM * pairs) if hi is None else hi, step, 0)

    def attend_forward(bs, q_ref, k_ref, v_ref, lengths_at, diagonal, bias_row, out_ref):
        def body(units):
            work = []
            for b, at in units:
                r0, n = buckets[b]
                rows = pl.ds(r0, n)
                q2, k2 = q_ref[rows, at], k_ref[rows, at]
                first = halves(n)
                for lanes in (first, ~first):
                    work.append(masked_scores(jnp.where(lanes, q2 * 0.125, jnp.zeros_like(q2)), k2, n, lengths_at[b], diagonal))
            work = [softmax(s).astype(bf16) for s in work]
            work = [dot_nn(prob, v_ref[pl.ds(*buckets[units[i // 2][0]]), units[i // 2][1]]) for i, prob in enumerate(work)]
            for i, (b, at) in enumerate(units):
                r0, n = buckets[b]
                att = jnp.where(halves(n), work[2 * i], work[2 * i + 1])
                if bias_row is not None:
                    att = att + vec[pl.ds(bias_row, 1), at]
                out_ref[pl.ds(r0, n), at] = att.astype(bf16)
        head_loop(bs, body)

    def attend_backward(bs, q_ref, k_ref, v_ref, lengths_at, diagonal, lo=0, hi=None):
        scale = HDIM ** -0.5

        def body(units):
            scores, ups = [], []
            for b, at in units:
                r0, n = buckets[b]
                rows = pl.ds(r0, n)
                q2, k2, v2, go2 = q_ref[rows, at], k_ref[rows, at], v_ref[rows, at], obuf[rows, at]
                first = halves(n)
                zero = jnp.zeros_like(q2)
                for lanes in (first, ~first):
                    scores.append(masked_scores(jnp.where(lanes, q2 * 0.125, zero), k2, n, lengths_at[b], diagonal))
                    ups.append(dot_nt(jnp.where(lanes, go2, zero), v2))
            probs = [softmax(s) for s in scores]
            gs = [(p * (gp - jnp.sum(p * gp, axis=-1, keepdims=True))).astype(bf16) for p, gp in zip(probs, ups)]
            for i, (b, at) in enumerate(units):
                r0, n = buckets[b]
                rows = pl.ds(r0, n)
                q2, k2, go2 = q_ref[rows, at], k_ref[rows, at], obuf[rows, at]
                first = halves(n)
                two = (2 * i, 2 * i + 1)
                gv = [dot_tn(probs[u].astype(bf16), go2) for u in two]
                gq = [dot_nn(gs[u], k2) for u in two]
                gk = [dot_tn(gs[u], q2) for u in two]
                q_ref[rows, at] = (jnp.where(first, gq[0], gq[1]) * scale).astype(bf16)
                k_ref[rows, at] = (jnp.where(first, gk[0], gk[1]) * scale).astype(bf16)
                v_ref[rows, at] = jnp.where(first, gv[0], gv[1]).astype(bf16)
        head_loop(bs, body, lo, hi)

    q_ref, k_ref, v_ref = gr.at[8], gr.at[9], gr.at[10]
    diagonal = (1 - st) * 4096
    bias_at = 5 + 10 * st
    ffn_at = 13 + 14 * st
    ffn_gain = 1 + 3 * st

    def by_tiles(fn):
        for t in range(tiles):
            fn(pl.ds(t * 256, 256))

    def self_project(bs):
        rows = at_rows(bs)

        def project(which, carry):
            for t in range(tiles):
                at = pl.ds(t * 256, 256)
                value = dot_nn(xb[rows, :], wproj[which, :, at])
                bias = vec[pl.ds(bias_at + which // 2, 1), at] * jnp.where(which == 1, 0.0, 1.0)
                gr[8 + which, rows, at] = (value + bias).astype(bf16)
            return carry
        lax.fori_loop(0, 3, project, 0)

    def self_output(bs):
        rows = at_rows(bs)

        def tile(at):
            acc[rows, at] = dot_nn(obuf[rows, :], wo[:, at])
        by_tiles(tile)
        norm_forward(bs, xb, u_self, bias_at + 2, 2 * st, bias_at + 3, hlow, grad)

    def ffn_forward(bs, residual, wait_in, wait_out):
        r0, n = span(bs)
        rows = pl.ds(r0, n)

        def ffn_slot(j, carry):
            for t in range(tiles):
                at = pl.ds(t * 256, 256)
                wide = pl.ds(pl.multiple_of(j * width + t * 256, 256), 256)
                zv = dot_nn(hlow[rows, :], win[:, wide]) + bias_in[pl.ds(st, 1), wide]
                cdf = 0.5 * (1.0 + lax.erf(zv * (0.5 ** 0.5)))
                pdf = jnp.exp(-0.5 * zv * zv) * 0.3989422804014327
                gr[1 + j, rows, at] = (zv * cdf).astype(bf16)
                dg[j, rows, at] = (cdf + zv * pdf).astype(bf16)
            return carry
        if wait_in:
            loads[3].wait()
        lax.fori_loop(0, slots, ffn_slot, 0)

        def ffn_out(at):
            total = dot_nn(gr[1, rows, :], wout[pl.ds(0, width), at])
            for j in range(1, slots):
                total = total + dot_nn(gr[1 + j, rows, :], wout[pl.ds(j * width, width), at])
            acc[rows, at] = total
        if wait_out:
            loads[4].wait()
        by_tiles(ffn_out)
        norm_forward(bs, residual, u_ffn, ffn_at, ffn_gain, ffn_at + 1, xb, None)

    def ffn_inner(bs, lo, hi, last):
        r0, n = span(bs)
        rows = pl.ds(r0, n)

        def ffn_inner_slot(j, carry):
            for t in range(tiles):
                at = pl.ds(t * 256, 256)
                wide = pl.ds(pl.multiple_of(j * width + t * 256, 256), 256)
                value = dot_nt(gr[0, rows, :], wout[wide, :])
                gr[1 + j, rows, at] = (value * dg[j, rows, at].astype(f32)).astype(bf16)
            if last:
                remote(gr.at[1 + j], grp.at[1 + j], gr_send.at[1 + j], gr_recv.at[1 + j], core_id).start()
            return carry
        lax.fori_loop(lo, hi, ffn_inner_slot, 0)

    def ffn_input(bs):
        rows = at_rows(bs)

        def tile(at):
            total = grad[rows, at]
            for j in range(slots):
                total = total + dot_nt(gr[1 + j, rows, :], win[at, pl.ds(j * width, width)])
            grad[rows, at] = total
        by_tiles(tile)

    def cross_forward(bs):
        rows = at_rows(bs)

        def memory_kv(which, carry):
            for t in range(tiles):
                at = pl.ds(t * 256, 256)
                value = dot_nn(mem[rows, pl.ds(0, half)], wx[2 * which, :, at]) + dot_nn(mem[rows, pl.ds(half, half)], wx[2 * which + 1, :, at])
                kv[which, rows, at] = value.astype(bf16)
            return carry
        lax.fori_loop(0, 2, memory_kv, 0)
        attend_forward(bs, gr.at[6], kv.at[0], kv.at[1], lens[:2], 4096, 20, obuf)

        def cross_out(at):
            acc[rows, at] = dot_nn(obuf[rows, :], wsecond[:, at])
        by_tiles(cross_out)
        norm_forward(bs, grad, u_cross, 21, 3, 22, hlow, hw)
        transposed(7, bs, obuf)

    def cross_backward(bs):
        rows = at_rows(bs)
        norm_backward(bs, u_cross, grad, 3, 22, hw, gr.at[5])

        def cross_up(at):
            obuf[rows, at] = dot_nt(gr[5, rows, :], wsecond[at, :]).astype(bf16)
        by_tiles(cross_up)
        attend_backward(bs, gr.at[6], kv.at[0], kv.at[1], lens[:2], 4096)

        def memory_half(h, carry):
            at = cols(h, half)
            gmem[rows, at] = (dot_nt(kv[0, rows, :], wx[h]) + dot_nt(kv[1, rows, :], wx[2 + h])).astype(bf16)
            return carry
        lax.fori_loop(0, 2, memory_half, 0)
        gm_copy[bs[0]].start()

    def cross_input(at):
        grad[:, at] = hw[:, at] + dot_nt(gr[6], wfirst[at, :])

    def lanes_of(h):
        return pl.ds(0, width) if h is None else cols(h, half)

    def sems(i, stage, h):
        k = 2 * stage + (0 if h is None else h)
        return sem_send.at[i, k], sem_recv.at[i, k]

    def first_copy(i, z_first, h):
        at = lanes_of(h)
        return remote(one_send.at[i % SEND_SLOTS, :, :, :, at], one_recv.at[i, :, :, :, at], *sems(i, 0, h),
                      near_id if z_first else y_id)

    def second_copy(i, z_first, h):
        at = lanes_of(h)
        source = one_recv.at[i, 1 - zh, :, :, at] if z_first else one_recv.at[i, :, 1 - zl, :, at]
        return remote(source, two_recv.at[i, :, :, at], *sems(i, 1, h), far_id if z_first else near_id)

    def third_copy(i, z_first, h):
        at = lanes_of(h)
        source = two_recv.at[i, 1 - y if z_first else 1 - zh, :, at]
        return remote(source, out_part.at[i, :, at], *sems(i, 2, h), y_id if z_first else far_id)

    def own_copy(i, z_first, h):
        at = lanes_of(h)
        return pltpu.make_async_copy(two_recv.at[i, y if z_first else zh, :, at], out_own.at[i, :, at], own_sem.at[i, 0 if h is None else h])

    def product(left, slot, z_first, other, at):
        if z_first:
            zz = 1 - zl if other else zl
            mine, theirs = lt[left, :, zz, :, c], ltp[left, :, zz]
        else:
            yy = 1 - y if other else y
            mine, theirs = lt[left, :, :, yy, c], ltp[left, :, :, yy]
        shape = (4 * PIECE, ROWS)
        return dot_nn(mine.reshape(shape), gr[slot, :, at]) + dot_nn(theirs.reshape(shape), grp[slot, :, at])

    def piece_tiles(h, fn):
        if h is None:
            loop(0, tiles, lambda t: fn(cols(t, 256), 256))
        else:
            fn(cols(h, half), half)

    def send_piece(i, left, slot, z_first=False, h=None):
        def tile(at, n):
            one_send[i % SEND_SLOTS, :, :, :, at] = product(left, slot, z_first, True, at).astype(bf16).reshape(2, 2, PIECE, n)
        piece_tiles(h, tile)
        first_copy(i, z_first, h).start()

    def keep_piece(i, left, slot, z_first=False, h=None):
        first_copy(i, z_first, h).wait()

        def tile(at, n):
            total = one_recv[i, :, :, :, at].reshape(4 * PIECE, n).astype(f32) + product(left, slot, z_first, False, at)
            one_recv[i, :, :, :, at] = total.astype(bf16).reshape(2, 2, PIECE, n)
        piece_tiles(h, tile)
        second_copy(i, z_first, h).start()

    def pass_piece(i, z_first=False, h=None):
        second_copy(i, z_first, h).wait()
        at = lanes_of(h)
        for k in range(2):
            mine = one_recv[i, zh, k, :, at] if z_first else one_recv[i, k, zl, :, at]
            two_recv[i, k, :, at] = (two_recv[i, k, :, at].astype(f32) + mine.astype(f32)).astype(bf16)
        third_copy(i, z_first, h).start()
        own_copy(i, z_first, h).start()

    def loop(lo, hi, fn):
        def step(i, carry):
            fn(i)
            return carry
        lax.fori_loop(lo, hi, step, 0)

    def wait_active():
        for i in range(4):
            lt_copy[i].wait()
        gr_first[0].wait()
        gr_first[1].wait()

    @pl.when(is_enc)
    def _():
        again = pltpu.make_async_copy(x_hbm, mem, load_sem.at[8])
        again.start()
        for bs in (long, short):
            self_project(bs)
            attend_forward(bs, q_ref, k_ref, v_ref, own_lens, diagonal, None, obuf)
            if bs == long:
                loads[2].wait()
            self_output(bs)
            ffn_forward(bs, grad, bs == long, bs == long)
            mem_copy[bs[0]].start()
        transposed_active(both)
        for k in range(4):
            lt_copy[k].start()
        again.wait()
        for i, ref in ((4, mem), (5, obuf), (6, hlow), (7, xb)):
            transposed(i, both, ref)
            lt_copy[i].start()
        loads[5].wait()
        loads[6].wait()
        for bs in (short, long):
            gm_copy[bs[0]].wait_recv()
            norm_backward(bs, u_ffn, up, ffn_gain, ffn_at + 1, grad, gr.at[0])
            gr_first[bs[0]].start()
            if bs == short:
                ffn_inner(bs, 0, slots, False)
                ffn_input(bs)
        ffn_inner(long, 0, 1, True)

    @pl.when(is_dec)
    def _():
        self_project(both)
        transposed(4, both, xb)
        lt_copy[4].start()

        def wx_forward(h):
            wx_first[h].wait_recv()
            wx_y[h].start()
            wx_near[h].start()
        wx_forward(0)
        attend_forward(both, q_ref, k_ref, v_ref, own_lens, diagonal, None, obuf)
        wx_forward(1)
        loads[2].wait()
        self_output(both)
        wx_forward(2)
        for cp in loads[5:]:
            cp.wait()

        def cross_query(at):
            gr[6, :, at] = (dot_nn(hlow[...], wfirst[:, at]) + vec[pl.ds(19, 1), at]).astype(bf16)
        by_tiles(cross_query)
        wx_forward(3)
        transposed(5, both, obuf)
        lt_copy[5].start()
        transposed(8, both, hlow)
        lt_copy[8].start()
        cot_load.wait()
        for h in range(WX_CHUNKS):
            wx_y[h].wait()
            wx_far[h].start()
        for h in range(WX_CHUNKS):
            wx_near[h].wait()
            wx_far[h].wait()
        for bs in (long, short):
            mem_copy[bs[0]].wait_recv()
            cross_forward(bs)
        lt_copy[7].start()
        ffn_forward(both, hw, True, True)
        transposed_active(both)
        for k in range(4):
            lt_copy[k].start()
        norm_backward(both, u_ffn, up, ffn_gain, ffn_at + 1, grad, gr.at[0])
        gr_first[0].start()
        gr_first[1].start()
        ffn_inner(both, 0, slots, True)
        ffn_input(both)
        for bs in (short, long):
            cross_backward(bs)
        transposed(6, both, hlow)
        lt_copy[6].start()

    wait_active()

    def first_sends(k):
        send_piece(2 + k, 2 + k, 0)
        send_piece(k, k, 0, True)
    loop(0, 2, first_sends)

    @pl.when(is_enc)
    def _():
        ffn_inner(long, 1, slots, True)
    lt_copy[6].wait()

    def inner_sends(j):
        remote(gr.at[1 + j], grp.at[1 + j], gr_send.at[1 + j], gr_recv.at[1 + j], core_id).wait()
        send_piece(4 + j, 6, 1 + j)
    loop(0, slots, inner_sends)

    @pl.when(is_enc)
    def _():
        ffn_input(long)

    @pl.when(is_dec)
    def _():
        gr_copy[5].start()
        gr_copy[6].start()
        by_tiles(cross_input)
        col_sum(obuf, 20)
        col_sum(gr.at[6], 19)
        col_sum(gr.at[5], 21)

    rows_copy = pltpu.make_async_copy(xb, out_rows, io_sem.at[0])
    rows_copy.start()

    norm_backward(both, u_self, grad, 2 * st, bias_at + 3, hw, gr.at[7])
    gr_copy[7].start()

    def self_up(at):
        obuf[:, at] = dot_nt(gr[7], wo[at, :]).astype(bf16)
    by_tiles(self_up)

    def keep_and_attend(k, carry):
        keep_piece(2 + k, 2 + k, 0)
        keep_piece(k, k, 0, True)
        attend_backward(both, q_ref, k_ref, v_ref, own_lens, diagonal, k * 3, k * 3 + 3)
        return carry
    lax.fori_loop(0, 2, keep_and_attend, 0)
    for j in range(3):
        gr_copy[8 + j].start()

    @pl.when(is_dec)
    def _():
        gk_copy[0].start()
        gk_copy[1].start()

    def self_input(at):
        total = hw[:, at]
        for j in range(3):
            total = total + dot_nt(gr[8 + j], wproj[j, at, :])
        hw[:, at] = total
    by_tiles(self_input)
    grad_copy = pltpu.make_async_copy(hw, out_grad, io_sem.at[1])
    grad_copy.start()
    loop(2, 4, pass_piece)
    for i in (4, 5, 7):
        lt_copy[i].wait()

    @pl.when(is_dec)
    def _():
        lt_copy[8].wait()
    for i in range(7, 11):
        gr_copy[i].wait()
    col_sum(gr.at[0], ffn_at)
    loop(0, slots, lambda j: col_sum(gr.at[1 + j], ffn_at - 4 + j))
    col_sum(gr.at[7], bias_at + 2)
    col_sum(gr.at[8], bias_at)
    col_sum(gr.at[10], bias_at + 1)
    own_half = pl.ds(pl.multiple_of(c * half, half), half)
    other_half = pl.ds(pl.multiple_of((1 - c) * half, half), half)
    v_copy = [remote(vg.at[:, other_half] if k == 0 else vbuf.at[2 * k], vbuf.at[2 * k + 1], v_send.at[k], v_recv.at[k], dev)
              for k, dev in enumerate((core_id, y_id, near_id, far_id, x_id))]
    v_last = remote(vboth.at[:, :, own_half], vboth.at[:, :, own_half], v_send.at[5], v_recv.at[5], core_id)
    vbuf[0] = vg[:, own_half]

    def v_next(k):
        v_copy[k].wait()
        vbuf[2 * k + 2] = vbuf[2 * k] + vbuf[2 * k + 1]
        v_copy[k + 1].start()
    v_copy[0].start()

    @pl.when(is_enc)
    def _():
        gk_copy[0].wait_recv()
        gk_copy[1].wait_recv()
        gr_copy[5].start()
        gr_copy[6].start()
    v_next(0)

    def attention_piece(k):
        return 8 + k, 5 - (k + 3) // 4, 7 + k

    def cross_piece(k):
        return 12 + k // 2, 7 + st * (k // 2), 5 + k // 2, False, k % 2

    def middle(k):
        send_piece(*attention_piece(k))
        keep_piece(4 + k, 6, 1 + k)

        @pl.when(k > 0)
        def _():
            pass_piece(3 + k)
    loop(0, 4, middle)
    for i in range(5, 7):
        gr_copy[i].wait()
    loop(0, 4, lambda k: send_piece(*cross_piece(k)))
    v_next(1)

    def later(k):
        keep_piece(*attention_piece(k))
        pass_piece(7 + k)
    loop(0, 4, later)
    v_next(2)
    loop(0, 2, lambda i: pass_piece(i, True))

    def ends(k):
        i, left, slot, z_first, h = cross_piece(k)
        keep_piece(i, left, slot, z_first, h)

        @pl.when(k == 0)
        def _():
            pass_piece(11)

        @pl.when(k > 0)
        def _():
            pass_piece(12 + (k - 1) // 2, False, (k + 1) % 2)

        @pl.when(k == 2)
        def _():
            v_next(3)
    loop(0, 4, ends)
    pass_piece(13, False, 1)
    v_copy[4].wait()
    vboth[st, :, own_half] = vbuf[8]
    vboth[1 - st, :, own_half] = vbuf[9]
    v_last.start()
    v_last.wait()
    vec_copy = pltpu.make_async_copy(vboth, out_vec, io_sem.at[2])
    vec_copy.start()

    def finish(i, z_first=False, h=None):
        third_copy(i, z_first, h).wait()
        own_copy(i, z_first, h).wait()
    loop(0, 2, lambda i: finish(i, True))
    loop(2, 12, finish)
    loop(0, 4, lambda k: finish(12 + k // 2, False, k % 2))
    rows_copy.wait()
    grad_copy.wait()
    vec_copy.wait()

    @pl.when(is_enc)
    def _():
        for h in range(WX_CHUNKS):
            wx_first[h].wait_send()
        for h in range(2):
            mem_copy[h].wait_send()

    @pl.when(is_dec)
    def _():
        for h in range(2):
            gm_copy[h].wait_send()
            gk_copy[h].wait_send()


def last_kernel(width, rows_in, grad_in, own, parts, vec_sum, rows_out, grad_out, *refs):
    outs, (vec_buf, rows_buf, grad_buf, own_buf, part_buf, sums, in_sem, through_sem, out_sem) = refs[:8], refs[8:]
    group = PIECES // 2
    loads = []
    for g in range(2):
        at = pl.ds(g * group, group)
        loads.append((pltpu.make_async_copy(own.at[at], own_buf.at[at], in_sem.at[g, 0]),
                      pltpu.make_async_copy(parts.at[at], part_buf.at[at], in_sem.at[g, 1])))
    vec_load = pltpu.make_async_copy(vec_sum, vec_buf, through_sem.at[2])
    into = [pltpu.make_async_copy(grad_in, grad_buf, through_sem.at[0]), pltpu.make_async_copy(rows_in, rows_buf, through_sem.at[1])]
    for cp in (*loads[0], into[0], *loads[1], into[1], vec_load):
        cp.start()
    stores = []

    def store(src, dst):
        stores.append(pltpu.make_async_copy(src, dst, out_sem.at[len(stores)]))
        stores[-1].start()
    for g in range(2):
        for cp in loads[g]:
            cp.wait()
        for i in range(g * group, (g + 1) * group):
            sums[i] = own_buf[i].astype(f32) + part_buf[i].astype(f32)
            if i < 4:
                store(sums.at[i], outs[0].at[pl.ds(i * PIECE, PIECE), :])
            elif i < 8:
                store(sums.at[i], outs[1].at[:, pl.ds((i - 4) * width, width)])
            elif i == 8:
                store(sums.at[i], outs[4])
            elif i == 11:
                store(sums.at[pl.ds(9, 3)], outs[5])
            elif i > 11:
                store(sums.at[i], outs[i - 10])
        into[g].wait()
        store(rows_buf if g else grad_buf, rows_out if g else grad_out)
    vec_load.wait()
    shift = lax.rem(width - lax.axis_index("dp") * PIECE, width)
    for s, (g0, g1, b0, b1) in enumerate(((0, 2, 0, 10), (2, 5, 10, 24))):
        turned = pltpu.roll(vec_buf[s], shift, 1)
        outs[6][pl.ds(g0, g1 - g0), :] = turned[:g1 - g0, :PIECE]
        outs[7][pl.ds(b0, b1 - b0), :] = turned[3:3 + b1 - b0, :PIECE]
    for cp in stores:
        cp.wait()


def whole_step(lengths, gains, biases, x, cot, wproj, wo, wfirst, wsecond, win, wout):
    width = x.shape[1]
    hidden = win.shape[1]
    half = width // 2
    any_space = pl.BlockSpec(memory_space=pl.ANY)
    vmem = pl.BlockSpec(memory_space=pltpu.VMEM)
    dma = pltpu.SemaphoreType.DMA
    slots = hidden // width
    small = (32, width)
    results = pl.pallas_call(
        functools.partial(step_kernel, width, hidden),
        out_shape=[
            jax.ShapeDtypeStruct((ROWS, width), bf16),
            jax.ShapeDtypeStruct((ROWS, width), f32),
            jax.ShapeDtypeStruct((PIECES, PIECE, width), bf16),
            jax.ShapeDtypeStruct((PIECES, PIECE, width), bf16),
            jax.ShapeDtypeStruct((2, VEC_ROWS, width), f32),
        ],
        in_specs=[pl.BlockSpec(memory_space=pltpu.SMEM), vmem, vmem] + [any_space] * 8,
        out_specs=[any_space] * 5,
        scratch_shapes=[
            pltpu.VMEM(small, f32), pltpu.VMEM((2, hidden), f32),
            pltpu.VMEM(wproj.shape, bf16), pltpu.VMEM(wo.shape, bf16), pltpu.VMEM(wfirst.shape, bf16),
            pltpu.VMEM(wsecond.shape, bf16), pltpu.VMEM(win.shape, bf16), pltpu.VMEM(wout.shape, bf16),
            pltpu.VMEM((4, half, width), bf16),
            pltpu.VMEM((ROWS, width), bf16),
            pltpu.VMEM((ROWS, width), bf16),
            pltpu.VMEM((ROWS, width), bf16),
            pltpu.VMEM((ROWS, width), bf16),
            pltpu.VMEM((ROWS, width), bf16),
            pltpu.VMEM((slots, ROWS, width), bf16),
            pltpu.VMEM((2, ROWS, width), bf16),
            pltpu.VMEM((ROWS, width), f32),
            pltpu.VMEM((ROWS, width), f32),
            pltpu.VMEM((ROWS, width), f32),
            pltpu.VMEM((ROWS, width), f32),
            pltpu.VMEM((ROWS, width), f32),
            pltpu.VMEM((ROWS, width), f32),
            pltpu.VMEM((11, ROWS, width), bf16),
            pltpu.VMEM((11, ROWS, width), bf16),
            pltpu.VMEM((9, 2, 2, 2, 2, PIECE, ROWS), bf16),
            pltpu.VMEM((9, 2, 2, 2, PIECE, ROWS), bf16),
            pltpu.VMEM((SEND_SLOTS, 2, 2, PIECE, width), bf16),
            pltpu.VMEM((PIECES, 2, 2, PIECE, width), bf16),
            pltpu.VMEM((PIECES, 2, PIECE, width), bf16),
            pltpu.VMEM((ROWS, width), bf16),
            pltpu.VMEM((VEC_ROWS, width), f32),
            pltpu.VMEM((10, VEC_ROWS, half), f32),
            pltpu.VMEM((2, VEC_ROWS, width), f32),
            dma((9,)), dma((4 * WX_CHUNKS,)), dma((4 * WX_CHUNKS,)), dma((2,)), dma((2,)), dma((2,)), dma((2,)), dma((2,)), dma((2,)),
            dma((9,)), dma((9,)), dma((12,)), dma((12,)),
            dma((PIECES, 6)), dma((PIECES, 6)), dma((PIECES, 2)), dma((3,)), dma((6,)), dma((6,)),
        ],
        compiler_params=pltpu.CompilerParams(collective_id=0, has_side_effects=True, vmem_limit_bytes=VMEM_LIMIT),
        name="step",
    )(lengths, gains, biases, x, cot, wproj, wo, wfirst, wsecond, win, wout)
    shapes = [(4 * PIECE, width), (PIECE, hidden), (PIECE, width), (PIECE, width), (PIECE, width), (3, PIECE, width),
              (5, PIECE), (24, PIECE)]
    return pl.pallas_call(
        functools.partial(last_kernel, width),
        out_shape=[jax.ShapeDtypeStruct((ROWS, width), bf16), jax.ShapeDtypeStruct((ROWS, width), f32)]
        + [jax.ShapeDtypeStruct(shape, f32) for shape in shapes],
        in_specs=[any_space] * 5,
        out_specs=[any_space] * 8 + [vmem] * 2,
        scratch_shapes=[
            pltpu.VMEM((2, VEC_ROWS, width), f32), pltpu.VMEM((ROWS, width), bf16), pltpu.VMEM((ROWS, width), f32),
            pltpu.VMEM((PIECES, PIECE, width), bf16), pltpu.VMEM((PIECES, PIECE, width), bf16),
            pltpu.VMEM((PIECES, PIECE, width), f32), dma((2, 2)), dma((3,)), dma((PIECES + 2,)),
        ],
        compiler_params=pltpu.CompilerParams(vmem_limit_bytes=VMEM_LIMIT),
        name="last",
    )(*results)


eps_norm = 1e-05
low_type = jnp.bfloat16
wide_type = jnp.float32


def as_sent(shard):
    return jax.tree.map(lambda a: a.astype(jnp.bfloat16) if a.dtype == jnp.float32 else a, shard)


def shifted(shard, axis, by):
    count = lax.axis_size(axis)
    pairs = [(i, i + by) for i in range(count) if 0 <= i + by < count]
    return lax.ppermute(shard, axis, pairs)


def matmul(left_mat, right_mat):
    return jnp.dot(left_mat, right_mat, preferred_element_type=wide_type)


def matmul_tn(left_mat, right_mat):
    return lax.dot_general(
        left_mat, right_mat, (((0,), (0,)), ((), ())), preferred_element_type=wide_type
    )


def matmul_nt(left_mat, right_mat):
    return lax.dot_general(
        left_mat, right_mat, (((1,), (1,)), ((), ())), preferred_element_type=wide_type
    )


def column_sum(tensor):
    return jnp.sum(tensor.astype(wide_type), axis=0)


def norm_rows(tensor, norm_gain, norm_shift):
    centre = tensor - jnp.mean(tensor, axis=-1, keepdims=True)
    spread = jnp.mean(centre * centre, axis=-1, keepdims=True)
    return centre * lax.rsqrt(spread + eps_norm) * norm_gain + norm_shift


def norm_back(tensor, norm_gain, norm_shift, upstream):
    unused, pullback = jax.vjp(norm_rows, tensor, norm_gain, norm_shift)
    return pullback(upstream)


def gelu_exact(tensor):
    return jax.nn.gelu(tensor, approximate=False)


def key_mask(row_count, key_count, length, causal):
    columns = lax.broadcasted_iota(jnp.int32, (row_count, key_count), 1)
    allowed = columns < length
    if causal:
        allowed = allowed & (columns <= lax.broadcasted_iota(jnp.int32, (row_count, key_count), 0))
    return allowed


def split_heads(tensor):
    return tensor.reshape(tensor.shape[0], -1, HDIM)


def attend_scores(queries, key_rows, allowed):
    scores = jnp.einsum(
        "qhd,khd->hqk",
        split_heads(queries),
        split_heads(key_rows),
        preferred_element_type=wide_type,
    )
    return jnp.where(allowed[None], scores * HDIM ** (-0.5), -1e30)


def attend_forward(queries, key_rows, values, allowed):
    scores = attend_scores(queries, key_rows, allowed)
    row_max = jnp.max(scores, axis=-1, keepdims=True)
    log_total = row_max + jnp.log(jnp.sum(jnp.exp(scores - row_max), axis=-1, keepdims=True))
    softmaxed = jnp.exp(scores - log_total).astype(low_type)
    attended = jnp.einsum(
        "hqk,khd->qhd", softmaxed, split_heads(values), preferred_element_type=wide_type
    )
    return (attended.reshape(queries.shape[0], -1), log_total)


def attend_backward(queries, key_rows, values, allowed, log_total, upstream):
    softmaxed = jnp.exp(attend_scores(queries, key_rows, allowed) - log_total)
    grad_heads = split_heads(upstream)
    grad_values = jnp.einsum(
        "hqk,qhd->khd", softmaxed.astype(low_type), grad_heads, preferred_element_type=wide_type
    )
    grad_probs = jnp.einsum(
        "qhd,khd->hqk", grad_heads, split_heads(values), preferred_element_type=wide_type
    )
    grad_scores = (
        softmaxed * (grad_probs - jnp.sum(softmaxed * grad_probs, axis=-1, keepdims=True))
    ).astype(low_type)
    scale_factor = HDIM ** (-0.5)
    grad_queries = (
        jnp.einsum(
            "hqk,khd->qhd", grad_scores, split_heads(key_rows), preferred_element_type=wide_type
        )
        * scale_factor
    )
    grad_keys = (
        jnp.einsum(
            "hqk,qhd->khd", grad_scores, split_heads(queries), preferred_element_type=wide_type
        )
        * scale_factor
    )
    key_count = key_rows.shape[0]
    return (
        grad_queries.reshape(queries.shape[0], -1),
        grad_keys.reshape(key_count, -1),
        grad_values.reshape(key_count, -1),
    )


def self_forward(row_block, length, causal, w_proj, w_out, vectors):
    bias_q, bias_v, bias_o, norm_gain, norm_shift = vectors
    row_count = row_block.shape[0]
    offsets = jnp.stack([bias_q, jnp.zeros_like(bias_q), bias_v])[:, None, :]
    projected = (
        jnp.einsum("rd,cde->cre", row_block, w_proj, preferred_element_type=wide_type) + offsets
    ).astype(low_type)
    allowed = key_mask(row_count, row_count, length, causal)
    attended, log_total = attend_forward(projected[0], projected[1], projected[2], allowed)
    attended = attended.astype(low_type)
    summed = row_block.astype(wide_type) + matmul(attended, w_out) + bias_o
    return (norm_rows(summed, norm_gain, norm_shift), (projected, log_total, attended, summed))


def self_backward(row_block, length, causal, w_proj, w_out, vectors, saved_fwd, upstream):
    projected, log_total, attended, summed = saved_fwd
    row_count = row_block.shape[0]
    grad_sum, grad_gain, grad_shift = norm_back(summed, vectors[3], vectors[4], upstream)
    grad_branch = grad_sum.astype(low_type)
    grad_attended = matmul_nt(grad_branch, w_out).astype(low_type)
    allowed = key_mask(row_count, row_count, length, causal)
    grad_q, grad_k, grad_v = attend_backward(
        projected[0], projected[1], projected[2], allowed, log_total, grad_attended
    )
    grad_proj = jnp.stack([grad_q, grad_k, grad_v]).astype(low_type)
    grad_rows = grad_sum + jnp.einsum(
        "cre,cde->rd", grad_proj, w_proj, preferred_element_type=wide_type
    )
    weight_grads = (
        jnp.einsum("rd,cre->cde", row_block, grad_proj, preferred_element_type=wide_type),
        matmul_tn(attended, grad_branch),
    )
    vector_grads = (
        column_sum(grad_proj[0]),
        column_sum(grad_proj[2]),
        column_sum(grad_branch),
        grad_gain,
        grad_shift,
    )
    return (grad_rows, weight_grads, vector_grads)


def ffn_forward(hidden, w_in, w_out, vectors):
    bias_in, bias_out, norm_gain, norm_shift = vectors
    low_hidden = hidden.astype(low_type)
    inner_act = matmul(low_hidden, w_in) + bias_in
    active = gelu_exact(inner_act).astype(low_type)
    summed = hidden + matmul(active, w_out) + bias_out
    return (norm_rows(summed, norm_gain, norm_shift), (low_hidden, inner_act, active, summed))


def ffn_backward(w_in, w_out, vectors, saved_fwd, upstream):
    low_hidden, inner_act, active, summed = saved_fwd
    grad_sum, grad_gain, grad_shift = norm_back(summed, vectors[2], vectors[3], upstream)
    grad_branch = grad_sum.astype(low_type)
    unused, pullback = jax.vjp(gelu_exact, inner_act)
    grad_inner = pullback(matmul_nt(grad_branch, w_out))[0].astype(low_type)
    grad_hidden = grad_sum + matmul_nt(grad_inner, w_in)
    weight_grads = (matmul_tn(low_hidden, grad_inner), matmul_tn(active, grad_branch))
    vector_grads = (column_sum(grad_inner), column_sum(grad_branch), grad_gain, grad_shift)
    return (grad_hidden, weight_grads, vector_grads)


def cross_forward(hidden, memory, src_len, w_query, w_out, vectors):
    bias_q, bias_v, bias_o, norm_gain, norm_shift = vectors
    low_hidden = hidden.astype(low_type)
    queries = (matmul(low_hidden, w_query) + bias_q).astype(low_type)
    allowed = key_mask(hidden.shape[0], memory.shape[1], src_len, False)
    attended, log_total = attend_forward(queries, memory[0], memory[1], allowed)
    attended = (attended + bias_v).astype(low_type)
    summed = hidden + matmul(attended, w_out) + bias_o
    return (
        norm_rows(summed, norm_gain, norm_shift),
        (low_hidden, queries, log_total, attended, summed),
    )


def cross_backward(memory, src_len, w_query, w_out, vectors, saved_fwd, upstream):
    low_hidden, queries, log_total, attended, summed = saved_fwd
    grad_sum, grad_gain, grad_shift = norm_back(summed, vectors[3], vectors[4], upstream)
    grad_branch = grad_sum.astype(low_type)
    grad_attended = matmul_nt(grad_branch, w_out).astype(low_type)
    allowed = key_mask(queries.shape[0], memory.shape[1], src_len, False)
    grad_q, grad_k, grad_v = attend_backward(
        queries, memory[0], memory[1], allowed, log_total, grad_attended
    )
    grad_query = grad_q.astype(low_type)
    grad_memory = jnp.stack([grad_k, grad_v]).astype(low_type)
    grad_hidden = grad_sum + matmul_nt(grad_query, w_query)
    weight_grads = (matmul_tn(low_hidden, grad_query), matmul_tn(attended, grad_branch))
    vector_grads = (
        column_sum(grad_query),
        column_sum(grad_attended),
        column_sum(grad_branch),
        grad_gain,
        grad_shift,
    )
    return (grad_hidden, grad_memory, weight_grads, vector_grads)


def self_vectors(gain_rows, bias_rows, decoder):
    base_row = 10 if decoder else 0
    gain_row = 2 if decoder else 0
    return (
        bias_rows[base_row],
        bias_rows[base_row + 1],
        bias_rows[base_row + 2],
        gain_rows[gain_row],
        bias_rows[base_row + 3],
    )


def ffn_vectors(gain_rows, bias_rows, decoder):
    base_row = 18 if decoder else 4
    gain_row = 4 if decoder else 1
    return (
        bias_rows[base_row : base_row + 4].reshape(-1),
        bias_rows[base_row + 4],
        gain_rows[gain_row],
        bias_rows[base_row + 5],
    )


def cross_vectors(gain_rows, bias_rows):
    return (bias_rows[14], bias_rows[15], bias_rows[16], gain_rows[3], bias_rows[17])


def self_plan(decoder, vector_grads):
    base_row = 10 if decoder else 0
    gain_row = 2 if decoder else 0
    return (
        ("biases", base_row, vector_grads[0]),
        ("biases", base_row + 1, vector_grads[1]),
        ("biases", base_row + 2, vector_grads[2]),
        ("gains", gain_row, vector_grads[3]),
        ("biases", base_row + 3, vector_grads[4]),
    )


def ffn_plan(decoder, vector_grads):
    base_row = 18 if decoder else 4
    gain_row = 4 if decoder else 1
    return (
        ("biases", base_row, vector_grads[0]),
        ("biases", base_row + 4, vector_grads[1]),
        ("gains", gain_row, vector_grads[2]),
        ("biases", base_row + 5, vector_grads[3]),
    )


def cross_plan(vector_grads):
    return (
        ("biases", 14, vector_grads[0]),
        ("biases", 15, vector_grads[1]),
        ("biases", 16, vector_grads[2]),
        ("gains", 3, vector_grads[3]),
        ("biases", 17, vector_grads[4]),
    )


def accumulate(totals, weight_names, weight_grads, vector_plan):
    merged = dict(totals)
    for key_name, tensor in zip(weight_names, weight_grads):
        merged[key_name] = merged[key_name] + tensor
    for table_name, row_at, tensor in vector_plan:
        table_now = merged[table_name]
        row_block = tensor.reshape(-1, table_now.shape[1])
        merged[table_name] = table_now.at[row_at : row_at + row_block.shape[0]].add(row_block)
    return merged


def updated(progress, key_name, position, tensor):
    copied = dict(progress)
    copied[key_name] = [
        tensor if slot_index == position else entry_now
        for slot_index, entry_now in enumerate(progress[key_name])
    ]
    return copied


def with_totals(progress, totals):
    copied = dict(progress)
    copied["totals"] = totals
    return copied


def forward_pass(tensor):
    return jax.tree.map(
        lambda part, own: part.astype(own.dtype), shifted(as_sent(tensor), "stream", 1), tensor
    )


def backward_pass(tensor):
    return jax.tree.map(
        lambda part, own: part.astype(own.dtype), shifted(as_sent(tensor), "stream", -1), tensor
    )


def keep_same(progress):
    return progress


def plain_body(
    inputs,
    lengths,
    cotangent,
    attn_in,
    attn_out,
    cross_first,
    cross_second,
    ffn_in,
    ffn_out,
    gains,
    biases,
):
    own_rows = inputs[0]
    model_width = own_rows.shape[1]
    hidden_width = ffn_in.shape[2]
    head_count = model_width // HDIM
    row_sizes = (SHORT, LONG)
    bucket_spans = ((0, SHORT), (SHORT, SHORT + LONG))
    row_pieces = [own_rows[start_row:stop_row] for start_row, stop_row in bucket_spans]
    grad_pieces = [
        cotangent[start_row:stop_row].astype(wide_type) for start_row, stop_row in bucket_spans
    ]
    src_lens = [lengths[0, 0, bucket_idx] for bucket_idx in range(2)]
    tgt_lens = [lengths[1, 0, bucket_idx] for bucket_idx in range(2)]
    w_proj = attn_in[0]
    w_attn_out = attn_out[0]
    w_first = cross_first[0]
    w_second = cross_second[0]
    w_ffn_in = ffn_in[0]
    w_ffn_out = ffn_out[0]
    gain_rows = gains.astype(wide_type)
    bias_rows = biases.astype(wide_type)
    enc_self = self_vectors(gain_rows, bias_rows, False)
    enc_ffn = ffn_vectors(gain_rows, bias_rows, False)
    dec_self = self_vectors(gain_rows, bias_rows, True)
    dec_ffn = ffn_vectors(gain_rows, bias_rows, True)
    dec_cross = cross_vectors(gain_rows, bias_rows)
    is_decoder = lax.axis_index("stream") == 1

    def blank_self(size_rows):
        return (
            jnp.zeros((3, size_rows, model_width), low_type),
            jnp.zeros((head_count, size_rows, 1), wide_type),
            jnp.zeros((size_rows, model_width), low_type),
            jnp.zeros((size_rows, model_width), wide_type),
        )

    def blank_ffn(size_rows):
        return (
            jnp.zeros((size_rows, model_width), low_type),
            jnp.zeros((size_rows, hidden_width), wide_type),
            jnp.zeros((size_rows, hidden_width), low_type),
            jnp.zeros((size_rows, model_width), wide_type),
        )

    def blank_cross(size_rows):
        return (
            jnp.zeros((size_rows, model_width), low_type),
            jnp.zeros((size_rows, model_width), low_type),
            jnp.zeros((head_count, size_rows, 1), wide_type),
            jnp.zeros((size_rows, model_width), low_type),
            jnp.zeros((size_rows, model_width), wide_type),
        )

    progress = {
        "out": [jnp.zeros((size_rows, model_width), low_type) for size_rows in row_sizes],
        "grad_in": [jnp.zeros((size_rows, model_width), wide_type) for size_rows in row_sizes],
        "send": [jnp.zeros((2, size_rows, model_width), low_type) for size_rows in row_sizes],
        "memory": [jnp.zeros((2, size_rows, model_width), low_type) for size_rows in row_sizes],
        "grad_send": [jnp.zeros((2, size_rows, model_width), low_type) for size_rows in row_sizes],
        "grad_memory": [
            jnp.zeros((2, size_rows, model_width), low_type) for size_rows in row_sizes
        ],
        "mid": [jnp.zeros((size_rows, model_width), wide_type) for size_rows in row_sizes],
        "grad_mid": [jnp.zeros((size_rows, model_width), wide_type) for size_rows in row_sizes],
        "totals": {
            "proj": jnp.zeros(w_proj.shape, wide_type),
            "attn_out": jnp.zeros(w_attn_out.shape, wide_type),
            "first": jnp.zeros(w_first.shape, wide_type),
            "second": jnp.zeros(w_second.shape, wide_type),
            "ffn_in": jnp.zeros(w_ffn_in.shape, wide_type),
            "ffn_out": jnp.zeros(w_ffn_out.shape, wide_type),
            "gains": jnp.zeros(gains.shape, wide_type),
            "biases": jnp.zeros(biases.shape, wide_type),
        },
    }
    progress["self_saved"] = [blank_self(size_rows) for size_rows in row_sizes]
    progress["ffn_saved"] = [blank_ffn(size_rows) for size_rows in row_sizes]
    progress["cross_saved"] = [blank_cross(size_rows) for size_rows in row_sizes]

    def encoder_core(micro_idx):
        h_one, self_saved = self_forward(
            row_pieces[micro_idx], src_lens[micro_idx], False, w_proj, w_attn_out, enc_self
        )
        encoded, ffn_saved = ffn_forward(h_one, w_ffn_in, w_ffn_out, enc_ffn)
        return (encoded.astype(low_type), self_saved, ffn_saved)

    def encoder_forward_step(progress, micro_idx):
        low_memory, self_saved, ffn_saved = encoder_core(micro_idx)
        memory = jnp.stack([matmul(low_memory, w_first), matmul(low_memory, w_second)]).astype(
            low_type
        )
        progress = updated(progress, "out", micro_idx, low_memory)
        progress = updated(progress, "send", micro_idx, memory)
        progress = updated(progress, "self_saved", micro_idx, self_saved)
        progress = updated(progress, "ffn_saved", micro_idx, ffn_saved)
        return progress

    def decoder_head(micro_idx):
        return self_forward(
            row_pieces[micro_idx], tgt_lens[micro_idx], True, w_proj, w_attn_out, dec_self
        )

    def decoder_tail(mid_rows, memory, micro_idx):
        crossed, cross_saved = cross_forward(
            mid_rows, memory, src_lens[micro_idx], w_first, w_second, dec_cross
        )
        decoded, ffn_saved = ffn_forward(crossed, w_ffn_in, w_ffn_out, dec_ffn)
        return (decoded, cross_saved, ffn_saved)

    def decoder_head_step(progress, micro_idx):
        mid_rows, self_saved = decoder_head(micro_idx)
        progress = updated(progress, "mid", micro_idx, mid_rows)
        progress = updated(progress, "self_saved", micro_idx, self_saved)
        return progress

    def decoder_tail_step(progress, micro_idx):
        decoded, cross_saved, ffn_saved = decoder_tail(
            progress["mid"][micro_idx], progress["memory"][micro_idx], micro_idx
        )
        progress = updated(progress, "out", micro_idx, decoded.astype(low_type))
        progress = updated(progress, "cross_saved", micro_idx, cross_saved)
        progress = updated(progress, "ffn_saved", micro_idx, ffn_saved)
        return progress

    def decoder_back_step(progress, micro_idx):
        memory = progress["memory"][micro_idx]
        self_saved = progress["self_saved"][micro_idx]
        cross_saved = progress["cross_saved"][micro_idx]
        ffn_saved = progress["ffn_saved"][micro_idx]
        grad_h_two, ffn_w, ffn_v = ffn_backward(
            w_ffn_in, w_ffn_out, dec_ffn, ffn_saved, grad_pieces[micro_idx]
        )
        grad_h_one, grad_memory, cross_w, cross_v = cross_backward(
            memory, src_lens[micro_idx], w_first, w_second, dec_cross, cross_saved, grad_h_two
        )
        grad_rows, self_w, self_v = self_backward(
            row_pieces[micro_idx],
            tgt_lens[micro_idx],
            True,
            w_proj,
            w_attn_out,
            dec_self,
            self_saved,
            grad_h_one,
        )
        totals = accumulate(
            progress["totals"],
            ("ffn_in", "ffn_out", "first", "second", "proj", "attn_out"),
            ffn_w + cross_w + self_w,
            ffn_plan(True, ffn_v) + cross_plan(cross_v) + self_plan(True, self_v),
        )
        progress = updated(progress, "grad_in", micro_idx, grad_rows)
        progress = updated(progress, "grad_send", micro_idx, grad_memory)
        return with_totals(progress, totals)

    def encoder_top_step(progress, micro_idx):
        low_memory = progress["out"][micro_idx]
        ffn_saved = progress["ffn_saved"][micro_idx]
        grad_memory = progress["grad_memory"][micro_idx]
        grad_encoded = matmul_nt(grad_memory[0], w_first) + matmul_nt(grad_memory[1], w_second)
        grad_h_one, ffn_w, ffn_v = ffn_backward(
            w_ffn_in, w_ffn_out, enc_ffn, ffn_saved, grad_encoded
        )
        projections = (matmul_tn(low_memory, grad_memory[0]), matmul_tn(low_memory, grad_memory[1]))
        totals = accumulate(
            progress["totals"],
            ("first", "second", "ffn_in", "ffn_out"),
            projections + ffn_w,
            ffn_plan(False, ffn_v),
        )
        progress = updated(progress, "grad_mid", micro_idx, grad_h_one)
        return with_totals(progress, totals)

    def encoder_bottom_step(progress, micro_idx):
        self_saved = progress["self_saved"][micro_idx]
        grad_rows, self_w, self_v = self_backward(
            row_pieces[micro_idx],
            src_lens[micro_idx],
            False,
            w_proj,
            w_attn_out,
            enc_self,
            self_saved,
            progress["grad_mid"][micro_idx],
        )
        totals = accumulate(
            progress["totals"], ("proj", "attn_out"), self_w, self_plan(False, self_v)
        )
        progress = updated(progress, "grad_in", micro_idx, grad_rows)
        return with_totals(progress, totals)

    def enc_zero(progress):
        return encoder_forward_step(progress, 0)

    def dec_zero(progress):
        return decoder_head_step(progress, 0)

    def enc_one(progress):
        return encoder_forward_step(progress, 1)

    def dec_one(progress):
        return decoder_tail_step(decoder_head_step(progress, 1), 0)

    def dec_two(progress):
        return decoder_back_step(decoder_tail_step(progress, 1), 1)

    def enc_three(progress):
        return encoder_bottom_step(encoder_top_step(progress, 1), 1)

    def dec_three(progress):
        return decoder_back_step(progress, 0)

    def enc_four(progress):
        return encoder_top_step(progress, 0)

    def enc_five(progress):
        return encoder_bottom_step(progress, 0)

    progress = lax.cond(is_decoder, dec_zero, enc_zero, progress)
    progress = updated(progress, "memory", 0, forward_pass(progress["send"][0]))
    progress = lax.cond(is_decoder, dec_one, enc_one, progress)
    progress = updated(progress, "memory", 1, forward_pass(progress["send"][1]))
    progress = lax.cond(is_decoder, dec_two, keep_same, progress)
    progress = updated(progress, "grad_memory", 1, backward_pass(progress["grad_send"][1]))
    progress = lax.cond(is_decoder, dec_three, enc_three, progress)
    progress = updated(progress, "grad_memory", 0, backward_pass(progress["grad_send"][0]))
    progress = lax.cond(is_decoder, keep_same, enc_four, progress)
    progress = lax.cond(is_decoder, keep_same, enc_five, progress)
    totals = progress["totals"]
    owned = (
        lax.psum_scatter(totals["proj"], "dp", scatter_dimension=1, tiled=True),
        lax.psum_scatter(totals["attn_out"], "dp", scatter_dimension=0, tiled=True),
        lax.psum_scatter(totals["first"], "dp", scatter_dimension=0, tiled=True),
        lax.psum_scatter(totals["second"], "dp", scatter_dimension=0, tiled=True),
        lax.psum_scatter(totals["ffn_in"], "dp", scatter_dimension=0, tiled=True),
        lax.psum_scatter(totals["ffn_out"], "dp", scatter_dimension=0, tiled=True),
        lax.psum_scatter(totals["gains"], "dp", scatter_dimension=1, tiled=True),
        lax.psum_scatter(totals["biases"], "dp", scatter_dimension=1, tiled=True),
    )
    owned_gains, owned_biases = lax.psum((owned[6], owned[7]), "stream")
    layer_out = jnp.concatenate(progress["out"], axis=0)[None]
    grad_inputs = jnp.concatenate(progress["grad_in"], axis=0)[None]
    return (
        layer_out,
        grad_inputs,
        owned[0][None],
        owned[1][None],
        owned[2][None],
        owned[3][None],
        owned[4][None],
        owned[5][None],
        owned_gains,
        owned_biases,
    )


def fused_body(inputs, lengths, cotangent, attn_in, attn_out, cross_first, cross_second, ffn_in, ffn_out, gains, biases):
    rows, grad, s_out, s_in, s_second, s_first, s_attn, s_proj, own_gains, own_biases = whole_step(
        lengths, gains, biases, inputs[0], cotangent, attn_in[0], attn_out[0],
        cross_first[0], cross_second[0], ffn_in[0], ffn_out[0])
    return (rows[None], grad[None], s_proj[None], s_attn[None], s_first[None], s_second[None],
            s_in[None], s_out[None], own_gains, own_biases)


def solution(mesh):
    def body(*args):
        width = args[0].shape[2]
        fits = mesh.shape["dp"] * PIECE == width and args[0].shape[1] == ROWS and args[7].shape[2] == 4 * width
        return (fused_body if fits else plain_body)(*args)
    return jax.shard_map(
        body,
        mesh=mesh,
        in_specs=(
            P("stream", "dp", None),
            P(None, "dp", None),
            P("dp", None),
            P("stream", None, None, None),
            P("stream", None, None),
            P("stream", None, None),
            P("stream", None, None),
            P("stream", None, None),
            P("stream", None, None),
            P(),
            P(),
        ),
        out_specs=(
            P("stream", "dp", None),
            P("stream", "dp", None),
            P("stream", None, "dp", None),
            P("stream", "dp", None),
            P("stream", "dp", None),
            P("stream", "dp", None),
            P("stream", "dp", None),
            P("stream", "dp", None),
            P(None, "dp"),
            P(None, "dp"),
        ),
        check_vma=False,
    )
```

```python
import functools

import jax
import jax.numpy as jnp
from jax import lax
from jax.experimental import pallas as pl
from jax.experimental.pallas import tpu as pltpu
from jax.sharding import PartitionSpec as P

HDIM = 64
SHORT = 128
LONG = 256
ROWS = SHORT + LONG
PIECE = 48
PIECES = 14
VEC_ROWS = 24
SEND_SLOTS = 8
MESH = pl.DeviceIdType.MESH
bf16, f32 = jnp.bfloat16, jnp.float32
VMEM_LIMIT = 64 << 20


def dot_nn(a, b):
    return jnp.dot(a, b, preferred_element_type=f32)


def dot_nt(a, b):
    return lax.dot_general(a, b, (((1,), (1,)), ((), ())), preferred_element_type=f32)


def dot_tn(a, b):
    return lax.dot_general(a, b, (((0,), (0,)), ((), ())), preferred_element_type=f32)


def cols(j, width):
    return pl.ds(pl.multiple_of(j * width, width), width)


def step_kernel(
    width, hidden,
    lengths, gains, biases, x_hbm, cot_hbm, wproj_hbm, wo_hbm, wfirst_hbm, wsecond_hbm, win_hbm, wout_hbm,
    out_rows, out_grad, out_own, out_part, out_vec,
    vec, bias_in, wproj, wo, wfirst, wsecond, win, wout, wx,
    xb, up, mem, obuf, hlow, dg, kv, acc, grad, hw, u_self, u_cross, u_ffn, gr, grp, lt, ltp, one_send, one_recv, two_recv, gmem, vg, vbuf, vboth,
    load_sem, wx_send, wx_recv, mem_send, mem_recv, gm_send, gm_recv, gv_send, gv_recv, lt_send, lt_recv, gr_send, gr_recv,
    sem_send, sem_recv, own_sem, io_sem, v_send, v_recv,
):
    st = lax.axis_index("stream")
    me = lax.axis_index("dp")
    z, y, c = me // 4, (me // 2) % 2, me % 2
    is_dec = st == 1
    is_enc = st == 0
    core_id = {"dp": z * 4 + y * 2 + (1 - c)}
    y_id = {"dp": z * 4 + (1 - y) * 2 + c}
    x_id = {"stream": 1 - st}
    tiles = width // 256
    slots = hidden // width

    zh, zl = z // 2, z % 2

    def z_id(other):
        return {"dp": other * 4 + y * 2 + c}
    near_id = z_id(zh * 2 + 1 - zl)
    far_id = z_id((1 - zh) * 2 + zl)
    over_id = {"stream": 1 - st, **far_id}

    def remote(src, dst, ss, rs, dev):
        return pltpu.make_async_remote_copy(
            src_ref=src, dst_ref=dst, send_sem=ss, recv_sem=rs, device_id=dev, device_id_type=MESH)

    loads = [
        pltpu.make_async_copy(src, dst, load_sem.at[i])
        for i, (src, dst) in enumerate((
            (x_hbm, xb), (wproj_hbm, wproj), (wo_hbm, wo), (win_hbm, win), (wout_hbm, wout),
            (wfirst_hbm, wfirst), (wsecond_hbm, wsecond)))
    ]
    cot_load = pltpu.make_async_copy(cot_hbm, up, load_sem.at[7])
    loads[0].start()
    loads[1].start()

    barrier = pltpu.get_barrier_semaphore()
    peers = [core_id, y_id, x_id, near_id, far_id, over_id]
    for p in peers:
        pl.semaphore_signal(barrier, inc=1, device_id=p, device_id_type=MESH)

    lens = [lengths[i // 2, 0, i % 2] for i in range(4)]
    own_lens = [jnp.where(is_dec, lens[2 + i], lens[i]) for i in range(2)]
    vec[pl.ds(0, 5), :] = gains[...].astype(f32)
    vec[pl.ds(5, 24), :] = biases[...].astype(f32)
    for i in range(slots):
        for s in range(2):
            bias_in[pl.ds(s, 1), pl.ds(i * width, width)] = vec[pl.ds(9 + 14 * s + i, 1), :]
    vg[...] = jnp.zeros_like(vg)
    half = width // 2
    chunks = width // 4 // PIECE

    def wx_block(yy, zz, cc, h):
        return wx.at[yy, pl.ds((zz * 2 + cc) * chunks * PIECE + h * PIECE, PIECE)]

    def wx_copy(src, dst, k, dev):
        return remote(src, dst, wx_send.at[k], wx_recv.at[k], dev)

    def wx_from(source, h):
        return wx_copy(source.at[pl.ds((zl * 2 + c) * chunks * PIECE + h * PIECE, PIECE)], wx_block(y, zl, c, h), h, x_id)
    wx_in = [wx_from(wfirst_hbm, h) for h in range(chunks)]
    wx_y = [wx_copy(wx_block(y, zl, c, h), wx_block(y, zl, c, h), chunks + h, y_id) for h in range(chunks)]
    wx_z = [wx_copy(wx_block(y, zl, c, h), wx_block(y, zl, c, h), 2 * chunks + h, near_id) for h in range(chunks)]
    wx_on = [wx_copy(wx_block(1 - y, zl, c, h), wx_block(1 - y, zl, c, h), 3 * chunks + h, near_id) if h < chunks // 2 else
             wx_copy(wx_block(y, 1 - zl, c, h), wx_block(y, 1 - zl, c, h), 3 * chunks + h, y_id) for h in range(chunks)]

    def wx_whole(yy, zz):
        return wx.at[yy, pl.ds((zz * 2 + c) * chunks * PIECE, chunks * PIECE)]
    wx_core = [wx_copy(wx_whole(yy, zz), wx_whole(yy, zz), 4 * chunks + k, core_id)
               for k, (yy, zz) in enumerate(((y, zl), (1 - y, zl), (y, 1 - zl), (1 - y, 1 - zl)))]

    def wx_start():
        pl.semaphore_wait(barrier, len(peers))

        @pl.when(is_enc & (y == 0))
        def _():
            for h in range(chunks):
                wx_in[h].start()

        @pl.when(is_enc & (y == 1))
        def _():
            for h in range(chunks):
                wx_from(wsecond_hbm, h).start()
    loads[0].wait()
    loads[1].wait()
    for cp in loads[2:]:
        cp.start()

    @pl.when(is_dec)
    def _():
        cot_load.start()

    gain_row = lambda r: pl.ds(r - 2 * st, 1)
    bias_row_of = lambda r: pl.ds(r - 2 - 10 * st, 1)
    lt_copy = [remote(lt.at[i, :, :, :, 1 - c], ltp.at[i], lt_send.at[i], lt_recv.at[i], core_id) for i in range(9)]
    gr_copy = {i: remote(gr.at[i], grp.at[i], gr_send.at[i], gr_recv.at[i], core_id) for i in range(5, 11)}
    buckets = ((0, SHORT), (SHORT, LONG))
    short, long, both = (0,), (1,), (0, 1)

    def span(bs):
        return buckets[bs[0]][0], sum(buckets[b][1] for b in bs)

    def at_rows(bs):
        return pl.ds(*span(bs))
    mem_copy = [remote(xb.at[at_rows((b,))], mem.at[at_rows((b,))], mem_send.at[b], mem_recv.at[b], x_id) for b in range(2)]
    gm_copy = [remote(gmem.at[at_rows((b,))], up.at[at_rows((b,))], gm_send.at[b], gm_recv.at[b], x_id) for b in range(2)]
    gv_copy = remote(kv.at[1], gr.at[5], gv_send, gv_recv, x_id)

    gr_first = [remote(gr.at[0, at_rows((b,))], grp.at[0, at_rows((b,))], gr_send.at[11 * b], gr_recv.at[11 * b], core_id)
                for b in range(2)]

    def row_loop(bs, block, body, unroll=1):
        r0, n = span(bs)

        def step(i, carry):
            body(pl.ds(pl.multiple_of(r0 + i * block, block), block))
            return carry
        lax.fori_loop(0, n // block, step, 0, unroll=unroll)

    def vrow(r):
        return vec[pl.ds(r, 1), :]

    def transposed(i, bs, ref):
        r0, n = span(bs)
        lt[i, :, :, :, :, :, pl.ds(r0, n)] = ref[pl.ds(r0, n), :].T.reshape(2, 2, 2, 2, PIECE, n)

    def transposed_slot(bs, j):
        r0, n = span(bs)
        turned = gr[1 + j, pl.ds(r0, n), :].T.reshape(2, 2, 4, PIECE, n)
        for k in range(4):
            lt[k, j // 2, j % 2, :, :, :, pl.ds(r0, n)] = turned[:, :, k]

    def transposed_active(bs):

        def step(j, carry):
            transposed_slot(bs, j)
            return carry
        lax.fori_loop(0, slots, step, 0)

    def col_sum(slot, row):
        def step(i, carry):
            block = slot[pl.ds(pl.multiple_of(i * 64, 64), 64), :].astype(f32)
            return carry + jnp.sum(block.reshape(8, 8, width), axis=0)
        total = lax.fori_loop(0, ROWS // 64, step, jnp.zeros((8, width), f32))
        vg[bias_row_of(row), :] = jnp.sum(total, axis=0, keepdims=True)

    def norm_forward(bs, residual, sum_ref, add_bias, gain, shift, out_low, out_wide):
        def body(rows):
            u = residual[rows, :].astype(f32) + acc[rows, :] + vrow(add_bias)
            sum_ref[rows, :] = u
            centre = u - jnp.mean(u, axis=-1, keepdims=True)
            spread = jnp.mean(centre * centre, axis=-1, keepdims=True)
            h = centre * lax.rsqrt(spread + 1e-05) * vrow(gain) + vrow(shift)
            if out_wide is not None:
                out_wide[rows, :] = h
            out_low[rows, :] = h.astype(bf16)
        row_loop(bs, 32, body, 4)

    def norm_backward(bs, sum_ref, source, gain, shift, out_wide, slot):
        r0, n = span(bs)

        def step(i, carry):
            rows = pl.ds(pl.multiple_of(r0 + i * 32, 32), 32)
            r = source[rows, :].astype(f32)
            u = sum_ref[rows, :]
            centre = u - jnp.mean(u, axis=-1, keepdims=True)
            spread = jnp.mean(centre * centre, axis=-1, keepdims=True)
            inv = lax.rsqrt(spread + 1e-05)
            uhat = centre * inv
            t = r * vrow(gain)
            gu = (t - jnp.mean(t, axis=-1, keepdims=True) - uhat * jnp.mean(t * uhat, axis=-1, keepdims=True)) * inv
            out_wide[rows, :] = gu
            slot[rows, :] = gu.astype(bf16)
            return (carry[0] + jnp.sum((r * uhat).reshape(4, 8, width), axis=0),
                    carry[1] + jnp.sum(r.reshape(4, 8, width), axis=0))
        zero = jnp.zeros((8, width), f32)
        total = lax.fori_loop(0, n // 32, step, (zero, zero), unroll=4)
        for row, part in ((gain_row(gain), total[0]), (bias_row_of(shift), total[1])):
            vg[row, :] = vg[row, :] + jnp.sum(part, axis=0, keepdims=True)

    def masked_scores(q_half, k2, n, length, diagonal):
        s = dot_nt(q_half, k2)
        column = lax.broadcasted_iota(jnp.int32, (n, n), 1)
        row = lax.broadcasted_iota(jnp.int32, (n, n), 0)
        return jnp.where((column < length) & (column <= row + diagonal), s, -1e30)

    def softmax(s):
        e = jnp.exp(s - jnp.max(s, axis=-1, keepdims=True))
        return e * (1.0 / jnp.sum(e, axis=-1, keepdims=True))

    def halves(n):
        lane = lax.broadcasted_iota(jnp.int32, (n, 2 * HDIM), 1)
        return lane < HDIM

    def head_loop(bs, body, lo=0, hi=None):
        pairs = {short: 3, long: 2, both: 1}[bs]

        def step(p, carry):
            body([(b, pl.ds(pl.multiple_of((p * pairs + i) * 2 * HDIM, 2 * HDIM), 2 * HDIM)) for b in bs for i in range(pairs)])
            return carry
        lax.fori_loop(lo, width // (2 * HDIM * pairs) if hi is None else hi, step, 0)

    def attend_forward(bs, q_ref, k_ref, v_ref, lengths_at, diagonal, bias_row, out_ref, lo=0, hi=None):
        def body(units):
            work = []
            for b, at in units:
                r0, n = buckets[b]
                rows = pl.ds(r0, n)
                q2, k2 = q_ref[rows, at], k_ref[rows, at]
                first = halves(n)
                for lanes in (first, ~first):
                    work.append(masked_scores(jnp.where(lanes, q2 * 0.125, jnp.zeros_like(q2)), k2, n, lengths_at[b], diagonal))
            work = [softmax(s).astype(bf16) for s in work]
            work = [dot_nn(prob, v_ref[pl.ds(*buckets[units[i // 2][0]]), units[i // 2][1]]) for i, prob in enumerate(work)]
            for i, (b, at) in enumerate(units):
                r0, n = buckets[b]
                att = jnp.where(halves(n), work[2 * i], work[2 * i + 1])
                if bias_row is not None:
                    att = att + vec[pl.ds(bias_row, 1), at]
                out_ref[pl.ds(r0, n), at] = att.astype(bf16)
        head_loop(bs, body, lo, hi)

    def attend_backward(bs, q_ref, k_ref, v_ref, lengths_at, diagonal, lo=0, hi=None):
        scale = HDIM ** -0.5

        def body(units):
            scores, ups = [], []
            for b, at in units:
                r0, n = buckets[b]
                rows = pl.ds(r0, n)
                q2, k2, v2, go2 = q_ref[rows, at], k_ref[rows, at], v_ref[rows, at], obuf[rows, at]
                first = halves(n)
                zero = jnp.zeros_like(q2)
                for lanes in (first, ~first):
                    scores.append(masked_scores(jnp.where(lanes, q2 * 0.125, zero), k2, n, lengths_at[b], diagonal))
                    ups.append(dot_nt(jnp.where(lanes, go2, zero), v2))
            probs = [softmax(s) for s in scores]
            gs = [(p * (gp - jnp.sum(p * gp, axis=-1, keepdims=True))).astype(bf16) for p, gp in zip(probs, ups)]
            for i, (b, at) in enumerate(units):
                r0, n = buckets[b]
                rows = pl.ds(r0, n)
                q2, k2, go2 = q_ref[rows, at], k_ref[rows, at], obuf[rows, at]
                first = halves(n)
                two = (2 * i, 2 * i + 1)
                gv = [dot_tn(probs[u].astype(bf16), go2) for u in two]
                gq = [dot_nn(gs[u], k2) for u in two]
                gk = [dot_tn(gs[u], q2) for u in two]
                q_ref[rows, at] = (jnp.where(first, gq[0], gq[1]) * scale).astype(bf16)
                k_ref[rows, at] = (jnp.where(first, gk[0], gk[1]) * scale).astype(bf16)
                v_ref[rows, at] = jnp.where(first, gv[0], gv[1]).astype(bf16)
        head_loop(bs, body, lo, hi)

    q_ref, k_ref, v_ref = gr.at[8], gr.at[9], gr.at[10]
    diagonal = (1 - st) * 4096
    bias_at = 5 + 10 * st
    ffn_at = 13 + 14 * st
    ffn_gain = 1 + 3 * st

    def by_tiles(fn):
        for t in range(tiles):
            fn(pl.ds(t * 256, 256))

    def self_project(bs):
        rows = at_rows(bs)

        def project(which, carry):
            for t in range(tiles):
                at = pl.ds(t * 256, 256)
                value = dot_nn(xb[rows, :], wproj[which, :, at])
                bias = vec[pl.ds(bias_at + which // 2, 1), at] * jnp.where(which == 1, 0.0, 1.0)
                gr[8 + which, rows, at] = (value + bias).astype(bf16)
            return carry
        lax.fori_loop(0, 3, project, 0)

    def self_output(bs):
        rows = at_rows(bs)

        def tile(at):
            acc[rows, at] = dot_nn(obuf[rows, :], wo[:, at])
        by_tiles(tile)
        norm_forward(bs, xb, u_self, bias_at + 2, 2 * st, bias_at + 3, hlow, grad)

    def ffn_forward(bs, residual, wait_in, wait_out, turn=False):
        r0, n = span(bs)
        rows = pl.ds(r0, n)

        def ffn_slot(j, carry):
            for t in range(tiles):
                at = pl.ds(t * 256, 256)
                wide = pl.ds(pl.multiple_of(j * width + t * 256, 256), 256)
                zv = dot_nn(hlow[rows, :], win[:, wide]) + bias_in[pl.ds(st, 1), wide]
                cdf = 0.5 * (1.0 + lax.erf(zv * (0.5 ** 0.5)))
                pdf = jnp.exp(-0.5 * zv * zv) * 0.3989422804014327
                gr[1 + j, rows, at] = (zv * cdf).astype(bf16)
                dg[j, rows, at] = (cdf + zv * pdf).astype(bf16)
            return carry
        if wait_in:
            loads[3].wait()
        lax.fori_loop(0, slots, ffn_slot, 0)

        def ffn_out(at):
            total = dot_nn(gr[1, rows, :], wout[pl.ds(0, width), at])
            for j in range(1, slots):
                total = total + dot_nn(gr[1 + j, rows, :], wout[pl.ds(j * width, width), at])
            acc[rows, at] = total
        if wait_out:
            loads[4].wait()
        by_tiles(ffn_out)
        if turn:
            for j in range(slots):
                transposed_slot(bs, j)
        norm_forward(bs, residual, u_ffn, ffn_at, ffn_gain, ffn_at + 1, xb, None)

    def ffn_inner(bs, lo, hi, last):
        r0, n = span(bs)
        rows = pl.ds(r0, n)

        def ffn_inner_slot(j, carry):
            for t in range(tiles):
                at = pl.ds(t * 256, 256)
                wide = pl.ds(pl.multiple_of(j * width + t * 256, 256), 256)
                value = dot_nt(gr[0, rows, :], wout[wide, :])
                gr[1 + j, rows, at] = (value * dg[j, rows, at].astype(f32)).astype(bf16)
            if last:
                remote(gr.at[1 + j], grp.at[1 + j], gr_send.at[1 + j], gr_recv.at[1 + j], core_id).start()
            return carry
        lax.fori_loop(lo, hi, ffn_inner_slot, 0)

    def ffn_input(bs):
        rows = at_rows(bs)

        def tile(at):
            total = grad[rows, at]
            for j in range(slots):
                total = total + dot_nt(gr[1 + j, rows, :], win[at, pl.ds(j * width, width)])
            grad[rows, at] = total
        by_tiles(tile)

    def cross_forward(bs):
        rows = at_rows(bs)

        def memory_kv(which, carry):
            for t in range(tiles):
                at = pl.ds(t * 256, 256)
                value = dot_nn(mem[rows, :], wx[which, :, at])
                kv[which, rows, at] = value.astype(bf16)
            return carry
        lax.fori_loop(0, 2, memory_kv, 0)
        attend_forward(bs, gr.at[6], kv.at[0], kv.at[1], lens[:2], 4096, 20, obuf)

        def cross_out(at):
            acc[rows, at] = dot_nn(obuf[rows, :], wsecond[:, at])
        by_tiles(cross_out)
        norm_forward(bs, grad, u_cross, 21, 3, 22, hlow, hw)
        transposed(7, bs, obuf)

    def cross_backward(bs):
        rows = at_rows(bs)
        norm_backward(bs, u_cross, grad, 3, 22, hw, gr.at[5])

        def cross_up(at):
            obuf[rows, at] = dot_nt(gr[5, rows, :], wsecond[at, :]).astype(bf16)
        by_tiles(cross_up)
        attend_backward(bs, gr.at[6], kv.at[0], kv.at[1], lens[:2], 4096)

        def memory_half(h, carry):
            at = cols(h, half)
            gmem[rows, at] = (dot_nt(kv[0, rows, :], wx[0, at, :]) + dot_nt(kv[1, rows, :], wx[1, at, :])).astype(bf16)
            return carry
        lax.fori_loop(0, 2, memory_half, 0)
        gm_copy[bs[0]].start()

    def cross_input(at):
        grad[:, at] = hw[:, at] + dot_nt(gr[6], wfirst[at, :])

    def lanes_of(h):
        return pl.ds(0, width) if h is None else cols(h, half)

    def unit(i, h):
        return i if h is None else 15 + 2 * (i - 12) + h

    def sems(i, stage, h):
        return sem_send.at[unit(i, h), stage], sem_recv.at[unit(i, h), stage]

    def first_copy(i, z_first, h):
        at = lanes_of(h)
        return remote(one_send.at[i % SEND_SLOTS, :, :, :, at], one_recv.at[i, :, :, :, at], *sems(i, 0, h),
                      near_id if z_first else y_id)

    def second_copy(i, z_first, h):
        at = lanes_of(h)
        source = one_recv.at[i, 1 - zh, :, :, at] if z_first else one_recv.at[i, :, 1 - zl, :, at]
        return remote(source, two_recv.at[i, :, :, at], *sems(i, 1, h), far_id if z_first else near_id)

    def third_copy(i, z_first, h):
        at = lanes_of(h)
        source = two_recv.at[i, 1 - y if z_first else 1 - zh, :, at]
        return remote(source, out_part.at[i, :, at], *sems(i, 2, h), y_id if z_first else far_id)

    def own_copy(i, z_first, h):
        at = lanes_of(h)
        return pltpu.make_async_copy(two_recv.at[i, y if z_first else zh, :, at], out_own.at[i, :, at], own_sem.at[unit(i, h)])

    def product(left, slot, z_first, other, at):
        if z_first:
            zz = 1 - zl if other else zl
            mine, theirs = lt[left, :, zz, :, c], ltp[left, :, zz]
        else:
            yy = 1 - y if other else y
            mine, theirs = lt[left, :, :, yy, c], ltp[left, :, :, yy]
        shape = (4 * PIECE, ROWS)
        return dot_nn(mine.reshape(shape), gr[slot, :, at]) + dot_nn(theirs.reshape(shape), grp[slot, :, at])

    def piece_tiles(h, fn):
        if h is None:
            loop(0, tiles, lambda t: fn(cols(t, 256), 256))
        else:
            fn(cols(h, half), half)

    def send_piece(i, left, slot, z_first=False, h=None):
        def tile(at, n):
            one_send[i % SEND_SLOTS, :, :, :, at] = product(left, slot, z_first, True, at).astype(bf16).reshape(2, 2, PIECE, n)
        piece_tiles(h, tile)
        first_copy(i, z_first, h).start()

    def keep_piece(i, left, slot, z_first=False, h=None):
        first_copy(i, z_first, h).wait()

        def tile(at, n):
            total = one_recv[i, :, :, :, at].reshape(4 * PIECE, n).astype(f32) + product(left, slot, z_first, False, at)
            one_recv[i, :, :, :, at] = total.astype(bf16).reshape(2, 2, PIECE, n)
        piece_tiles(h, tile)
        second_copy(i, z_first, h).start()

    def merge_piece(i, z_first=False, h=None):
        second_copy(i, z_first, h).wait()
        at = lanes_of(h)
        for k in range(2):
            mine = one_recv[i, zh, k, :, at] if z_first else one_recv[i, k, zl, :, at]
            two_recv[i, k, :, at] = (two_recv[i, k, :, at].astype(f32) + mine.astype(f32)).astype(bf16)

    def pass_piece(i, z_first=False, h=None):
        merge_piece(i, z_first, h)
        third_copy(i, z_first, h).start()
        own_copy(i, z_first, h).start()

    extra = PIECES
    extra_part = remote(two_recv.at[extra, 1 - zh], out_part.at[13], sem_send.at[extra, 2], sem_recv.at[13, 2], over_id)
    extra_own = remote(two_recv.at[extra, zh], out_own.at[13], sem_send.at[13, 0], sem_recv.at[13, 0], x_id)
    extra_left = remote(lt.at[0, :, :, :, 1 - c], ltp.at[0], lt_send.at[0], lt_recv.at[0], core_id)
    extra_right = remote(gr.at[0], grp.at[0], gr_send.at[0], gr_recv.at[0], core_id)

    def loop(lo, hi, fn):
        def step(i, carry):
            fn(i)
            return carry
        lax.fori_loop(lo, hi, step, 0)

    def wait_active():
        for i in range(4):
            lt_copy[i].wait()
        gr_first[0].wait()
        gr_first[1].wait()

    @pl.when(is_enc)
    def _():
        again = pltpu.make_async_copy(x_hbm, mem, load_sem.at[8])
        again.start()
        for bs in (long, short):
            self_project(bs)
            if bs == long:
                wx_start()
            attend_forward(bs, q_ref, k_ref, v_ref, own_lens, diagonal, None, obuf)
            if bs == long:
                loads[2].wait()
            self_output(bs)
            ffn_forward(bs, grad, bs == long, bs == long)
            mem_copy[bs[0]].start()
        transposed_active(both)
        for k in range(4):
            lt_copy[k].start()
        again.wait()
        for i, ref in ((4, mem), (5, obuf), (6, hlow), (7, xb)):
            transposed(i, both, ref)
            lt_copy[i].start()
        loads[5].wait()
        loads[6].wait()
        for bs in (short, long):
            gm_copy[bs[0]].wait_recv()
            norm_backward(bs, u_ffn, up, ffn_gain, ffn_at + 1, grad, gr.at[0])
            gr_first[bs[0]].start()
            if bs == short:
                ffn_inner(bs, 0, slots, False)
                ffn_input(bs)
        ffn_inner(long, 0, 1, True)

    @pl.when(is_dec)
    def _():
        self_project(both)
        wx_start()
        transposed(4, both, xb)
        lt_copy[4].start()

        def wx_forward(h):
            wx_in[h].wait_recv()
            wx_y[h].start()
            wx_z[h].start()
        attend_forward(both, q_ref, k_ref, v_ref, own_lens, diagonal, None, obuf, 0, 3)
        wx_forward(0)
        attend_forward(both, q_ref, k_ref, v_ref, own_lens, diagonal, None, obuf, 3, 6)
        wx_forward(1)
        loads[2].wait()
        self_output(both)
        wx_forward(2)
        wx_y[0].wait()
        wx_on[0].start()
        loads[5].wait()

        def cross_query(at):
            gr[6, :, at] = (dot_nn(hlow[...], wfirst[:, at]) + vec[pl.ds(19, 1), at]).astype(bf16)
        by_tiles(cross_query)
        wx_forward(3)
        wx_core[0].start()
        transposed(5, both, obuf)
        lt_copy[5].start()
        transposed(8, both, hlow)
        lt_copy[8].start()
        loads[6].wait()
        cot_load.wait()
        wx_y[1].wait()
        wx_on[1].start()
        wx_z[0].wait()
        wx_z[1].wait()
        wx_z[2].wait()
        wx_on[2].start()
        wx_y[2].wait()
        wx_z[3].wait()
        wx_on[3].start()
        wx_y[3].wait()
        wx_core[1].start()
        wx_core[2].start()
        for h in range(chunks):
            wx_on[h].wait()
        wx_core[3].start()
        for k in range(4):
            wx_core[k].wait()
        for bs in (long, short):
            mem_copy[bs[0]].wait_recv()
            cross_forward(bs)
        lt_copy[7].start()
        ffn_forward(both, hw, True, True, True)
        for k in range(4):
            lt_copy[k].start()
        norm_backward(both, u_ffn, up, ffn_gain, ffn_at + 1, grad, gr.at[0])
        gr_first[0].start()
        gr_first[1].start()
        ffn_inner(both, 0, slots, True)
        ffn_input(both)
        for bs in (short, long):
            cross_backward(bs)
        transposed(6, both, hlow)
        lt_copy[6].start()

    wait_active()

    def first_sends(k):
        send_piece(2 + k, 2 + k, 0)
        send_piece(k, k, 0, True)
    loop(0, 2, first_sends)

    @pl.when(is_enc)
    def _():
        ffn_inner(long, 1, slots, True)
    lt_copy[6].wait()

    def inner_sends(j):
        remote(gr.at[1 + j], grp.at[1 + j], gr_send.at[1 + j], gr_recv.at[1 + j], core_id).wait()
        send_piece(4 + j, 6, 1 + j)
    loop(0, slots, inner_sends)

    @pl.when(is_enc)
    def _():
        ffn_input(long)

    @pl.when(is_dec)
    def _():
        gr_copy[5].start()
        gr_copy[6].start()
        by_tiles(cross_input)
        col_sum(obuf, 20)
        col_sum(gr.at[6], 19)
        col_sum(gr.at[5], 21)

    rows_copy = pltpu.make_async_copy(xb, out_rows, io_sem.at[0])
    rows_copy.start()

    norm_backward(both, u_self, grad, 2 * st, bias_at + 3, hw, gr.at[7])
    gr_copy[7].start()

    def self_up(at):
        obuf[:, at] = dot_nt(gr[7], wo[at, :]).astype(bf16)
    by_tiles(self_up)

    def keep_and_attend(k, carry):
        keep_piece(2 + k, 2 + k, 0)
        keep_piece(k, k, 0, True)
        attend_backward(both, q_ref, k_ref, v_ref, own_lens, diagonal, k * 3, k * 3 + 3)
        return carry
    lax.fori_loop(0, 2, keep_and_attend, 0)
    for j in range(3):
        gr_copy[8 + j].start()

    @pl.when(is_dec)
    def _():
        gv_copy.start()

    def self_input(at):
        total = hw[:, at]
        for j in range(3):
            total = total + dot_nt(gr[8 + j], wproj[j, at, :])
        hw[:, at] = total
    by_tiles(self_input)
    grad_copy = pltpu.make_async_copy(hw, out_grad, io_sem.at[1])
    grad_copy.start()
    loop(2, 4, pass_piece)
    for i in (4, 5, 7):
        lt_copy[i].wait()

    @pl.when(is_dec)
    def _():
        lt_copy[8].wait()
    for i in range(7, 11):
        gr_copy[i].wait()
    col_sum(gr.at[0], ffn_at)
    loop(0, slots, lambda j: col_sum(gr.at[1 + j], ffn_at - 4 + j))
    col_sum(gr.at[7], bias_at + 2)
    col_sum(gr.at[8], bias_at)
    col_sum(gr.at[10], bias_at + 1)
    own_half = pl.ds(pl.multiple_of(c * half, half), half)
    other_half = pl.ds(pl.multiple_of((1 - c) * half, half), half)
    v_copy = [remote(vg.at[:, other_half] if k == 0 else vbuf.at[2 * k], vbuf.at[2 * k + 1], v_send.at[k], v_recv.at[k], dev)
              for k, dev in enumerate((core_id, y_id, near_id, far_id, x_id))]
    v_last = remote(vboth.at[:, :, own_half], vboth.at[:, :, own_half], v_send.at[5], v_recv.at[5], core_id)
    vbuf[0] = vg[:, own_half]

    @pl.when(is_dec)
    def _():
        transposed(0, both, mem)
        extra_left.start()
        gr[0] = kv[0]
        extra_right.start()

    def v_next(k):
        v_copy[k].wait()
        vbuf[2 * k + 2] = vbuf[2 * k] + vbuf[2 * k + 1]
        v_copy[k + 1].start()
    v_copy[0].start()
    v_next(0)

    def attention_piece(k):
        return 8 + k, 5 - (k + 3) // 4, 7 + k

    def cross_piece(k):
        return 12 + k // 2, 7 + st * (k // 2), 5 + k // 2, False, k % 2

    def middle(k):
        send_piece(*attention_piece(k))
        keep_piece(4 + k, 6, 1 + k)

        @pl.when(k > 0)
        def _():
            pass_piece(3 + k)
    loop(0, 4, middle)

    @pl.when(is_enc)
    def _():
        gv_copy.wait_recv()
        gr_copy[5].start()

    @pl.when(is_dec)
    def _():
        extra_left.wait()
        extra_right.wait()
        send_piece(extra, 0, 0)
        gr_copy[6].wait()
    v_next(1)
    cross_units = 2 + 2 * st

    def later(k):
        keep_piece(*attention_piece(k))

        @pl.when(k == 0)
        def _():
            gr_copy[5].wait()
            loop(0, cross_units, lambda k: send_piece(*cross_piece(k)))
        pass_piece(7 + k)
    loop(0, 4, later)

    @pl.when(is_dec)
    def _():
        keep_piece(extra, 0, 0)
    v_next(2)
    loop(0, 2, lambda i: pass_piece(i, True))

    def ends(k):
        i, left, slot, z_first, h = cross_piece(k)
        keep_piece(i, left, slot, z_first, h)

        @pl.when(k == 0)
        def _():
            pass_piece(11)

        @pl.when(k > 0)
        def _():
            pass_piece(12 + (k - 1) // 2, False, (k + 1) % 2)

        @pl.when(k == 1)
        def _():
            v_next(3)

        @pl.when(is_dec & (k == 1))
        def _():
            merge_piece(extra)
            extra_part.start()
            extra_own.start()
    loop(0, cross_units, ends)
    pass_piece(12 + st, False, 1)
    v_copy[4].wait()
    vboth[st, :, own_half] = vbuf[8]
    vboth[1 - st, :, own_half] = vbuf[9]
    v_last.start()
    v_last.wait()
    vec_copy = pltpu.make_async_copy(vboth, out_vec, io_sem.at[2])
    vec_copy.start()

    def finish(i, z_first=False, h=None):
        third_copy(i, z_first, h).wait()
        own_copy(i, z_first, h).wait()
    loop(0, 2, lambda i: finish(i, True))
    loop(2, 12, finish)
    loop(0, cross_units, lambda k: finish(12 + k // 2, False, k % 2))
    rows_copy.wait()
    grad_copy.wait()
    vec_copy.wait()

    @pl.when(is_enc)
    def _():
        for h in range(chunks):
            wx_in[h].wait_send()
        for h in range(2):
            mem_copy[h].wait_send()
        extra_part.wait_recv()
        extra_own.wait_recv()

    @pl.when(is_dec)
    def _():
        for h in range(2):
            gm_copy[h].wait_send()
        gv_copy.wait_send()
        extra_part.wait_send()
        extra_own.wait_send()


def last_kernel(width, rows_in, grad_in, own, parts, vec_sum, rows_out, grad_out, *refs):
    outs, (vec_buf, rows_buf, grad_buf, own_buf, part_buf, sums, in_sem, through_sem, out_sem) = refs[:8], refs[8:]
    group = PIECES // 2
    loads = []
    for g in range(2):
        at = pl.ds(g * group, group)
        loads.append((pltpu.make_async_copy(own.at[at], own_buf.at[at], in_sem.at[g, 0]),
                      pltpu.make_async_copy(parts.at[at], part_buf.at[at], in_sem.at[g, 1])))
    vec_load = pltpu.make_async_copy(vec_sum, vec_buf, through_sem.at[2])
    into = [pltpu.make_async_copy(grad_in, grad_buf, through_sem.at[0]), pltpu.make_async_copy(rows_in, rows_buf, through_sem.at[1])]
    for cp in (*loads[0], into[0], *loads[1], into[1], vec_load):
        cp.start()
    stores = []

    def store(src, dst):
        stores.append(pltpu.make_async_copy(src, dst, out_sem.at[len(stores)]))
        stores[-1].start()
    for g in range(2):
        for cp in loads[g]:
            cp.wait()
        for i in range(g * group, (g + 1) * group):
            sums[i] = own_buf[i].astype(f32) + part_buf[i].astype(f32)
            if i < 4:
                store(sums.at[i], outs[0].at[pl.ds(i * PIECE, PIECE), :])
            elif i < 8:
                store(sums.at[i], outs[1].at[:, pl.ds((i - 4) * width, width)])
            elif i == 8:
                store(sums.at[i], outs[4])
            elif i == 11:
                store(sums.at[pl.ds(9, 3)], outs[5])
            elif i > 11:
                store(sums.at[i], outs[i - 10])
        into[g].wait()
        store(rows_buf if g else grad_buf, rows_out if g else grad_out)
    vec_load.wait()
    shift = lax.rem(width - lax.axis_index("dp") * PIECE, width)
    for s, (g0, g1, b0, b1) in enumerate(((0, 2, 0, 10), (2, 5, 10, 24))):
        turned = pltpu.roll(vec_buf[s], shift, 1)
        outs[6][pl.ds(g0, g1 - g0), :] = turned[:g1 - g0, :PIECE]
        outs[7][pl.ds(b0, b1 - b0), :] = turned[3:3 + b1 - b0, :PIECE]
    for cp in stores:
        cp.wait()


def whole_step(lengths, gains, biases, x, cot, wproj, wo, wfirst, wsecond, win, wout):
    width = x.shape[1]
    hidden = win.shape[1]
    half = width // 2
    any_space = pl.BlockSpec(memory_space=pl.ANY)
    vmem = pl.BlockSpec(memory_space=pltpu.VMEM)
    dma = pltpu.SemaphoreType.DMA
    slots = hidden // width
    small = (32, width)
    results = pl.pallas_call(
        functools.partial(step_kernel, width, hidden),
        out_shape=[
            jax.ShapeDtypeStruct((ROWS, width), bf16),
            jax.ShapeDtypeStruct((ROWS, width), f32),
            jax.ShapeDtypeStruct((PIECES, PIECE, width), bf16),
            jax.ShapeDtypeStruct((PIECES, PIECE, width), bf16),
            jax.ShapeDtypeStruct((2, VEC_ROWS, width), f32),
        ],
        in_specs=[pl.BlockSpec(memory_space=pltpu.SMEM), vmem, vmem] + [any_space] * 8,
        out_specs=[any_space] * 5,
        scratch_shapes=[
            pltpu.VMEM(small, f32), pltpu.VMEM((2, hidden), f32),
            pltpu.VMEM(wproj.shape, bf16), pltpu.VMEM(wo.shape, bf16), pltpu.VMEM(wfirst.shape, bf16),
            pltpu.VMEM(wsecond.shape, bf16), pltpu.VMEM(win.shape, bf16), pltpu.VMEM(wout.shape, bf16),
            pltpu.VMEM((2, width, width), bf16),
            pltpu.VMEM((ROWS, width), bf16),
            pltpu.VMEM((ROWS, width), bf16),
            pltpu.VMEM((ROWS, width), bf16),
            pltpu.VMEM((ROWS, width), bf16),
            pltpu.VMEM((ROWS, width), bf16),
            pltpu.VMEM((slots, ROWS, width), bf16),
            pltpu.VMEM((2, ROWS, width), bf16),
            pltpu.VMEM((ROWS, width), f32),
            pltpu.VMEM((ROWS, width), f32),
            pltpu.VMEM((ROWS, width), f32),
            pltpu.VMEM((ROWS, width), f32),
            pltpu.VMEM((ROWS, width), f32),
            pltpu.VMEM((ROWS, width), f32),
            pltpu.VMEM((11, ROWS, width), bf16),
            pltpu.VMEM((11, ROWS, width), bf16),
            pltpu.VMEM((9, 2, 2, 2, 2, PIECE, ROWS), bf16),
            pltpu.VMEM((9, 2, 2, 2, PIECE, ROWS), bf16),
            pltpu.VMEM((SEND_SLOTS, 2, 2, PIECE, width), bf16),
            pltpu.VMEM((PIECES + 1, 2, 2, PIECE, width), bf16),
            pltpu.VMEM((PIECES + 1, 2, PIECE, width), bf16),
            pltpu.VMEM((ROWS, width), bf16),
            pltpu.VMEM((VEC_ROWS, width), f32),
            pltpu.VMEM((10, VEC_ROWS, half), f32),
            pltpu.VMEM((2, VEC_ROWS, width), f32),
            dma((9,)), dma((20,)), dma((20,)), dma((2,)), dma((2,)), dma((2,)), dma((2,)), dma, dma,
            dma((9,)), dma((9,)), dma((12,)), dma((12,)),
            dma((19, 3)), dma((19, 3)), dma((19,)), dma((3,)), dma((6,)), dma((6,)),
        ],
        compiler_params=pltpu.CompilerParams(collective_id=0, has_side_effects=True, vmem_limit_bytes=VMEM_LIMIT),
        name="step",
    )(lengths, gains, biases, x, cot, wproj, wo, wfirst, wsecond, win, wout)
    shapes = [(4 * PIECE, width), (PIECE, hidden), (PIECE, width), (PIECE, width), (PIECE, width), (3, PIECE, width),
              (5, PIECE), (24, PIECE)]
    return pl.pallas_call(
        functools.partial(last_kernel, width),
        out_shape=[jax.ShapeDtypeStruct((ROWS, width), bf16), jax.ShapeDtypeStruct((ROWS, width), f32)]
        + [jax.ShapeDtypeStruct(shape, f32) for shape in shapes],
        in_specs=[any_space] * 5,
        out_specs=[any_space] * 8 + [vmem] * 2,
        scratch_shapes=[
            pltpu.VMEM((2, VEC_ROWS, width), f32), pltpu.VMEM((ROWS, width), bf16), pltpu.VMEM((ROWS, width), f32),
            pltpu.VMEM((PIECES, PIECE, width), bf16), pltpu.VMEM((PIECES, PIECE, width), bf16),
            pltpu.VMEM((PIECES, PIECE, width), f32), dma((2, 2)), dma((3,)), dma((PIECES + 2,)),
        ],
        compiler_params=pltpu.CompilerParams(vmem_limit_bytes=VMEM_LIMIT),
        name="last",
    )(*results)


eps_norm = 1e-05
low_type = jnp.bfloat16
wide_type = jnp.float32


def as_sent(shard):
    return jax.tree.map(lambda a: a.astype(jnp.bfloat16) if a.dtype == jnp.float32 else a, shard)


def shifted(shard, axis, by):
    count = lax.axis_size(axis)
    pairs = [(i, i + by) for i in range(count) if 0 <= i + by < count]
    return lax.ppermute(shard, axis, pairs)


def matmul(left_mat, right_mat):
    return jnp.dot(left_mat, right_mat, preferred_element_type=wide_type)


def matmul_tn(left_mat, right_mat):
    return lax.dot_general(
        left_mat, right_mat, (((0,), (0,)), ((), ())), preferred_element_type=wide_type
    )


def matmul_nt(left_mat, right_mat):
    return lax.dot_general(
        left_mat, right_mat, (((1,), (1,)), ((), ())), preferred_element_type=wide_type
    )


def column_sum(tensor):
    return jnp.sum(tensor.astype(wide_type), axis=0)


def norm_rows(tensor, norm_gain, norm_shift):
    centre = tensor - jnp.mean(tensor, axis=-1, keepdims=True)
    spread = jnp.mean(centre * centre, axis=-1, keepdims=True)
    return centre * lax.rsqrt(spread + eps_norm) * norm_gain + norm_shift


def norm_back(tensor, norm_gain, norm_shift, upstream):
    unused, pullback = jax.vjp(norm_rows, tensor, norm_gain, norm_shift)
    return pullback(upstream)


def gelu_exact(tensor):
    return jax.nn.gelu(tensor, approximate=False)


def key_mask(row_count, key_count, length, causal):
    columns = lax.broadcasted_iota(jnp.int32, (row_count, key_count), 1)
    allowed = columns < length
    if causal:
        allowed = allowed & (columns <= lax.broadcasted_iota(jnp.int32, (row_count, key_count), 0))
    return allowed


def split_heads(tensor):
    return tensor.reshape(tensor.shape[0], -1, HDIM)


def attend_scores(queries, key_rows, allowed):
    scores = jnp.einsum(
        "qhd,khd->hqk",
        split_heads(queries),
        split_heads(key_rows),
        preferred_element_type=wide_type,
    )
    return jnp.where(allowed[None], scores * HDIM ** (-0.5), -1e30)


def attend_forward(queries, key_rows, values, allowed):
    scores = attend_scores(queries, key_rows, allowed)
    row_max = jnp.max(scores, axis=-1, keepdims=True)
    log_total = row_max + jnp.log(jnp.sum(jnp.exp(scores - row_max), axis=-1, keepdims=True))
    softmaxed = jnp.exp(scores - log_total).astype(low_type)
    attended = jnp.einsum(
        "hqk,khd->qhd", softmaxed, split_heads(values), preferred_element_type=wide_type
    )
    return (attended.reshape(queries.shape[0], -1), log_total)


def attend_backward(queries, key_rows, values, allowed, log_total, upstream):
    softmaxed = jnp.exp(attend_scores(queries, key_rows, allowed) - log_total)
    grad_heads = split_heads(upstream)
    grad_values = jnp.einsum(
        "hqk,qhd->khd", softmaxed.astype(low_type), grad_heads, preferred_element_type=wide_type
    )
    grad_probs = jnp.einsum(
        "qhd,khd->hqk", grad_heads, split_heads(values), preferred_element_type=wide_type
    )
    grad_scores = (
        softmaxed * (grad_probs - jnp.sum(softmaxed * grad_probs, axis=-1, keepdims=True))
    ).astype(low_type)
    scale_factor = HDIM ** (-0.5)
    grad_queries = (
        jnp.einsum(
            "hqk,khd->qhd", grad_scores, split_heads(key_rows), preferred_element_type=wide_type
        )
        * scale_factor
    )
    grad_keys = (
        jnp.einsum(
            "hqk,qhd->khd", grad_scores, split_heads(queries), preferred_element_type=wide_type
        )
        * scale_factor
    )
    key_count = key_rows.shape[0]
    return (
        grad_queries.reshape(queries.shape[0], -1),
        grad_keys.reshape(key_count, -1),
        grad_values.reshape(key_count, -1),
    )


def self_forward(row_block, length, causal, w_proj, w_out, vectors):
    bias_q, bias_v, bias_o, norm_gain, norm_shift = vectors
    row_count = row_block.shape[0]
    offsets = jnp.stack([bias_q, jnp.zeros_like(bias_q), bias_v])[:, None, :]
    projected = (
        jnp.einsum("rd,cde->cre", row_block, w_proj, preferred_element_type=wide_type) + offsets
    ).astype(low_type)
    allowed = key_mask(row_count, row_count, length, causal)
    attended, log_total = attend_forward(projected[0], projected[1], projected[2], allowed)
    attended = attended.astype(low_type)
    summed = row_block.astype(wide_type) + matmul(attended, w_out) + bias_o
    return (norm_rows(summed, norm_gain, norm_shift), (projected, log_total, attended, summed))


def self_backward(row_block, length, causal, w_proj, w_out, vectors, saved_fwd, upstream):
    projected, log_total, attended, summed = saved_fwd
    row_count = row_block.shape[0]
    grad_sum, grad_gain, grad_shift = norm_back(summed, vectors[3], vectors[4], upstream)
    grad_branch = grad_sum.astype(low_type)
    grad_attended = matmul_nt(grad_branch, w_out).astype(low_type)
    allowed = key_mask(row_count, row_count, length, causal)
    grad_q, grad_k, grad_v = attend_backward(
        projected[0], projected[1], projected[2], allowed, log_total, grad_attended
    )
    grad_proj = jnp.stack([grad_q, grad_k, grad_v]).astype(low_type)
    grad_rows = grad_sum + jnp.einsum(
        "cre,cde->rd", grad_proj, w_proj, preferred_element_type=wide_type
    )
    weight_grads = (
        jnp.einsum("rd,cre->cde", row_block, grad_proj, preferred_element_type=wide_type),
        matmul_tn(attended, grad_branch),
    )
    vector_grads = (
        column_sum(grad_proj[0]),
        column_sum(grad_proj[2]),
        column_sum(grad_branch),
        grad_gain,
        grad_shift,
    )
    return (grad_rows, weight_grads, vector_grads)


def ffn_forward(hidden, w_in, w_out, vectors):
    bias_in, bias_out, norm_gain, norm_shift = vectors
    low_hidden = hidden.astype(low_type)
    inner_act = matmul(low_hidden, w_in) + bias_in
    active = gelu_exact(inner_act).astype(low_type)
    summed = hidden + matmul(active, w_out) + bias_out
    return (norm_rows(summed, norm_gain, norm_shift), (low_hidden, inner_act, active, summed))


def ffn_backward(w_in, w_out, vectors, saved_fwd, upstream):
    low_hidden, inner_act, active, summed = saved_fwd
    grad_sum, grad_gain, grad_shift = norm_back(summed, vectors[2], vectors[3], upstream)
    grad_branch = grad_sum.astype(low_type)
    unused, pullback = jax.vjp(gelu_exact, inner_act)
    grad_inner = pullback(matmul_nt(grad_branch, w_out))[0].astype(low_type)
    grad_hidden = grad_sum + matmul_nt(grad_inner, w_in)
    weight_grads = (matmul_tn(low_hidden, grad_inner), matmul_tn(active, grad_branch))
    vector_grads = (column_sum(grad_inner), column_sum(grad_branch), grad_gain, grad_shift)
    return (grad_hidden, weight_grads, vector_grads)


def cross_forward(hidden, memory, src_len, w_query, w_out, vectors):
    bias_q, bias_v, bias_o, norm_gain, norm_shift = vectors
    low_hidden = hidden.astype(low_type)
    queries = (matmul(low_hidden, w_query) + bias_q).astype(low_type)
    allowed = key_mask(hidden.shape[0], memory.shape[1], src_len, False)
    attended, log_total = attend_forward(queries, memory[0], memory[1], allowed)
    attended = (attended + bias_v).astype(low_type)
    summed = hidden + matmul(attended, w_out) + bias_o
    return (
        norm_rows(summed, norm_gain, norm_shift),
        (low_hidden, queries, log_total, attended, summed),
    )


def cross_backward(memory, src_len, w_query, w_out, vectors, saved_fwd, upstream):
    low_hidden, queries, log_total, attended, summed = saved_fwd
    grad_sum, grad_gain, grad_shift = norm_back(summed, vectors[3], vectors[4], upstream)
    grad_branch = grad_sum.astype(low_type)
    grad_attended = matmul_nt(grad_branch, w_out).astype(low_type)
    allowed = key_mask(queries.shape[0], memory.shape[1], src_len, False)
    grad_q, grad_k, grad_v = attend_backward(
        queries, memory[0], memory[1], allowed, log_total, grad_attended
    )
    grad_query = grad_q.astype(low_type)
    grad_memory = jnp.stack([grad_k, grad_v]).astype(low_type)
    grad_hidden = grad_sum + matmul_nt(grad_query, w_query)
    weight_grads = (matmul_tn(low_hidden, grad_query), matmul_tn(attended, grad_branch))
    vector_grads = (
        column_sum(grad_query),
        column_sum(grad_attended),
        column_sum(grad_branch),
        grad_gain,
        grad_shift,
    )
    return (grad_hidden, grad_memory, weight_grads, vector_grads)


def self_vectors(gain_rows, bias_rows, decoder):
    base_row = 10 if decoder else 0
    gain_row = 2 if decoder else 0
    return (
        bias_rows[base_row],
        bias_rows[base_row + 1],
        bias_rows[base_row + 2],
        gain_rows[gain_row],
        bias_rows[base_row + 3],
    )


def ffn_vectors(gain_rows, bias_rows, decoder):
    base_row = 18 if decoder else 4
    gain_row = 4 if decoder else 1
    return (
        bias_rows[base_row : base_row + 4].reshape(-1),
        bias_rows[base_row + 4],
        gain_rows[gain_row],
        bias_rows[base_row + 5],
    )


def cross_vectors(gain_rows, bias_rows):
    return (bias_rows[14], bias_rows[15], bias_rows[16], gain_rows[3], bias_rows[17])


def self_plan(decoder, vector_grads):
    base_row = 10 if decoder else 0
    gain_row = 2 if decoder else 0
    return (
        ("biases", base_row, vector_grads[0]),
        ("biases", base_row + 1, vector_grads[1]),
        ("biases", base_row + 2, vector_grads[2]),
        ("gains", gain_row, vector_grads[3]),
        ("biases", base_row + 3, vector_grads[4]),
    )


def ffn_plan(decoder, vector_grads):
    base_row = 18 if decoder else 4
    gain_row = 4 if decoder else 1
    return (
        ("biases", base_row, vector_grads[0]),
        ("biases", base_row + 4, vector_grads[1]),
        ("gains", gain_row, vector_grads[2]),
        ("biases", base_row + 5, vector_grads[3]),
    )


def cross_plan(vector_grads):
    return (
        ("biases", 14, vector_grads[0]),
        ("biases", 15, vector_grads[1]),
        ("biases", 16, vector_grads[2]),
        ("gains", 3, vector_grads[3]),
        ("biases", 17, vector_grads[4]),
    )


def accumulate(totals, weight_names, weight_grads, vector_plan):
    merged = dict(totals)
    for key_name, tensor in zip(weight_names, weight_grads):
        merged[key_name] = merged[key_name] + tensor
    for table_name, row_at, tensor in vector_plan:
        table_now = merged[table_name]
        row_block = tensor.reshape(-1, table_now.shape[1])
        merged[table_name] = table_now.at[row_at : row_at + row_block.shape[0]].add(row_block)
    return merged


def updated(progress, key_name, position, tensor):
    copied = dict(progress)
    copied[key_name] = [
        tensor if slot_index == position else entry_now
        for slot_index, entry_now in enumerate(progress[key_name])
    ]
    return copied


def with_totals(progress, totals):
    copied = dict(progress)
    copied["totals"] = totals
    return copied


def forward_pass(tensor):
    return jax.tree.map(
        lambda part, own: part.astype(own.dtype), shifted(as_sent(tensor), "stream", 1), tensor
    )


def backward_pass(tensor):
    return jax.tree.map(
        lambda part, own: part.astype(own.dtype), shifted(as_sent(tensor), "stream", -1), tensor
    )


def keep_same(progress):
    return progress


def plain_body(
    inputs,
    lengths,
    cotangent,
    attn_in,
    attn_out,
    cross_first,
    cross_second,
    ffn_in,
    ffn_out,
    gains,
    biases,
):
    own_rows = inputs[0]
    model_width = own_rows.shape[1]
    hidden_width = ffn_in.shape[2]
    head_count = model_width // HDIM
    row_sizes = (SHORT, LONG)
    bucket_spans = ((0, SHORT), (SHORT, SHORT + LONG))
    row_pieces = [own_rows[start_row:stop_row] for start_row, stop_row in bucket_spans]
    grad_pieces = [
        cotangent[start_row:stop_row].astype(wide_type) for start_row, stop_row in bucket_spans
    ]
    src_lens = [lengths[0, 0, bucket_idx] for bucket_idx in range(2)]
    tgt_lens = [lengths[1, 0, bucket_idx] for bucket_idx in range(2)]
    w_proj = attn_in[0]
    w_attn_out = attn_out[0]
    w_first = cross_first[0]
    w_second = cross_second[0]
    w_ffn_in = ffn_in[0]
    w_ffn_out = ffn_out[0]
    gain_rows = gains.astype(wide_type)
    bias_rows = biases.astype(wide_type)
    enc_self = self_vectors(gain_rows, bias_rows, False)
    enc_ffn = ffn_vectors(gain_rows, bias_rows, False)
    dec_self = self_vectors(gain_rows, bias_rows, True)
    dec_ffn = ffn_vectors(gain_rows, bias_rows, True)
    dec_cross = cross_vectors(gain_rows, bias_rows)
    is_decoder = lax.axis_index("stream") == 1

    def blank_self(size_rows):
        return (
            jnp.zeros((3, size_rows, model_width), low_type),
            jnp.zeros((head_count, size_rows, 1), wide_type),
            jnp.zeros((size_rows, model_width), low_type),
            jnp.zeros((size_rows, model_width), wide_type),
        )

    def blank_ffn(size_rows):
        return (
            jnp.zeros((size_rows, model_width), low_type),
            jnp.zeros((size_rows, hidden_width), wide_type),
            jnp.zeros((size_rows, hidden_width), low_type),
            jnp.zeros((size_rows, model_width), wide_type),
        )

    def blank_cross(size_rows):
        return (
            jnp.zeros((size_rows, model_width), low_type),
            jnp.zeros((size_rows, model_width), low_type),
            jnp.zeros((head_count, size_rows, 1), wide_type),
            jnp.zeros((size_rows, model_width), low_type),
            jnp.zeros((size_rows, model_width), wide_type),
        )

    progress = {
        "out": [jnp.zeros((size_rows, model_width), low_type) for size_rows in row_sizes],
        "grad_in": [jnp.zeros((size_rows, model_width), wide_type) for size_rows in row_sizes],
        "send": [jnp.zeros((2, size_rows, model_width), low_type) for size_rows in row_sizes],
        "memory": [jnp.zeros((2, size_rows, model_width), low_type) for size_rows in row_sizes],
        "grad_send": [jnp.zeros((2, size_rows, model_width), low_type) for size_rows in row_sizes],
        "grad_memory": [
            jnp.zeros((2, size_rows, model_width), low_type) for size_rows in row_sizes
        ],
        "mid": [jnp.zeros((size_rows, model_width), wide_type) for size_rows in row_sizes],
        "grad_mid": [jnp.zeros((size_rows, model_width), wide_type) for size_rows in row_sizes],
        "totals": {
            "proj": jnp.zeros(w_proj.shape, wide_type),
            "attn_out": jnp.zeros(w_attn_out.shape, wide_type),
            "first": jnp.zeros(w_first.shape, wide_type),
            "second": jnp.zeros(w_second.shape, wide_type),
            "ffn_in": jnp.zeros(w_ffn_in.shape, wide_type),
            "ffn_out": jnp.zeros(w_ffn_out.shape, wide_type),
            "gains": jnp.zeros(gains.shape, wide_type),
            "biases": jnp.zeros(biases.shape, wide_type),
        },
    }
    progress["self_saved"] = [blank_self(size_rows) for size_rows in row_sizes]
    progress["ffn_saved"] = [blank_ffn(size_rows) for size_rows in row_sizes]
    progress["cross_saved"] = [blank_cross(size_rows) for size_rows in row_sizes]

    def encoder_core(micro_idx):
        h_one, self_saved = self_forward(
            row_pieces[micro_idx], src_lens[micro_idx], False, w_proj, w_attn_out, enc_self
        )
        encoded, ffn_saved = ffn_forward(h_one, w_ffn_in, w_ffn_out, enc_ffn)
        return (encoded.astype(low_type), self_saved, ffn_saved)

    def encoder_forward_step(progress, micro_idx):
        low_memory, self_saved, ffn_saved = encoder_core(micro_idx)
        memory = jnp.stack([matmul(low_memory, w_first), matmul(low_memory, w_second)]).astype(
            low_type
        )
        progress = updated(progress, "out", micro_idx, low_memory)
        progress = updated(progress, "send", micro_idx, memory)
        progress = updated(progress, "self_saved", micro_idx, self_saved)
        progress = updated(progress, "ffn_saved", micro_idx, ffn_saved)
        return progress

    def decoder_head(micro_idx):
        return self_forward(
            row_pieces[micro_idx], tgt_lens[micro_idx], True, w_proj, w_attn_out, dec_self
        )

    def decoder_tail(mid_rows, memory, micro_idx):
        crossed, cross_saved = cross_forward(
            mid_rows, memory, src_lens[micro_idx], w_first, w_second, dec_cross
        )
        decoded, ffn_saved = ffn_forward(crossed, w_ffn_in, w_ffn_out, dec_ffn)
        return (decoded, cross_saved, ffn_saved)

    def decoder_head_step(progress, micro_idx):
        mid_rows, self_saved = decoder_head(micro_idx)
        progress = updated(progress, "mid", micro_idx, mid_rows)
        progress = updated(progress, "self_saved", micro_idx, self_saved)
        return progress

    def decoder_tail_step(progress, micro_idx):
        decoded, cross_saved, ffn_saved = decoder_tail(
            progress["mid"][micro_idx], progress["memory"][micro_idx], micro_idx
        )
        progress = updated(progress, "out", micro_idx, decoded.astype(low_type))
        progress = updated(progress, "cross_saved", micro_idx, cross_saved)
        progress = updated(progress, "ffn_saved", micro_idx, ffn_saved)
        return progress

    def decoder_back_step(progress, micro_idx):
        memory = progress["memory"][micro_idx]
        self_saved = progress["self_saved"][micro_idx]
        cross_saved = progress["cross_saved"][micro_idx]
        ffn_saved = progress["ffn_saved"][micro_idx]
        grad_h_two, ffn_w, ffn_v = ffn_backward(
            w_ffn_in, w_ffn_out, dec_ffn, ffn_saved, grad_pieces[micro_idx]
        )
        grad_h_one, grad_memory, cross_w, cross_v = cross_backward(
            memory, src_lens[micro_idx], w_first, w_second, dec_cross, cross_saved, grad_h_two
        )
        grad_rows, self_w, self_v = self_backward(
            row_pieces[micro_idx],
            tgt_lens[micro_idx],
            True,
            w_proj,
            w_attn_out,
            dec_self,
            self_saved,
            grad_h_one,
        )
        totals = accumulate(
            progress["totals"],
            ("ffn_in", "ffn_out", "first", "second", "proj", "attn_out"),
            ffn_w + cross_w + self_w,
            ffn_plan(True, ffn_v) + cross_plan(cross_v) + self_plan(True, self_v),
        )
        progress = updated(progress, "grad_in", micro_idx, grad_rows)
        progress = updated(progress, "grad_send", micro_idx, grad_memory)
        return with_totals(progress, totals)

    def encoder_top_step(progress, micro_idx):
        low_memory = progress["out"][micro_idx]
        ffn_saved = progress["ffn_saved"][micro_idx]
        grad_memory = progress["grad_memory"][micro_idx]
        grad_encoded = matmul_nt(grad_memory[0], w_first) + matmul_nt(grad_memory[1], w_second)
        grad_h_one, ffn_w, ffn_v = ffn_backward(
            w_ffn_in, w_ffn_out, enc_ffn, ffn_saved, grad_encoded
        )
        projections = (matmul_tn(low_memory, grad_memory[0]), matmul_tn(low_memory, grad_memory[1]))
        totals = accumulate(
            progress["totals"],
            ("first", "second", "ffn_in", "ffn_out"),
            projections + ffn_w,
            ffn_plan(False, ffn_v),
        )
        progress = updated(progress, "grad_mid", micro_idx, grad_h_one)
        return with_totals(progress, totals)

    def encoder_bottom_step(progress, micro_idx):
        self_saved = progress["self_saved"][micro_idx]
        grad_rows, self_w, self_v = self_backward(
            row_pieces[micro_idx],
            src_lens[micro_idx],
            False,
            w_proj,
            w_attn_out,
            enc_self,
            self_saved,
            progress["grad_mid"][micro_idx],
        )
        totals = accumulate(
            progress["totals"], ("proj", "attn_out"), self_w, self_plan(False, self_v)
        )
        progress = updated(progress, "grad_in", micro_idx, grad_rows)
        return with_totals(progress, totals)

    def enc_zero(progress):
        return encoder_forward_step(progress, 0)

    def dec_zero(progress):
        return decoder_head_step(progress, 0)

    def enc_one(progress):
        return encoder_forward_step(progress, 1)

    def dec_one(progress):
        return decoder_tail_step(decoder_head_step(progress, 1), 0)

    def dec_two(progress):
        return decoder_back_step(decoder_tail_step(progress, 1), 1)

    def enc_three(progress):
        return encoder_bottom_step(encoder_top_step(progress, 1), 1)

    def dec_three(progress):
        return decoder_back_step(progress, 0)

    def enc_four(progress):
        return encoder_top_step(progress, 0)

    def enc_five(progress):
        return encoder_bottom_step(progress, 0)

    progress = lax.cond(is_decoder, dec_zero, enc_zero, progress)
    progress = updated(progress, "memory", 0, forward_pass(progress["send"][0]))
    progress = lax.cond(is_decoder, dec_one, enc_one, progress)
    progress = updated(progress, "memory", 1, forward_pass(progress["send"][1]))
    progress = lax.cond(is_decoder, dec_two, keep_same, progress)
    progress = updated(progress, "grad_memory", 1, backward_pass(progress["grad_send"][1]))
    progress = lax.cond(is_decoder, dec_three, enc_three, progress)
    progress = updated(progress, "grad_memory", 0, backward_pass(progress["grad_send"][0]))
    progress = lax.cond(is_decoder, keep_same, enc_four, progress)
    progress = lax.cond(is_decoder, keep_same, enc_five, progress)
    totals = progress["totals"]
    owned = (
        lax.psum_scatter(totals["proj"], "dp", scatter_dimension=1, tiled=True),
        lax.psum_scatter(totals["attn_out"], "dp", scatter_dimension=0, tiled=True),
        lax.psum_scatter(totals["first"], "dp", scatter_dimension=0, tiled=True),
        lax.psum_scatter(totals["second"], "dp", scatter_dimension=0, tiled=True),
        lax.psum_scatter(totals["ffn_in"], "dp", scatter_dimension=0, tiled=True),
        lax.psum_scatter(totals["ffn_out"], "dp", scatter_dimension=0, tiled=True),
        lax.psum_scatter(totals["gains"], "dp", scatter_dimension=1, tiled=True),
        lax.psum_scatter(totals["biases"], "dp", scatter_dimension=1, tiled=True),
    )
    owned_gains, owned_biases = lax.psum((owned[6], owned[7]), "stream")
    layer_out = jnp.concatenate(progress["out"], axis=0)[None]
    grad_inputs = jnp.concatenate(progress["grad_in"], axis=0)[None]
    return (
        layer_out,
        grad_inputs,
        owned[0][None],
        owned[1][None],
        owned[2][None],
        owned[3][None],
        owned[4][None],
        owned[5][None],
        owned_gains,
        owned_biases,
    )


def fused_body(inputs, lengths, cotangent, attn_in, attn_out, cross_first, cross_second, ffn_in, ffn_out, gains, biases):
    rows, grad, s_out, s_in, s_second, s_first, s_attn, s_proj, own_gains, own_biases = whole_step(
        lengths, gains, biases, inputs[0], cotangent, attn_in[0], attn_out[0],
        cross_first[0], cross_second[0], ffn_in[0], ffn_out[0])
    return (rows[None], grad[None], s_proj[None], s_attn[None], s_first[None], s_second[None],
            s_in[None], s_out[None], own_gains, own_biases)


def solution(mesh):
    def body(*args):
        width = args[0].shape[2]
        fits = mesh.shape["dp"] * PIECE == width and args[0].shape[1] == ROWS and args[7].shape[2] == 4 * width
        return (fused_body if fits else plain_body)(*args)
    return jax.shard_map(
        body,
        mesh=mesh,
        in_specs=(
            P("stream", "dp", None),
            P(None, "dp", None),
            P("dp", None),
            P("stream", None, None, None),
            P("stream", None, None),
            P("stream", None, None),
            P("stream", None, None),
            P("stream", None, None),
            P("stream", None, None),
            P(),
            P(),
        ),
        out_specs=(
            P("stream", "dp", None),
            P("stream", "dp", None),
            P("stream", None, "dp", None),
            P("stream", "dp", None),
            P("stream", "dp", None),
            P("stream", "dp", None),
            P("stream", "dp", None),
            P("stream", "dp", None),
            P(None, "dp"),
            P(None, "dp"),
        ),
        check_vma=False,
    )
```

```python
import functools

import jax
import jax.numpy as jnp
from jax import lax
from jax.experimental import pallas as pl
from jax.experimental.pallas import tpu as pltpu
from jax.sharding import PartitionSpec as P

HDIM = 64
SHORT = 128
LONG = 256
ROWS = SHORT + LONG
PIECE = 48
PIECES = 14
VEC_ROWS = 24
SEND_SLOTS = 8
MESH = pl.DeviceIdType.MESH
bf16, f32 = jnp.bfloat16, jnp.float32
VMEM_LIMIT = 64 << 20


def dot_nn(a, b):
    return jnp.dot(a, b, preferred_element_type=f32)


def dot_nt(a, b):
    return lax.dot_general(a, b, (((1,), (1,)), ((), ())), preferred_element_type=f32)


def dot_tn(a, b):
    return lax.dot_general(a, b, (((0,), (0,)), ((), ())), preferred_element_type=f32)


def cols(j, width):
    return pl.ds(pl.multiple_of(j * width, width), width)


def step_kernel(
    width, hidden,
    lengths, gains, biases, x_hbm, cot_hbm, wproj_hbm, wo_hbm, wfirst_hbm, wsecond_hbm, win_hbm, wout_hbm,
    out_rows, out_grad, out_own, out_part, out_vec,
    vec, bias_in, wproj, wo, wfirst, wsecond, win, wout, wx,
    xb, up, mem, obuf, hlow, dg, kv, acc, grad, hw, u_self, u_cross, u_ffn, gr, grp, lt, ltp, one_send, one_recv, two_recv, gmem, vg, vbuf, vboth,
    load_sem, wx_send, wx_recv, mem_send, mem_recv, gm_send, gm_recv, gv_send, gv_recv, lt_send, lt_recv, gr_send, gr_recv,
    sem_send, sem_recv, own_sem, io_sem, v_send, v_recv,
):
    st = lax.axis_index("stream")
    me = lax.axis_index("dp")
    z, y, c = me // 4, (me // 2) % 2, me % 2
    is_dec = st == 1
    is_enc = st == 0
    core_id = {"dp": z * 4 + y * 2 + (1 - c)}
    y_id = {"dp": z * 4 + (1 - y) * 2 + c}
    x_id = {"stream": 1 - st}
    tiles = width // 256
    slots = hidden // width

    zh, zl = z // 2, z % 2

    def z_id(other):
        return {"dp": other * 4 + y * 2 + c}
    near_id = z_id(zh * 2 + 1 - zl)
    far_id = z_id((1 - zh) * 2 + zl)
    over_id = {"stream": 1 - st, **far_id}

    def remote(src, dst, ss, rs, dev):
        return pltpu.make_async_remote_copy(
            src_ref=src, dst_ref=dst, send_sem=ss, recv_sem=rs, device_id=dev, device_id_type=MESH)

    loads = [
        pltpu.make_async_copy(src, dst, load_sem.at[i])
        for i, (src, dst) in enumerate((
            (x_hbm, xb), (x_hbm, mem), (wo_hbm, wo), (win_hbm, win), (wout_hbm, wout),
            (wfirst_hbm, wfirst), (wsecond_hbm, wsecond)))
    ]
    cot_load = pltpu.make_async_copy(cot_hbm, up, load_sem.at[7])
    def proj_load(which):
        return pltpu.make_async_copy(wproj_hbm.at[which], wproj.at[which], load_sem.at[9 + which])
    loads[0].start()
    for which in range(3):
        proj_load(which).start()

    barrier = pltpu.get_barrier_semaphore()
    peers = [core_id, y_id, x_id, near_id, far_id, over_id]
    for p in peers:
        pl.semaphore_signal(barrier, inc=1, device_id=p, device_id_type=MESH)

    lens = [lengths[i // 2, 0, i % 2] for i in range(4)]
    own_lens = [jnp.where(is_dec, lens[2 + i], lens[i]) for i in range(2)]
    vec[pl.ds(0, 5), :] = gains[...].astype(f32)
    vec[pl.ds(5, 24), :] = biases[...].astype(f32)
    for i in range(slots):
        for s in range(2):
            bias_in[pl.ds(s, 1), pl.ds(i * width, width)] = vec[pl.ds(9 + 14 * s + i, 1), :]
    vg[...] = jnp.zeros_like(vg)
    half = width // 2
    chunks = width // 4 // PIECE

    def wx_block(yy, zz, cc, h):
        return wx.at[yy, pl.ds((zz * 2 + cc) * chunks * PIECE + h * PIECE, PIECE)]

    def wx_copy(src, dst, k, dev):
        return remote(src, dst, wx_send.at[k], wx_recv.at[k], dev)

    def wx_from(source, h):
        return wx_copy(source.at[pl.ds((zl * 2 + c) * chunks * PIECE + h * PIECE, PIECE)], wx_block(y, zl, c, h), h, x_id)
    wx_in = [wx_from(wfirst_hbm, h) for h in range(chunks)]
    wx_y = [wx_copy(wx_block(y, zl, c, h), wx_block(y, zl, c, h), chunks + h, y_id) for h in range(chunks)]
    wx_z = [wx_copy(wx_block(y, zl, c, h), wx_block(y, zl, c, h), 2 * chunks + h, near_id) for h in range(chunks)]
    wx_on = [wx_copy(wx_block(1 - y, zl, c, h), wx_block(1 - y, zl, c, h), 3 * chunks + h, near_id) if h < chunks // 2 else
             wx_copy(wx_block(y, 1 - zl, c, h), wx_block(y, 1 - zl, c, h), 3 * chunks + h, y_id) for h in range(chunks)]

    def wx_whole(yy, zz):
        return wx.at[yy, pl.ds((zz * 2 + c) * chunks * PIECE, chunks * PIECE)]
    wx_core = [wx_copy(wx_whole(yy, zz), wx_whole(yy, zz), 4 * chunks + k, core_id)
               for k, (yy, zz) in enumerate(((y, zl), (1 - y, zl), (y, 1 - zl), (1 - y, 1 - zl)))]

    def wx_start():
        pl.semaphore_wait(barrier, len(peers))

        @pl.when(is_enc & (y == 0))
        def _():
            for h in range(chunks):
                wx_in[h].start()

        @pl.when(is_enc & (y == 1))
        def _():
            for h in range(chunks):
                wx_from(wsecond_hbm, h).start()
    for cp in loads[2:]:
        cp.start()
    loads[0].wait()

    @pl.when(is_dec)
    def _():
        cot_load.start()

    gain_row = lambda r: pl.ds(r - 2 * st, 1)
    bias_row_of = lambda r: pl.ds(r - 2 - 10 * st, 1)
    lt_copy = [remote(lt.at[i, :, :, :, 1 - c], ltp.at[i], lt_send.at[i], lt_recv.at[i], core_id) for i in range(9)]
    gr_copy = {i: remote(gr.at[i], grp.at[i], gr_send.at[i], gr_recv.at[i], core_id) for i in range(5, 11)}
    buckets = ((0, SHORT), (SHORT, LONG))
    short, long, both = (0,), (1,), (0, 1)

    def span(bs):
        return buckets[bs[0]][0], sum(buckets[b][1] for b in bs)

    def at_rows(bs):
        return pl.ds(*span(bs))
    mem_copy = [remote(xb.at[at_rows((b,))], mem.at[at_rows((b,))], mem_send.at[b], mem_recv.at[b], x_id) for b in range(2)]

    def gm_part(b, h):
        at = cols(h, half)
        return remote(gmem.at[at_rows((b,)), at], up.at[at_rows((b,)), at], gm_send.at[2 * b + h], gm_recv.at[2 * b + h], x_id)
    gv_copy = remote(kv.at[1], gr.at[5], gv_send, gv_recv, x_id)

    gr_first = [remote(gr.at[0, at_rows((b,))], grp.at[0, at_rows((b,))], gr_send.at[11 * b], gr_recv.at[11 * b], core_id)
                for b in range(2)]

    def row_loop(bs, block, body, unroll=1):
        r0, n = span(bs)

        def step(i, carry):
            body(pl.ds(pl.multiple_of(r0 + i * block, block), block))
            return carry
        lax.fori_loop(0, n // block, step, 0, unroll=unroll)

    def vrow(r):
        return vec[pl.ds(r, 1), :]

    def transposed(i, bs, ref):
        r0, n = span(bs)
        lt[i, :, :, :, :, :, pl.ds(r0, n)] = ref[pl.ds(r0, n), :].T.reshape(2, 2, 2, 2, PIECE, n)

    def transposed_slot(bs, j):
        r0, n = span(bs)
        turned = gr[1 + j, pl.ds(r0, n), :].T.reshape(2, 2, 4, PIECE, n)
        for k in range(4):
            lt[k, j // 2, j % 2, :, :, :, pl.ds(r0, n)] = turned[:, :, k]

    def transposed_active(bs):

        def step(j, carry):
            transposed_slot(bs, j)
            return carry
        lax.fori_loop(0, slots, step, 0)

    def col_sum(slot, row):
        def step(i, carry):
            block = slot[pl.ds(pl.multiple_of(i * 64, 64), 64), :].astype(f32)
            return carry + jnp.sum(block.reshape(8, 8, width), axis=0)
        total = lax.fori_loop(0, ROWS // 64, step, jnp.zeros((8, width), f32))
        vg[bias_row_of(row), :] = jnp.sum(total, axis=0, keepdims=True)

    def norm_forward(bs, residual, sum_ref, add_bias, gain, shift, out_low, out_wide):
        def body(rows):
            u = residual[rows, :].astype(f32) + acc[rows, :] + vrow(add_bias)
            sum_ref[rows, :] = u
            centre = u - jnp.mean(u, axis=-1, keepdims=True)
            spread = jnp.mean(centre * centre, axis=-1, keepdims=True)
            h = centre * lax.rsqrt(spread + 1e-05) * vrow(gain) + vrow(shift)
            if out_wide is not None:
                out_wide[rows, :] = h
            out_low[rows, :] = h.astype(bf16)
        row_loop(bs, 32, body, 4)

    def norm_backward(bs, sum_ref, source, gain, shift, out_wide, slot):
        r0, n = span(bs)

        def step(i, carry):
            rows = pl.ds(pl.multiple_of(r0 + i * 32, 32), 32)
            r = source[rows, :].astype(f32)
            u = sum_ref[rows, :]
            centre = u - jnp.mean(u, axis=-1, keepdims=True)
            spread = jnp.mean(centre * centre, axis=-1, keepdims=True)
            inv = lax.rsqrt(spread + 1e-05)
            uhat = centre * inv
            t = r * vrow(gain)
            gu = (t - jnp.mean(t, axis=-1, keepdims=True) - uhat * jnp.mean(t * uhat, axis=-1, keepdims=True)) * inv
            out_wide[rows, :] = gu
            slot[rows, :] = gu.astype(bf16)
            return (carry[0] + jnp.sum((r * uhat).reshape(4, 8, width), axis=0),
                    carry[1] + jnp.sum(r.reshape(4, 8, width), axis=0))
        zero = jnp.zeros((8, width), f32)
        total = lax.fori_loop(0, n // 32, step, (zero, zero), unroll=4)
        for row, part in ((gain_row(gain), total[0]), (bias_row_of(shift), total[1])):
            vg[row, :] = vg[row, :] + jnp.sum(part, axis=0, keepdims=True)

    def masked_scores(q_half, k2, n, length, diagonal):
        s = dot_nt(q_half, k2)
        column = lax.broadcasted_iota(jnp.int32, (n, n), 1)
        row = lax.broadcasted_iota(jnp.int32, (n, n), 0)
        return jnp.where((column < length) & (column <= row + diagonal), s, -1e30)

    def softmax(s):
        e = jnp.exp(s - jnp.max(s, axis=-1, keepdims=True))
        return e * (1.0 / jnp.sum(e, axis=-1, keepdims=True))

    def halves(n):
        lane = lax.broadcasted_iota(jnp.int32, (n, 2 * HDIM), 1)
        return lane < HDIM

    def head_loop(bs, body, lo=0, hi=None):
        pairs = {short: 3, long: 2, both: 1}[bs]

        def step(p, carry):
            body([(b, pl.ds(pl.multiple_of((p * pairs + i) * 2 * HDIM, 2 * HDIM), 2 * HDIM)) for b in bs for i in range(pairs)])
            return carry
        lax.fori_loop(lo, width // (2 * HDIM * pairs) if hi is None else hi, step, 0)

    def attend_forward(bs, q_ref, k_ref, v_ref, lengths_at, diagonal, bias_row, out_ref, lo=0, hi=None):
        def body(units):
            work = []
            for b, at in units:
                r0, n = buckets[b]
                rows = pl.ds(r0, n)
                q2, k2 = q_ref[rows, at], k_ref[rows, at]
                first = halves(n)
                for lanes in (first, ~first):
                    work.append(masked_scores(jnp.where(lanes, q2 * 0.125, jnp.zeros_like(q2)), k2, n, lengths_at[b], diagonal))
            work = [softmax(s).astype(bf16) for s in work]
            work = [dot_nn(prob, v_ref[pl.ds(*buckets[units[i // 2][0]]), units[i // 2][1]]) for i, prob in enumerate(work)]
            for i, (b, at) in enumerate(units):
                r0, n = buckets[b]
                att = jnp.where(halves(n), work[2 * i], work[2 * i + 1])
                if bias_row is not None:
                    att = att + vec[pl.ds(bias_row, 1), at]
                out_ref[pl.ds(r0, n), at] = att.astype(bf16)
        head_loop(bs, body, lo, hi)

    def attend_backward(bs, q_ref, k_ref, v_ref, lengths_at, diagonal, lo=0, hi=None):
        scale = HDIM ** -0.5

        def body(units):
            scores, ups = [], []
            for b, at in units:
                r0, n = buckets[b]
                rows = pl.ds(r0, n)
                q2, k2, v2, go2 = q_ref[rows, at], k_ref[rows, at], v_ref[rows, at], obuf[rows, at]
                first = halves(n)
                zero = jnp.zeros_like(q2)
                for lanes in (first, ~first):
                    scores.append(masked_scores(jnp.where(lanes, q2 * 0.125, zero), k2, n, lengths_at[b], diagonal))
                    ups.append(dot_nt(jnp.where(lanes, go2, zero), v2))
            probs = [softmax(s) for s in scores]
            gs = [(p * (gp - jnp.sum(p * gp, axis=-1, keepdims=True))).astype(bf16) for p, gp in zip(probs, ups)]
            for i, (b, at) in enumerate(units):
                r0, n = buckets[b]
                rows = pl.ds(r0, n)
                q2, k2, go2 = q_ref[rows, at], k_ref[rows, at], obuf[rows, at]
                first = halves(n)
                two = (2 * i, 2 * i + 1)
                gv = [dot_tn(probs[u].astype(bf16), go2) for u in two]
                gq = [dot_nn(gs[u], k2) for u in two]
                gk = [dot_tn(gs[u], q2) for u in two]
                q_ref[rows, at] = (jnp.where(first, gq[0], gq[1]) * scale).astype(bf16)
                k_ref[rows, at] = (jnp.where(first, gk[0], gk[1]) * scale).astype(bf16)
                v_ref[rows, at] = jnp.where(first, gv[0], gv[1]).astype(bf16)
        head_loop(bs, body, lo, hi)

    q_ref, k_ref, v_ref = gr.at[8], gr.at[9], gr.at[10]
    diagonal = (1 - st) * 4096
    bias_at = 5 + 10 * st
    ffn_at = 13 + 14 * st
    ffn_gain = 1 + 3 * st

    def by_tiles(fn):
        for t in range(tiles):
            fn(pl.ds(t * 256, 256))

    def self_project(bs, wait):
        rows = at_rows(bs)

        def project(which, carry):
            if wait:
                proj_load(which).wait()
            for t in range(tiles):
                at = pl.ds(t * 256, 256)
                value = dot_nn(xb[rows, :], wproj[which, :, at])
                bias = vec[pl.ds(bias_at + which // 2, 1), at] * jnp.where(which == 1, 0.0, 1.0)
                gr[8 + which, rows, at] = (value + bias).astype(bf16)
            return carry
        lax.fori_loop(0, 3, project, 0)

    def self_output(bs):
        rows = at_rows(bs)

        def tile(at):
            acc[rows, at] = dot_nn(obuf[rows, :], wo[:, at])
        by_tiles(tile)
        norm_forward(bs, xb, u_self, bias_at + 2, 2 * st, bias_at + 3, hlow, grad)

    def ffn_forward(bs, residual, wait_in, wait_out, turn=False):
        r0, n = span(bs)
        rows = pl.ds(r0, n)

        def ffn_slot(j, carry):
            for t in range(tiles):
                at = pl.ds(t * 256, 256)
                wide = pl.ds(pl.multiple_of(j * width + t * 256, 256), 256)
                zv = dot_nn(hlow[rows, :], win[:, wide]) + bias_in[pl.ds(st, 1), wide]
                cdf = 0.5 * (1.0 + lax.erf(zv * (0.5 ** 0.5)))
                pdf = jnp.exp(-0.5 * zv * zv) * 0.3989422804014327
                gr[1 + j, rows, at] = (zv * cdf).astype(bf16)
                dg[j, rows, at] = (cdf + zv * pdf).astype(bf16)
            return carry
        if wait_in:
            loads[3].wait()
        lax.fori_loop(0, slots, ffn_slot, 0)

        def ffn_out(at):
            total = dot_nn(gr[1, rows, :], wout[pl.ds(0, width), at])
            for j in range(1, slots):
                total = total + dot_nn(gr[1 + j, rows, :], wout[pl.ds(j * width, width), at])
            acc[rows, at] = total
        if wait_out:
            loads[4].wait()
        by_tiles(ffn_out)
        if turn:
            for j in range(slots):
                transposed_slot(bs, j)
        norm_forward(bs, residual, u_ffn, ffn_at, ffn_gain, ffn_at + 1, xb, None)

    def ffn_inner(bs, lo, hi, last):
        r0, n = span(bs)
        rows = pl.ds(r0, n)

        def ffn_inner_slot(j, carry):
            for t in range(tiles):
                at = pl.ds(t * 256, 256)
                wide = pl.ds(pl.multiple_of(j * width + t * 256, 256), 256)
                value = dot_nt(gr[0, rows, :], wout[wide, :])
                gr[1 + j, rows, at] = (value * dg[j, rows, at].astype(f32)).astype(bf16)
            if last:
                remote(gr.at[1 + j], grp.at[1 + j], gr_send.at[1 + j], gr_recv.at[1 + j], core_id).start()
            return carry
        lax.fori_loop(lo, hi, ffn_inner_slot, 0)

    def ffn_input(bs):
        rows = at_rows(bs)

        def tile(at):
            total = grad[rows, at]
            for j in range(slots):
                total = total + dot_nt(gr[1 + j, rows, :], win[at, pl.ds(j * width, width)])
            grad[rows, at] = total
        by_tiles(tile)

    def cross_forward(bs):
        rows = at_rows(bs)

        def memory_kv(which, carry):
            for t in range(tiles):
                at = pl.ds(t * 256, 256)
                value = dot_nn(mem[rows, :], wx[which, :, at])
                kv[which, rows, at] = value.astype(bf16)
            return carry
        lax.fori_loop(0, 2, memory_kv, 0)
        attend_forward(bs, gr.at[6], kv.at[0], kv.at[1], lens[:2], 4096, 20, obuf)

        def cross_out(at):
            acc[rows, at] = dot_nn(obuf[rows, :], wsecond[:, at])
        by_tiles(cross_out)
        norm_forward(bs, grad, u_cross, 21, 3, 22, hlow, hw)
        transposed(7, bs, obuf)

    def cross_branch():
        norm_backward(both, u_cross, grad, 3, 22, hw, gr.at[5])

        def cross_up(at):
            obuf[:, at] = dot_nt(gr[5], wsecond[at, :]).astype(bf16)
        by_tiles(cross_up)

    def cross_backward(bs):
        rows = at_rows(bs)
        attend_backward(bs, gr.at[6], kv.at[0], kv.at[1], lens[:2], 4096)

        def memory_half(h, carry):
            at = cols(h, half)
            gmem[rows, at] = (dot_nt(kv[0, rows, :], wx[0, at, :]) + dot_nt(kv[1, rows, :], wx[1, at, :])).astype(bf16)
            gm_part(bs[0], h).start()
            return carry
        lax.fori_loop(0, 2, memory_half, 0)

    def cross_input(at):
        grad[:, at] = hw[:, at] + dot_nt(gr[6], wfirst[at, :])

    def lanes_of(h):
        return pl.ds(0, width) if h is None else cols(h, half)

    def unit(i, h):
        return i if h is None else 15 + 2 * (i - 12) + h

    def sems(i, stage, h):
        return sem_send.at[unit(i, h), stage], sem_recv.at[unit(i, h), stage]

    def first_copy(i, z_first, h):
        at = lanes_of(h)
        return remote(one_send.at[i % SEND_SLOTS, :, :, :, at], one_recv.at[i, :, :, :, at], *sems(i, 0, h),
                      near_id if z_first else y_id)

    def second_copy(i, z_first, h):
        at = lanes_of(h)
        source = one_recv.at[i, 1 - zh, :, :, at] if z_first else one_recv.at[i, :, 1 - zl, :, at]
        return remote(source, two_recv.at[i, :, :, at], *sems(i, 1, h), far_id if z_first else near_id)

    def third_copy(i, z_first, h):
        at = lanes_of(h)
        source = two_recv.at[i, 1 - y if z_first else 1 - zh, :, at]
        return remote(source, out_part.at[i, :, at], *sems(i, 2, h), y_id if z_first else far_id)

    def own_copy(i, z_first, h):
        at = lanes_of(h)
        return pltpu.make_async_copy(two_recv.at[i, y if z_first else zh, :, at], out_own.at[i, :, at], own_sem.at[unit(i, h)])

    def product(left, slot, z_first, other, at):
        if z_first:
            zz = 1 - zl if other else zl
            mine, theirs = lt[left, :, zz, :, c], ltp[left, :, zz]
        else:
            yy = 1 - y if other else y
            mine, theirs = lt[left, :, :, yy, c], ltp[left, :, :, yy]
        shape = (4 * PIECE, ROWS)
        return dot_nn(mine.reshape(shape), gr[slot, :, at]) + dot_nn(theirs.reshape(shape), grp[slot, :, at])

    def piece_tiles(h, fn):
        if h is None:
            loop(0, tiles, lambda t: fn(cols(t, 256), 256))
        else:
            fn(cols(h, half), half)

    def send_piece(i, left, slot, z_first=False, h=None):
        def tile(at, n):
            one_send[i % SEND_SLOTS, :, :, :, at] = product(left, slot, z_first, True, at).astype(bf16).reshape(2, 2, PIECE, n)
        piece_tiles(h, tile)
        first_copy(i, z_first, h).start()

    def keep_piece(i, left, slot, z_first=False, h=None):
        first_copy(i, z_first, h).wait()

        def tile(at, n):
            total = one_recv[i, :, :, :, at].reshape(4 * PIECE, n).astype(f32) + product(left, slot, z_first, False, at)
            one_recv[i, :, :, :, at] = total.astype(bf16).reshape(2, 2, PIECE, n)
        piece_tiles(h, tile)
        second_copy(i, z_first, h).start()

    def merge_piece(i, z_first=False, h=None):
        second_copy(i, z_first, h).wait()
        at = lanes_of(h)
        for k in range(2):
            mine = one_recv[i, zh, k, :, at] if z_first else one_recv[i, k, zl, :, at]
            two_recv[i, k, :, at] = (two_recv[i, k, :, at].astype(f32) + mine.astype(f32)).astype(bf16)

    def pass_piece(i, z_first=False, h=None):
        merge_piece(i, z_first, h)
        third_copy(i, z_first, h).start()
        own_copy(i, z_first, h).start()

    extra = PIECES
    extra_part = remote(two_recv.at[extra, 1 - zh], out_part.at[13], sem_send.at[extra, 2], sem_recv.at[13, 2], over_id)
    extra_own = remote(two_recv.at[extra, zh], out_own.at[13], sem_send.at[13, 0], sem_recv.at[13, 0], x_id)
    extra_left = remote(lt.at[0, :, :, :, 1 - c], ltp.at[0], lt_send.at[0], lt_recv.at[0], core_id)
    extra_right = remote(gr.at[0], grp.at[0], gr_send.at[0], gr_recv.at[0], core_id)

    def loop(lo, hi, fn):
        def step(i, carry):
            fn(i)
            return carry
        lax.fori_loop(lo, hi, step, 0)

    def wait_active():
        for i in range(4):
            lt_copy[i].wait()
        gr_first[0].wait()
        gr_first[1].wait()

    @pl.when(is_enc)
    def _():
        again = loads[1]
        again.start()
        for bs in (long, short):
            self_project(bs, bs == long)
            if bs == long:
                wx_start()
            attend_forward(bs, q_ref, k_ref, v_ref, own_lens, diagonal, None, obuf)
            if bs == long:
                loads[2].wait()
            self_output(bs)
            ffn_forward(bs, grad, bs == long, bs == long)
            mem_copy[bs[0]].start()
        transposed_active(both)
        for k in range(4):
            lt_copy[k].start()
        again.wait()
        for i, ref in ((4, mem), (5, obuf), (6, hlow), (7, xb)):
            transposed(i, both, ref)
            lt_copy[i].start()
        loads[5].wait()
        loads[6].wait()
        for bs in (short, long):
            for h in range(2):
                gm_part(bs[0], h).wait_recv()
            norm_backward(bs, u_ffn, up, ffn_gain, ffn_at + 1, grad, gr.at[0])
            gr_first[bs[0]].start()
            if bs == short:
                ffn_inner(bs, 0, slots, False)
                ffn_input(bs)
        ffn_inner(long, 0, 1, True)

    @pl.when(is_dec)
    def _():
        self_project(both, True)
        wx_start()
        transposed(4, both, xb)
        lt_copy[4].start()

        def wx_forward(h):
            wx_in[h].wait_recv()
            wx_y[h].start()
            wx_z[h].start()
        attend_forward(both, q_ref, k_ref, v_ref, own_lens, diagonal, None, obuf, 0, 3)
        wx_forward(0)
        attend_forward(both, q_ref, k_ref, v_ref, own_lens, diagonal, None, obuf, 3, 6)
        wx_forward(1)
        loads[2].wait()
        self_output(both)
        wx_forward(2)
        wx_y[0].wait()
        wx_on[0].start()
        loads[5].wait()

        def cross_query(at):
            gr[6, :, at] = (dot_nn(hlow[...], wfirst[:, at]) + vec[pl.ds(19, 1), at]).astype(bf16)
        by_tiles(cross_query)
        wx_forward(3)
        wx_core[0].start()
        transposed(5, both, obuf)
        lt_copy[5].start()
        transposed(8, both, hlow)
        lt_copy[8].start()
        loads[6].wait()
        cot_load.wait()
        wx_y[1].wait()
        wx_on[1].start()
        wx_z[0].wait()
        wx_z[1].wait()
        wx_z[2].wait()
        wx_on[2].start()
        wx_y[2].wait()
        wx_z[3].wait()
        wx_on[3].start()
        wx_y[3].wait()
        wx_core[1].start()
        wx_core[2].start()
        for h in range(chunks):
            wx_on[h].wait()
        wx_core[3].start()
        for k in range(4):
            wx_core[k].wait()
        for bs in (long, short):
            mem_copy[bs[0]].wait_recv()
            cross_forward(bs)
        lt_copy[7].start()
        ffn_forward(both, hw, True, True, True)
        for k in range(4):
            lt_copy[k].start()
        norm_backward(both, u_ffn, up, ffn_gain, ffn_at + 1, grad, gr.at[0])
        gr_first[0].start()
        gr_first[1].start()
        ffn_inner(both, 0, slots, True)
        ffn_input(both)
        cross_branch()
        for bs in (short, long):
            cross_backward(bs)
        transposed(6, both, hlow)
        lt_copy[6].start()

    wait_active()

    def first_sends(k):
        send_piece(2 + k, 2 + k, 0)
        send_piece(k, k, 0, True)
    loop(0, 2, first_sends)

    @pl.when(is_enc)
    def _():
        ffn_inner(long, 1, slots, True)
    lt_copy[6].wait()

    def inner_sends(j):
        remote(gr.at[1 + j], grp.at[1 + j], gr_send.at[1 + j], gr_recv.at[1 + j], core_id).wait()
        send_piece(4 + j, 6, 1 + j)
    loop(0, slots, inner_sends)

    @pl.when(is_enc)
    def _():
        ffn_input(long)

    @pl.when(is_dec)
    def _():
        gr_copy[5].start()
        gr_copy[6].start()
        by_tiles(cross_input)
        col_sum(obuf, 20)
        col_sum(gr.at[6], 19)
        col_sum(gr.at[5], 21)

    rows_copy = pltpu.make_async_copy(xb, out_rows, io_sem.at[0])
    rows_copy.start()

    norm_backward(both, u_self, grad, 2 * st, bias_at + 3, hw, gr.at[7])
    gr_copy[7].start()

    def self_up(at):
        obuf[:, at] = dot_nt(gr[7], wo[at, :]).astype(bf16)
    by_tiles(self_up)

    def keep_and_attend(k, carry):
        keep_piece(2 + k, 2 + k, 0)
        keep_piece(k, k, 0, True)
        attend_backward(both, q_ref, k_ref, v_ref, own_lens, diagonal, k * 3, k * 3 + 3)
        return carry
    lax.fori_loop(0, 2, keep_and_attend, 0)
    for j in range(3):
        gr_copy[8 + j].start()

    @pl.when(is_dec)
    def _():
        gv_copy.start()

    def self_input(at):
        total = hw[:, at]
        for j in range(3):
            total = total + dot_nt(gr[8 + j], wproj[j, at, :])
        hw[:, at] = total
    by_tiles(self_input)
    grad_copy = pltpu.make_async_copy(hw, out_grad, io_sem.at[1])
    grad_copy.start()
    loop(2, 4, pass_piece)
    for i in (4, 5, 7):
        lt_copy[i].wait()

    @pl.when(is_dec)
    def _():
        lt_copy[8].wait()
    for i in range(7, 11):
        gr_copy[i].wait()
    col_sum(gr.at[0], ffn_at)
    loop(0, slots, lambda j: col_sum(gr.at[1 + j], ffn_at - 4 + j))
    col_sum(gr.at[7], bias_at + 2)
    col_sum(gr.at[8], bias_at)
    col_sum(gr.at[10], bias_at + 1)
    own_half = pl.ds(pl.multiple_of(c * half, half), half)
    other_half = pl.ds(pl.multiple_of((1 - c) * half, half), half)
    v_copy = [remote(vg.at[:, other_half] if k == 0 else vbuf.at[2 * k], vbuf.at[2 * k + 1], v_send.at[k], v_recv.at[k], dev)
              for k, dev in enumerate((core_id, y_id, near_id, far_id, x_id))]
    v_last = remote(vboth.at[:, :, own_half], vboth.at[:, :, own_half], v_send.at[5], v_recv.at[5], core_id)
    vbuf[0] = vg[:, own_half]

    @pl.when(is_dec)
    def _():
        transposed(0, both, mem)
        extra_left.start()
        gr[0] = kv[0]
        extra_right.start()

    def v_next(k):
        v_copy[k].wait()
        vbuf[2 * k + 2] = vbuf[2 * k] + vbuf[2 * k + 1]
        v_copy[k + 1].start()
    v_copy[0].start()
    v_next(0)

    def attention_piece(k):
        return 8 + k, 5 - (k + 3) // 4, 7 + k

    def cross_piece(k):
        return 12 + k // 2, 7 + st * (k // 2), 5 + k // 2, False, k % 2

    def middle(k):
        send_piece(*attention_piece(k))
        keep_piece(4 + k, 6, 1 + k)

        @pl.when(k > 0)
        def _():
            pass_piece(3 + k)
    loop(0, 4, middle)

    @pl.when(is_enc)
    def _():
        gv_copy.wait_recv()
        gr_copy[5].start()

    @pl.when(is_dec)
    def _():
        extra_left.wait()
        extra_right.wait()
        send_piece(extra, 0, 0)
        gr_copy[6].wait()
    v_next(1)
    cross_units = 2 + 2 * st

    def later(k):
        keep_piece(*attention_piece(k))

        @pl.when(k == 0)
        def _():
            gr_copy[5].wait()
            loop(0, cross_units, lambda k: send_piece(*cross_piece(k)))
        pass_piece(7 + k)
    loop(0, 4, later)

    @pl.when(is_dec)
    def _():
        keep_piece(extra, 0, 0)
    v_next(2)
    loop(0, 2, lambda i: pass_piece(i, True))

    def ends(k):
        i, left, slot, z_first, h = cross_piece(k)
        keep_piece(i, left, slot, z_first, h)

        @pl.when(k == 0)
        def _():
            pass_piece(11)

        @pl.when(k > 0)
        def _():
            pass_piece(12 + (k - 1) // 2, False, (k + 1) % 2)

        @pl.when(k == 1)
        def _():
            v_next(3)

        @pl.when(is_dec & (k == 1))
        def _():
            merge_piece(extra)
            extra_part.start()
            extra_own.start()
    loop(0, cross_units, ends)
    pass_piece(12 + st, False, 1)
    v_copy[4].wait()
    vboth[st, :, own_half] = vbuf[8]
    vboth[1 - st, :, own_half] = vbuf[9]
    v_last.start()
    v_last.wait()
    vec_copy = pltpu.make_async_copy(vboth, out_vec, io_sem.at[2])
    vec_copy.start()

    def finish(i, z_first=False, h=None):
        third_copy(i, z_first, h).wait()
        own_copy(i, z_first, h).wait()
    loop(0, 2, lambda i: finish(i, True))
    loop(2, 12, finish)
    loop(0, cross_units, lambda k: finish(12 + k // 2, False, k % 2))
    rows_copy.wait()
    grad_copy.wait()
    vec_copy.wait()

    @pl.when(is_enc)
    def _():
        for h in range(chunks):
            wx_in[h].wait_send()
        for h in range(2):
            mem_copy[h].wait_send()
        extra_part.wait_recv()
        extra_own.wait_recv()

    @pl.when(is_dec)
    def _():
        for h in range(2):
            for b in range(2):
                gm_part(b, h).wait_send()
        gv_copy.wait_send()
        extra_part.wait_send()
        extra_own.wait_send()


def last_kernel(width, rows_in, grad_in, own, parts, vec_sum, rows_out, grad_out, *refs):
    outs, (vec_buf, rows_buf, grad_buf, own_buf, part_buf, sums, in_sem, through_sem, out_sem) = refs[:8], refs[8:]
    group = PIECES // 2
    loads = []
    for g in range(2):
        at = pl.ds(g * group, group)
        loads.append((pltpu.make_async_copy(own.at[at], own_buf.at[at], in_sem.at[g, 0]),
                      pltpu.make_async_copy(parts.at[at], part_buf.at[at], in_sem.at[g, 1])))
    vec_load = pltpu.make_async_copy(vec_sum, vec_buf, through_sem.at[2])
    into = [pltpu.make_async_copy(grad_in, grad_buf, through_sem.at[0]), pltpu.make_async_copy(rows_in, rows_buf, through_sem.at[1])]
    for cp in (*loads[0], into[0], *loads[1], into[1], vec_load):
        cp.start()
    stores = []

    def store(src, dst):
        stores.append(pltpu.make_async_copy(src, dst, out_sem.at[len(stores)]))
        stores[-1].start()
    for g in range(2):
        for cp in loads[g]:
            cp.wait()
        for i in range(g * group, (g + 1) * group):
            sums[i] = own_buf[i].astype(f32) + part_buf[i].astype(f32)
            if i < 4:
                store(sums.at[i], outs[0].at[pl.ds(i * PIECE, PIECE), :])
            elif i < 8:
                store(sums.at[i], outs[1].at[:, pl.ds((i - 4) * width, width)])
            elif i == 8:
                store(sums.at[i], outs[4])
            elif i == 11:
                store(sums.at[pl.ds(9, 3)], outs[5])
            elif i > 11:
                store(sums.at[i], outs[i - 10])
        into[g].wait()
        store(rows_buf if g else grad_buf, rows_out if g else grad_out)
    vec_load.wait()
    shift = lax.rem(width - lax.axis_index("dp") * PIECE, width)
    for s, (g0, g1, b0, b1) in enumerate(((0, 2, 0, 10), (2, 5, 10, 24))):
        turned = pltpu.roll(vec_buf[s], shift, 1)
        outs[6][pl.ds(g0, g1 - g0), :] = turned[:g1 - g0, :PIECE]
        outs[7][pl.ds(b0, b1 - b0), :] = turned[3:3 + b1 - b0, :PIECE]
    for cp in stores:
        cp.wait()


def whole_step(lengths, gains, biases, x, cot, wproj, wo, wfirst, wsecond, win, wout):
    width = x.shape[1]
    hidden = win.shape[1]
    half = width // 2
    any_space = pl.BlockSpec(memory_space=pl.ANY)
    vmem = pl.BlockSpec(memory_space=pltpu.VMEM)
    dma = pltpu.SemaphoreType.DMA
    slots = hidden // width
    small = (32, width)
    results = pl.pallas_call(
        functools.partial(step_kernel, width, hidden),
        out_shape=[
            jax.ShapeDtypeStruct((ROWS, width), bf16),
            jax.ShapeDtypeStruct((ROWS, width), f32),
            jax.ShapeDtypeStruct((PIECES, PIECE, width), bf16),
            jax.ShapeDtypeStruct((PIECES, PIECE, width), bf16),
            jax.ShapeDtypeStruct((2, VEC_ROWS, width), f32),
        ],
        in_specs=[pl.BlockSpec(memory_space=pltpu.SMEM), vmem, vmem] + [any_space] * 8,
        out_specs=[any_space] * 5,
        scratch_shapes=[
            pltpu.VMEM(small, f32), pltpu.VMEM((2, hidden), f32),
            pltpu.VMEM(wproj.shape, bf16), pltpu.VMEM(wo.shape, bf16), pltpu.VMEM(wfirst.shape, bf16),
            pltpu.VMEM(wsecond.shape, bf16), pltpu.VMEM(win.shape, bf16), pltpu.VMEM(wout.shape, bf16),
            pltpu.VMEM((2, width, width), bf16),
            pltpu.VMEM((ROWS, width), bf16),
            pltpu.VMEM((ROWS, width), bf16),
            pltpu.VMEM((ROWS, width), bf16),
            pltpu.VMEM((ROWS, width), bf16),
            pltpu.VMEM((ROWS, width), bf16),
            pltpu.VMEM((slots, ROWS, width), bf16),
            pltpu.VMEM((2, ROWS, width), bf16),
            pltpu.VMEM((ROWS, width), f32),
            pltpu.VMEM((ROWS, width), f32),
            pltpu.VMEM((ROWS, width), f32),
            pltpu.VMEM((ROWS, width), f32),
            pltpu.VMEM((ROWS, width), f32),
            pltpu.VMEM((ROWS, width), f32),
            pltpu.VMEM((11, ROWS, width), bf16),
            pltpu.VMEM((11, ROWS, width), bf16),
            pltpu.VMEM((9, 2, 2, 2, 2, PIECE, ROWS), bf16),
            pltpu.VMEM((9, 2, 2, 2, PIECE, ROWS), bf16),
            pltpu.VMEM((SEND_SLOTS, 2, 2, PIECE, width), bf16),
            pltpu.VMEM((PIECES + 1, 2, 2, PIECE, width), bf16),
            pltpu.VMEM((PIECES + 1, 2, PIECE, width), bf16),
            pltpu.VMEM((ROWS, width), bf16),
            pltpu.VMEM((VEC_ROWS, width), f32),
            pltpu.VMEM((10, VEC_ROWS, half), f32),
            pltpu.VMEM((2, VEC_ROWS, width), f32),
            dma((12,)), dma((20,)), dma((20,)), dma((2,)), dma((2,)), dma((4,)), dma((4,)), dma, dma,
            dma((9,)), dma((9,)), dma((12,)), dma((12,)),
            dma((19, 3)), dma((19, 3)), dma((19,)), dma((3,)), dma((6,)), dma((6,)),
        ],
        compiler_params=pltpu.CompilerParams(collective_id=0, has_side_effects=True, vmem_limit_bytes=VMEM_LIMIT),
        name="step",
    )(lengths, gains, biases, x, cot, wproj, wo, wfirst, wsecond, win, wout)
    shapes = [(4 * PIECE, width), (PIECE, hidden), (PIECE, width), (PIECE, width), (PIECE, width), (3, PIECE, width),
              (5, PIECE), (24, PIECE)]
    return pl.pallas_call(
        functools.partial(last_kernel, width),
        out_shape=[jax.ShapeDtypeStruct((ROWS, width), bf16), jax.ShapeDtypeStruct((ROWS, width), f32)]
        + [jax.ShapeDtypeStruct(shape, f32) for shape in shapes],
        in_specs=[any_space] * 5,
        out_specs=[any_space] * 8 + [vmem] * 2,
        scratch_shapes=[
            pltpu.VMEM((2, VEC_ROWS, width), f32), pltpu.VMEM((ROWS, width), bf16), pltpu.VMEM((ROWS, width), f32),
            pltpu.VMEM((PIECES, PIECE, width), bf16), pltpu.VMEM((PIECES, PIECE, width), bf16),
            pltpu.VMEM((PIECES, PIECE, width), f32), dma((2, 2)), dma((3,)), dma((PIECES + 2,)),
        ],
        compiler_params=pltpu.CompilerParams(vmem_limit_bytes=VMEM_LIMIT),
        name="last",
    )(*results)


eps_norm = 1e-05
low_type = jnp.bfloat16
wide_type = jnp.float32


def as_sent(shard):
    return jax.tree.map(lambda a: a.astype(jnp.bfloat16) if a.dtype == jnp.float32 else a, shard)


def shifted(shard, axis, by):
    count = lax.axis_size(axis)
    pairs = [(i, i + by) for i in range(count) if 0 <= i + by < count]
    return lax.ppermute(shard, axis, pairs)


def matmul(left_mat, right_mat):
    return jnp.dot(left_mat, right_mat, preferred_element_type=wide_type)


def matmul_tn(left_mat, right_mat):
    return lax.dot_general(
        left_mat, right_mat, (((0,), (0,)), ((), ())), preferred_element_type=wide_type
    )


def matmul_nt(left_mat, right_mat):
    return lax.dot_general(
        left_mat, right_mat, (((1,), (1,)), ((), ())), preferred_element_type=wide_type
    )


def column_sum(tensor):
    return jnp.sum(tensor.astype(wide_type), axis=0)


def norm_rows(tensor, norm_gain, norm_shift):
    centre = tensor - jnp.mean(tensor, axis=-1, keepdims=True)
    spread = jnp.mean(centre * centre, axis=-1, keepdims=True)
    return centre * lax.rsqrt(spread + eps_norm) * norm_gain + norm_shift


def norm_back(tensor, norm_gain, norm_shift, upstream):
    unused, pullback = jax.vjp(norm_rows, tensor, norm_gain, norm_shift)
    return pullback(upstream)


def gelu_exact(tensor):
    return jax.nn.gelu(tensor, approximate=False)


def key_mask(row_count, key_count, length, causal):
    columns = lax.broadcasted_iota(jnp.int32, (row_count, key_count), 1)
    allowed = columns < length
    if causal:
        allowed = allowed & (columns <= lax.broadcasted_iota(jnp.int32, (row_count, key_count), 0))
    return allowed


def split_heads(tensor):
    return tensor.reshape(tensor.shape[0], -1, HDIM)


def attend_scores(queries, key_rows, allowed):
    scores = jnp.einsum(
        "qhd,khd->hqk",
        split_heads(queries),
        split_heads(key_rows),
        preferred_element_type=wide_type,
    )
    return jnp.where(allowed[None], scores * HDIM ** (-0.5), -1e30)


def attend_forward(queries, key_rows, values, allowed):
    scores = attend_scores(queries, key_rows, allowed)
    row_max = jnp.max(scores, axis=-1, keepdims=True)
    log_total = row_max + jnp.log(jnp.sum(jnp.exp(scores - row_max), axis=-1, keepdims=True))
    softmaxed = jnp.exp(scores - log_total).astype(low_type)
    attended = jnp.einsum(
        "hqk,khd->qhd", softmaxed, split_heads(values), preferred_element_type=wide_type
    )
    return (attended.reshape(queries.shape[0], -1), log_total)


def attend_backward(queries, key_rows, values, allowed, log_total, upstream):
    softmaxed = jnp.exp(attend_scores(queries, key_rows, allowed) - log_total)
    grad_heads = split_heads(upstream)
    grad_values = jnp.einsum(
        "hqk,qhd->khd", softmaxed.astype(low_type), grad_heads, preferred_element_type=wide_type
    )
    grad_probs = jnp.einsum(
        "qhd,khd->hqk", grad_heads, split_heads(values), preferred_element_type=wide_type
    )
    grad_scores = (
        softmaxed * (grad_probs - jnp.sum(softmaxed * grad_probs, axis=-1, keepdims=True))
    ).astype(low_type)
    scale_factor = HDIM ** (-0.5)
    grad_queries = (
        jnp.einsum(
            "hqk,khd->qhd", grad_scores, split_heads(key_rows), preferred_element_type=wide_type
        )
        * scale_factor
    )
    grad_keys = (
        jnp.einsum(
            "hqk,qhd->khd", grad_scores, split_heads(queries), preferred_element_type=wide_type
        )
        * scale_factor
    )
    key_count = key_rows.shape[0]
    return (
        grad_queries.reshape(queries.shape[0], -1),
        grad_keys.reshape(key_count, -1),
        grad_values.reshape(key_count, -1),
    )


def self_forward(row_block, length, causal, w_proj, w_out, vectors):
    bias_q, bias_v, bias_o, norm_gain, norm_shift = vectors
    row_count = row_block.shape[0]
    offsets = jnp.stack([bias_q, jnp.zeros_like(bias_q), bias_v])[:, None, :]
    projected = (
        jnp.einsum("rd,cde->cre", row_block, w_proj, preferred_element_type=wide_type) + offsets
    ).astype(low_type)
    allowed = key_mask(row_count, row_count, length, causal)
    attended, log_total = attend_forward(projected[0], projected[1], projected[2], allowed)
    attended = attended.astype(low_type)
    summed = row_block.astype(wide_type) + matmul(attended, w_out) + bias_o
    return (norm_rows(summed, norm_gain, norm_shift), (projected, log_total, attended, summed))


def self_backward(row_block, length, causal, w_proj, w_out, vectors, saved_fwd, upstream):
    projected, log_total, attended, summed = saved_fwd
    row_count = row_block.shape[0]
    grad_sum, grad_gain, grad_shift = norm_back(summed, vectors[3], vectors[4], upstream)
    grad_branch = grad_sum.astype(low_type)
    grad_attended = matmul_nt(grad_branch, w_out).astype(low_type)
    allowed = key_mask(row_count, row_count, length, causal)
    grad_q, grad_k, grad_v = attend_backward(
        projected[0], projected[1], projected[2], allowed, log_total, grad_attended
    )
    grad_proj = jnp.stack([grad_q, grad_k, grad_v]).astype(low_type)
    grad_rows = grad_sum + jnp.einsum(
        "cre,cde->rd", grad_proj, w_proj, preferred_element_type=wide_type
    )
    weight_grads = (
        jnp.einsum("rd,cre->cde", row_block, grad_proj, preferred_element_type=wide_type),
        matmul_tn(attended, grad_branch),
    )
    vector_grads = (
        column_sum(grad_proj[0]),
        column_sum(grad_proj[2]),
        column_sum(grad_branch),
        grad_gain,
        grad_shift,
    )
    return (grad_rows, weight_grads, vector_grads)


def ffn_forward(hidden, w_in, w_out, vectors):
    bias_in, bias_out, norm_gain, norm_shift = vectors
    low_hidden = hidden.astype(low_type)
    inner_act = matmul(low_hidden, w_in) + bias_in
    active = gelu_exact(inner_act).astype(low_type)
    summed = hidden + matmul(active, w_out) + bias_out
    return (norm_rows(summed, norm_gain, norm_shift), (low_hidden, inner_act, active, summed))


def ffn_backward(w_in, w_out, vectors, saved_fwd, upstream):
    low_hidden, inner_act, active, summed = saved_fwd
    grad_sum, grad_gain, grad_shift = norm_back(summed, vectors[2], vectors[3], upstream)
    grad_branch = grad_sum.astype(low_type)
    unused, pullback = jax.vjp(gelu_exact, inner_act)
    grad_inner = pullback(matmul_nt(grad_branch, w_out))[0].astype(low_type)
    grad_hidden = grad_sum + matmul_nt(grad_inner, w_in)
    weight_grads = (matmul_tn(low_hidden, grad_inner), matmul_tn(active, grad_branch))
    vector_grads = (column_sum(grad_inner), column_sum(grad_branch), grad_gain, grad_shift)
    return (grad_hidden, weight_grads, vector_grads)


def cross_forward(hidden, memory, src_len, w_query, w_out, vectors):
    bias_q, bias_v, bias_o, norm_gain, norm_shift = vectors
    low_hidden = hidden.astype(low_type)
    queries = (matmul(low_hidden, w_query) + bias_q).astype(low_type)
    allowed = key_mask(hidden.shape[0], memory.shape[1], src_len, False)
    attended, log_total = attend_forward(queries, memory[0], memory[1], allowed)
    attended = (attended + bias_v).astype(low_type)
    summed = hidden + matmul(attended, w_out) + bias_o
    return (
        norm_rows(summed, norm_gain, norm_shift),
        (low_hidden, queries, log_total, attended, summed),
    )


def cross_backward(memory, src_len, w_query, w_out, vectors, saved_fwd, upstream):
    low_hidden, queries, log_total, attended, summed = saved_fwd
    grad_sum, grad_gain, grad_shift = norm_back(summed, vectors[3], vectors[4], upstream)
    grad_branch = grad_sum.astype(low_type)
    grad_attended = matmul_nt(grad_branch, w_out).astype(low_type)
    allowed = key_mask(queries.shape[0], memory.shape[1], src_len, False)
    grad_q, grad_k, grad_v = attend_backward(
        queries, memory[0], memory[1], allowed, log_total, grad_attended
    )
    grad_query = grad_q.astype(low_type)
    grad_memory = jnp.stack([grad_k, grad_v]).astype(low_type)
    grad_hidden = grad_sum + matmul_nt(grad_query, w_query)
    weight_grads = (matmul_tn(low_hidden, grad_query), matmul_tn(attended, grad_branch))
    vector_grads = (
        column_sum(grad_query),
        column_sum(grad_attended),
        column_sum(grad_branch),
        grad_gain,
        grad_shift,
    )
    return (grad_hidden, grad_memory, weight_grads, vector_grads)


def self_vectors(gain_rows, bias_rows, decoder):
    base_row = 10 if decoder else 0
    gain_row = 2 if decoder else 0
    return (
        bias_rows[base_row],
        bias_rows[base_row + 1],
        bias_rows[base_row + 2],
        gain_rows[gain_row],
        bias_rows[base_row + 3],
    )


def ffn_vectors(gain_rows, bias_rows, decoder):
    base_row = 18 if decoder else 4
    gain_row = 4 if decoder else 1
    return (
        bias_rows[base_row : base_row + 4].reshape(-1),
        bias_rows[base_row + 4],
        gain_rows[gain_row],
        bias_rows[base_row + 5],
    )


def cross_vectors(gain_rows, bias_rows):
    return (bias_rows[14], bias_rows[15], bias_rows[16], gain_rows[3], bias_rows[17])


def self_plan(decoder, vector_grads):
    base_row = 10 if decoder else 0
    gain_row = 2 if decoder else 0
    return (
        ("biases", base_row, vector_grads[0]),
        ("biases", base_row + 1, vector_grads[1]),
        ("biases", base_row + 2, vector_grads[2]),
        ("gains", gain_row, vector_grads[3]),
        ("biases", base_row + 3, vector_grads[4]),
    )


def ffn_plan(decoder, vector_grads):
    base_row = 18 if decoder else 4
    gain_row = 4 if decoder else 1
    return (
        ("biases", base_row, vector_grads[0]),
        ("biases", base_row + 4, vector_grads[1]),
        ("gains", gain_row, vector_grads[2]),
        ("biases", base_row + 5, vector_grads[3]),
    )


def cross_plan(vector_grads):
    return (
        ("biases", 14, vector_grads[0]),
        ("biases", 15, vector_grads[1]),
        ("biases", 16, vector_grads[2]),
        ("gains", 3, vector_grads[3]),
        ("biases", 17, vector_grads[4]),
    )


def accumulate(totals, weight_names, weight_grads, vector_plan):
    merged = dict(totals)
    for key_name, tensor in zip(weight_names, weight_grads):
        merged[key_name] = merged[key_name] + tensor
    for table_name, row_at, tensor in vector_plan:
        table_now = merged[table_name]
        row_block = tensor.reshape(-1, table_now.shape[1])
        merged[table_name] = table_now.at[row_at : row_at + row_block.shape[0]].add(row_block)
    return merged


def updated(progress, key_name, position, tensor):
    copied = dict(progress)
    copied[key_name] = [
        tensor if slot_index == position else entry_now
        for slot_index, entry_now in enumerate(progress[key_name])
    ]
    return copied


def with_totals(progress, totals):
    copied = dict(progress)
    copied["totals"] = totals
    return copied


def forward_pass(tensor):
    return jax.tree.map(
        lambda part, own: part.astype(own.dtype), shifted(as_sent(tensor), "stream", 1), tensor
    )


def backward_pass(tensor):
    return jax.tree.map(
        lambda part, own: part.astype(own.dtype), shifted(as_sent(tensor), "stream", -1), tensor
    )


def keep_same(progress):
    return progress


def plain_body(
    inputs,
    lengths,
    cotangent,
    attn_in,
    attn_out,
    cross_first,
    cross_second,
    ffn_in,
    ffn_out,
    gains,
    biases,
):
    own_rows = inputs[0]
    model_width = own_rows.shape[1]
    hidden_width = ffn_in.shape[2]
    head_count = model_width // HDIM
    row_sizes = (SHORT, LONG)
    bucket_spans = ((0, SHORT), (SHORT, SHORT + LONG))
    row_pieces = [own_rows[start_row:stop_row] for start_row, stop_row in bucket_spans]
    grad_pieces = [
        cotangent[start_row:stop_row].astype(wide_type) for start_row, stop_row in bucket_spans
    ]
    src_lens = [lengths[0, 0, bucket_idx] for bucket_idx in range(2)]
    tgt_lens = [lengths[1, 0, bucket_idx] for bucket_idx in range(2)]
    w_proj = attn_in[0]
    w_attn_out = attn_out[0]
    w_first = cross_first[0]
    w_second = cross_second[0]
    w_ffn_in = ffn_in[0]
    w_ffn_out = ffn_out[0]
    gain_rows = gains.astype(wide_type)
    bias_rows = biases.astype(wide_type)
    enc_self = self_vectors(gain_rows, bias_rows, False)
    enc_ffn = ffn_vectors(gain_rows, bias_rows, False)
    dec_self = self_vectors(gain_rows, bias_rows, True)
    dec_ffn = ffn_vectors(gain_rows, bias_rows, True)
    dec_cross = cross_vectors(gain_rows, bias_rows)
    is_decoder = lax.axis_index("stream") == 1

    def blank_self(size_rows):
        return (
            jnp.zeros((3, size_rows, model_width), low_type),
            jnp.zeros((head_count, size_rows, 1), wide_type),
            jnp.zeros((size_rows, model_width), low_type),
            jnp.zeros((size_rows, model_width), wide_type),
        )

    def blank_ffn(size_rows):
        return (
            jnp.zeros((size_rows, model_width), low_type),
            jnp.zeros((size_rows, hidden_width), wide_type),
            jnp.zeros((size_rows, hidden_width), low_type),
            jnp.zeros((size_rows, model_width), wide_type),
        )

    def blank_cross(size_rows):
        return (
            jnp.zeros((size_rows, model_width), low_type),
            jnp.zeros((size_rows, model_width), low_type),
            jnp.zeros((head_count, size_rows, 1), wide_type),
            jnp.zeros((size_rows, model_width), low_type),
            jnp.zeros((size_rows, model_width), wide_type),
        )

    progress = {
        "out": [jnp.zeros((size_rows, model_width), low_type) for size_rows in row_sizes],
        "grad_in": [jnp.zeros((size_rows, model_width), wide_type) for size_rows in row_sizes],
        "send": [jnp.zeros((2, size_rows, model_width), low_type) for size_rows in row_sizes],
        "memory": [jnp.zeros((2, size_rows, model_width), low_type) for size_rows in row_sizes],
        "grad_send": [jnp.zeros((2, size_rows, model_width), low_type) for size_rows in row_sizes],
        "grad_memory": [
            jnp.zeros((2, size_rows, model_width), low_type) for size_rows in row_sizes
        ],
        "mid": [jnp.zeros((size_rows, model_width), wide_type) for size_rows in row_sizes],
        "grad_mid": [jnp.zeros((size_rows, model_width), wide_type) for size_rows in row_sizes],
        "totals": {
            "proj": jnp.zeros(w_proj.shape, wide_type),
            "attn_out": jnp.zeros(w_attn_out.shape, wide_type),
            "first": jnp.zeros(w_first.shape, wide_type),
            "second": jnp.zeros(w_second.shape, wide_type),
            "ffn_in": jnp.zeros(w_ffn_in.shape, wide_type),
            "ffn_out": jnp.zeros(w_ffn_out.shape, wide_type),
            "gains": jnp.zeros(gains.shape, wide_type),
            "biases": jnp.zeros(biases.shape, wide_type),
        },
    }
    progress["self_saved"] = [blank_self(size_rows) for size_rows in row_sizes]
    progress["ffn_saved"] = [blank_ffn(size_rows) for size_rows in row_sizes]
    progress["cross_saved"] = [blank_cross(size_rows) for size_rows in row_sizes]

    def encoder_core(micro_idx):
        h_one, self_saved = self_forward(
            row_pieces[micro_idx], src_lens[micro_idx], False, w_proj, w_attn_out, enc_self
        )
        encoded, ffn_saved = ffn_forward(h_one, w_ffn_in, w_ffn_out, enc_ffn)
        return (encoded.astype(low_type), self_saved, ffn_saved)

    def encoder_forward_step(progress, micro_idx):
        low_memory, self_saved, ffn_saved = encoder_core(micro_idx)
        memory = jnp.stack([matmul(low_memory, w_first), matmul(low_memory, w_second)]).astype(
            low_type
        )
        progress = updated(progress, "out", micro_idx, low_memory)
        progress = updated(progress, "send", micro_idx, memory)
        progress = updated(progress, "self_saved", micro_idx, self_saved)
        progress = updated(progress, "ffn_saved", micro_idx, ffn_saved)
        return progress

    def decoder_head(micro_idx):
        return self_forward(
            row_pieces[micro_idx], tgt_lens[micro_idx], True, w_proj, w_attn_out, dec_self
        )

    def decoder_tail(mid_rows, memory, micro_idx):
        crossed, cross_saved = cross_forward(
            mid_rows, memory, src_lens[micro_idx], w_first, w_second, dec_cross
        )
        decoded, ffn_saved = ffn_forward(crossed, w_ffn_in, w_ffn_out, dec_ffn)
        return (decoded, cross_saved, ffn_saved)

    def decoder_head_step(progress, micro_idx):
        mid_rows, self_saved = decoder_head(micro_idx)
        progress = updated(progress, "mid", micro_idx, mid_rows)
        progress = updated(progress, "self_saved", micro_idx, self_saved)
        return progress

    def decoder_tail_step(progress, micro_idx):
        decoded, cross_saved, ffn_saved = decoder_tail(
            progress["mid"][micro_idx], progress["memory"][micro_idx], micro_idx
        )
        progress = updated(progress, "out", micro_idx, decoded.astype(low_type))
        progress = updated(progress, "cross_saved", micro_idx, cross_saved)
        progress = updated(progress, "ffn_saved", micro_idx, ffn_saved)
        return progress

    def decoder_back_step(progress, micro_idx):
        memory = progress["memory"][micro_idx]
        self_saved = progress["self_saved"][micro_idx]
        cross_saved = progress["cross_saved"][micro_idx]
        ffn_saved = progress["ffn_saved"][micro_idx]
        grad_h_two, ffn_w, ffn_v = ffn_backward(
            w_ffn_in, w_ffn_out, dec_ffn, ffn_saved, grad_pieces[micro_idx]
        )
        grad_h_one, grad_memory, cross_w, cross_v = cross_backward(
            memory, src_lens[micro_idx], w_first, w_second, dec_cross, cross_saved, grad_h_two
        )
        grad_rows, self_w, self_v = self_backward(
            row_pieces[micro_idx],
            tgt_lens[micro_idx],
            True,
            w_proj,
            w_attn_out,
            dec_self,
            self_saved,
            grad_h_one,
        )
        totals = accumulate(
            progress["totals"],
            ("ffn_in", "ffn_out", "first", "second", "proj", "attn_out"),
            ffn_w + cross_w + self_w,
            ffn_plan(True, ffn_v) + cross_plan(cross_v) + self_plan(True, self_v),
        )
        progress = updated(progress, "grad_in", micro_idx, grad_rows)
        progress = updated(progress, "grad_send", micro_idx, grad_memory)
        return with_totals(progress, totals)

    def encoder_top_step(progress, micro_idx):
        low_memory = progress["out"][micro_idx]
        ffn_saved = progress["ffn_saved"][micro_idx]
        grad_memory = progress["grad_memory"][micro_idx]
        grad_encoded = matmul_nt(grad_memory[0], w_first) + matmul_nt(grad_memory[1], w_second)
        grad_h_one, ffn_w, ffn_v = ffn_backward(
            w_ffn_in, w_ffn_out, enc_ffn, ffn_saved, grad_encoded
        )
        projections = (matmul_tn(low_memory, grad_memory[0]), matmul_tn(low_memory, grad_memory[1]))
        totals = accumulate(
            progress["totals"],
            ("first", "second", "ffn_in", "ffn_out"),
            projections + ffn_w,
            ffn_plan(False, ffn_v),
        )
        progress = updated(progress, "grad_mid", micro_idx, grad_h_one)
        return with_totals(progress, totals)

    def encoder_bottom_step(progress, micro_idx):
        self_saved = progress["self_saved"][micro_idx]
        grad_rows, self_w, self_v = self_backward(
            row_pieces[micro_idx],
            src_lens[micro_idx],
            False,
            w_proj,
            w_attn_out,
            enc_self,
            self_saved,
            progress["grad_mid"][micro_idx],
        )
        totals = accumulate(
            progress["totals"], ("proj", "attn_out"), self_w, self_plan(False, self_v)
        )
        progress = updated(progress, "grad_in", micro_idx, grad_rows)
        return with_totals(progress, totals)

    def enc_zero(progress):
        return encoder_forward_step(progress, 0)

    def dec_zero(progress):
        return decoder_head_step(progress, 0)

    def enc_one(progress):
        return encoder_forward_step(progress, 1)

    def dec_one(progress):
        return decoder_tail_step(decoder_head_step(progress, 1), 0)

    def dec_two(progress):
        return decoder_back_step(decoder_tail_step(progress, 1), 1)

    def enc_three(progress):
        return encoder_bottom_step(encoder_top_step(progress, 1), 1)

    def dec_three(progress):
        return decoder_back_step(progress, 0)

    def enc_four(progress):
        return encoder_top_step(progress, 0)

    def enc_five(progress):
        return encoder_bottom_step(progress, 0)

    progress = lax.cond(is_decoder, dec_zero, enc_zero, progress)
    progress = updated(progress, "memory", 0, forward_pass(progress["send"][0]))
    progress = lax.cond(is_decoder, dec_one, enc_one, progress)
    progress = updated(progress, "memory", 1, forward_pass(progress["send"][1]))
    progress = lax.cond(is_decoder, dec_two, keep_same, progress)
    progress = updated(progress, "grad_memory", 1, backward_pass(progress["grad_send"][1]))
    progress = lax.cond(is_decoder, dec_three, enc_three, progress)
    progress = updated(progress, "grad_memory", 0, backward_pass(progress["grad_send"][0]))
    progress = lax.cond(is_decoder, keep_same, enc_four, progress)
    progress = lax.cond(is_decoder, keep_same, enc_five, progress)
    totals = progress["totals"]
    owned = (
        lax.psum_scatter(totals["proj"], "dp", scatter_dimension=1, tiled=True),
        lax.psum_scatter(totals["attn_out"], "dp", scatter_dimension=0, tiled=True),
        lax.psum_scatter(totals["first"], "dp", scatter_dimension=0, tiled=True),
        lax.psum_scatter(totals["second"], "dp", scatter_dimension=0, tiled=True),
        lax.psum_scatter(totals["ffn_in"], "dp", scatter_dimension=0, tiled=True),
        lax.psum_scatter(totals["ffn_out"], "dp", scatter_dimension=0, tiled=True),
        lax.psum_scatter(totals["gains"], "dp", scatter_dimension=1, tiled=True),
        lax.psum_scatter(totals["biases"], "dp", scatter_dimension=1, tiled=True),
    )
    owned_gains, owned_biases = lax.psum((owned[6], owned[7]), "stream")
    layer_out = jnp.concatenate(progress["out"], axis=0)[None]
    grad_inputs = jnp.concatenate(progress["grad_in"], axis=0)[None]
    return (
        layer_out,
        grad_inputs,
        owned[0][None],
        owned[1][None],
        owned[2][None],
        owned[3][None],
        owned[4][None],
        owned[5][None],
        owned_gains,
        owned_biases,
    )


def fused_body(inputs, lengths, cotangent, attn_in, attn_out, cross_first, cross_second, ffn_in, ffn_out, gains, biases):
    rows, grad, s_out, s_in, s_second, s_first, s_attn, s_proj, own_gains, own_biases = whole_step(
        lengths, gains, biases, inputs[0], cotangent, attn_in[0], attn_out[0],
        cross_first[0], cross_second[0], ffn_in[0], ffn_out[0])
    return (rows[None], grad[None], s_proj[None], s_attn[None], s_first[None], s_second[None],
            s_in[None], s_out[None], own_gains, own_biases)


def solution(mesh):
    def body(*args):
        width = args[0].shape[2]
        fits = mesh.shape["dp"] * PIECE == width and args[0].shape[1] == ROWS and args[7].shape[2] == 4 * width
        return (fused_body if fits else plain_body)(*args)
    return jax.shard_map(
        body,
        mesh=mesh,
        in_specs=(
            P("stream", "dp", None),
            P(None, "dp", None),
            P("dp", None),
            P("stream", None, None, None),
            P("stream", None, None),
            P("stream", None, None),
            P("stream", None, None),
            P("stream", None, None),
            P("stream", None, None),
            P(),
            P(),
        ),
        out_specs=(
            P("stream", "dp", None),
            P("stream", "dp", None),
            P("stream", None, "dp", None),
            P("stream", "dp", None),
            P("stream", "dp", None),
            P("stream", "dp", None),
            P("stream", "dp", None),
            P("stream", "dp", None),
            P(None, "dp"),
            P(None, "dp"),
        ),
        check_vma=False,
    )
```

```python
import functools

import jax
import jax.numpy as jnp
from jax import lax
from jax.experimental import pallas as pl
from jax.experimental.pallas import tpu as pltpu
from jax.sharding import PartitionSpec as P

HDIM = 64
SHORT = 128
LONG = 256
ROWS = SHORT + LONG
PIECE = 48
PIECES = 14
VEC_ROWS = 24
SEND_SLOTS = 8
MESH = pl.DeviceIdType.MESH
bf16, f32 = jnp.bfloat16, jnp.float32
VMEM_LIMIT = 64 << 20


def dot_nn(a, b):
    return jnp.dot(a, b, preferred_element_type=f32)


def dot_nt(a, b):
    return lax.dot_general(a, b, (((1,), (1,)), ((), ())), preferred_element_type=f32)


def dot_tn(a, b):
    return lax.dot_general(a, b, (((0,), (0,)), ((), ())), preferred_element_type=f32)


def cols(j, width):
    return pl.ds(pl.multiple_of(j * width, width), width)


def step_kernel(
    width, hidden,
    lengths, gains, biases, x_hbm, cot_hbm, wproj_hbm, wo_hbm, wfirst_hbm, wsecond_hbm, win_hbm, wout_hbm,
    out_rows, out_grad, out_own, out_part, out_vec,
    vec, bias_in, wproj, wo, wfirst, wsecond, win, wout, wx,
    xb, up, mem, obuf, hlow, dg, kv, acc, grad, hw, u_self, u_cross, u_ffn, gr, grp, lt, ltp, one_send, one_recv, two_recv, gmem, vg, vbuf, vboth,
    load_sem, wx_send, wx_recv, mem_send, mem_recv, gm_send, gm_recv, gv_send, gv_recv, lt_send, lt_recv, gr_send, gr_recv,
    sem_send, sem_recv, own_sem, io_sem, v_send, v_recv,
):
    st = lax.axis_index("stream")
    me = lax.axis_index("dp")
    z, y, c = me // 4, (me // 2) % 2, me % 2
    is_dec = st == 1
    is_enc = st == 0
    core_id = {"dp": z * 4 + y * 2 + (1 - c)}
    y_id = {"dp": z * 4 + (1 - y) * 2 + c}
    x_id = {"stream": 1 - st}
    tiles = width // 256
    slots = hidden // width

    zh, zl = z // 2, z % 2

    def z_id(other):
        return {"dp": other * 4 + y * 2 + c}
    near_id = z_id(zh * 2 + 1 - zl)
    far_id = z_id((1 - zh) * 2 + zl)
    over_id = {"stream": 1 - st, **far_id}

    def remote(src, dst, ss, rs, dev):
        return pltpu.make_async_remote_copy(
            src_ref=src, dst_ref=dst, send_sem=ss, recv_sem=rs, device_id=dev, device_id_type=MESH)

    loads = [
        pltpu.make_async_copy(src, dst, load_sem.at[i])
        for i, (src, dst) in enumerate((
            (x_hbm, xb), (x_hbm, mem), (wo_hbm, wo), (win_hbm, win), (wout_hbm, wout),
            (wfirst_hbm, wfirst), (wsecond_hbm, wsecond)))
    ]
    cot_load = pltpu.make_async_copy(cot_hbm, up, load_sem.at[7])
    def proj_load(which):
        return pltpu.make_async_copy(wproj_hbm.at[which], wproj.at[which], load_sem.at[9 + which])
    loads[0].start()
    for which in range(3):
        proj_load(which).start()

    barrier = pltpu.get_barrier_semaphore()
    peers = [core_id, y_id, x_id, near_id, far_id, over_id]
    for p in peers:
        pl.semaphore_signal(barrier, inc=1, device_id=p, device_id_type=MESH)

    lens = [lengths[i // 2, 0, i % 2] for i in range(4)]
    own_lens = [jnp.where(is_dec, lens[2 + i], lens[i]) for i in range(2)]
    vec[pl.ds(0, 5), :] = gains[...].astype(f32)
    vec[pl.ds(5, 24), :] = biases[...].astype(f32)
    for i in range(slots):
        for s in range(2):
            bias_in[pl.ds(s, 1), pl.ds(i * width, width)] = vec[pl.ds(9 + 14 * s + i, 1), :]
    vg[...] = jnp.zeros_like(vg)
    half = width // 2
    chunks = width // 4 // PIECE

    def wx_block(yy, zz, cc, h):
        return wx.at[yy, pl.ds((zz * 2 + cc) * chunks * PIECE + h * PIECE, PIECE)]

    def wx_copy(src, dst, k, dev):
        return remote(src, dst, wx_send.at[k], wx_recv.at[k], dev)

    def wx_from(source, h):
        return wx_copy(source.at[pl.ds((zl * 2 + c) * chunks * PIECE + h * PIECE, PIECE)], wx_block(y, zl, c, h), h, x_id)
    wx_in = [wx_from(wfirst_hbm, h) for h in range(chunks)]
    wx_y = [wx_copy(wx_block(y, zl, c, h), wx_block(y, zl, c, h), chunks + h, y_id) for h in range(chunks)]
    wx_z = [wx_copy(wx_block(y, zl, c, h), wx_block(y, zl, c, h), 2 * chunks + h, near_id) for h in range(chunks)]
    wx_on = [wx_copy(wx_block(1 - y, zl, c, h), wx_block(1 - y, zl, c, h), 3 * chunks + h, near_id) if h < chunks // 2 else
             wx_copy(wx_block(y, 1 - zl, c, h), wx_block(y, 1 - zl, c, h), 3 * chunks + h, y_id) for h in range(chunks)]

    def wx_whole(yy, zz):
        return wx.at[yy, pl.ds((zz * 2 + c) * chunks * PIECE, chunks * PIECE)]
    wx_core = [wx_copy(wx_whole(yy, zz), wx_whole(yy, zz), 4 * chunks + k, core_id)
               for k, (yy, zz) in enumerate(((y, zl), (1 - y, zl), (y, 1 - zl), (1 - y, 1 - zl)))]

    def wx_start():
        pl.semaphore_wait(barrier, len(peers))

        @pl.when(is_enc & (y == 0))
        def _():
            for h in range(chunks):
                wx_in[h].start()

        @pl.when(is_enc & (y == 1))
        def _():
            for h in range(chunks):
                wx_from(wsecond_hbm, h).start()
    for cp in loads[2:]:
        cp.start()
    loads[0].wait()

    @pl.when(is_dec)
    def _():
        cot_load.start()

    gain_row = lambda r: pl.ds(r - 2 * st, 1)
    bias_row_of = lambda r: pl.ds(r - 2 - 10 * st, 1)
    lt_copy = [remote(lt.at[i, :, :, :, 1 - c], ltp.at[i], lt_send.at[i], lt_recv.at[i], core_id) for i in range(9)]
    gr_copy = {i: remote(gr.at[i], grp.at[i], gr_send.at[i], gr_recv.at[i], core_id) for i in range(5, 11)}
    buckets = ((0, SHORT), (SHORT, LONG))
    short, long, both = (0,), (1,), (0, 1)

    def span(bs):
        return buckets[bs[0]][0], sum(buckets[b][1] for b in bs)

    def at_rows(bs):
        return pl.ds(*span(bs))
    mem_copy = [remote(xb.at[at_rows((b,))], mem.at[at_rows((b,))], mem_send.at[b], mem_recv.at[b], x_id) for b in range(2)]

    def gm_part(b, h):
        at = cols(h, half)
        return remote(gmem.at[at_rows((b,)), at], up.at[at_rows((b,)), at], gm_send.at[2 * b + h], gm_recv.at[2 * b + h], x_id)
    gv_copy = remote(kv.at[1], gr.at[5], gv_send, gv_recv, x_id)

    gr_first = [remote(gr.at[0, at_rows((b,))], grp.at[0, at_rows((b,))], gr_send.at[11 * b], gr_recv.at[11 * b], core_id)
                for b in range(2)]

    def row_loop(bs, block, body, unroll=1):
        r0, n = span(bs)

        def step(i, carry):
            body(pl.ds(pl.multiple_of(r0 + i * block, block), block))
            return carry
        lax.fori_loop(0, n // block, step, 0, unroll=unroll)

    def vrow(r):
        return vec[pl.ds(r, 1), :]

    def transposed(i, bs, ref):
        r0, n = span(bs)
        lt[i, :, :, :, :, :, pl.ds(r0, n)] = ref[pl.ds(r0, n), :].T.reshape(2, 2, 2, 2, PIECE, n)

    def transposed_slot(bs, j):
        r0, n = span(bs)
        turned = gr[1 + j, pl.ds(r0, n), :].T.reshape(2, 2, 4, PIECE, n)
        for k in range(4):
            lt[k, j // 2, j % 2, :, :, :, pl.ds(r0, n)] = turned[:, :, k]

    def transposed_active(bs):

        def step(j, carry):
            transposed_slot(bs, j)
            return carry
        lax.fori_loop(0, slots, step, 0)

    def col_sum(slot, row):
        def step(i, carry):
            block = slot[pl.ds(pl.multiple_of(i * 64, 64), 64), :].astype(f32)
            return carry + jnp.sum(block.reshape(8, 8, width), axis=0)
        total = lax.fori_loop(0, ROWS // 64, step, jnp.zeros((8, width), f32))
        vg[bias_row_of(row), :] = jnp.sum(total, axis=0, keepdims=True)

    def norm_forward(bs, residual, sum_ref, add_bias, gain, shift, out_low, out_wide):
        def body(rows):
            u = residual[rows, :].astype(f32) + acc[rows, :] + vrow(add_bias)
            sum_ref[rows, :] = u
            centre = u - jnp.mean(u, axis=-1, keepdims=True)
            spread = jnp.mean(centre * centre, axis=-1, keepdims=True)
            h = centre * lax.rsqrt(spread + 1e-05) * vrow(gain) + vrow(shift)
            if out_wide is not None:
                out_wide[rows, :] = h
            out_low[rows, :] = h.astype(bf16)
        row_loop(bs, 32, body, 4)

    def norm_backward(bs, sum_ref, source, gain, shift, out_wide, slot, again=None):
        r0, n = span(bs)

        def step(i, carry):
            rows = pl.ds(pl.multiple_of(r0 + i * 32, 32), 32)
            r = source[rows, :].astype(f32)
            u = sum_ref[rows, :]
            centre = u - jnp.mean(u, axis=-1, keepdims=True)
            spread = jnp.mean(centre * centre, axis=-1, keepdims=True)
            inv = lax.rsqrt(spread + 1e-05)
            uhat = centre * inv
            t = r * vrow(gain)
            gu = (t - jnp.mean(t, axis=-1, keepdims=True) - uhat * jnp.mean(t * uhat, axis=-1, keepdims=True)) * inv
            out_wide[rows, :] = gu
            slot[rows, :] = gu.astype(bf16)
            if again is not None:
                again[rows, :] = gu.astype(bf16)
            return (carry[0] + jnp.sum((r * uhat).reshape(4, 8, width), axis=0),
                    carry[1] + jnp.sum(r.reshape(4, 8, width), axis=0))
        zero = jnp.zeros((8, width), f32)
        total = lax.fori_loop(0, n // 32, step, (zero, zero), unroll=4)
        for row, part in ((gain_row(gain), total[0]), (bias_row_of(shift), total[1])):
            vg[row, :] = vg[row, :] + jnp.sum(part, axis=0, keepdims=True)

    def masked_scores(q_half, k2, n, length, diagonal):
        s = dot_nt(q_half, k2)
        column = lax.broadcasted_iota(jnp.int32, (n, n), 1)
        row = lax.broadcasted_iota(jnp.int32, (n, n), 0)
        return jnp.where((column < length) & (column <= row + diagonal), s, -1e30)

    def softmax(s):
        e = jnp.exp(s - jnp.max(s, axis=-1, keepdims=True))
        return e * (1.0 / jnp.sum(e, axis=-1, keepdims=True))

    def halves(n):
        lane = lax.broadcasted_iota(jnp.int32, (n, 2 * HDIM), 1)
        return lane < HDIM

    def head_loop(bs, body, lo=0, hi=None):
        pairs = {short: 3, long: 2, both: 1}[bs]

        def step(p, carry):
            body([(b, pl.ds(pl.multiple_of((p * pairs + i) * 2 * HDIM, 2 * HDIM), 2 * HDIM)) for b in bs for i in range(pairs)])
            return carry
        lax.fori_loop(lo, width // (2 * HDIM * pairs) if hi is None else hi, step, 0)

    def attend_forward(bs, q_ref, k_ref, v_ref, lengths_at, diagonal, bias_row, out_ref, lo=0, hi=None):
        def body(units):
            work = []
            for b, at in units:
                r0, n = buckets[b]
                rows = pl.ds(r0, n)
                q2, k2 = q_ref[rows, at], k_ref[rows, at]
                first = halves(n)
                for lanes in (first, ~first):
                    work.append(masked_scores(jnp.where(lanes, q2 * 0.125, jnp.zeros_like(q2)), k2, n, lengths_at[b], diagonal))
            work = [softmax(s).astype(bf16) for s in work]
            work = [dot_nn(prob, v_ref[pl.ds(*buckets[units[i // 2][0]]), units[i // 2][1]]) for i, prob in enumerate(work)]
            for i, (b, at) in enumerate(units):
                r0, n = buckets[b]
                att = jnp.where(halves(n), work[2 * i], work[2 * i + 1])
                if bias_row is not None:
                    att = att + vec[pl.ds(bias_row, 1), at]
                out_ref[pl.ds(r0, n), at] = att.astype(bf16)
        head_loop(bs, body, lo, hi)

    def attend_backward(bs, q_ref, k_ref, v_ref, lengths_at, diagonal, lo=0, hi=None):
        scale = HDIM ** -0.5

        def body(units):
            scores, ups = [], []
            for b, at in units:
                r0, n = buckets[b]
                rows = pl.ds(r0, n)
                q2, k2, v2, go2 = q_ref[rows, at], k_ref[rows, at], v_ref[rows, at], obuf[rows, at]
                first = halves(n)
                zero = jnp.zeros_like(q2)
                for lanes in (first, ~first):
                    scores.append(masked_scores(jnp.where(lanes, q2 * 0.125, zero), k2, n, lengths_at[b], diagonal))
                    ups.append(dot_nt(jnp.where(lanes, go2, zero), v2))
            probs = [softmax(s) for s in scores]
            gs = [(p * (gp - jnp.sum(p * gp, axis=-1, keepdims=True))).astype(bf16) for p, gp in zip(probs, ups)]
            results = []
            for i, (b, at) in enumerate(units):
                r0, n = buckets[b]
                rows = pl.ds(r0, n)
                q2, k2, go2 = q_ref[rows, at], k_ref[rows, at], obuf[rows, at]
                first = halves(n)
                two = (2 * i, 2 * i + 1)
                gv = [dot_tn(probs[u].astype(bf16), go2) for u in two]
                gq = [dot_nn(gs[u], k2) for u in two]
                gk = [dot_tn(gs[u], q2) for u in two]
                results.append(((jnp.where(first, gq[0], gq[1]) * scale).astype(bf16),
                                (jnp.where(first, gk[0], gk[1]) * scale).astype(bf16),
                                jnp.where(first, gv[0], gv[1]).astype(bf16)))
            for (b, at), (gq, gk, gv) in zip(units, results):
                rows = pl.ds(*buckets[b])
                q_ref[rows, at] = gq
                k_ref[rows, at] = gk
                v_ref[rows, at] = gv
        head_loop(bs, body, lo, hi)

    q_ref, k_ref, v_ref = gr.at[8], gr.at[9], gr.at[10]
    diagonal = (1 - st) * 4096
    bias_at = 5 + 10 * st
    ffn_at = 13 + 14 * st
    ffn_gain = 1 + 3 * st

    def by_tiles(fn):
        for t in range(tiles):
            fn(pl.ds(t * 256, 256))

    def self_project(bs, wait):
        rows = at_rows(bs)

        def project(which, carry):
            if wait:
                proj_load(which).wait()
            for t in range(tiles):
                at = pl.ds(t * 256, 256)
                value = dot_nn(xb[rows, :], wproj[which, :, at])
                bias = vec[pl.ds(bias_at + which // 2, 1), at] * jnp.where(which == 1, 0.0, 1.0)
                gr[8 + which, rows, at] = (value + bias).astype(bf16)
            return carry
        lax.fori_loop(0, 3, project, 0)

    def self_output(bs):
        rows = at_rows(bs)

        def tile(at):
            acc[rows, at] = dot_nn(obuf[rows, :], wo[:, at])
        by_tiles(tile)
        norm_forward(bs, xb, u_self, bias_at + 2, 2 * st, bias_at + 3, hlow, grad)

    def ffn_forward(bs, residual, wait_in, wait_out, turn=False):
        r0, n = span(bs)
        rows = pl.ds(r0, n)

        def ffn_slot(j, carry):
            for t in range(tiles):
                at = pl.ds(t * 256, 256)
                wide = pl.ds(pl.multiple_of(j * width + t * 256, 256), 256)
                zv = dot_nn(hlow[rows, :], win[:, wide]) + bias_in[pl.ds(st, 1), wide]
                cdf = 0.5 * (1.0 + lax.erf(zv * (0.5 ** 0.5)))
                pdf = jnp.exp(-0.5 * zv * zv) * 0.3989422804014327
                gr[1 + j, rows, at] = (zv * cdf).astype(bf16)
                dg[j, rows, at] = (cdf + zv * pdf).astype(bf16)
            return carry
        if wait_in:
            loads[3].wait()
        lax.fori_loop(0, slots, ffn_slot, 0)

        def ffn_out(at):
            total = dot_nn(gr[1, rows, :], wout[pl.ds(0, width), at])
            for j in range(1, slots):
                total = total + dot_nn(gr[1 + j, rows, :], wout[pl.ds(j * width, width), at])
            acc[rows, at] = total
        if wait_out:
            loads[4].wait()
        by_tiles(ffn_out)
        if turn:
            for j in range(slots):
                transposed_slot(bs, j)
        norm_forward(bs, residual, u_ffn, ffn_at, ffn_gain, ffn_at + 1, xb, None)

    def ffn_inner(bs, lo, hi, last):
        r0, n = span(bs)
        rows = pl.ds(r0, n)

        def ffn_inner_slot(j, carry):
            for t in range(tiles):
                at = pl.ds(t * 256, 256)
                wide = pl.ds(pl.multiple_of(j * width + t * 256, 256), 256)
                value = dot_nt(obuf[rows, :], wout[wide, :])
                gr[1 + j, rows, at] = (value * dg[j, rows, at].astype(f32)).astype(bf16)
            if last:
                remote(gr.at[1 + j], grp.at[1 + j], gr_send.at[1 + j], gr_recv.at[1 + j], core_id).start()
            return carry
        lax.fori_loop(lo, hi, ffn_inner_slot, 0)

    def ffn_input(bs):
        rows = at_rows(bs)

        def tile(at):
            total = grad[rows, at]
            for j in range(slots):
                total = total + dot_nt(gr[1 + j, rows, :], win[at, pl.ds(j * width, width)])
            grad[rows, at] = total
        by_tiles(tile)

    def cross_forward(bs):
        rows = at_rows(bs)

        def memory_kv(which, carry):
            for t in range(tiles):
                at = pl.ds(t * 256, 256)
                value = dot_nn(mem[rows, :], wx[which, :, at])
                kv[which, rows, at] = value.astype(bf16)
            return carry
        lax.fori_loop(0, 2, memory_kv, 0)
        attend_forward(bs, gr.at[6], kv.at[0], kv.at[1], lens[:2], 4096, 20, obuf)

        def cross_out(at):
            acc[rows, at] = dot_nn(obuf[rows, :], wsecond[:, at])
        by_tiles(cross_out)
        norm_forward(bs, grad, u_cross, 21, 3, 22, hlow, hw)
        transposed(7, bs, obuf)

    def cross_branch():
        norm_backward(both, u_cross, grad, 3, 22, hw, gr.at[5])

        def cross_up(at):
            obuf[:, at] = dot_nt(gr[5], wsecond[at, :]).astype(bf16)
        by_tiles(cross_up)

    def cross_backward(bs):
        rows = at_rows(bs)
        attend_backward(bs, gr.at[6], kv.at[0], kv.at[1], lens[:2], 4096)

        def memory_half(h, carry):
            at = cols(h, half)
            gmem[rows, at] = (dot_nt(kv[0, rows, :], wx[0, at, :]) + dot_nt(kv[1, rows, :], wx[1, at, :])).astype(bf16)
            gm_part(bs[0], h).start()
            return carry
        lax.fori_loop(0, 2, memory_half, 0)

    def cross_input(at):
        grad[:, at] = hw[:, at] + dot_nt(gr[6], wfirst[at, :])

    def lanes_of(h):
        return pl.ds(0, width) if h is None else cols(h, half)

    def unit(i, h):
        return i if h is None else 15 + 2 * (i - 12) + h

    def sems(i, stage, h):
        return sem_send.at[unit(i, h), stage], sem_recv.at[unit(i, h), stage]

    def first_copy(i, z_first, h):
        at = lanes_of(h)
        return remote(one_send.at[i % SEND_SLOTS, :, :, :, at], one_recv.at[i, :, :, :, at], *sems(i, 0, h),
                      near_id if z_first else y_id)

    def second_copy(i, z_first, h):
        at = lanes_of(h)
        source = one_recv.at[i, 1 - zh, :, :, at] if z_first else one_recv.at[i, :, 1 - zl, :, at]
        return remote(source, two_recv.at[i, :, :, at], *sems(i, 1, h), far_id if z_first else near_id)

    def third_copy(i, z_first, h):
        at = lanes_of(h)
        source = two_recv.at[i, 1 - y if z_first else 1 - zh, :, at]
        return remote(source, out_part.at[i, :, at], *sems(i, 2, h), y_id if z_first else far_id)

    def own_copy(i, z_first, h):
        at = lanes_of(h)
        return pltpu.make_async_copy(two_recv.at[i, y if z_first else zh, :, at], out_own.at[i, :, at], own_sem.at[unit(i, h)])

    def product(left, slot, z_first, other, at):
        if z_first:
            zz = 1 - zl if other else zl
            mine, theirs = lt[left, :, zz, :, c], ltp[left, :, zz]
        else:
            yy = 1 - y if other else y
            mine, theirs = lt[left, :, :, yy, c], ltp[left, :, :, yy]
        shape = (4 * PIECE, ROWS)
        return dot_nn(mine.reshape(shape), gr[slot, :, at]) + dot_nn(theirs.reshape(shape), grp[slot, :, at])

    def piece_tiles(h, fn):
        if h is None:
            loop(0, tiles, lambda t: fn(cols(t, 256), 256))
        else:
            fn(cols(h, half), half)

    def send_piece(i, left, slot, z_first=False, h=None):
        def tile(at, n):
            one_send[i % SEND_SLOTS, :, :, :, at] = product(left, slot, z_first, True, at).astype(bf16).reshape(2, 2, PIECE, n)
        piece_tiles(h, tile)
        first_copy(i, z_first, h).start()

    def keep_piece(i, left, slot, z_first=False, h=None):
        first_copy(i, z_first, h).wait()

        def tile(at, n):
            total = one_recv[i, :, :, :, at].reshape(4 * PIECE, n).astype(f32) + product(left, slot, z_first, False, at)
            one_recv[i, :, :, :, at] = total.astype(bf16).reshape(2, 2, PIECE, n)
        piece_tiles(h, tile)
        second_copy(i, z_first, h).start()

    def merge_piece(i, z_first=False, h=None):
        second_copy(i, z_first, h).wait()
        at = lanes_of(h)
        for k in range(2):
            mine = one_recv[i, zh, k, :, at] if z_first else one_recv[i, k, zl, :, at]
            two_recv[i, k, :, at] = (two_recv[i, k, :, at].astype(f32) + mine.astype(f32)).astype(bf16)

    def pass_piece(i, z_first=False, h=None):
        merge_piece(i, z_first, h)
        third_copy(i, z_first, h).start()
        own_copy(i, z_first, h).start()

    extra = PIECES
    extra_part = remote(two_recv.at[extra, 1 - zh], out_part.at[13], sem_send.at[extra, 2], sem_recv.at[13, 2], over_id)
    extra_own = remote(two_recv.at[extra, zh], out_own.at[13], sem_send.at[13, 0], sem_recv.at[13, 0], x_id)
    extra_left = remote(lt.at[0, :, :, :, 1 - c], ltp.at[0], lt_send.at[0], lt_recv.at[0], core_id)
    extra_right = remote(gr.at[0], grp.at[0], gr_send.at[0], gr_recv.at[0], core_id)

    def loop(lo, hi, fn):
        def step(i, carry):
            fn(i)
            return carry
        lax.fori_loop(lo, hi, step, 0)

    def wait_active():
        for i in range(4):
            lt_copy[i].wait()
        gr_first[0].wait()
        gr_first[1].wait()

    @pl.when(is_enc)
    def _():
        again = loads[1]
        again.start()
        for bs in (long, short):
            self_project(bs, bs == long)
            if bs == long:
                wx_start()
            attend_forward(bs, q_ref, k_ref, v_ref, own_lens, diagonal, None, obuf)
            if bs == long:
                loads[2].wait()
            self_output(bs)
            ffn_forward(bs, grad, bs == long, bs == long)
            mem_copy[bs[0]].start()
        transposed_active(both)
        for k in range(4):
            lt_copy[k].start()
        again.wait()
        for i, ref in ((4, mem), (5, obuf), (6, hlow), (7, xb)):
            transposed(i, both, ref)
            lt_copy[i].start()
        loads[5].wait()
        loads[6].wait()
        for bs in (short, long):
            for h in range(2):
                gm_part(bs[0], h).wait_recv()
            norm_backward(bs, u_ffn, up, ffn_gain, ffn_at + 1, grad, gr.at[0], obuf)
            gr_first[bs[0]].start()
            if bs == short:
                ffn_inner(bs, 0, slots, False)
                ffn_input(bs)
        ffn_inner(long, 0, 1, True)

    @pl.when(is_dec)
    def _():
        self_project(both, True)
        wx_start()
        transposed(4, both, xb)
        lt_copy[4].start()

        def wx_forward(h):
            wx_in[h].wait_recv()
            wx_y[h].start()
            wx_z[h].start()
        attend_forward(both, q_ref, k_ref, v_ref, own_lens, diagonal, None, obuf, 0, 3)
        wx_forward(0)
        attend_forward(both, q_ref, k_ref, v_ref, own_lens, diagonal, None, obuf, 3, 6)
        wx_forward(1)
        loads[2].wait()
        self_output(both)
        wx_forward(2)
        wx_y[0].wait()
        wx_on[0].start()
        loads[5].wait()

        def cross_query(at):
            gr[6, :, at] = (dot_nn(hlow[...], wfirst[:, at]) + vec[pl.ds(19, 1), at]).astype(bf16)
        by_tiles(cross_query)
        wx_forward(3)
        wx_core[0].start()
        transposed(5, both, obuf)
        lt_copy[5].start()
        transposed(8, both, hlow)
        lt_copy[8].start()
        loads[6].wait()
        cot_load.wait()
        wx_y[1].wait()
        wx_on[1].start()
        wx_z[0].wait()
        wx_z[1].wait()
        wx_z[2].wait()
        wx_on[2].start()
        wx_y[2].wait()
        wx_z[3].wait()
        wx_on[3].start()
        wx_y[3].wait()
        wx_core[1].start()
        wx_core[2].start()
        for h in range(chunks):
            wx_on[h].wait()
        wx_core[3].start()
        for k in range(4):
            wx_core[k].wait()
        for bs in (long, short):
            mem_copy[bs[0]].wait_recv()
            cross_forward(bs)
        lt_copy[7].start()
        ffn_forward(both, hw, True, True, True)
        for k in range(4):
            lt_copy[k].start()
        norm_backward(both, u_ffn, up, ffn_gain, ffn_at + 1, grad, gr.at[0], obuf)
        gr_first[0].start()
        gr_first[1].start()
        ffn_inner(both, 0, slots, True)
        ffn_input(both)
        cross_branch()
        for bs in (short, long):
            cross_backward(bs)
        transposed(6, both, hlow)
        lt_copy[6].start()

    wait_active()

    def first_sends(k):
        send_piece(2 + k, 2 + k, 0)
        send_piece(k, k, 0, True)
    loop(0, 2, first_sends)

    @pl.when(is_enc)
    def _():
        ffn_inner(long, 1, slots, True)
    lt_copy[6].wait()

    def inner_sends(j):
        remote(gr.at[1 + j], grp.at[1 + j], gr_send.at[1 + j], gr_recv.at[1 + j], core_id).wait()
        send_piece(4 + j, 6, 1 + j)
    loop(0, slots, inner_sends)

    @pl.when(is_enc)
    def _():
        ffn_input(long)

    @pl.when(is_dec)
    def _():
        gr_copy[5].start()
        gr_copy[6].start()
        by_tiles(cross_input)
        col_sum(obuf, 20)
        col_sum(gr.at[6], 19)
        col_sum(gr.at[5], 21)

    rows_copy = pltpu.make_async_copy(xb, out_rows, io_sem.at[0])
    rows_copy.start()

    norm_backward(both, u_self, grad, 2 * st, bias_at + 3, hw, gr.at[7])
    gr_copy[7].start()

    def self_up(at):
        obuf[:, at] = dot_nt(gr[7], wo[at, :]).astype(bf16)
    by_tiles(self_up)

    def keep_and_attend(k, carry):
        keep_piece(2 + k, 2 + k, 0)
        keep_piece(k, k, 0, True)
        attend_backward(both, q_ref, k_ref, v_ref, own_lens, diagonal, k * 3, k * 3 + 3)
        return carry
    lax.fori_loop(0, 2, keep_and_attend, 0)
    for j in range(3):
        gr_copy[8 + j].start()

    @pl.when(is_dec)
    def _():
        gv_copy.start()

    def self_input(at):
        total = hw[:, at]
        for j in range(3):
            total = total + dot_nt(gr[8 + j], wproj[j, at, :])
        hw[:, at] = total
    by_tiles(self_input)
    grad_copy = pltpu.make_async_copy(hw, out_grad, io_sem.at[1])
    grad_copy.start()
    loop(2, 4, pass_piece)
    for i in (4, 5, 7):
        lt_copy[i].wait()

    @pl.when(is_dec)
    def _():
        lt_copy[8].wait()
    for i in range(7, 11):
        gr_copy[i].wait()
    col_sum(gr.at[0], ffn_at)
    loop(0, slots, lambda j: col_sum(gr.at[1 + j], ffn_at - 4 + j))
    col_sum(gr.at[7], bias_at + 2)
    col_sum(gr.at[8], bias_at)
    col_sum(gr.at[10], bias_at + 1)
    own_half = pl.ds(pl.multiple_of(c * half, half), half)
    other_half = pl.ds(pl.multiple_of((1 - c) * half, half), half)
    v_copy = [remote(vg.at[:, other_half] if k == 0 else vbuf.at[2 * k], vbuf.at[2 * k + 1], v_send.at[k], v_recv.at[k], dev)
              for k, dev in enumerate((core_id, y_id, near_id, far_id, x_id))]
    v_last = remote(vboth.at[:, :, own_half], vboth.at[:, :, own_half], v_send.at[5], v_recv.at[5], core_id)
    vbuf[0] = vg[:, own_half]

    @pl.when(is_dec)
    def _():
        transposed(0, both, mem)
        extra_left.start()
        gr[0] = kv[0]
        extra_right.start()

    def v_next(k):
        v_copy[k].wait()
        vbuf[2 * k + 2] = vbuf[2 * k] + vbuf[2 * k + 1]
        v_copy[k + 1].start()
    v_copy[0].start()
    v_next(0)

    def attention_piece(k):
        return 8 + k, 5 - (k + 3) // 4, 7 + k

    def cross_piece(k):
        return 12 + k // 2, 7 + st * (k // 2), 5 + k // 2, False, k % 2

    def middle(k):
        send_piece(*attention_piece(k))
        keep_piece(4 + k, 6, 1 + k)

        @pl.when(k > 0)
        def _():
            pass_piece(3 + k)
    loop(0, 4, middle)

    @pl.when(is_enc)
    def _():
        gv_copy.wait_recv()
        gr_copy[5].start()

    @pl.when(is_dec)
    def _():
        extra_left.wait()
        extra_right.wait()
        send_piece(extra, 0, 0)
        gr_copy[6].wait()
    v_next(1)
    cross_units = 2 + 2 * st

    def later(k):
        keep_piece(*attention_piece(k))

        @pl.when(k == 0)
        def _():
            gr_copy[5].wait()
            loop(0, cross_units, lambda k: send_piece(*cross_piece(k)))
        pass_piece(7 + k)
    loop(0, 4, later)

    @pl.when(is_dec)
    def _():
        keep_piece(extra, 0, 0)
    v_next(2)
    loop(0, 2, lambda i: pass_piece(i, True))

    def ends(k):
        i, left, slot, z_first, h = cross_piece(k)
        keep_piece(i, left, slot, z_first, h)

        @pl.when(k == 0)
        def _():
            pass_piece(11)

        @pl.when(k > 0)
        def _():
            pass_piece(12 + (k - 1) // 2, False, (k + 1) % 2)

        @pl.when(k == 1)
        def _():
            v_next(3)

        @pl.when(is_dec & (k == 1))
        def _():
            merge_piece(extra)
            extra_part.start()
            extra_own.start()
    loop(0, cross_units, ends)
    pass_piece(12 + st, False, 1)
    v_copy[4].wait()
    vboth[st, :, own_half] = vbuf[8]
    vboth[1 - st, :, own_half] = vbuf[9]
    v_last.start()
    v_last.wait()
    vec_copy = pltpu.make_async_copy(vboth, out_vec, io_sem.at[2])
    vec_copy.start()

    def finish(i, z_first=False, h=None):
        third_copy(i, z_first, h).wait()
        own_copy(i, z_first, h).wait()
    loop(0, 2, lambda i: finish(i, True))
    loop(2, 12, finish)
    loop(0, cross_units, lambda k: finish(12 + k // 2, False, k % 2))
    rows_copy.wait()
    grad_copy.wait()
    vec_copy.wait()

    @pl.when(is_enc)
    def _():
        for h in range(chunks):
            wx_in[h].wait_send()
        for h in range(2):
            mem_copy[h].wait_send()
        extra_part.wait_recv()
        extra_own.wait_recv()

    @pl.when(is_dec)
    def _():
        for h in range(2):
            for b in range(2):
                gm_part(b, h).wait_send()
        gv_copy.wait_send()
        extra_part.wait_send()
        extra_own.wait_send()


def last_kernel(width, rows_in, grad_in, own, parts, vec_sum, rows_out, grad_out, *refs):
    outs, (vec_buf, rows_buf, grad_buf, own_buf, part_buf, sums, in_sem, through_sem, out_sem) = refs[:8], refs[8:]
    group = PIECES // 2
    loads = []
    for g in range(2):
        at = pl.ds(g * group, group)
        loads.append((pltpu.make_async_copy(own.at[at], own_buf.at[at], in_sem.at[g, 0]),
                      pltpu.make_async_copy(parts.at[at], part_buf.at[at], in_sem.at[g, 1])))
    vec_load = pltpu.make_async_copy(vec_sum, vec_buf, through_sem.at[2])
    into = [pltpu.make_async_copy(grad_in, grad_buf, through_sem.at[0]), pltpu.make_async_copy(rows_in, rows_buf, through_sem.at[1])]
    for cp in (*loads[0], into[0], *loads[1], into[1], vec_load):
        cp.start()
    stores = []

    def store(src, dst):
        stores.append(pltpu.make_async_copy(src, dst, out_sem.at[len(stores)]))
        stores[-1].start()
    for g in range(2):
        for cp in loads[g]:
            cp.wait()
        for i in range(g * group, (g + 1) * group):
            sums[i] = own_buf[i].astype(f32) + part_buf[i].astype(f32)
            if i < 4:
                store(sums.at[i], outs[0].at[pl.ds(i * PIECE, PIECE), :])
            elif i < 8:
                store(sums.at[i], outs[1].at[:, pl.ds((i - 4) * width, width)])
            elif i == 8:
                store(sums.at[i], outs[4])
            elif i == 11:
                store(sums.at[pl.ds(9, 3)], outs[5])
            elif i > 11:
                store(sums.at[i], outs[i - 10])
        into[g].wait()
        store(rows_buf if g else grad_buf, rows_out if g else grad_out)
    vec_load.wait()
    shift = lax.rem(width - lax.axis_index("dp") * PIECE, width)
    for s, (g0, g1, b0, b1) in enumerate(((0, 2, 0, 10), (2, 5, 10, 24))):
        turned = pltpu.roll(vec_buf[s], shift, 1)
        outs[6][pl.ds(g0, g1 - g0), :] = turned[:g1 - g0, :PIECE]
        outs[7][pl.ds(b0, b1 - b0), :] = turned[3:3 + b1 - b0, :PIECE]
    for cp in stores:
        cp.wait()


def whole_step(lengths, gains, biases, x, cot, wproj, wo, wfirst, wsecond, win, wout):
    width = x.shape[1]
    hidden = win.shape[1]
    half = width // 2
    any_space = pl.BlockSpec(memory_space=pl.ANY)
    vmem = pl.BlockSpec(memory_space=pltpu.VMEM)
    dma = pltpu.SemaphoreType.DMA
    slots = hidden // width
    small = (32, width)
    results = pl.pallas_call(
        functools.partial(step_kernel, width, hidden),
        out_shape=[
            jax.ShapeDtypeStruct((ROWS, width), bf16),
            jax.ShapeDtypeStruct((ROWS, width), f32),
            jax.ShapeDtypeStruct((PIECES, PIECE, width), bf16),
            jax.ShapeDtypeStruct((PIECES, PIECE, width), bf16),
            jax.ShapeDtypeStruct((2, VEC_ROWS, width), f32),
        ],
        in_specs=[pl.BlockSpec(memory_space=pltpu.SMEM), vmem, vmem] + [any_space] * 8,
        out_specs=[any_space] * 5,
        scratch_shapes=[
            pltpu.VMEM(small, f32), pltpu.VMEM((2, hidden), f32),
            pltpu.VMEM(wproj.shape, bf16), pltpu.VMEM(wo.shape, bf16), pltpu.VMEM(wfirst.shape, bf16),
            pltpu.VMEM(wsecond.shape, bf16), pltpu.VMEM(win.shape, bf16), pltpu.VMEM(wout.shape, bf16),
            pltpu.VMEM((2, width, width), bf16),
            pltpu.VMEM((ROWS, width), bf16),
            pltpu.VMEM((ROWS, width), bf16),
            pltpu.VMEM((ROWS, width), bf16),
            pltpu.VMEM((ROWS, width), bf16),
            pltpu.VMEM((ROWS, width), bf16),
            pltpu.VMEM((slots, ROWS, width), bf16),
            pltpu.VMEM((2, ROWS, width), bf16),
            pltpu.VMEM((ROWS, width), f32),
            pltpu.VMEM((ROWS, width), f32),
            pltpu.VMEM((ROWS, width), f32),
            pltpu.VMEM((ROWS, width), f32),
            pltpu.VMEM((ROWS, width), f32),
            pltpu.VMEM((ROWS, width), f32),
            pltpu.VMEM((11, ROWS, width), bf16),
            pltpu.VMEM((11, ROWS, width), bf16),
            pltpu.VMEM((9, 2, 2, 2, 2, PIECE, ROWS), bf16),
            pltpu.VMEM((9, 2, 2, 2, PIECE, ROWS), bf16),
            pltpu.VMEM((SEND_SLOTS, 2, 2, PIECE, width), bf16),
            pltpu.VMEM((PIECES + 1, 2, 2, PIECE, width), bf16),
            pltpu.VMEM((PIECES + 1, 2, PIECE, width), bf16),
            pltpu.VMEM((ROWS, width), bf16),
            pltpu.VMEM((VEC_ROWS, width), f32),
            pltpu.VMEM((10, VEC_ROWS, half), f32),
            pltpu.VMEM((2, VEC_ROWS, width), f32),
            dma((12,)), dma((20,)), dma((20,)), dma((2,)), dma((2,)), dma((4,)), dma((4,)), dma, dma,
            dma((9,)), dma((9,)), dma((12,)), dma((12,)),
            dma((19, 3)), dma((19, 3)), dma((19,)), dma((3,)), dma((6,)), dma((6,)),
        ],
        compiler_params=pltpu.CompilerParams(collective_id=0, has_side_effects=True, vmem_limit_bytes=VMEM_LIMIT),
        name="step",
    )(lengths, gains, biases, x, cot, wproj, wo, wfirst, wsecond, win, wout)
    shapes = [(4 * PIECE, width), (PIECE, hidden), (PIECE, width), (PIECE, width), (PIECE, width), (3, PIECE, width),
              (5, PIECE), (24, PIECE)]
    return pl.pallas_call(
        functools.partial(last_kernel, width),
        out_shape=[jax.ShapeDtypeStruct((ROWS, width), bf16), jax.ShapeDtypeStruct((ROWS, width), f32)]
        + [jax.ShapeDtypeStruct(shape, f32) for shape in shapes],
        in_specs=[any_space] * 5,
        out_specs=[any_space] * 8 + [vmem] * 2,
        scratch_shapes=[
            pltpu.VMEM((2, VEC_ROWS, width), f32), pltpu.VMEM((ROWS, width), bf16), pltpu.VMEM((ROWS, width), f32),
            pltpu.VMEM((PIECES, PIECE, width), bf16), pltpu.VMEM((PIECES, PIECE, width), bf16),
            pltpu.VMEM((PIECES, PIECE, width), f32), dma((2, 2)), dma((3,)), dma((PIECES + 2,)),
        ],
        compiler_params=pltpu.CompilerParams(vmem_limit_bytes=VMEM_LIMIT),
        name="last",
    )(*results)


eps_norm = 1e-05
low_type = jnp.bfloat16
wide_type = jnp.float32


def as_sent(shard):
    return jax.tree.map(lambda a: a.astype(jnp.bfloat16) if a.dtype == jnp.float32 else a, shard)


def shifted(shard, axis, by):
    count = lax.axis_size(axis)
    pairs = [(i, i + by) for i in range(count) if 0 <= i + by < count]
    return lax.ppermute(shard, axis, pairs)


def matmul(left_mat, right_mat):
    return jnp.dot(left_mat, right_mat, preferred_element_type=wide_type)


def matmul_tn(left_mat, right_mat):
    return lax.dot_general(
        left_mat, right_mat, (((0,), (0,)), ((), ())), preferred_element_type=wide_type
    )


def matmul_nt(left_mat, right_mat):
    return lax.dot_general(
        left_mat, right_mat, (((1,), (1,)), ((), ())), preferred_element_type=wide_type
    )


def column_sum(tensor):
    return jnp.sum(tensor.astype(wide_type), axis=0)


def norm_rows(tensor, norm_gain, norm_shift):
    centre = tensor - jnp.mean(tensor, axis=-1, keepdims=True)
    spread = jnp.mean(centre * centre, axis=-1, keepdims=True)
    return centre * lax.rsqrt(spread + eps_norm) * norm_gain + norm_shift


def norm_back(tensor, norm_gain, norm_shift, upstream):
    unused, pullback = jax.vjp(norm_rows, tensor, norm_gain, norm_shift)
    return pullback(upstream)


def gelu_exact(tensor):
    return jax.nn.gelu(tensor, approximate=False)


def key_mask(row_count, key_count, length, causal):
    columns = lax.broadcasted_iota(jnp.int32, (row_count, key_count), 1)
    allowed = columns < length
    if causal:
        allowed = allowed & (columns <= lax.broadcasted_iota(jnp.int32, (row_count, key_count), 0))
    return allowed


def split_heads(tensor):
    return tensor.reshape(tensor.shape[0], -1, HDIM)


def attend_scores(queries, key_rows, allowed):
    scores = jnp.einsum(
        "qhd,khd->hqk",
        split_heads(queries),
        split_heads(key_rows),
        preferred_element_type=wide_type,
    )
    return jnp.where(allowed[None], scores * HDIM ** (-0.5), -1e30)


def attend_forward(queries, key_rows, values, allowed):
    scores = attend_scores(queries, key_rows, allowed)
    row_max = jnp.max(scores, axis=-1, keepdims=True)
    log_total = row_max + jnp.log(jnp.sum(jnp.exp(scores - row_max), axis=-1, keepdims=True))
    softmaxed = jnp.exp(scores - log_total).astype(low_type)
    attended = jnp.einsum(
        "hqk,khd->qhd", softmaxed, split_heads(values), preferred_element_type=wide_type
    )
    return (attended.reshape(queries.shape[0], -1), log_total)


def attend_backward(queries, key_rows, values, allowed, log_total, upstream):
    softmaxed = jnp.exp(attend_scores(queries, key_rows, allowed) - log_total)
    grad_heads = split_heads(upstream)
    grad_values = jnp.einsum(
        "hqk,qhd->khd", softmaxed.astype(low_type), grad_heads, preferred_element_type=wide_type
    )
    grad_probs = jnp.einsum(
        "qhd,khd->hqk", grad_heads, split_heads(values), preferred_element_type=wide_type
    )
    grad_scores = (
        softmaxed * (grad_probs - jnp.sum(softmaxed * grad_probs, axis=-1, keepdims=True))
    ).astype(low_type)
    scale_factor = HDIM ** (-0.5)
    grad_queries = (
        jnp.einsum(
            "hqk,khd->qhd", grad_scores, split_heads(key_rows), preferred_element_type=wide_type
        )
        * scale_factor
    )
    grad_keys = (
        jnp.einsum(
            "hqk,qhd->khd", grad_scores, split_heads(queries), preferred_element_type=wide_type
        )
        * scale_factor
    )
    key_count = key_rows.shape[0]
    return (
        grad_queries.reshape(queries.shape[0], -1),
        grad_keys.reshape(key_count, -1),
        grad_values.reshape(key_count, -1),
    )


def self_forward(row_block, length, causal, w_proj, w_out, vectors):
    bias_q, bias_v, bias_o, norm_gain, norm_shift = vectors
    row_count = row_block.shape[0]
    offsets = jnp.stack([bias_q, jnp.zeros_like(bias_q), bias_v])[:, None, :]
    projected = (
        jnp.einsum("rd,cde->cre", row_block, w_proj, preferred_element_type=wide_type) + offsets
    ).astype(low_type)
    allowed = key_mask(row_count, row_count, length, causal)
    attended, log_total = attend_forward(projected[0], projected[1], projected[2], allowed)
    attended = attended.astype(low_type)
    summed = row_block.astype(wide_type) + matmul(attended, w_out) + bias_o
    return (norm_rows(summed, norm_gain, norm_shift), (projected, log_total, attended, summed))


def self_backward(row_block, length, causal, w_proj, w_out, vectors, saved_fwd, upstream):
    projected, log_total, attended, summed = saved_fwd
    row_count = row_block.shape[0]
    grad_sum, grad_gain, grad_shift = norm_back(summed, vectors[3], vectors[4], upstream)
    grad_branch = grad_sum.astype(low_type)
    grad_attended = matmul_nt(grad_branch, w_out).astype(low_type)
    allowed = key_mask(row_count, row_count, length, causal)
    grad_q, grad_k, grad_v = attend_backward(
        projected[0], projected[1], projected[2], allowed, log_total, grad_attended
    )
    grad_proj = jnp.stack([grad_q, grad_k, grad_v]).astype(low_type)
    grad_rows = grad_sum + jnp.einsum(
        "cre,cde->rd", grad_proj, w_proj, preferred_element_type=wide_type
    )
    weight_grads = (
        jnp.einsum("rd,cre->cde", row_block, grad_proj, preferred_element_type=wide_type),
        matmul_tn(attended, grad_branch),
    )
    vector_grads = (
        column_sum(grad_proj[0]),
        column_sum(grad_proj[2]),
        column_sum(grad_branch),
        grad_gain,
        grad_shift,
    )
    return (grad_rows, weight_grads, vector_grads)


def ffn_forward(hidden, w_in, w_out, vectors):
    bias_in, bias_out, norm_gain, norm_shift = vectors
    low_hidden = hidden.astype(low_type)
    inner_act = matmul(low_hidden, w_in) + bias_in
    active = gelu_exact(inner_act).astype(low_type)
    summed = hidden + matmul(active, w_out) + bias_out
    return (norm_rows(summed, norm_gain, norm_shift), (low_hidden, inner_act, active, summed))


def ffn_backward(w_in, w_out, vectors, saved_fwd, upstream):
    low_hidden, inner_act, active, summed = saved_fwd
    grad_sum, grad_gain, grad_shift = norm_back(summed, vectors[2], vectors[3], upstream)
    grad_branch = grad_sum.astype(low_type)
    unused, pullback = jax.vjp(gelu_exact, inner_act)
    grad_inner = pullback(matmul_nt(grad_branch, w_out))[0].astype(low_type)
    grad_hidden = grad_sum + matmul_nt(grad_inner, w_in)
    weight_grads = (matmul_tn(low_hidden, grad_inner), matmul_tn(active, grad_branch))
    vector_grads = (column_sum(grad_inner), column_sum(grad_branch), grad_gain, grad_shift)
    return (grad_hidden, weight_grads, vector_grads)


def cross_forward(hidden, memory, src_len, w_query, w_out, vectors):
    bias_q, bias_v, bias_o, norm_gain, norm_shift = vectors
    low_hidden = hidden.astype(low_type)
    queries = (matmul(low_hidden, w_query) + bias_q).astype(low_type)
    allowed = key_mask(hidden.shape[0], memory.shape[1], src_len, False)
    attended, log_total = attend_forward(queries, memory[0], memory[1], allowed)
    attended = (attended + bias_v).astype(low_type)
    summed = hidden + matmul(attended, w_out) + bias_o
    return (
        norm_rows(summed, norm_gain, norm_shift),
        (low_hidden, queries, log_total, attended, summed),
    )


def cross_backward(memory, src_len, w_query, w_out, vectors, saved_fwd, upstream):
    low_hidden, queries, log_total, attended, summed = saved_fwd
    grad_sum, grad_gain, grad_shift = norm_back(summed, vectors[3], vectors[4], upstream)
    grad_branch = grad_sum.astype(low_type)
    grad_attended = matmul_nt(grad_branch, w_out).astype(low_type)
    allowed = key_mask(queries.shape[0], memory.shape[1], src_len, False)
    grad_q, grad_k, grad_v = attend_backward(
        queries, memory[0], memory[1], allowed, log_total, grad_attended
    )
    grad_query = grad_q.astype(low_type)
    grad_memory = jnp.stack([grad_k, grad_v]).astype(low_type)
    grad_hidden = grad_sum + matmul_nt(grad_query, w_query)
    weight_grads = (matmul_tn(low_hidden, grad_query), matmul_tn(attended, grad_branch))
    vector_grads = (
        column_sum(grad_query),
        column_sum(grad_attended),
        column_sum(grad_branch),
        grad_gain,
        grad_shift,
    )
    return (grad_hidden, grad_memory, weight_grads, vector_grads)


def self_vectors(gain_rows, bias_rows, decoder):
    base_row = 10 if decoder else 0
    gain_row = 2 if decoder else 0
    return (
        bias_rows[base_row],
        bias_rows[base_row + 1],
        bias_rows[base_row + 2],
        gain_rows[gain_row],
        bias_rows[base_row + 3],
    )


def ffn_vectors(gain_rows, bias_rows, decoder):
    base_row = 18 if decoder else 4
    gain_row = 4 if decoder else 1
    return (
        bias_rows[base_row : base_row + 4].reshape(-1),
        bias_rows[base_row + 4],
        gain_rows[gain_row],
        bias_rows[base_row + 5],
    )


def cross_vectors(gain_rows, bias_rows):
    return (bias_rows[14], bias_rows[15], bias_rows[16], gain_rows[3], bias_rows[17])


def self_plan(decoder, vector_grads):
    base_row = 10 if decoder else 0
    gain_row = 2 if decoder else 0
    return (
        ("biases", base_row, vector_grads[0]),
        ("biases", base_row + 1, vector_grads[1]),
        ("biases", base_row + 2, vector_grads[2]),
        ("gains", gain_row, vector_grads[3]),
        ("biases", base_row + 3, vector_grads[4]),
    )


def ffn_plan(decoder, vector_grads):
    base_row = 18 if decoder else 4
    gain_row = 4 if decoder else 1
    return (
        ("biases", base_row, vector_grads[0]),
        ("biases", base_row + 4, vector_grads[1]),
        ("gains", gain_row, vector_grads[2]),
        ("biases", base_row + 5, vector_grads[3]),
    )


def cross_plan(vector_grads):
    return (
        ("biases", 14, vector_grads[0]),
        ("biases", 15, vector_grads[1]),
        ("biases", 16, vector_grads[2]),
        ("gains", 3, vector_grads[3]),
        ("biases", 17, vector_grads[4]),
    )


def accumulate(totals, weight_names, weight_grads, vector_plan):
    merged = dict(totals)
    for key_name, tensor in zip(weight_names, weight_grads):
        merged[key_name] = merged[key_name] + tensor
    for table_name, row_at, tensor in vector_plan:
        table_now = merged[table_name]
        row_block = tensor.reshape(-1, table_now.shape[1])
        merged[table_name] = table_now.at[row_at : row_at + row_block.shape[0]].add(row_block)
    return merged


def updated(progress, key_name, position, tensor):
    copied = dict(progress)
    copied[key_name] = [
        tensor if slot_index == position else entry_now
        for slot_index, entry_now in enumerate(progress[key_name])
    ]
    return copied


def with_totals(progress, totals):
    copied = dict(progress)
    copied["totals"] = totals
    return copied


def forward_pass(tensor):
    return jax.tree.map(
        lambda part, own: part.astype(own.dtype), shifted(as_sent(tensor), "stream", 1), tensor
    )


def backward_pass(tensor):
    return jax.tree.map(
        lambda part, own: part.astype(own.dtype), shifted(as_sent(tensor), "stream", -1), tensor
    )


def keep_same(progress):
    return progress


def plain_body(
    inputs,
    lengths,
    cotangent,
    attn_in,
    attn_out,
    cross_first,
    cross_second,
    ffn_in,
    ffn_out,
    gains,
    biases,
):
    own_rows = inputs[0]
    model_width = own_rows.shape[1]
    hidden_width = ffn_in.shape[2]
    head_count = model_width // HDIM
    row_sizes = (SHORT, LONG)
    bucket_spans = ((0, SHORT), (SHORT, SHORT + LONG))
    row_pieces = [own_rows[start_row:stop_row] for start_row, stop_row in bucket_spans]
    grad_pieces = [
        cotangent[start_row:stop_row].astype(wide_type) for start_row, stop_row in bucket_spans
    ]
    src_lens = [lengths[0, 0, bucket_idx] for bucket_idx in range(2)]
    tgt_lens = [lengths[1, 0, bucket_idx] for bucket_idx in range(2)]
    w_proj = attn_in[0]
    w_attn_out = attn_out[0]
    w_first = cross_first[0]
    w_second = cross_second[0]
    w_ffn_in = ffn_in[0]
    w_ffn_out = ffn_out[0]
    gain_rows = gains.astype(wide_type)
    bias_rows = biases.astype(wide_type)
    enc_self = self_vectors(gain_rows, bias_rows, False)
    enc_ffn = ffn_vectors(gain_rows, bias_rows, False)
    dec_self = self_vectors(gain_rows, bias_rows, True)
    dec_ffn = ffn_vectors(gain_rows, bias_rows, True)
    dec_cross = cross_vectors(gain_rows, bias_rows)
    is_decoder = lax.axis_index("stream") == 1

    def blank_self(size_rows):
        return (
            jnp.zeros((3, size_rows, model_width), low_type),
            jnp.zeros((head_count, size_rows, 1), wide_type),
            jnp.zeros((size_rows, model_width), low_type),
            jnp.zeros((size_rows, model_width), wide_type),
        )

    def blank_ffn(size_rows):
        return (
            jnp.zeros((size_rows, model_width), low_type),
            jnp.zeros((size_rows, hidden_width), wide_type),
            jnp.zeros((size_rows, hidden_width), low_type),
            jnp.zeros((size_rows, model_width), wide_type),
        )

    def blank_cross(size_rows):
        return (
            jnp.zeros((size_rows, model_width), low_type),
            jnp.zeros((size_rows, model_width), low_type),
            jnp.zeros((head_count, size_rows, 1), wide_type),
            jnp.zeros((size_rows, model_width), low_type),
            jnp.zeros((size_rows, model_width), wide_type),
        )

    progress = {
        "out": [jnp.zeros((size_rows, model_width), low_type) for size_rows in row_sizes],
        "grad_in": [jnp.zeros((size_rows, model_width), wide_type) for size_rows in row_sizes],
        "send": [jnp.zeros((2, size_rows, model_width), low_type) for size_rows in row_sizes],
        "memory": [jnp.zeros((2, size_rows, model_width), low_type) for size_rows in row_sizes],
        "grad_send": [jnp.zeros((2, size_rows, model_width), low_type) for size_rows in row_sizes],
        "grad_memory": [
            jnp.zeros((2, size_rows, model_width), low_type) for size_rows in row_sizes
        ],
        "mid": [jnp.zeros((size_rows, model_width), wide_type) for size_rows in row_sizes],
        "grad_mid": [jnp.zeros((size_rows, model_width), wide_type) for size_rows in row_sizes],
        "totals": {
            "proj": jnp.zeros(w_proj.shape, wide_type),
            "attn_out": jnp.zeros(w_attn_out.shape, wide_type),
            "first": jnp.zeros(w_first.shape, wide_type),
            "second": jnp.zeros(w_second.shape, wide_type),
            "ffn_in": jnp.zeros(w_ffn_in.shape, wide_type),
            "ffn_out": jnp.zeros(w_ffn_out.shape, wide_type),
            "gains": jnp.zeros(gains.shape, wide_type),
            "biases": jnp.zeros(biases.shape, wide_type),
        },
    }
    progress["self_saved"] = [blank_self(size_rows) for size_rows in row_sizes]
    progress["ffn_saved"] = [blank_ffn(size_rows) for size_rows in row_sizes]
    progress["cross_saved"] = [blank_cross(size_rows) for size_rows in row_sizes]

    def encoder_core(micro_idx):
        h_one, self_saved = self_forward(
            row_pieces[micro_idx], src_lens[micro_idx], False, w_proj, w_attn_out, enc_self
        )
        encoded, ffn_saved = ffn_forward(h_one, w_ffn_in, w_ffn_out, enc_ffn)
        return (encoded.astype(low_type), self_saved, ffn_saved)

    def encoder_forward_step(progress, micro_idx):
        low_memory, self_saved, ffn_saved = encoder_core(micro_idx)
        memory = jnp.stack([matmul(low_memory, w_first), matmul(low_memory, w_second)]).astype(
            low_type
        )
        progress = updated(progress, "out", micro_idx, low_memory)
        progress = updated(progress, "send", micro_idx, memory)
        progress = updated(progress, "self_saved", micro_idx, self_saved)
        progress = updated(progress, "ffn_saved", micro_idx, ffn_saved)
        return progress

    def decoder_head(micro_idx):
        return self_forward(
            row_pieces[micro_idx], tgt_lens[micro_idx], True, w_proj, w_attn_out, dec_self
        )

    def decoder_tail(mid_rows, memory, micro_idx):
        crossed, cross_saved = cross_forward(
            mid_rows, memory, src_lens[micro_idx], w_first, w_second, dec_cross
        )
        decoded, ffn_saved = ffn_forward(crossed, w_ffn_in, w_ffn_out, dec_ffn)
        return (decoded, cross_saved, ffn_saved)

    def decoder_head_step(progress, micro_idx):
        mid_rows, self_saved = decoder_head(micro_idx)
        progress = updated(progress, "mid", micro_idx, mid_rows)
        progress = updated(progress, "self_saved", micro_idx, self_saved)
        return progress

    def decoder_tail_step(progress, micro_idx):
        decoded, cross_saved, ffn_saved = decoder_tail(
            progress["mid"][micro_idx], progress["memory"][micro_idx], micro_idx
        )
        progress = updated(progress, "out", micro_idx, decoded.astype(low_type))
        progress = updated(progress, "cross_saved", micro_idx, cross_saved)
        progress = updated(progress, "ffn_saved", micro_idx, ffn_saved)
        return progress

    def decoder_back_step(progress, micro_idx):
        memory = progress["memory"][micro_idx]
        self_saved = progress["self_saved"][micro_idx]
        cross_saved = progress["cross_saved"][micro_idx]
        ffn_saved = progress["ffn_saved"][micro_idx]
        grad_h_two, ffn_w, ffn_v = ffn_backward(
            w_ffn_in, w_ffn_out, dec_ffn, ffn_saved, grad_pieces[micro_idx]
        )
        grad_h_one, grad_memory, cross_w, cross_v = cross_backward(
            memory, src_lens[micro_idx], w_first, w_second, dec_cross, cross_saved, grad_h_two
        )
        grad_rows, self_w, self_v = self_backward(
            row_pieces[micro_idx],
            tgt_lens[micro_idx],
            True,
            w_proj,
            w_attn_out,
            dec_self,
            self_saved,
            grad_h_one,
        )
        totals = accumulate(
            progress["totals"],
            ("ffn_in", "ffn_out", "first", "second", "proj", "attn_out"),
            ffn_w + cross_w + self_w,
            ffn_plan(True, ffn_v) + cross_plan(cross_v) + self_plan(True, self_v),
        )
        progress = updated(progress, "grad_in", micro_idx, grad_rows)
        progress = updated(progress, "grad_send", micro_idx, grad_memory)
        return with_totals(progress, totals)

    def encoder_top_step(progress, micro_idx):
        low_memory = progress["out"][micro_idx]
        ffn_saved = progress["ffn_saved"][micro_idx]
        grad_memory = progress["grad_memory"][micro_idx]
        grad_encoded = matmul_nt(grad_memory[0], w_first) + matmul_nt(grad_memory[1], w_second)
        grad_h_one, ffn_w, ffn_v = ffn_backward(
            w_ffn_in, w_ffn_out, enc_ffn, ffn_saved, grad_encoded
        )
        projections = (matmul_tn(low_memory, grad_memory[0]), matmul_tn(low_memory, grad_memory[1]))
        totals = accumulate(
            progress["totals"],
            ("first", "second", "ffn_in", "ffn_out"),
            projections + ffn_w,
            ffn_plan(False, ffn_v),
        )
        progress = updated(progress, "grad_mid", micro_idx, grad_h_one)
        return with_totals(progress, totals)

    def encoder_bottom_step(progress, micro_idx):
        self_saved = progress["self_saved"][micro_idx]
        grad_rows, self_w, self_v = self_backward(
            row_pieces[micro_idx],
            src_lens[micro_idx],
            False,
            w_proj,
            w_attn_out,
            enc_self,
            self_saved,
            progress["grad_mid"][micro_idx],
        )
        totals = accumulate(
            progress["totals"], ("proj", "attn_out"), self_w, self_plan(False, self_v)
        )
        progress = updated(progress, "grad_in", micro_idx, grad_rows)
        return with_totals(progress, totals)

    def enc_zero(progress):
        return encoder_forward_step(progress, 0)

    def dec_zero(progress):
        return decoder_head_step(progress, 0)

    def enc_one(progress):
        return encoder_forward_step(progress, 1)

    def dec_one(progress):
        return decoder_tail_step(decoder_head_step(progress, 1), 0)

    def dec_two(progress):
        return decoder_back_step(decoder_tail_step(progress, 1), 1)

    def enc_three(progress):
        return encoder_bottom_step(encoder_top_step(progress, 1), 1)

    def dec_three(progress):
        return decoder_back_step(progress, 0)

    def enc_four(progress):
        return encoder_top_step(progress, 0)

    def enc_five(progress):
        return encoder_bottom_step(progress, 0)

    progress = lax.cond(is_decoder, dec_zero, enc_zero, progress)
    progress = updated(progress, "memory", 0, forward_pass(progress["send"][0]))
    progress = lax.cond(is_decoder, dec_one, enc_one, progress)
    progress = updated(progress, "memory", 1, forward_pass(progress["send"][1]))
    progress = lax.cond(is_decoder, dec_two, keep_same, progress)
    progress = updated(progress, "grad_memory", 1, backward_pass(progress["grad_send"][1]))
    progress = lax.cond(is_decoder, dec_three, enc_three, progress)
    progress = updated(progress, "grad_memory", 0, backward_pass(progress["grad_send"][0]))
    progress = lax.cond(is_decoder, keep_same, enc_four, progress)
    progress = lax.cond(is_decoder, keep_same, enc_five, progress)
    totals = progress["totals"]
    owned = (
        lax.psum_scatter(totals["proj"], "dp", scatter_dimension=1, tiled=True),
        lax.psum_scatter(totals["attn_out"], "dp", scatter_dimension=0, tiled=True),
        lax.psum_scatter(totals["first"], "dp", scatter_dimension=0, tiled=True),
        lax.psum_scatter(totals["second"], "dp", scatter_dimension=0, tiled=True),
        lax.psum_scatter(totals["ffn_in"], "dp", scatter_dimension=0, tiled=True),
        lax.psum_scatter(totals["ffn_out"], "dp", scatter_dimension=0, tiled=True),
        lax.psum_scatter(totals["gains"], "dp", scatter_dimension=1, tiled=True),
        lax.psum_scatter(totals["biases"], "dp", scatter_dimension=1, tiled=True),
    )
    owned_gains, owned_biases = lax.psum((owned[6], owned[7]), "stream")
    layer_out = jnp.concatenate(progress["out"], axis=0)[None]
    grad_inputs = jnp.concatenate(progress["grad_in"], axis=0)[None]
    return (
        layer_out,
        grad_inputs,
        owned[0][None],
        owned[1][None],
        owned[2][None],
        owned[3][None],
        owned[4][None],
        owned[5][None],
        owned_gains,
        owned_biases,
    )


def fused_body(inputs, lengths, cotangent, attn_in, attn_out, cross_first, cross_second, ffn_in, ffn_out, gains, biases):
    rows, grad, s_out, s_in, s_second, s_first, s_attn, s_proj, own_gains, own_biases = whole_step(
        lengths, gains, biases, inputs[0], cotangent, attn_in[0], attn_out[0],
        cross_first[0], cross_second[0], ffn_in[0], ffn_out[0])
    return (rows[None], grad[None], s_proj[None], s_attn[None], s_first[None], s_second[None],
            s_in[None], s_out[None], own_gains, own_biases)


def solution(mesh):
    def body(*args):
        width = args[0].shape[2]
        fits = mesh.shape["dp"] * PIECE == width and args[0].shape[1] == ROWS and args[7].shape[2] == 4 * width
        return (fused_body if fits else plain_body)(*args)
    return jax.shard_map(
        body,
        mesh=mesh,
        in_specs=(
            P("stream", "dp", None),
            P(None, "dp", None),
            P("dp", None),
            P("stream", None, None, None),
            P("stream", None, None),
            P("stream", None, None),
            P("stream", None, None),
            P("stream", None, None),
            P("stream", None, None),
            P(),
            P(),
        ),
        out_specs=(
            P("stream", "dp", None),
            P("stream", "dp", None),
            P("stream", None, "dp", None),
            P("stream", "dp", None),
            P("stream", "dp", None),
            P("stream", "dp", None),
            P("stream", "dp", None),
            P("stream", "dp", None),
            P(None, "dp"),
            P(None, "dp"),
        ),
        check_vma=False,
    )
```

```python
import functools

import jax
import jax.numpy as jnp
from jax import lax
from jax.experimental import pallas as pl
from jax.experimental.pallas import tpu as pltpu
from jax.sharding import PartitionSpec as P

HDIM = 64
SHORT = 128
LONG = 256
ROWS = SHORT + LONG
PIECE = 48
PIECES = 14
VEC_ROWS = 24
SEND_SLOTS = 8
MESH = pl.DeviceIdType.MESH
bf16, f32 = jnp.bfloat16, jnp.float32
VMEM_LIMIT = 64 << 20


def dot_nn(a, b):
    return jnp.dot(a, b, preferred_element_type=f32)


def dot_nt(a, b):
    return lax.dot_general(a, b, (((1,), (1,)), ((), ())), preferred_element_type=f32)


def dot_tn(a, b):
    return lax.dot_general(a, b, (((0,), (0,)), ((), ())), preferred_element_type=f32)


def cols(j, width):
    return pl.ds(pl.multiple_of(j * width, width), width)


def step_kernel(
    width, hidden,
    lengths, gains, biases, x_hbm, cot_hbm, wproj_hbm, wo_hbm, wfirst_hbm, wsecond_hbm, win_hbm, wout_hbm,
    out_rows, out_grad, out_own, out_part, out_vec,
    vec, bias_in, wproj, wo, wfirst, wsecond, win, wout, wx,
    xb, up, mem, obuf, hlow, dg, kv, acc, grad, hw, u_self, u_cross, u_ffn, gr, grp, lt, ltp, one_send, one_recv, two_recv, gmem, vg, vbuf, vboth,
    load_sem, wx_send, wx_recv, mem_send, mem_recv, gm_send, gm_recv, gv_send, gv_recv, lt_send, lt_recv, gr_send, gr_recv,
    sem_send, sem_recv, own_sem, io_sem, v_send, v_recv,
):
    st = lax.axis_index("stream")
    me = lax.axis_index("dp")
    z, y, c = me // 4, (me // 2) % 2, me % 2
    is_dec = st == 1
    is_enc = st == 0
    core_id = {"dp": z * 4 + y * 2 + (1 - c)}
    y_id = {"dp": z * 4 + (1 - y) * 2 + c}
    x_id = {"stream": 1 - st}
    tiles = width // 256
    slots = hidden // width

    zh, zl = z // 2, z % 2

    def z_id(other):
        return {"dp": other * 4 + y * 2 + c}
    near_id = z_id(zh * 2 + 1 - zl)
    far_id = z_id((1 - zh) * 2 + zl)
    over_id = {"stream": 1 - st, **far_id}

    def remote(src, dst, ss, rs, dev):
        return pltpu.make_async_remote_copy(
            src_ref=src, dst_ref=dst, send_sem=ss, recv_sem=rs, device_id=dev, device_id_type=MESH)

    loads = [
        pltpu.make_async_copy(src, dst, load_sem.at[i])
        for i, (src, dst) in enumerate((
            (x_hbm, xb), (x_hbm, mem), (wo_hbm, wo), (win_hbm, win), (wout_hbm, wout),
            (wfirst_hbm, wfirst), (wsecond_hbm, wsecond)))
    ]
    cot_load = pltpu.make_async_copy(cot_hbm, up, load_sem.at[7])
    def proj_load(which):
        return pltpu.make_async_copy(wproj_hbm.at[which], wproj.at[which], load_sem.at[9 + which])
    loads[0].start()
    for which in range(3):
        proj_load(which).start()

    barrier = pltpu.get_barrier_semaphore()
    peers = [core_id, y_id, x_id, near_id, far_id, over_id]
    for p in peers:
        pl.semaphore_signal(barrier, inc=1, device_id=p, device_id_type=MESH)

    lens = [lengths[i // 2, 0, i % 2] for i in range(4)]
    own_lens = [jnp.where(is_dec, lens[2 + i], lens[i]) for i in range(2)]
    vec[pl.ds(0, 5), :] = gains[...].astype(f32)
    vec[pl.ds(5, 24), :] = biases[...].astype(f32)
    for i in range(slots):
        for s in range(2):
            bias_in[pl.ds(s, 1), pl.ds(i * width, width)] = vec[pl.ds(9 + 14 * s + i, 1), :]
    vg[...] = jnp.zeros_like(vg)
    half = width // 2
    chunks = width // 4 // PIECE

    def wx_block(yy, zz, cc, h):
        return wx.at[yy, pl.ds((zz * 2 + cc) * chunks * PIECE + h * PIECE, PIECE)]

    def wx_copy(src, dst, k, dev):
        return remote(src, dst, wx_send.at[k], wx_recv.at[k], dev)

    def wx_from(source, h):
        return wx_copy(source.at[pl.ds((zl * 2 + c) * chunks * PIECE + h * PIECE, PIECE)], wx_block(y, zl, c, h), h, x_id)
    wx_in = [wx_from(wfirst_hbm, h) for h in range(chunks)]
    wx_y = [wx_copy(wx_block(y, zl, c, h), wx_block(y, zl, c, h), chunks + h, y_id) for h in range(chunks)]
    wx_z = [wx_copy(wx_block(y, zl, c, h), wx_block(y, zl, c, h), 2 * chunks + h, near_id) for h in range(chunks)]
    wx_on = [wx_copy(wx_block(1 - y, zl, c, h), wx_block(1 - y, zl, c, h), 3 * chunks + h, near_id) if h < chunks // 2 else
             wx_copy(wx_block(y, 1 - zl, c, h), wx_block(y, 1 - zl, c, h), 3 * chunks + h, y_id) for h in range(chunks)]

    def wx_whole(yy, zz):
        return wx.at[yy, pl.ds((zz * 2 + c) * chunks * PIECE, chunks * PIECE)]
    wx_core = [wx_copy(wx_whole(yy, zz), wx_whole(yy, zz), 4 * chunks + k, core_id)
               for k, (yy, zz) in enumerate(((y, zl), (1 - y, zl), (y, 1 - zl), (1 - y, 1 - zl)))]

    def wx_start():
        pl.semaphore_wait(barrier, len(peers))

        @pl.when(is_enc & (y == 0))
        def _():
            for h in range(chunks):
                wx_in[h].start()

        @pl.when(is_enc & (y == 1))
        def _():
            for h in range(chunks):
                wx_from(wsecond_hbm, h).start()
    for cp in loads[2:]:
        cp.start()
    loads[0].wait()

    @pl.when(is_dec)
    def _():
        cot_load.start()

    gain_row = lambda r: pl.ds(r - 2 * st, 1)
    bias_row_of = lambda r: pl.ds(r - 2 - 10 * st, 1)
    lt_copy = [remote(lt.at[i, :, :, :, 1 - c], ltp.at[i], lt_send.at[i], lt_recv.at[i], core_id) for i in range(9)]
    gr_copy = {i: remote(gr.at[i], grp.at[i], gr_send.at[i], gr_recv.at[i], core_id) for i in range(5, 11)}
    buckets = ((0, SHORT), (SHORT, LONG))
    short, long, both = (0,), (1,), (0, 1)

    def span(bs):
        return buckets[bs[0]][0], sum(buckets[b][1] for b in bs)

    def at_rows(bs):
        return pl.ds(*span(bs))
    mem_copy = [remote(xb.at[at_rows((b,))], mem.at[at_rows((b,))], mem_send.at[b], mem_recv.at[b], x_id) for b in range(2)]

    def gm_part(b, h):
        at = cols(h, half)
        return remote(gmem.at[at_rows((b,)), at], up.at[at_rows((b,)), at], gm_send.at[2 * b + h], gm_recv.at[2 * b + h], x_id)
    gv_copy = remote(kv.at[1], gr.at[5], gv_send, gv_recv, x_id)

    gr_first = [remote(gr.at[0, at_rows((b,))], grp.at[0, at_rows((b,))], gr_send.at[11 * b], gr_recv.at[11 * b], core_id)
                for b in range(2)]

    def row_loop(bs, block, body, unroll=1):
        r0, n = span(bs)

        def step(i, carry):
            body(pl.ds(pl.multiple_of(r0 + i * block, block), block))
            return carry
        lax.fori_loop(0, n // block, step, 0, unroll=unroll)

    def vrow(r):
        return vec[pl.ds(r, 1), :]

    def transposed(i, bs, ref):
        r0, n = span(bs)
        lt[i, :, :, :, :, :, pl.ds(r0, n)] = ref[pl.ds(r0, n), :].T.reshape(2, 2, 2, 2, PIECE, n)

    def transposed_slot(bs, j):
        r0, n = span(bs)
        turned = gr[1 + j, pl.ds(r0, n), :].T.reshape(2, 2, 4, PIECE, n)
        for k in range(4):
            lt[k, j // 2, j % 2, :, :, :, pl.ds(r0, n)] = turned[:, :, k]

    def transposed_active(bs):

        def step(j, carry):
            transposed_slot(bs, j)
            return carry
        lax.fori_loop(0, slots, step, 0)

    def col_sum(slot, row):
        def step(i, carry):
            block = slot[pl.ds(pl.multiple_of(i * 64, 64), 64), :].astype(f32)
            return carry + jnp.sum(block.reshape(8, 8, width), axis=0)
        total = lax.fori_loop(0, ROWS // 64, step, jnp.zeros((8, width), f32))
        vg[bias_row_of(row), :] = jnp.sum(total, axis=0, keepdims=True)

    def norm_forward(bs, residual, sum_ref, add_bias, gain, shift, out_low, out_wide):
        def body(rows):
            u = residual[rows, :].astype(f32) + acc[rows, :] + vrow(add_bias)
            sum_ref[rows, :] = u
            centre = u - jnp.mean(u, axis=-1, keepdims=True)
            spread = jnp.mean(centre * centre, axis=-1, keepdims=True)
            h = centre * lax.rsqrt(spread + 1e-05) * vrow(gain) + vrow(shift)
            if out_wide is not None:
                out_wide[rows, :] = h
            out_low[rows, :] = h.astype(bf16)
        row_loop(bs, 32, body, 4)

    def norm_backward(bs, sum_ref, source, gain, shift, out_wide, slot, again=None):
        r0, n = span(bs)

        def step(i, carry):
            rows = pl.ds(pl.multiple_of(r0 + i * 32, 32), 32)
            r = source[rows, :].astype(f32)
            u = sum_ref[rows, :]
            centre = u - jnp.mean(u, axis=-1, keepdims=True)
            spread = jnp.mean(centre * centre, axis=-1, keepdims=True)
            inv = lax.rsqrt(spread + 1e-05)
            uhat = centre * inv
            t = r * vrow(gain)
            gu = (t - jnp.mean(t, axis=-1, keepdims=True) - uhat * jnp.mean(t * uhat, axis=-1, keepdims=True)) * inv
            out_wide[rows, :] = gu
            slot[rows, :] = gu.astype(bf16)
            if again is not None:
                again[rows, :] = gu.astype(bf16)
            return (carry[0] + jnp.sum((r * uhat).reshape(4, 8, width), axis=0),
                    carry[1] + jnp.sum(r.reshape(4, 8, width), axis=0))
        zero = jnp.zeros((8, width), f32)
        total = lax.fori_loop(0, n // 32, step, (zero, zero), unroll=4)
        for row, part in ((gain_row(gain), total[0]), (bias_row_of(shift), total[1])):
            vg[row, :] = vg[row, :] + jnp.sum(part, axis=0, keepdims=True)

    def masked_scores(q_half, k2, n, length, diagonal):
        s = dot_nt(q_half, k2)
        column = lax.broadcasted_iota(jnp.int32, (n, n), 1)
        if diagonal is None:
            return jnp.where(column < length, s, -1e30)
        row = lax.broadcasted_iota(jnp.int32, (n, n), 0)
        return jnp.where((column < length) & (column <= row + diagonal), s, -1e30)

    def softmax(s):
        e = jnp.exp(s - jnp.max(s, axis=-1, keepdims=True))
        return e * (1.0 / jnp.sum(e, axis=-1, keepdims=True))

    def halves(n):
        lane = lax.broadcasted_iota(jnp.int32, (n, 2 * HDIM), 1)
        return lane < HDIM

    def head_loop(bs, body, lo=0, hi=None, more=False):
        pairs = {short: 6 if more else 3, long: 3 if more else 2, both: 1}[bs]

        def step(p, carry):
            body([(b, pl.ds(pl.multiple_of((p * pairs + i) * 2 * HDIM, 2 * HDIM), 2 * HDIM)) for b in bs for i in range(pairs)])
            return carry
        lax.fori_loop(lo, width // (2 * HDIM * pairs) if hi is None else hi, step, 0)

    def attend_forward(bs, q_ref, k_ref, v_ref, lengths_at, diagonal, bias_row, out_ref, lo=0, hi=None):
        def body(units):
            work = []
            for b, at in units:
                r0, n = buckets[b]
                rows = pl.ds(r0, n)
                q2, k2 = q_ref[rows, at], k_ref[rows, at]
                first = halves(n)
                for lanes in (first, ~first):
                    work.append(masked_scores(jnp.where(lanes, q2 * 0.125, jnp.zeros_like(q2)), k2, n, lengths_at[b], diagonal))
            work = [softmax(s).astype(bf16) for s in work]
            work = [dot_nn(prob, v_ref[pl.ds(*buckets[units[i // 2][0]]), units[i // 2][1]]) for i, prob in enumerate(work)]
            for i, (b, at) in enumerate(units):
                r0, n = buckets[b]
                att = jnp.where(halves(n), work[2 * i], work[2 * i + 1])
                if bias_row is not None:
                    att = att + vec[pl.ds(bias_row, 1), at]
                out_ref[pl.ds(r0, n), at] = att.astype(bf16)
        head_loop(bs, body, lo, hi, True)

    def attend_backward(bs, q_ref, k_ref, v_ref, lengths_at, diagonal, lo=0, hi=None):
        scale = HDIM ** -0.5

        def body(units):
            scores, ups = [], []
            for b, at in units:
                r0, n = buckets[b]
                rows = pl.ds(r0, n)
                q2, k2, v2, go2 = q_ref[rows, at], k_ref[rows, at], v_ref[rows, at], obuf[rows, at]
                first = halves(n)
                zero = jnp.zeros_like(q2)
                for lanes in (first, ~first):
                    scores.append(masked_scores(jnp.where(lanes, q2 * 0.125, zero), k2, n, lengths_at[b], diagonal))
                    ups.append(dot_nt(jnp.where(lanes, go2, zero), v2))
            probs = [softmax(s) for s in scores]
            gs = [(p * (gp - jnp.sum(p * gp, axis=-1, keepdims=True))).astype(bf16) for p, gp in zip(probs, ups)]
            results = []
            for i, (b, at) in enumerate(units):
                r0, n = buckets[b]
                rows = pl.ds(r0, n)
                q2, k2, go2 = q_ref[rows, at], k_ref[rows, at], obuf[rows, at]
                first = halves(n)
                two = (2 * i, 2 * i + 1)
                gv = [dot_tn(probs[u].astype(bf16), go2) for u in two]
                gq = [dot_nn(gs[u], k2) for u in two]
                gk = [dot_tn(gs[u], q2) for u in two]
                results.append(((jnp.where(first, gq[0], gq[1]) * scale).astype(bf16),
                                (jnp.where(first, gk[0], gk[1]) * scale).astype(bf16),
                                jnp.where(first, gv[0], gv[1]).astype(bf16)))
            for (b, at), (gq, gk, gv) in zip(units, results):
                rows = pl.ds(*buckets[b])
                q_ref[rows, at] = gq
                k_ref[rows, at] = gk
                v_ref[rows, at] = gv
        head_loop(bs, body, lo, hi)

    q_ref, k_ref, v_ref = gr.at[8], gr.at[9], gr.at[10]
    diagonal = (1 - st) * 4096
    bias_at = 5 + 10 * st
    ffn_at = 13 + 14 * st
    ffn_gain = 1 + 3 * st

    def by_tiles(fn):
        for t in range(tiles):
            fn(pl.ds(t * 256, 256))

    def self_project(bs, wait):
        rows = at_rows(bs)

        def project(which, carry):
            if wait:
                proj_load(which).wait()
            for t in range(tiles):
                at = pl.ds(t * 256, 256)
                value = dot_nn(xb[rows, :], wproj[which, :, at])
                bias = vec[pl.ds(bias_at + which // 2, 1), at] * jnp.where(which == 1, 0.0, 1.0)
                gr[8 + which, rows, at] = (value + bias).astype(bf16)
            return carry
        lax.fori_loop(0, 3, project, 0)

    def self_output(bs):
        rows = at_rows(bs)

        def tile(at):
            acc[rows, at] = dot_nn(obuf[rows, :], wo[:, at])
        by_tiles(tile)
        norm_forward(bs, xb, u_self, bias_at + 2, 2 * st, bias_at + 3, hlow, grad)

    def ffn_forward(bs, residual, wait_in, wait_out, turn=False):
        r0, n = span(bs)
        rows = pl.ds(r0, n)

        def ffn_slot(j, carry):
            for t in range(tiles):
                at = pl.ds(t * 256, 256)
                wide = pl.ds(pl.multiple_of(j * width + t * 256, 256), 256)
                zv = dot_nn(hlow[rows, :], win[:, wide]) + bias_in[pl.ds(st, 1), wide]
                cdf = 0.5 * (1.0 + lax.erf(zv * (0.5 ** 0.5)))
                pdf = jnp.exp(-0.5 * zv * zv) * 0.3989422804014327
                gr[1 + j, rows, at] = (zv * cdf).astype(bf16)
                dg[j, rows, at] = (cdf + zv * pdf).astype(bf16)
            return carry
        if wait_in:
            loads[3].wait()
        lax.fori_loop(0, slots, ffn_slot, 0)

        def ffn_out(at):
            total = dot_nn(gr[1, rows, :], wout[pl.ds(0, width), at])
            for j in range(1, slots):
                total = total + dot_nn(gr[1 + j, rows, :], wout[pl.ds(j * width, width), at])
            acc[rows, at] = total
        if wait_out:
            loads[4].wait()
        by_tiles(ffn_out)
        if turn:
            for j in range(slots):
                transposed_slot(bs, j)
        norm_forward(bs, residual, u_ffn, ffn_at, ffn_gain, ffn_at + 1, xb, None)

    def ffn_inner(bs, lo, hi, last):
        r0, n = span(bs)
        rows = pl.ds(r0, n)

        def ffn_inner_slot(j, carry):
            for t in range(tiles):
                at = pl.ds(t * 256, 256)
                wide = pl.ds(pl.multiple_of(j * width + t * 256, 256), 256)
                value = dot_nt(obuf[rows, :], wout[wide, :])
                gr[1 + j, rows, at] = (value * dg[j, rows, at].astype(f32)).astype(bf16)
            if last:
                remote(gr.at[1 + j], grp.at[1 + j], gr_send.at[1 + j], gr_recv.at[1 + j], core_id).start()
            return carry
        lax.fori_loop(lo, hi, ffn_inner_slot, 0)

    def ffn_input(bs):
        rows = at_rows(bs)

        def tile(at):
            total = grad[rows, at]
            for j in range(slots):
                total = total + dot_nt(gr[1 + j, rows, :], win[at, pl.ds(j * width, width)])
            grad[rows, at] = total
        by_tiles(tile)

    def cross_forward(bs):
        rows = at_rows(bs)

        def memory_kv(which, carry):
            for t in range(tiles):
                at = pl.ds(t * 256, 256)
                value = dot_nn(mem[rows, :], wx[which, :, at])
                kv[which, rows, at] = value.astype(bf16)
            return carry
        lax.fori_loop(0, 2, memory_kv, 0)
        attend_forward(bs, gr.at[6], kv.at[0], kv.at[1], lens[:2], None, 20, obuf)

        def cross_out(at):
            acc[rows, at] = dot_nn(obuf[rows, :], wsecond[:, at])
        by_tiles(cross_out)
        norm_forward(bs, grad, u_cross, 21, 3, 22, hlow, hw)
        transposed(7, bs, obuf)

    def cross_branch():
        norm_backward(both, u_cross, grad, 3, 22, hw, gr.at[5])

        def cross_up(at):
            obuf[:, at] = dot_nt(gr[5], wsecond[at, :]).astype(bf16)
        by_tiles(cross_up)

    def cross_backward(bs):
        rows = at_rows(bs)
        attend_backward(bs, gr.at[6], kv.at[0], kv.at[1], lens[:2], None)

        def memory_half(h, carry):
            at = cols(h, half)
            gmem[rows, at] = (dot_nt(kv[0, rows, :], wx[0, at, :]) + dot_nt(kv[1, rows, :], wx[1, at, :])).astype(bf16)
            gm_part(bs[0], h).start()
            return carry
        lax.fori_loop(0, 2, memory_half, 0)

    def cross_input(at):
        grad[:, at] = hw[:, at] + dot_nt(gr[6], wfirst[at, :])

    def lanes_of(h):
        return pl.ds(0, width) if h is None else cols(h, half)

    def unit(i, h):
        return i if h is None else 15 + 2 * (i - 12) + h

    def sems(i, stage, h):
        return sem_send.at[unit(i, h), stage], sem_recv.at[unit(i, h), stage]

    def first_copy(i, z_first, h):
        at = lanes_of(h)
        return remote(one_send.at[i % SEND_SLOTS, :, :, :, at], one_recv.at[i, :, :, :, at], *sems(i, 0, h),
                      near_id if z_first else y_id)

    def second_copy(i, z_first, h):
        at = lanes_of(h)
        source = one_recv.at[i, 1 - zh, :, :, at] if z_first else one_recv.at[i, :, 1 - zl, :, at]
        return remote(source, two_recv.at[i, :, :, at], *sems(i, 1, h), far_id if z_first else near_id)

    def third_copy(i, z_first, h):
        at = lanes_of(h)
        source = two_recv.at[i, 1 - y if z_first else 1 - zh, :, at]
        return remote(source, out_part.at[i, :, at], *sems(i, 2, h), y_id if z_first else far_id)

    def own_copy(i, z_first, h):
        at = lanes_of(h)
        return pltpu.make_async_copy(two_recv.at[i, y if z_first else zh, :, at], out_own.at[i, :, at], own_sem.at[unit(i, h)])

    def product(left, slot, z_first, other, at):
        if z_first:
            zz = 1 - zl if other else zl
            mine, theirs = lt[left, :, zz, :, c], ltp[left, :, zz]
        else:
            yy = 1 - y if other else y
            mine, theirs = lt[left, :, :, yy, c], ltp[left, :, :, yy]
        shape = (4 * PIECE, ROWS)
        return dot_nn(mine.reshape(shape), gr[slot, :, at]) + dot_nn(theirs.reshape(shape), grp[slot, :, at])

    def piece_tiles(h, fn):
        if h is None:
            loop(0, tiles, lambda t: fn(cols(t, 256), 256))
        else:
            fn(cols(h, half), half)

    def send_piece(i, left, slot, z_first=False, h=None):
        def tile(at, n):
            one_send[i % SEND_SLOTS, :, :, :, at] = product(left, slot, z_first, True, at).astype(bf16).reshape(2, 2, PIECE, n)
        piece_tiles(h, tile)
        first_copy(i, z_first, h).start()

    def keep_piece(i, left, slot, z_first=False, h=None):
        first_copy(i, z_first, h).wait()

        def tile(at, n):
            total = one_recv[i, :, :, :, at].reshape(4 * PIECE, n).astype(f32) + product(left, slot, z_first, False, at)
            one_recv[i, :, :, :, at] = total.astype(bf16).reshape(2, 2, PIECE, n)
        piece_tiles(h, tile)
        second_copy(i, z_first, h).start()

    def merge_piece(i, z_first=False, h=None):
        second_copy(i, z_first, h).wait()
        at = lanes_of(h)
        for k in range(2):
            mine = one_recv[i, zh, k, :, at] if z_first else one_recv[i, k, zl, :, at]
            two_recv[i, k, :, at] = (two_recv[i, k, :, at].astype(f32) + mine.astype(f32)).astype(bf16)

    def pass_piece(i, z_first=False, h=None):
        merge_piece(i, z_first, h)
        third_copy(i, z_first, h).start()
        own_copy(i, z_first, h).start()

    extra = PIECES
    extra_part = remote(two_recv.at[extra, 1 - zh], out_part.at[13], sem_send.at[extra, 2], sem_recv.at[13, 2], over_id)
    extra_own = remote(two_recv.at[extra, zh], out_own.at[13], sem_send.at[13, 0], sem_recv.at[13, 0], x_id)
    extra_left = remote(lt.at[0, :, :, :, 1 - c], ltp.at[0], lt_send.at[0], lt_recv.at[0], core_id)
    extra_right = remote(gr.at[0], grp.at[0], gr_send.at[0], gr_recv.at[0], core_id)

    def loop(lo, hi, fn):
        def step(i, carry):
            fn(i)
            return carry
        lax.fori_loop(lo, hi, step, 0)

    def wait_active():
        for i in range(4):
            lt_copy[i].wait()
        gr_first[0].wait()
        gr_first[1].wait()

    @pl.when(is_enc)
    def _():
        again = loads[1]
        again.start()
        for bs in (long, short):
            self_project(bs, bs == long)
            if bs == long:
                wx_start()
            attend_forward(bs, q_ref, k_ref, v_ref, own_lens, None, None, obuf)
            if bs == long:
                loads[2].wait()
            self_output(bs)
            ffn_forward(bs, grad, bs == long, bs == long)
            mem_copy[bs[0]].start()
        transposed_active(both)
        for k in range(4):
            lt_copy[k].start()
        again.wait()
        for i, ref in ((4, mem), (5, obuf), (6, hlow), (7, xb)):
            transposed(i, both, ref)
            lt_copy[i].start()
        loads[5].wait()
        loads[6].wait()
        for bs in (short, long):
            for h in range(2):
                gm_part(bs[0], h).wait_recv()
            norm_backward(bs, u_ffn, up, ffn_gain, ffn_at + 1, grad, gr.at[0], obuf)
            gr_first[bs[0]].start()
            if bs == short:
                ffn_inner(bs, 0, slots, False)
                ffn_input(bs)
        ffn_inner(long, 0, 1, True)

    @pl.when(is_dec)
    def _():
        self_project(both, True)
        wx_start()
        transposed(4, both, xb)
        lt_copy[4].start()

        def wx_forward(h):
            wx_in[h].wait_recv()
            wx_y[h].start()
            wx_z[h].start()
        attend_forward(both, q_ref, k_ref, v_ref, own_lens, diagonal, None, obuf, 0, 3)
        wx_forward(0)
        attend_forward(both, q_ref, k_ref, v_ref, own_lens, diagonal, None, obuf, 3, 6)
        wx_forward(1)
        loads[2].wait()
        self_output(both)
        wx_forward(2)
        wx_y[0].wait()
        wx_on[0].start()
        loads[5].wait()

        def cross_query(at):
            gr[6, :, at] = (dot_nn(hlow[...], wfirst[:, at]) + vec[pl.ds(19, 1), at]).astype(bf16)
        by_tiles(cross_query)
        wx_forward(3)
        wx_core[0].start()
        transposed(5, both, obuf)
        lt_copy[5].start()
        transposed(8, both, hlow)
        lt_copy[8].start()
        loads[6].wait()
        cot_load.wait()
        wx_y[1].wait()
        wx_on[1].start()
        wx_z[0].wait()
        wx_z[1].wait()
        wx_z[2].wait()
        wx_on[2].start()
        wx_y[2].wait()
        wx_z[3].wait()
        wx_on[3].start()
        wx_y[3].wait()
        wx_core[1].start()
        wx_core[2].start()
        for h in range(chunks):
            wx_on[h].wait()
        wx_core[3].start()
        for k in range(4):
            wx_core[k].wait()
        for bs in (long, short):
            mem_copy[bs[0]].wait_recv()
            cross_forward(bs)
        lt_copy[7].start()
        ffn_forward(both, hw, True, True, True)
        for k in range(4):
            lt_copy[k].start()
        norm_backward(both, u_ffn, up, ffn_gain, ffn_at + 1, grad, gr.at[0], obuf)
        gr_first[0].start()
        gr_first[1].start()
        ffn_inner(both, 0, slots, True)
        ffn_input(both)
        cross_branch()
        for bs in (short, long):
            cross_backward(bs)
        transposed(6, both, hlow)
        lt_copy[6].start()

    wait_active()

    def first_sends(k):
        send_piece(2 + k, 2 + k, 0)
        send_piece(k, k, 0, True)
    loop(0, 2, first_sends)

    @pl.when(is_enc)
    def _():
        ffn_inner(long, 1, slots, True)
    lt_copy[6].wait()

    def inner_sends(j):
        remote(gr.at[1 + j], grp.at[1 + j], gr_send.at[1 + j], gr_recv.at[1 + j], core_id).wait()
        send_piece(4 + j, 6, 1 + j)
    loop(0, slots, inner_sends)

    @pl.when(is_enc)
    def _():
        ffn_input(long)

    @pl.when(is_dec)
    def _():
        gr_copy[5].start()
        gr_copy[6].start()
        by_tiles(cross_input)
        col_sum(obuf, 20)
        col_sum(gr.at[6], 19)
        col_sum(gr.at[5], 21)

    rows_copy = pltpu.make_async_copy(xb, out_rows, io_sem.at[0])
    rows_copy.start()

    norm_backward(both, u_self, grad, 2 * st, bias_at + 3, hw, gr.at[7])
    gr_copy[7].start()

    def self_up(at):
        obuf[:, at] = dot_nt(gr[7], wo[at, :]).astype(bf16)
    by_tiles(self_up)

    def keep_and_attend(k, carry):
        keep_piece(2 + k, 2 + k, 0)
        keep_piece(k, k, 0, True)
        attend_backward(both, q_ref, k_ref, v_ref, own_lens, diagonal, k * 3, k * 3 + 3)
        return carry
    lax.fori_loop(0, 2, keep_and_attend, 0)
    for j in range(3):
        gr_copy[8 + j].start()

    @pl.when(is_dec)
    def _():
        gv_copy.start()

    def self_input(at):
        total = hw[:, at]
        for j in range(3):
            total = total + dot_nt(gr[8 + j], wproj[j, at, :])
        hw[:, at] = total
    by_tiles(self_input)
    grad_copy = pltpu.make_async_copy(hw, out_grad, io_sem.at[1])
    grad_copy.start()
    loop(2, 4, pass_piece)
    for i in (4, 5, 7):
        lt_copy[i].wait()

    @pl.when(is_dec)
    def _():
        lt_copy[8].wait()
    for i in range(7, 11):
        gr_copy[i].wait()
    col_sum(gr.at[0], ffn_at)
    loop(0, slots, lambda j: col_sum(gr.at[1 + j], ffn_at - 4 + j))
    col_sum(gr.at[7], bias_at + 2)
    col_sum(gr.at[8], bias_at)
    col_sum(gr.at[10], bias_at + 1)
    own_half = pl.ds(pl.multiple_of(c * half, half), half)
    other_half = pl.ds(pl.multiple_of((1 - c) * half, half), half)
    v_copy = [remote(vg.at[:, other_half] if k == 0 else vbuf.at[2 * k], vbuf.at[2 * k + 1], v_send.at[k], v_recv.at[k], dev)
              for k, dev in enumerate((core_id, y_id, near_id, far_id, x_id))]
    v_last = remote(vboth.at[:, :, own_half], vboth.at[:, :, own_half], v_send.at[5], v_recv.at[5], core_id)
    vbuf[0] = vg[:, own_half]

    @pl.when(is_dec)
    def _():
        transposed(0, both, mem)
        extra_left.start()
        gr[0] = kv[0]
        extra_right.start()

    def v_next(k):
        v_copy[k].wait()
        vbuf[2 * k + 2] = vbuf[2 * k] + vbuf[2 * k + 1]
        v_copy[k + 1].start()
    v_copy[0].start()
    v_next(0)

    def attention_piece(k):
        return 8 + k, 5 - (k + 3) // 4, 7 + k

    def cross_piece(k):
        return 12 + k // 2, 7 + st * (k // 2), 5 + k // 2, False, k % 2

    def middle(k):
        send_piece(*attention_piece(k))
        keep_piece(4 + k, 6, 1 + k)

        @pl.when(k > 0)
        def _():
            pass_piece(3 + k)
    loop(0, 4, middle)

    @pl.when(is_enc)
    def _():
        gv_copy.wait_recv()
        gr_copy[5].start()

    @pl.when(is_dec)
    def _():
        extra_left.wait()
        extra_right.wait()
        send_piece(extra, 0, 0)
        gr_copy[6].wait()
    v_next(1)
    cross_units = 2 + 2 * st

    def later(k):
        keep_piece(*attention_piece(k))

        @pl.when(k == 0)
        def _():
            gr_copy[5].wait()
            loop(0, cross_units, lambda k: send_piece(*cross_piece(k)))
        pass_piece(7 + k)
    loop(0, 4, later)

    @pl.when(is_dec)
    def _():
        keep_piece(extra, 0, 0)
    v_next(2)
    loop(0, 2, lambda i: pass_piece(i, True))

    def ends(k):
        i, left, slot, z_first, h = cross_piece(k)
        keep_piece(i, left, slot, z_first, h)

        @pl.when(k == 0)
        def _():
            pass_piece(11)

        @pl.when(k > 0)
        def _():
            pass_piece(12 + (k - 1) // 2, False, (k + 1) % 2)

        @pl.when(k == 1)
        def _():
            v_next(3)

        @pl.when(is_dec & (k == 1))
        def _():
            merge_piece(extra)
            extra_part.start()
            extra_own.start()
    loop(0, cross_units, ends)
    pass_piece(12 + st, False, 1)
    v_copy[4].wait()
    vboth[st, :, own_half] = vbuf[8]
    vboth[1 - st, :, own_half] = vbuf[9]
    v_last.start()
    v_last.wait()
    vec_copy = pltpu.make_async_copy(vboth, out_vec, io_sem.at[2])
    vec_copy.start()

    def finish(i, z_first=False, h=None):
        third_copy(i, z_first, h).wait()
        own_copy(i, z_first, h).wait()
    loop(0, 2, lambda i: finish(i, True))
    loop(2, 12, finish)
    loop(0, cross_units, lambda k: finish(12 + k // 2, False, k % 2))
    rows_copy.wait()
    grad_copy.wait()
    vec_copy.wait()

    @pl.when(is_enc)
    def _():
        for h in range(chunks):
            wx_in[h].wait_send()
        for h in range(2):
            mem_copy[h].wait_send()
        extra_part.wait_recv()
        extra_own.wait_recv()

    @pl.when(is_dec)
    def _():
        for h in range(2):
            for b in range(2):
                gm_part(b, h).wait_send()
        gv_copy.wait_send()
        extra_part.wait_send()
        extra_own.wait_send()


def last_kernel(width, rows_in, grad_in, own, parts, vec_sum, rows_out, grad_out, *refs):
    outs, (vec_buf, rows_buf, grad_buf, own_buf, part_buf, sums, in_sem, through_sem, out_sem) = refs[:8], refs[8:]
    group = PIECES // 2
    loads = []
    for g in range(2):
        at = pl.ds(g * group, group)
        loads.append((pltpu.make_async_copy(own.at[at], own_buf.at[at], in_sem.at[g, 0]),
                      pltpu.make_async_copy(parts.at[at], part_buf.at[at], in_sem.at[g, 1])))
    vec_load = pltpu.make_async_copy(vec_sum, vec_buf, through_sem.at[2])
    into = [pltpu.make_async_copy(grad_in, grad_buf, through_sem.at[0]), pltpu.make_async_copy(rows_in, rows_buf, through_sem.at[1])]
    for cp in (*loads[0], into[0], *loads[1], into[1], vec_load):
        cp.start()
    stores = []

    def store(src, dst):
        stores.append(pltpu.make_async_copy(src, dst, out_sem.at[len(stores)]))
        stores[-1].start()
    for g in range(2):
        for cp in loads[g]:
            cp.wait()
        for i in range(g * group, (g + 1) * group):
            sums[i] = own_buf[i].astype(f32) + part_buf[i].astype(f32)
            if i < 4:
                store(sums.at[i], outs[0].at[pl.ds(i * PIECE, PIECE), :])
            elif i < 8:
                store(sums.at[i], outs[1].at[:, pl.ds((i - 4) * width, width)])
            elif i == 8:
                store(sums.at[i], outs[4])
            elif i == 11:
                store(sums.at[pl.ds(9, 3)], outs[5])
            elif i > 11:
                store(sums.at[i], outs[i - 10])
        into[g].wait()
        store(rows_buf if g else grad_buf, rows_out if g else grad_out)
    vec_load.wait()
    shift = lax.rem(width - lax.axis_index("dp") * PIECE, width)
    for s, (g0, g1, b0, b1) in enumerate(((0, 2, 0, 10), (2, 5, 10, 24))):
        turned = pltpu.roll(vec_buf[s], shift, 1)
        outs[6][pl.ds(g0, g1 - g0), :] = turned[:g1 - g0, :PIECE]
        outs[7][pl.ds(b0, b1 - b0), :] = turned[3:3 + b1 - b0, :PIECE]
    for cp in stores:
        cp.wait()


def whole_step(lengths, gains, biases, x, cot, wproj, wo, wfirst, wsecond, win, wout):
    width = x.shape[1]
    hidden = win.shape[1]
    half = width // 2
    any_space = pl.BlockSpec(memory_space=pl.ANY)
    vmem = pl.BlockSpec(memory_space=pltpu.VMEM)
    dma = pltpu.SemaphoreType.DMA
    slots = hidden // width
    small = (32, width)
    results = pl.pallas_call(
        functools.partial(step_kernel, width, hidden),
        out_shape=[
            jax.ShapeDtypeStruct((ROWS, width), bf16),
            jax.ShapeDtypeStruct((ROWS, width), f32),
            jax.ShapeDtypeStruct((PIECES, PIECE, width), bf16),
            jax.ShapeDtypeStruct((PIECES, PIECE, width), bf16),
            jax.ShapeDtypeStruct((2, VEC_ROWS, width), f32),
        ],
        in_specs=[pl.BlockSpec(memory_space=pltpu.SMEM), vmem, vmem] + [any_space] * 8,
        out_specs=[any_space] * 5,
        scratch_shapes=[
            pltpu.VMEM(small, f32), pltpu.VMEM((2, hidden), f32),
            pltpu.VMEM(wproj.shape, bf16), pltpu.VMEM(wo.shape, bf16), pltpu.VMEM(wfirst.shape, bf16),
            pltpu.VMEM(wsecond.shape, bf16), pltpu.VMEM(win.shape, bf16), pltpu.VMEM(wout.shape, bf16),
            pltpu.VMEM((2, width, width), bf16),
            pltpu.VMEM((ROWS, width), bf16),
            pltpu.VMEM((ROWS, width), bf16),
            pltpu.VMEM((ROWS, width), bf16),
            pltpu.VMEM((ROWS, width), bf16),
            pltpu.VMEM((ROWS, width), bf16),
            pltpu.VMEM((slots, ROWS, width), bf16),
            pltpu.VMEM((2, ROWS, width), bf16),
            pltpu.VMEM((ROWS, width), f32),
            pltpu.VMEM((ROWS, width), f32),
            pltpu.VMEM((ROWS, width), f32),
            pltpu.VMEM((ROWS, width), f32),
            pltpu.VMEM((ROWS, width), f32),
            pltpu.VMEM((ROWS, width), f32),
            pltpu.VMEM((11, ROWS, width), bf16),
            pltpu.VMEM((11, ROWS, width), bf16),
            pltpu.VMEM((9, 2, 2, 2, 2, PIECE, ROWS), bf16),
            pltpu.VMEM((9, 2, 2, 2, PIECE, ROWS), bf16),
            pltpu.VMEM((SEND_SLOTS, 2, 2, PIECE, width), bf16),
            pltpu.VMEM((PIECES + 1, 2, 2, PIECE, width), bf16),
            pltpu.VMEM((PIECES + 1, 2, PIECE, width), bf16),
            pltpu.VMEM((ROWS, width), bf16),
            pltpu.VMEM((VEC_ROWS, width), f32),
            pltpu.VMEM((10, VEC_ROWS, half), f32),
            pltpu.VMEM((2, VEC_ROWS, width), f32),
            dma((12,)), dma((20,)), dma((20,)), dma((2,)), dma((2,)), dma((4,)), dma((4,)), dma, dma,
            dma((9,)), dma((9,)), dma((12,)), dma((12,)),
            dma((19, 3)), dma((19, 3)), dma((19,)), dma((3,)), dma((6,)), dma((6,)),
        ],
        compiler_params=pltpu.CompilerParams(collective_id=0, has_side_effects=True, vmem_limit_bytes=VMEM_LIMIT),
        name="step",
    )(lengths, gains, biases, x, cot, wproj, wo, wfirst, wsecond, win, wout)
    shapes = [(4 * PIECE, width), (PIECE, hidden), (PIECE, width), (PIECE, width), (PIECE, width), (3, PIECE, width),
              (5, PIECE), (24, PIECE)]
    return pl.pallas_call(
        functools.partial(last_kernel, width),
        out_shape=[jax.ShapeDtypeStruct((ROWS, width), bf16), jax.ShapeDtypeStruct((ROWS, width), f32)]
        + [jax.ShapeDtypeStruct(shape, f32) for shape in shapes],
        in_specs=[any_space] * 5,
        out_specs=[any_space] * 8 + [vmem] * 2,
        scratch_shapes=[
            pltpu.VMEM((2, VEC_ROWS, width), f32), pltpu.VMEM((ROWS, width), bf16), pltpu.VMEM((ROWS, width), f32),
            pltpu.VMEM((PIECES, PIECE, width), bf16), pltpu.VMEM((PIECES, PIECE, width), bf16),
            pltpu.VMEM((PIECES, PIECE, width), f32), dma((2, 2)), dma((3,)), dma((PIECES + 2,)),
        ],
        compiler_params=pltpu.CompilerParams(vmem_limit_bytes=VMEM_LIMIT),
        name="last",
    )(*results)


eps_norm = 1e-05
low_type = jnp.bfloat16
wide_type = jnp.float32


def as_sent(shard):
    return jax.tree.map(lambda a: a.astype(jnp.bfloat16) if a.dtype == jnp.float32 else a, shard)


def shifted(shard, axis, by):
    count = lax.axis_size(axis)
    pairs = [(i, i + by) for i in range(count) if 0 <= i + by < count]
    return lax.ppermute(shard, axis, pairs)


def matmul(left_mat, right_mat):
    return jnp.dot(left_mat, right_mat, preferred_element_type=wide_type)


def matmul_tn(left_mat, right_mat):
    return lax.dot_general(
        left_mat, right_mat, (((0,), (0,)), ((), ())), preferred_element_type=wide_type
    )


def matmul_nt(left_mat, right_mat):
    return lax.dot_general(
        left_mat, right_mat, (((1,), (1,)), ((), ())), preferred_element_type=wide_type
    )


def column_sum(tensor):
    return jnp.sum(tensor.astype(wide_type), axis=0)


def norm_rows(tensor, norm_gain, norm_shift):
    centre = tensor - jnp.mean(tensor, axis=-1, keepdims=True)
    spread = jnp.mean(centre * centre, axis=-1, keepdims=True)
    return centre * lax.rsqrt(spread + eps_norm) * norm_gain + norm_shift


def norm_back(tensor, norm_gain, norm_shift, upstream):
    unused, pullback = jax.vjp(norm_rows, tensor, norm_gain, norm_shift)
    return pullback(upstream)


def gelu_exact(tensor):
    return jax.nn.gelu(tensor, approximate=False)


def key_mask(row_count, key_count, length, causal):
    columns = lax.broadcasted_iota(jnp.int32, (row_count, key_count), 1)
    allowed = columns < length
    if causal:
        allowed = allowed & (columns <= lax.broadcasted_iota(jnp.int32, (row_count, key_count), 0))
    return allowed


def split_heads(tensor):
    return tensor.reshape(tensor.shape[0], -1, HDIM)


def attend_scores(queries, key_rows, allowed):
    scores = jnp.einsum(
        "qhd,khd->hqk",
        split_heads(queries),
        split_heads(key_rows),
        preferred_element_type=wide_type,
    )
    return jnp.where(allowed[None], scores * HDIM ** (-0.5), -1e30)


def attend_forward(queries, key_rows, values, allowed):
    scores = attend_scores(queries, key_rows, allowed)
    row_max = jnp.max(scores, axis=-1, keepdims=True)
    log_total = row_max + jnp.log(jnp.sum(jnp.exp(scores - row_max), axis=-1, keepdims=True))
    softmaxed = jnp.exp(scores - log_total).astype(low_type)
    attended = jnp.einsum(
        "hqk,khd->qhd", softmaxed, split_heads(values), preferred_element_type=wide_type
    )
    return (attended.reshape(queries.shape[0], -1), log_total)


def attend_backward(queries, key_rows, values, allowed, log_total, upstream):
    softmaxed = jnp.exp(attend_scores(queries, key_rows, allowed) - log_total)
    grad_heads = split_heads(upstream)
    grad_values = jnp.einsum(
        "hqk,qhd->khd", softmaxed.astype(low_type), grad_heads, preferred_element_type=wide_type
    )
    grad_probs = jnp.einsum(
        "qhd,khd->hqk", grad_heads, split_heads(values), preferred_element_type=wide_type
    )
    grad_scores = (
        softmaxed * (grad_probs - jnp.sum(softmaxed * grad_probs, axis=-1, keepdims=True))
    ).astype(low_type)
    scale_factor = HDIM ** (-0.5)
    grad_queries = (
        jnp.einsum(
            "hqk,khd->qhd", grad_scores, split_heads(key_rows), preferred_element_type=wide_type
        )
        * scale_factor
    )
    grad_keys = (
        jnp.einsum(
            "hqk,qhd->khd", grad_scores, split_heads(queries), preferred_element_type=wide_type
        )
        * scale_factor
    )
    key_count = key_rows.shape[0]
    return (
        grad_queries.reshape(queries.shape[0], -1),
        grad_keys.reshape(key_count, -1),
        grad_values.reshape(key_count, -1),
    )


def self_forward(row_block, length, causal, w_proj, w_out, vectors):
    bias_q, bias_v, bias_o, norm_gain, norm_shift = vectors
    row_count = row_block.shape[0]
    offsets = jnp.stack([bias_q, jnp.zeros_like(bias_q), bias_v])[:, None, :]
    projected = (
        jnp.einsum("rd,cde->cre", row_block, w_proj, preferred_element_type=wide_type) + offsets
    ).astype(low_type)
    allowed = key_mask(row_count, row_count, length, causal)
    attended, log_total = attend_forward(projected[0], projected[1], projected[2], allowed)
    attended = attended.astype(low_type)
    summed = row_block.astype(wide_type) + matmul(attended, w_out) + bias_o
    return (norm_rows(summed, norm_gain, norm_shift), (projected, log_total, attended, summed))


def self_backward(row_block, length, causal, w_proj, w_out, vectors, saved_fwd, upstream):
    projected, log_total, attended, summed = saved_fwd
    row_count = row_block.shape[0]
    grad_sum, grad_gain, grad_shift = norm_back(summed, vectors[3], vectors[4], upstream)
    grad_branch = grad_sum.astype(low_type)
    grad_attended = matmul_nt(grad_branch, w_out).astype(low_type)
    allowed = key_mask(row_count, row_count, length, causal)
    grad_q, grad_k, grad_v = attend_backward(
        projected[0], projected[1], projected[2], allowed, log_total, grad_attended
    )
    grad_proj = jnp.stack([grad_q, grad_k, grad_v]).astype(low_type)
    grad_rows = grad_sum + jnp.einsum(
        "cre,cde->rd", grad_proj, w_proj, preferred_element_type=wide_type
    )
    weight_grads = (
        jnp.einsum("rd,cre->cde", row_block, grad_proj, preferred_element_type=wide_type),
        matmul_tn(attended, grad_branch),
    )
    vector_grads = (
        column_sum(grad_proj[0]),
        column_sum(grad_proj[2]),
        column_sum(grad_branch),
        grad_gain,
        grad_shift,
    )
    return (grad_rows, weight_grads, vector_grads)


def ffn_forward(hidden, w_in, w_out, vectors):
    bias_in, bias_out, norm_gain, norm_shift = vectors
    low_hidden = hidden.astype(low_type)
    inner_act = matmul(low_hidden, w_in) + bias_in
    active = gelu_exact(inner_act).astype(low_type)
    summed = hidden + matmul(active, w_out) + bias_out
    return (norm_rows(summed, norm_gain, norm_shift), (low_hidden, inner_act, active, summed))


def ffn_backward(w_in, w_out, vectors, saved_fwd, upstream):
    low_hidden, inner_act, active, summed = saved_fwd
    grad_sum, grad_gain, grad_shift = norm_back(summed, vectors[2], vectors[3], upstream)
    grad_branch = grad_sum.astype(low_type)
    unused, pullback = jax.vjp(gelu_exact, inner_act)
    grad_inner = pullback(matmul_nt(grad_branch, w_out))[0].astype(low_type)
    grad_hidden = grad_sum + matmul_nt(grad_inner, w_in)
    weight_grads = (matmul_tn(low_hidden, grad_inner), matmul_tn(active, grad_branch))
    vector_grads = (column_sum(grad_inner), column_sum(grad_branch), grad_gain, grad_shift)
    return (grad_hidden, weight_grads, vector_grads)


def cross_forward(hidden, memory, src_len, w_query, w_out, vectors):
    bias_q, bias_v, bias_o, norm_gain, norm_shift = vectors
    low_hidden = hidden.astype(low_type)
    queries = (matmul(low_hidden, w_query) + bias_q).astype(low_type)
    allowed = key_mask(hidden.shape[0], memory.shape[1], src_len, False)
    attended, log_total = attend_forward(queries, memory[0], memory[1], allowed)
    attended = (attended + bias_v).astype(low_type)
    summed = hidden + matmul(attended, w_out) + bias_o
    return (
        norm_rows(summed, norm_gain, norm_shift),
        (low_hidden, queries, log_total, attended, summed),
    )


def cross_backward(memory, src_len, w_query, w_out, vectors, saved_fwd, upstream):
    low_hidden, queries, log_total, attended, summed = saved_fwd
    grad_sum, grad_gain, grad_shift = norm_back(summed, vectors[3], vectors[4], upstream)
    grad_branch = grad_sum.astype(low_type)
    grad_attended = matmul_nt(grad_branch, w_out).astype(low_type)
    allowed = key_mask(queries.shape[0], memory.shape[1], src_len, False)
    grad_q, grad_k, grad_v = attend_backward(
        queries, memory[0], memory[1], allowed, log_total, grad_attended
    )
    grad_query = grad_q.astype(low_type)
    grad_memory = jnp.stack([grad_k, grad_v]).astype(low_type)
    grad_hidden = grad_sum + matmul_nt(grad_query, w_query)
    weight_grads = (matmul_tn(low_hidden, grad_query), matmul_tn(attended, grad_branch))
    vector_grads = (
        column_sum(grad_query),
        column_sum(grad_attended),
        column_sum(grad_branch),
        grad_gain,
        grad_shift,
    )
    return (grad_hidden, grad_memory, weight_grads, vector_grads)


def self_vectors(gain_rows, bias_rows, decoder):
    base_row = 10 if decoder else 0
    gain_row = 2 if decoder else 0
    return (
        bias_rows[base_row],
        bias_rows[base_row + 1],
        bias_rows[base_row + 2],
        gain_rows[gain_row],
        bias_rows[base_row + 3],
    )


def ffn_vectors(gain_rows, bias_rows, decoder):
    base_row = 18 if decoder else 4
    gain_row = 4 if decoder else 1
    return (
        bias_rows[base_row : base_row + 4].reshape(-1),
        bias_rows[base_row + 4],
        gain_rows[gain_row],
        bias_rows[base_row + 5],
    )


def cross_vectors(gain_rows, bias_rows):
    return (bias_rows[14], bias_rows[15], bias_rows[16], gain_rows[3], bias_rows[17])


def self_plan(decoder, vector_grads):
    base_row = 10 if decoder else 0
    gain_row = 2 if decoder else 0
    return (
        ("biases", base_row, vector_grads[0]),
        ("biases", base_row + 1, vector_grads[1]),
        ("biases", base_row + 2, vector_grads[2]),
        ("gains", gain_row, vector_grads[3]),
        ("biases", base_row + 3, vector_grads[4]),
    )


def ffn_plan(decoder, vector_grads):
    base_row = 18 if decoder else 4
    gain_row = 4 if decoder else 1
    return (
        ("biases", base_row, vector_grads[0]),
        ("biases", base_row + 4, vector_grads[1]),
        ("gains", gain_row, vector_grads[2]),
        ("biases", base_row + 5, vector_grads[3]),
    )


def cross_plan(vector_grads):
    return (
        ("biases", 14, vector_grads[0]),
        ("biases", 15, vector_grads[1]),
        ("biases", 16, vector_grads[2]),
        ("gains", 3, vector_grads[3]),
        ("biases", 17, vector_grads[4]),
    )


def accumulate(totals, weight_names, weight_grads, vector_plan):
    merged = dict(totals)
    for key_name, tensor in zip(weight_names, weight_grads):
        merged[key_name] = merged[key_name] + tensor
    for table_name, row_at, tensor in vector_plan:
        table_now = merged[table_name]
        row_block = tensor.reshape(-1, table_now.shape[1])
        merged[table_name] = table_now.at[row_at : row_at + row_block.shape[0]].add(row_block)
    return merged


def updated(progress, key_name, position, tensor):
    copied = dict(progress)
    copied[key_name] = [
        tensor if slot_index == position else entry_now
        for slot_index, entry_now in enumerate(progress[key_name])
    ]
    return copied


def with_totals(progress, totals):
    copied = dict(progress)
    copied["totals"] = totals
    return copied


def forward_pass(tensor):
    return jax.tree.map(
        lambda part, own: part.astype(own.dtype), shifted(as_sent(tensor), "stream", 1), tensor
    )


def backward_pass(tensor):
    return jax.tree.map(
        lambda part, own: part.astype(own.dtype), shifted(as_sent(tensor), "stream", -1), tensor
    )


def keep_same(progress):
    return progress


def plain_body(
    inputs,
    lengths,
    cotangent,
    attn_in,
    attn_out,
    cross_first,
    cross_second,
    ffn_in,
    ffn_out,
    gains,
    biases,
):
    own_rows = inputs[0]
    model_width = own_rows.shape[1]
    hidden_width = ffn_in.shape[2]
    head_count = model_width // HDIM
    row_sizes = (SHORT, LONG)
    bucket_spans = ((0, SHORT), (SHORT, SHORT + LONG))
    row_pieces = [own_rows[start_row:stop_row] for start_row, stop_row in bucket_spans]
    grad_pieces = [
        cotangent[start_row:stop_row].astype(wide_type) for start_row, stop_row in bucket_spans
    ]
    src_lens = [lengths[0, 0, bucket_idx] for bucket_idx in range(2)]
    tgt_lens = [lengths[1, 0, bucket_idx] for bucket_idx in range(2)]
    w_proj = attn_in[0]
    w_attn_out = attn_out[0]
    w_first = cross_first[0]
    w_second = cross_second[0]
    w_ffn_in = ffn_in[0]
    w_ffn_out = ffn_out[0]
    gain_rows = gains.astype(wide_type)
    bias_rows = biases.astype(wide_type)
    enc_self = self_vectors(gain_rows, bias_rows, False)
    enc_ffn = ffn_vectors(gain_rows, bias_rows, False)
    dec_self = self_vectors(gain_rows, bias_rows, True)
    dec_ffn = ffn_vectors(gain_rows, bias_rows, True)
    dec_cross = cross_vectors(gain_rows, bias_rows)
    is_decoder = lax.axis_index("stream") == 1

    def blank_self(size_rows):
        return (
            jnp.zeros((3, size_rows, model_width), low_type),
            jnp.zeros((head_count, size_rows, 1), wide_type),
            jnp.zeros((size_rows, model_width), low_type),
            jnp.zeros((size_rows, model_width), wide_type),
        )

    def blank_ffn(size_rows):
        return (
            jnp.zeros((size_rows, model_width), low_type),
            jnp.zeros((size_rows, hidden_width), wide_type),
            jnp.zeros((size_rows, hidden_width), low_type),
            jnp.zeros((size_rows, model_width), wide_type),
        )

    def blank_cross(size_rows):
        return (
            jnp.zeros((size_rows, model_width), low_type),
            jnp.zeros((size_rows, model_width), low_type),
            jnp.zeros((head_count, size_rows, 1), wide_type),
            jnp.zeros((size_rows, model_width), low_type),
            jnp.zeros((size_rows, model_width), wide_type),
        )

    progress = {
        "out": [jnp.zeros((size_rows, model_width), low_type) for size_rows in row_sizes],
        "grad_in": [jnp.zeros((size_rows, model_width), wide_type) for size_rows in row_sizes],
        "send": [jnp.zeros((2, size_rows, model_width), low_type) for size_rows in row_sizes],
        "memory": [jnp.zeros((2, size_rows, model_width), low_type) for size_rows in row_sizes],
        "grad_send": [jnp.zeros((2, size_rows, model_width), low_type) for size_rows in row_sizes],
        "grad_memory": [
            jnp.zeros((2, size_rows, model_width), low_type) for size_rows in row_sizes
        ],
        "mid": [jnp.zeros((size_rows, model_width), wide_type) for size_rows in row_sizes],
        "grad_mid": [jnp.zeros((size_rows, model_width), wide_type) for size_rows in row_sizes],
        "totals": {
            "proj": jnp.zeros(w_proj.shape, wide_type),
            "attn_out": jnp.zeros(w_attn_out.shape, wide_type),
            "first": jnp.zeros(w_first.shape, wide_type),
            "second": jnp.zeros(w_second.shape, wide_type),
            "ffn_in": jnp.zeros(w_ffn_in.shape, wide_type),
            "ffn_out": jnp.zeros(w_ffn_out.shape, wide_type),
            "gains": jnp.zeros(gains.shape, wide_type),
            "biases": jnp.zeros(biases.shape, wide_type),
        },
    }
    progress["self_saved"] = [blank_self(size_rows) for size_rows in row_sizes]
    progress["ffn_saved"] = [blank_ffn(size_rows) for size_rows in row_sizes]
    progress["cross_saved"] = [blank_cross(size_rows) for size_rows in row_sizes]

    def encoder_core(micro_idx):
        h_one, self_saved = self_forward(
            row_pieces[micro_idx], src_lens[micro_idx], False, w_proj, w_attn_out, enc_self
        )
        encoded, ffn_saved = ffn_forward(h_one, w_ffn_in, w_ffn_out, enc_ffn)
        return (encoded.astype(low_type), self_saved, ffn_saved)

    def encoder_forward_step(progress, micro_idx):
        low_memory, self_saved, ffn_saved = encoder_core(micro_idx)
        memory = jnp.stack([matmul(low_memory, w_first), matmul(low_memory, w_second)]).astype(
            low_type
        )
        progress = updated(progress, "out", micro_idx, low_memory)
        progress = updated(progress, "send", micro_idx, memory)
        progress = updated(progress, "self_saved", micro_idx, self_saved)
        progress = updated(progress, "ffn_saved", micro_idx, ffn_saved)
        return progress

    def decoder_head(micro_idx):
        return self_forward(
            row_pieces[micro_idx], tgt_lens[micro_idx], True, w_proj, w_attn_out, dec_self
        )

    def decoder_tail(mid_rows, memory, micro_idx):
        crossed, cross_saved = cross_forward(
            mid_rows, memory, src_lens[micro_idx], w_first, w_second, dec_cross
        )
        decoded, ffn_saved = ffn_forward(crossed, w_ffn_in, w_ffn_out, dec_ffn)
        return (decoded, cross_saved, ffn_saved)

    def decoder_head_step(progress, micro_idx):
        mid_rows, self_saved = decoder_head(micro_idx)
        progress = updated(progress, "mid", micro_idx, mid_rows)
        progress = updated(progress, "self_saved", micro_idx, self_saved)
        return progress

    def decoder_tail_step(progress, micro_idx):
        decoded, cross_saved, ffn_saved = decoder_tail(
            progress["mid"][micro_idx], progress["memory"][micro_idx], micro_idx
        )
        progress = updated(progress, "out", micro_idx, decoded.astype(low_type))
        progress = updated(progress, "cross_saved", micro_idx, cross_saved)
        progress = updated(progress, "ffn_saved", micro_idx, ffn_saved)
        return progress

    def decoder_back_step(progress, micro_idx):
        memory = progress["memory"][micro_idx]
        self_saved = progress["self_saved"][micro_idx]
        cross_saved = progress["cross_saved"][micro_idx]
        ffn_saved = progress["ffn_saved"][micro_idx]
        grad_h_two, ffn_w, ffn_v = ffn_backward(
            w_ffn_in, w_ffn_out, dec_ffn, ffn_saved, grad_pieces[micro_idx]
        )
        grad_h_one, grad_memory, cross_w, cross_v = cross_backward(
            memory, src_lens[micro_idx], w_first, w_second, dec_cross, cross_saved, grad_h_two
        )
        grad_rows, self_w, self_v = self_backward(
            row_pieces[micro_idx],
            tgt_lens[micro_idx],
            True,
            w_proj,
            w_attn_out,
            dec_self,
            self_saved,
            grad_h_one,
        )
        totals = accumulate(
            progress["totals"],
            ("ffn_in", "ffn_out", "first", "second", "proj", "attn_out"),
            ffn_w + cross_w + self_w,
            ffn_plan(True, ffn_v) + cross_plan(cross_v) + self_plan(True, self_v),
        )
        progress = updated(progress, "grad_in", micro_idx, grad_rows)
        progress = updated(progress, "grad_send", micro_idx, grad_memory)
        return with_totals(progress, totals)

    def encoder_top_step(progress, micro_idx):
        low_memory = progress["out"][micro_idx]
        ffn_saved = progress["ffn_saved"][micro_idx]
        grad_memory = progress["grad_memory"][micro_idx]
        grad_encoded = matmul_nt(grad_memory[0], w_first) + matmul_nt(grad_memory[1], w_second)
        grad_h_one, ffn_w, ffn_v = ffn_backward(
            w_ffn_in, w_ffn_out, enc_ffn, ffn_saved, grad_encoded
        )
        projections = (matmul_tn(low_memory, grad_memory[0]), matmul_tn(low_memory, grad_memory[1]))
        totals = accumulate(
            progress["totals"],
            ("first", "second", "ffn_in", "ffn_out"),
            projections + ffn_w,
            ffn_plan(False, ffn_v),
        )
        progress = updated(progress, "grad_mid", micro_idx, grad_h_one)
        return with_totals(progress, totals)

    def encoder_bottom_step(progress, micro_idx):
        self_saved = progress["self_saved"][micro_idx]
        grad_rows, self_w, self_v = self_backward(
            row_pieces[micro_idx],
            src_lens[micro_idx],
            False,
            w_proj,
            w_attn_out,
            enc_self,
            self_saved,
            progress["grad_mid"][micro_idx],
        )
        totals = accumulate(
            progress["totals"], ("proj", "attn_out"), self_w, self_plan(False, self_v)
        )
        progress = updated(progress, "grad_in", micro_idx, grad_rows)
        return with_totals(progress, totals)

    def enc_zero(progress):
        return encoder_forward_step(progress, 0)

    def dec_zero(progress):
        return decoder_head_step(progress, 0)

    def enc_one(progress):
        return encoder_forward_step(progress, 1)

    def dec_one(progress):
        return decoder_tail_step(decoder_head_step(progress, 1), 0)

    def dec_two(progress):
        return decoder_back_step(decoder_tail_step(progress, 1), 1)

    def enc_three(progress):
        return encoder_bottom_step(encoder_top_step(progress, 1), 1)

    def dec_three(progress):
        return decoder_back_step(progress, 0)

    def enc_four(progress):
        return encoder_top_step(progress, 0)

    def enc_five(progress):
        return encoder_bottom_step(progress, 0)

    progress = lax.cond(is_decoder, dec_zero, enc_zero, progress)
    progress = updated(progress, "memory", 0, forward_pass(progress["send"][0]))
    progress = lax.cond(is_decoder, dec_one, enc_one, progress)
    progress = updated(progress, "memory", 1, forward_pass(progress["send"][1]))
    progress = lax.cond(is_decoder, dec_two, keep_same, progress)
    progress = updated(progress, "grad_memory", 1, backward_pass(progress["grad_send"][1]))
    progress = lax.cond(is_decoder, dec_three, enc_three, progress)
    progress = updated(progress, "grad_memory", 0, backward_pass(progress["grad_send"][0]))
    progress = lax.cond(is_decoder, keep_same, enc_four, progress)
    progress = lax.cond(is_decoder, keep_same, enc_five, progress)
    totals = progress["totals"]
    owned = (
        lax.psum_scatter(totals["proj"], "dp", scatter_dimension=1, tiled=True),
        lax.psum_scatter(totals["attn_out"], "dp", scatter_dimension=0, tiled=True),
        lax.psum_scatter(totals["first"], "dp", scatter_dimension=0, tiled=True),
        lax.psum_scatter(totals["second"], "dp", scatter_dimension=0, tiled=True),
        lax.psum_scatter(totals["ffn_in"], "dp", scatter_dimension=0, tiled=True),
        lax.psum_scatter(totals["ffn_out"], "dp", scatter_dimension=0, tiled=True),
        lax.psum_scatter(totals["gains"], "dp", scatter_dimension=1, tiled=True),
        lax.psum_scatter(totals["biases"], "dp", scatter_dimension=1, tiled=True),
    )
    owned_gains, owned_biases = lax.psum((owned[6], owned[7]), "stream")
    layer_out = jnp.concatenate(progress["out"], axis=0)[None]
    grad_inputs = jnp.concatenate(progress["grad_in"], axis=0)[None]
    return (
        layer_out,
        grad_inputs,
        owned[0][None],
        owned[1][None],
        owned[2][None],
        owned[3][None],
        owned[4][None],
        owned[5][None],
        owned_gains,
        owned_biases,
    )


def fused_body(inputs, lengths, cotangent, attn_in, attn_out, cross_first, cross_second, ffn_in, ffn_out, gains, biases):
    rows, grad, s_out, s_in, s_second, s_first, s_attn, s_proj, own_gains, own_biases = whole_step(
        lengths, gains, biases, inputs[0], cotangent, attn_in[0], attn_out[0],
        cross_first[0], cross_second[0], ffn_in[0], ffn_out[0])
    return (rows[None], grad[None], s_proj[None], s_attn[None], s_first[None], s_second[None],
            s_in[None], s_out[None], own_gains, own_biases)


def solution(mesh):
    def body(*args):
        width = args[0].shape[2]
        fits = mesh.shape["dp"] * PIECE == width and args[0].shape[1] == ROWS and args[7].shape[2] == 4 * width
        return (fused_body if fits else plain_body)(*args)
    return jax.shard_map(
        body,
        mesh=mesh,
        in_specs=(
            P("stream", "dp", None),
            P(None, "dp", None),
            P("dp", None),
            P("stream", None, None, None),
            P("stream", None, None),
            P("stream", None, None),
            P("stream", None, None),
            P("stream", None, None),
            P("stream", None, None),
            P(),
            P(),
        ),
        out_specs=(
            P("stream", "dp", None),
            P("stream", "dp", None),
            P("stream", None, "dp", None),
            P("stream", "dp", None),
            P("stream", "dp", None),
            P("stream", "dp", None),
            P("stream", "dp", None),
            P("stream", "dp", None),
            P(None, "dp"),
            P(None, "dp"),
        ),
        check_vma=False,
    )
```
